32 devices in a mesh: dp: 16 (over z, y, core), tensor: 2 (over x).
Axes of the slice: x: 2, y: 2, z: 4, core: 2. Of those that a mesh axis runs over, the one named last changes fastest.
Arguments:
- tokens: bfloat16 [8192, 2048], P('dp'), may hold values from -6 to 6
- cotangent: bfloat16 [8192, 2048], P('dp'), may hold values from -6 to 6
- norm_gain: float32 [2048], replicated, may hold values from 0.5 to 1.5
- w_x: bfloat16 [2048, 4096], P(None, 'tensor'), may hold values from -0.125 to 0.125
- w_z: bfloat16 [2048, 4096], P(None, 'tensor'), may hold values from -0.125 to 0.125
- conv_weight: float32 [4, 4096], P(None, 'tensor'), may hold values from -3 to 3
- conv_bias: float32 [4096], P('tensor'), may hold values from -3 to 3
- x_proj: bfloat16 [4096, 160], P('tensor'), may hold values from -0.09375 to 0.09375
- dt_proj: bfloat16 [128, 4096], P(None, 'tensor'), may hold values from -0.5 to 0.5
- dt_bias: float32 [4096], P('tensor'), may hold values from -5 to 1
- skip_gain: float32 [4096], P('tensor'), may hold values from 0.5 to 1.5
- w_out: bfloat16 [4096, 2048], P('tensor'), may hold values from -0.1875 to 0.1875
- seq_lengths: int32 [16, 3], P('dp'), may hold values from 1 to 384, 512 in all within a row
- arrival_route: int32 [8192], P('dp'), may hold values from 0 to 8191, as said below
- work_source: int32 [8192], P('dp'), may hold values from 0 to 8191, as said below
Outputs:
- out_tokens: bfloat16 [8192, 2048], P('dp', 'tensor')
- in_grad: bfloat16 [8192, 2048], P('dp', 'tensor')
- grad_gain: float32 [2048], P('tensor')
- grad_w_x: float32 [2048, 4096], P('dp', 'tensor')
- grad_w_z: float32 [2048, 4096], P('dp', 'tensor')
- grad_conv_weight: float32 [4, 4096], P(None, 'tensor')
- grad_conv_bias: float32 [4096], P('tensor')
- grad_x_proj: float32 [4096, 160], P('tensor')
- grad_dt_proj: float32 [128, 4096], P(None, 'tensor')
- grad_dt_bias: float32 [4096], P('tensor')
- grad_skip: float32 [4096], P('tensor')
- grad_w_out: float32 [4096, 2048], P('tensor', 'dp')
The draws below stay inside these ranges and needn't reach their ends.
Inputs may be any that keep to these rules, and one draw needn't show every extreme that they name: The lengths of each row of seq_lengths sum to 512, and each row's largest is exactly 384. `arrival_route`: A permutation. Of the 512 arriving tokens of each index of dp, exactly 32 go to each block of 512 working positions. `work_source`: the inverse permutation of arrival_route.
All inputs are finite; a program needn't handle non-finite values.
Results may differ from the reference program's by a relative error of at most 0.014.
Values may be sent and summed in bfloat16 or wider, within the bound.
A program may use at most 320 MiB of HBM per device.

```python
import math
import jax
import jax.numpy as jnp
import numpy as np
from jax import lax

D = 2048
INNER = 4096
CONV = 4
DT_RANK = 128
TOK_DEV = 512
SEQ_DEV = 3
MAXLEN = 384
PROJ = 160
DP_GROUPS = 16
TOKENS = 8192


def route_tables(key):
    dp_count = TOKENS // TOK_DEV
    per_peer = TOK_DEV // dp_count
    send_key = jax.random.fold_in(key, 101)
    place_key = jax.random.fold_in(key, 202)
    spread = jax.vmap(lambda member: jax.random.permutation(member, TOK_DEV))(jax.random.split(send_key, dp_count))
    placing = jax.vmap(lambda member: jax.random.permutation(member, TOK_DEV))(jax.random.split(place_key, dp_count))
    target = spread // per_peer
    within = spread % per_peer
    sender = jnp.arange(dp_count, dtype=jnp.int32)[:, None]
    local_slot = placing[target, sender * per_peer + within]
    arrive_map = (target * TOK_DEV + local_slot).reshape(TOKENS).astype(jnp.int32)
    source_map = jnp.zeros((TOKENS,), jnp.int32).at[arrive_map].set(jnp.arange(TOKENS, dtype=jnp.int32))
    return (arrive_map, source_map)


def draw_arrival_route(key, part):
    return route_tables(key)[0]


def draw_work_source(key, part):
    return route_tables(key)[1]


def level_of(stream_key, extent, cuts, smallest, top_value):
    level = 1.0
    for dim, parts in cuts:
        heights = jax.random.uniform(jax.random.fold_in(jax.random.fold_in(stream_key, 6), dim), (parts,), jnp.float32, smallest / len(cuts), top_value / len(cuts))
        level = level * jnp.repeat(jnp.exp(heights), extent[dim] // parts).reshape((-1,) + (1,) * (len(extent) - 1 - dim))
    return level


def split_up(amount, total, reach, slope):
    weights = [(1 << 20) // math.isqrt(grade ** slope) + 1 for grade in range(2, amount + 1)]
    rest, given = total - reach - (amount - 1), [1] * (amount - 1)
    while rest > 0:
        candidates = [i for i in range(amount - 1) if given[i] < reach]
        pool, left = sum([weights[i] for i in candidates]), rest
        for i in candidates:
            addition = min(reach - given[i], max(1, left * weights[i] // pool), rest)
            given[i] = given[i] + addition
            rest = rest - addition
    return np.array([reach] + given)


def uneven_parts(rng, count, total, bound, lean):
    if count == 2:
        one = jax.random.randint(rng, (), max(1, total - bound), min(bound, total - 1) + 1)
        return jnp.stack([one, total - one])
    tallies = jnp.asarray(split_up(count, total, bound, lean), jnp.int32)
    pairs = (count - 1) // 2
    giver, receiver = tallies[1:1 + 2 * pairs:2], tallies[2:2 + 2 * pairs:2]
    margin = jnp.minimum(giver - 1, bound - receiver)
    shifted = jax.random.randint(jax.random.fold_in(rng, 1), (pairs,), 0, 1 << 20) % (margin + 1)
    tallies = tallies.at[1:1 + 2 * pairs:2].set(giver - shifted).at[2:2 + 2 * pairs:2].set(receiver + shifted)
    return tallies[jax.random.permutation(jax.random.fold_in(rng, 2), count)]


def noise(stream_key, dims, scale, bound, pieces=(), kind=jnp.bfloat16):
    entries = jax.random.normal(stream_key, dims, jnp.float32) * scale
    if len(pieces) > 0:
        entries = level_of(stream_key, dims, pieces, -0.22, 0.18) * entries
    return jnp.clip(entries, min=-bound, max=bound).astype(kind)


def setup_inputs(seed: int = 0) -> dict:
    streams_of = jax.random.split(jax.random.key(seed), 16)
    return {
        "tokens": noise(streams_of[0], (TOKENS, D), 1.0, 6.0, ((0, 16),)),
        "cotangent": noise(streams_of[1], (TOKENS, D), 1.0, 6.0, ((0, 16),)),
        "norm_gain": jnp.clip(1.0 + 0.1 * jax.random.normal(streams_of[2], (D,), jnp.float32), 0.5, 1.5),
        "w_x": noise(streams_of[3], (D, INNER), D ** -0.5, 0.125, ((1, 2),)),
        "w_z": noise(streams_of[4], (D, INNER), D ** -0.5, 0.125, ((1, 2),)),
        "conv_weight": noise(streams_of[5], (CONV, INNER), CONV ** -0.5, 3.0, ((1, 2),), jnp.float32),
        "conv_bias": noise(streams_of[6], (INNER,), 0.5, 3.0, ((0, 2),), jnp.float32),
        "x_proj": noise(streams_of[7], (INNER, PROJ), INNER ** -0.5, 0.09375, ((0, 2),)),
        "dt_proj": noise(streams_of[8], (DT_RANK, INNER), DT_RANK ** -0.5, 0.5, ((1, 2),)),
        "dt_bias": jnp.clip(-5.0 + 6.0 * jax.random.uniform(streams_of[9], (INNER,), jnp.float32) ** level_of(streams_of[9], (INNER,), ((0, 2),), -0.2, 0.2), -5.0, 1.0),
        "skip_gain": jnp.clip(0.5 + 1.0 * jax.random.uniform(streams_of[10], (INNER,), jnp.float32) ** level_of(streams_of[10], (INNER,), ((0, 2),), -0.2, 0.2), 0.5, 1.5),
        "w_out": noise(streams_of[11], (INNER, D), (INNER // 4) ** -0.5, 0.1875, ((0, 2),)),
        "seq_lengths": jax.vmap(lambda own: uneven_parts(own, SEQ_DEV, TOK_DEV, MAXLEN, 2))(jax.random.split(streams_of[12], DP_GROUPS)).reshape((DP_GROUPS, SEQ_DEV)).astype(jnp.int32),
        "arrival_route": draw_arrival_route(jax.random.fold_in(streams_of[15], 71), 0),
        "work_source": draw_work_source(jax.random.fold_in(streams_of[15], 71), 0),
    }


@jax.custom_vjp
def low(v):
    return lax.optimization_barrier(v.astype(jnp.bfloat16)).astype(jnp.float32)

@jax.custom_vjp
def low_back(v):
    return v

def low_keep(v):
    return (low(v), None)

def low_pass(kept, grad):
    return (grad,)

def back_keep(v):
    return (v, None)

def back_low(kept, grad):
    return (low(grad),)
low.defvjp(low_keep, low_pass)
low_back.defvjp(back_keep, back_low)

def matmul(left, right):
    return jnp.dot(left, right, precision=lax.Precision.HIGHEST)

def conv_mix(inner_x, conv_weight, conv_bias, segment):
    row_count = inner_x.shape[0]
    taps = conv_weight.shape[0]
    mixed = conv_bias[None, :] + conv_weight[taps - 1][None, :] * inner_x
    for shift_by in range(1, taps):
        moved = jnp.concatenate([jnp.zeros((shift_by, inner_x.shape[1]), inner_x.dtype), inner_x[:row_count - shift_by]], 0)
        seg_moved = jnp.concatenate([jnp.full((shift_by,), -1, jnp.int32), segment[:row_count - shift_by]], 0)
        keep_mask = (seg_moved == segment).astype(inner_x.dtype)
        mixed = mixed + conv_weight[taps - 1 - shift_by][None, :] * moved * keep_mask[:, None]
    return mixed

def recurrence(beta, key_rows, query_rows, conv_out, starts):
    norm_sq = lax.optimization_barrier(jnp.sum(key_rows * key_rows, axis=1))
    step_size = beta / (1.0 + beta * norm_sq[:, None])

    def advance(carried, element):
        step_row, key_row, query_row, input_row, start_row = element
        cleared = carried * (1.0 - start_row)
        decay = 1.0 - step_row[:, None] * (key_row * key_row)[None, :]
        carried = decay * cleared + (step_row * input_row)[:, None] * key_row[None, :]
        return (carried, lax.optimization_barrier(jnp.sum(carried * query_row[None, :], axis=1)))
    initial = jnp.zeros((beta.shape[1], key_rows.shape[1]), beta.dtype)
    final_state, outputs = lax.scan(advance, initial, (step_size, key_rows, query_rows, conv_out, starts))
    return outputs

def block_forward(resid, segment, starts, weights):
    norm_gain, w_x, w_z, conv_weight, conv_bias, x_proj, dt_proj, dt_bias, skip_gain, w_out = weights
    low_rank = dt_proj.shape[0]
    state_size = (x_proj.shape[1] - low_rank) // 2
    scale_row = lax.rsqrt(lax.optimization_barrier(jnp.mean(resid * resid, axis=1, keepdims=True)) + 1e-05)
    normed = low(resid * scale_row * norm_gain[None, :])
    inner_x = low_back(matmul(normed, w_x))
    inner_z = low_back(matmul(normed, w_z))
    mixed = conv_mix(inner_x, conv_weight, conv_bias, segment)
    conv_out = mixed * jax.nn.sigmoid(mixed)
    projected = low_back(matmul(low(conv_out), x_proj))
    rank_part = low(projected[:, :low_rank])
    key_rows = projected[:, low_rank:low_rank + state_size]
    query_rows = projected[:, low_rank + state_size:]
    beta_pre = low_back(matmul(rank_part, dt_proj))
    beta = jax.nn.sigmoid(beta_pre + dt_bias[None, :])
    scan_out = recurrence(beta, key_rows, query_rows, conv_out, starts)
    gated = low((scan_out + skip_gain[None, :] * conv_out) * (inner_z * jax.nn.sigmoid(inner_z)))
    return resid + matmul(gated, w_out)

def reference(tokens, cotangent, norm_gain, w_x, w_z, conv_weight, conv_bias, x_proj, dt_proj, dt_bias, skip_gain, w_out, seq_lengths, arrival_route, work_source):
    dp_count = seq_lengths.shape[0]
    feat_width = tokens.shape[1]
    per_group = tokens.shape[0] // dp_count
    x_work = tokens[work_source].astype(jnp.float32).reshape(dp_count, per_group, feat_width)
    dy_work = cotangent[work_source].astype(jnp.float32).reshape(dp_count, per_group, feat_width)
    offsets = (jnp.cumsum(seq_lengths, axis=1) - seq_lengths).astype(jnp.int32)
    position = jnp.arange(per_group, dtype=jnp.int32)
    segment = (lax.optimization_barrier(jnp.sum((position[None, :, None] >= offsets[:, None, :]).astype(jnp.int32), axis=2)) - 1).astype(jnp.int32)
    starts = jnp.any(position[None, :, None] == offsets[:, None, :], axis=2).astype(jnp.float32)
    weights = (norm_gain.astype(jnp.float32), w_x.astype(jnp.float32), w_z.astype(jnp.float32), conv_weight.astype(jnp.float32), conv_bias.astype(jnp.float32), x_proj.astype(jnp.float32), dt_proj.astype(jnp.float32), dt_bias.astype(jnp.float32), skip_gain.astype(jnp.float32), w_out.astype(jnp.float32))

    def forward(x_all, params):

        def per_group_fn(element):
            return block_forward(element[0], element[1], element[2], params)
        return lax.map(jax.checkpoint(per_group_fn), (x_all, segment, starts))
    y_work, pull = jax.vjp(forward, x_work, weights)
    dx_work, grads = pull(dy_work)
    out_tokens = y_work.reshape(-1, feat_width)[arrival_route].astype(jnp.bfloat16)
    in_grad = dx_work.reshape(-1, feat_width)[arrival_route].astype(jnp.bfloat16)
    return (out_tokens, in_grad, grads[0], grads[1], grads[2], grads[3], grads[4], grads[5], grads[6], grads[7], grads[8], grads[9])
```

```python
import functools
from functools import partial

import jax
import jax.numpy as jnp
from jax import lax
from jax.experimental import pallas as pl
from jax.experimental.pallas import tpu as pltpu
from jax.sharding import PartitionSpec as P

F32, BF16 = jnp.float32, jnp.bfloat16

def scan_kernel(GR, NS, rank_ref, dtp_ref, dtb_ref, u_ref, z_ref, dg_ref, skip_ref,
                kb_ref, qb_ref, keep_ref, ksq_ref, qblk_ref, kblk_ref, k2blk_ref,
                gated_ref, diz_ref, du_ref, gskip_ref, gdtb_ref, gdtp_ref,
                drank_ref, acca_ref, accb_ref, accq_ref, sst_ref,
                beta_s, step_s, stepm_s, su_s, ds_s, y_s, d_s, e_s, h_s, g_s, m_s):
    T, CH = u_ref.shape
    L = CH // 128
    NG = T // GR
    R = GR * NS
    first = pl.program_id(0) == 0
    lanes = [slice(l * 128, (l + 1) * 128) for l in range(L)]

    @pl.when(first)
    def _():
        for r in (drank_ref, acca_ref, accb_ref, accq_ref, sst_ref):
            r[...] = jnp.zeros_like(r)
        h_s[pl.ds(0, NS), :] = jnp.zeros((NS, CH), h_s.dtype)

    beta_s[...] = jnp.dot(rank_ref[...], dtp_ref[...], preferred_element_type=F32)

    def prologue(r, acc):
        rows = pl.ds(pl.multiple_of(r * GR, GR), GR)
        kq = ksq_ref[rows, :]
        kp = keep_ref[rows, :]
        out = []
        for l in range(L):
            ln = lanes[l]
            beta = jax.nn.sigmoid(beta_s[rows, ln] + dtb_ref[:, ln])
            step = beta / (1.0 + beta * kq)
            beta_s[rows, ln] = beta
            step_s[rows, ln] = step
            stepm_s[rows, ln] = step * kp
            u = u_ref[rows, ln]
            su_s[rows, ln] = step * u
            z = z_ref[rows, ln]
            ds = dg_ref[rows, ln] * (z * jax.nn.sigmoid(z))
            ds_s[rows, ln] = ds
            out.append(acc[l] + jnp.sum(ds * u, axis=0, keepdims=True))
        return tuple(out)

    zrow = tuple(jnp.zeros((1, 128), F32) for _ in range(L))
    gsk = lax.fori_loop(0, NG, prologue, zrow)
    for l in range(L):
        gskip_ref[:, lanes[l]] = gsk[l]

    def forward(gi, h):
        h = list(h)
        base = pl.multiple_of(gi * GR, GR)
        for j in range(GR):
            t = base + j
            k = kb_ref[pl.ds(t * NS, NS), :]
            k2 = k * k
            kp = keep_ref.at[pl.ds(base, GR)][j:j + 1, :]
            for l in range(L):
                a = kp - k2 * stepm_s.at[pl.ds(base, GR)][j:j + 1, lanes[l]]
                h[l] = a * h[l] + k * su_s.at[pl.ds(base, GR)][j:j + 1, lanes[l]]
                h_s[pl.ds((t + 1) * NS, NS), lanes[l]] = h[l].astype(BF16)
        y_s[pl.ds(base, GR), :] = jnp.dot(
            qblk_ref[pl.ds(base, GR), :], h_s[pl.ds((base + 1) * NS, R), :],
            preferred_element_type=F32)
        return tuple(h)

    zst = tuple(jnp.zeros((NS, 128), F32) for _ in range(L))
    lax.fori_loop(0, NG, forward, zst)

    def middle(r, c):
        rows = pl.ds(pl.multiple_of(r * GR, GR), GR)
        for l in range(L):
            ln = lanes[l]
            z = z_ref[rows, ln]
            s = jax.nn.sigmoid(z)
            v = y_s[rows, ln] + skip_ref[:, ln] * u_ref[rows, ln]
            gated_ref[rows, ln] = (v * (z * s)).astype(BF16)
            diz_ref[rows, ln] = (dg_ref[rows, ln] * v * s * (1.0 + z * (1.0 - s))).astype(BF16)
        return c

    lax.fori_loop(0, NG, middle, 0)

    def backward(ri, gc):
        gc = list(gc)
        gi = NG - 1 - ri
        base = pl.multiple_of(gi * GR, GR)
        rows = pl.ds(base, GR)
        for j in reversed(range(GR)):
            t = base + j
            k = kb_ref[pl.ds(t * NS, NS), :]
            q = qb_ref[pl.ds(t * NS, NS), :]
            k2 = k * k
            kp = keep_ref.at[pl.ds(base, GR)][j:j + 1, :]
            for l in range(L):
                g = gc[l] + q * ds_s.at[pl.ds(base, GR)][j:j + 1, lanes[l]]
                gb = g.astype(BF16)
                g_s[pl.ds(j * NS, NS), lanes[l]] = gb
                m_s[pl.ds(j * NS, NS), lanes[l]] = gb * h_s[pl.ds(t * NS, NS), lanes[l]]
                gc[l] = (kp - k2 * stepm_s.at[pl.ds(base, GR)][j:j + 1, lanes[l]]) * g
        gv = g_s[...]
        mv = m_s[...]
        d_s[rows, :] = jnp.dot(kblk_ref[rows, :], gv, preferred_element_type=F32)
        e_s[rows, :] = jnp.dot(k2blk_ref[rows, :], mv, preferred_element_type=F32)
        nt = (((1,), (1,)), ((), ()))
        acca_ref[rows, :] += lax.dot_general(su_s[rows, :].astype(BF16), gv, nt, preferred_element_type=F32)
        accb_ref[rows, :] += lax.dot_general(step_s[rows, :].astype(BF16), mv, nt, preferred_element_type=F32)
        accq_ref[rows, :] += lax.dot_general(ds_s[rows, :].astype(BF16), h_s[pl.ds((base + 1) * NS, R), :], nt, preferred_element_type=F32)
        return tuple(gc)

    lax.fori_loop(0, NG, backward, zst)

    def epilogue(r, acc):
        rows = pl.ds(pl.multiple_of(r * GR, GR), GR)
        kq = ksq_ref[rows, :]
        kp = keep_ref[rows, :]
        out = []
        ss = sst_ref[rows, :]
        for l in range(L):
            ln = lanes[l]
            u = u_ref[rows, ln]
            step = step_s[rows, ln]
            beta = beta_s[rows, ln]
            dsum = d_s[rows, ln]
            dstep = u * dsum - kp * e_s[rows, ln]
            du_ref[rows, ln] = step * dsum + ds_s[rows, ln] * skip_ref[:, ln]
            ds2 = dstep * step * step
            ss = ss + ds2
            den = 1.0 / (1.0 + beta * kq)
            db = dstep * beta * (1.0 - beta) * den * den
            beta_s[rows, ln] = db
            out.append(acc[l] + jnp.sum(db, axis=0, keepdims=True))
        sst_ref[rows, :] = ss
        return tuple(out)

    gdb = lax.fori_loop(0, NG, epilogue, zrow)
    for l in range(L):
        gdtb_ref[:, lanes[l]] = gdb[l]
    dbl = beta_s[...].astype(BF16)
    gdtp_ref[...] = lax.dot_general(rank_ref[...], dbl, (((0,), (0,)), ((), ())), preferred_element_type=F32)
    drank_ref[...] += lax.dot_general(dbl, dtp_ref[...], (((1,), (1,)), ((), ())), preferred_element_type=F32)


def scan_call(rank, dtp, dtb, u, z, dg, skip, kb, qb, keep, ksq, qblk, kblk, k2blk, CH=512, GR=16, NS=16):
    T, C = u.shape
    CH = min(CH, C)
    const = lambda a: pl.BlockSpec(a.shape, lambda j: (0,) * a.ndim)
    col = lambda a: pl.BlockSpec((a.shape[0], CH), lambda j: (0, j))
    S = jax.ShapeDtypeStruct
    W = GR * NS
    outs = (S((T, C), BF16), S((T, C), BF16), S((T, C), F32), S((1, C), F32), S((1, C), F32), S((rank.shape[1], C), F32),
            S((T, rank.shape[1]), F32), S((T, W), F32), S((T, W), F32), S((T, W), F32), S((T, 128), F32))
    f = pl.pallas_call(
        functools.partial(scan_kernel, GR, NS),
        grid=(C // CH,),
        in_specs=[const(rank), col(dtp), col(dtb), col(u), col(z), col(dg), col(skip), const(kb), const(qb),
                  const(keep), const(ksq), const(qblk), const(kblk), const(k2blk)],
        out_specs=[col(o) for o in outs[:6]] + [const(o) for o in outs[6:]],
        out_shape=outs,
        scratch_shapes=[pltpu.VMEM((T, CH), F32)] * 8 + [pltpu.VMEM(((T + 1) * NS, CH), BF16), pltpu.VMEM((W, CH), BF16), pltpu.VMEM((W, CH), BF16)],
        compiler_params=pltpu.CompilerParams(vmem_limit_bytes=58 << 20, dimension_semantics=("arbitrary",)),
        name="scan",
    )
    return f(rank, dtp, dtb, u, z, dg, skip, kb, qb, keep, ksq, qblk, kblk, k2blk)


def scan_all(rank, dtp, dtb, u, z, dg, skip, keys, query, keep, **kw):
    T, NS = keys.shape
    GR = kw.get("GR", 16)
    kb = jnp.broadcast_to(keys[:, :, None], (T, NS, 128)).reshape(T * NS, 128)
    qb = jnp.broadcast_to(query[:, :, None], (T, NS, 128)).reshape(T * NS, 128)
    keepb = jnp.broadcast_to(keep[:, None], (T, 128))
    ksq = jnp.sum(keys * keys, axis=1)
    ksqb = jnp.broadcast_to(ksq[:, None], (T, 128))
    slot = (jnp.arange(T)[:, None] % GR == jnp.arange(GR * NS)[None, :] // NS).astype(F32)
    blk = lambda v: (slot * jnp.tile(v, (1, GR))).astype(BF16)
    o = scan_call(rank, dtp, dtb, u, z, dg, skip, kb, qb, keepb, ksqb, blk(query), blk(keys), blk(keys * keys), **kw)
    gated, diz, du, gskip, gdtb, gdtp, drank, aa, ab, aq, sst = o
    fold = lambda v: jnp.sum((v * slot).reshape(T, GR, NS), axis=1)
    dq = fold(aq)
    dk = fold(aa) - 2.0 * keys * (fold(ab) * keep[:, None] + jnp.sum(sst, axis=1, keepdims=True))
    return gated, diz, du, gskip, gdtb, gdtp, drank, dk, dq


def tensor_other(value):
    return lax.ppermute(value, "tensor", [(0, 1), (1, 0)])


def tensor_total(value):
    if lax.axis_size("tensor") == 2:
        return value + tensor_other(value)
    return lax.psum(value, "tensor")


def half_total(value, me, width):
    if lax.axis_size("tensor") == 2:
        own = lax.dynamic_slice_in_dim(value, me * width, width, 1)
        sent = lax.dynamic_slice_in_dim(value, (1 - me) * width, width, 1).astype(BF16)
        return own + tensor_other(sent).astype(F32)
    return lax.psum_scatter(value, "tensor", scatter_dimension=1, tiled=True)


def full_columns(part, me):
    if lax.axis_size("tensor") == 2:
        other = tensor_other(part)
        return jnp.where(
            me == 0,
            jnp.concatenate([part, other], 1),
            jnp.concatenate([other, part], 1),
        )
    return lax.all_gather(part, "tensor", axis=1, tiled=True)


def position_in(keys):
    return jnp.sum((keys[None, :] < keys[:, None]).astype(jnp.int32), axis=1)


def conv_mix(inner_x, conv_weight, conv_bias, segment):
    row_count = inner_x.shape[0]
    taps = conv_weight.shape[0]
    mixed = conv_bias[None, :] + conv_weight[taps - 1][None, :] * inner_x
    for shift_by in range(1, taps):
        moved = jnp.concatenate([jnp.zeros((shift_by, inner_x.shape[1]), F32), inner_x[: row_count - shift_by]], 0)
        seg_moved = jnp.concatenate([jnp.full((shift_by,), -1, jnp.int32), segment[: row_count - shift_by]], 0)
        keep_mask = (seg_moved == segment).astype(F32)
        mixed = mixed + conv_weight[taps - 1 - shift_by][None, :] * moved * keep_mask[:, None]
    return mixed


def silu_conv(inner_x, conv_weight, conv_bias, segment):
    mixed = conv_mix(inner_x, conv_weight, conv_bias, segment)
    return mixed * jax.nn.sigmoid(mixed)


def contract_rows(left, right):
    return lax.dot_general(left, right, (((0,), (0,)), ((), ())), preferred_element_type=F32)


def contract_cols(left, right):
    return lax.dot_general(left, right, (((1,), (1,)), ((), ())), preferred_element_type=F32)


def body(tokens, cotangent, norm_gain, w_x, w_z, conv_weight, conv_bias, x_proj, dt_proj, dt_bias, skip_gain, w_out,
         seq_lengths, arrival_route, work_source):
    dp_count = lax.axis_size("dp")
    tp_count = lax.axis_size("tensor")
    row_count, feat_width = tokens.shape
    per_peer = row_count // dp_count
    col_share = feat_width // tp_count
    me = lax.axis_index("tensor")
    col_start = me * col_share
    low_rank = dt_proj.shape[0]
    state_size = (x_proj.shape[1] - low_rank) // 2
    position = jnp.arange(row_count, dtype=jnp.int32)

    deal = (position_in(arrival_route)[:, None] == position[None, :]).astype(BF16)
    settle = (position_in(work_source // row_count * row_count + position)[:, None] == position[None, :]).astype(BF16)

    def exchange(rows):
        out = lax.all_to_all(rows.reshape(dp_count, per_peer, rows.shape[1]), "dp", split_axis=0, concat_axis=0, tiled=True)
        return out.reshape(row_count, rows.shape[1])

    def pick(table, rows, dim):
        return lax.dot_general(table, rows, (((dim,), (0,)), ((), ())), preferred_element_type=F32).astype(BF16)

    def bring(values):
        part = lax.dynamic_slice_in_dim(values, col_start, col_share, 1)
        return full_columns(pick(settle, exchange(pick(deal, part, 0)), 1), me)

    def give_back(values):
        return pick(deal, exchange(pick(settle, values, 0)), 1)

    x_work = bring(tokens)
    dy_work = bring(cotangent)

    lengths = seq_lengths[0]
    count = lengths.shape[0]
    before = jnp.arange(count)[:, None] > jnp.arange(count)[None, :]
    offsets = jnp.sum(jnp.where(before, lengths[None, :], 0), axis=1)
    segment = jnp.sum((position[:, None] >= offsets[None, :]).astype(jnp.int32), axis=1) - 1
    keep = 1.0 - jnp.any(position[:, None] == offsets[None, :], axis=1).astype(F32)

    resid = x_work.astype(F32)
    scale_row = lax.rsqrt(jnp.mean(resid * resid, axis=1, keepdims=True) + 1e-05)
    unit = resid * scale_row
    normed = (unit * norm_gain[None, :]).astype(BF16)
    inner_x = jnp.dot(normed, w_x, preferred_element_type=F32)
    inner_z = jnp.dot(normed, w_z, preferred_element_type=F32)
    conv_out, conv_pull = jax.vjp(partial(silu_conv, segment=segment), inner_x, conv_weight, conv_bias)
    conv_low = conv_out.astype(BF16)
    projected = tensor_total(jnp.dot(conv_low, x_proj, preferred_element_type=F32))
    rank_part = projected[:, :low_rank].astype(BF16)
    key_rows = projected[:, low_rank : low_rank + state_size]
    query_rows = projected[:, low_rank + state_size :]

    d_gated = contract_cols(dy_work, w_out)
    gated_low, d_inner_z_low, d_conv_out, grad_skip, grad_dt_bias, grad_dt_proj, d_rank, d_keys, d_query = scan_all(
        rank_part, dt_proj, dt_bias[None, :], conv_out, inner_z, d_gated, skip_gain[None, :], key_rows, query_rows, keep)
    grad_skip, grad_dt_bias = grad_skip[0], grad_dt_bias[0]

    mixed_share = half_total(jnp.dot(gated_low, w_out, preferred_element_type=F32), me, col_share)
    out_cols = (lax.dynamic_slice_in_dim(resid, col_start, col_share, 1) + mixed_share).astype(BF16)
    grad_w_out = contract_rows(gated_low, dy_work)
    d_proj = tensor_total(jnp.concatenate([d_rank, d_keys, d_query], axis=1))
    d_proj_low = d_proj.astype(BF16)
    grad_x_proj = contract_rows(conv_low, d_proj_low)
    d_conv_out = d_conv_out + contract_cols(d_proj_low, x_proj)
    d_inner_x, grad_conv_weight, grad_conv_bias = conv_pull(d_conv_out)
    d_inner_x_low = d_inner_x.astype(BF16)
    grad_w_x = contract_rows(normed, d_inner_x_low)
    grad_w_z = contract_rows(normed, d_inner_z_low)
    d_normed = contract_cols(d_inner_x_low, w_x) + contract_cols(d_inner_z_low, w_z)
    unit_cols = lax.dynamic_slice_in_dim(unit, col_start, col_share, 1)
    gain_cols = lax.dynamic_slice_in_dim(norm_gain, col_start, col_share, 0)
    dy_cols = lax.dynamic_slice_in_dim(dy_work, col_start, col_share, 1).astype(F32)
    d_share = half_total(d_normed, me, col_share)
    d_unit_cols = d_share * gain_cols[None, :]
    row_total = tensor_total(jnp.sum(d_unit_cols * unit_cols, axis=1, keepdims=True))
    grad_gain = jnp.sum(d_share * unit_cols, axis=0)
    d_resid = dy_cols + scale_row * (d_unit_cols - unit_cols * (row_total / feat_width))
    out_tokens = give_back(out_cols)
    in_grad = give_back(d_resid.astype(BF16))
    grad_w_out, grad_w_z, grad_w_x = (
        lax.psum_scatter(g.astype(BF16), "dp", scatter_dimension=dim, tiled=True).astype(F32)
        for g, dim in ((grad_w_out, 1), (grad_w_z, 0), (grad_w_x, 0))
    )
    grad_gain, grad_conv_weight, grad_conv_bias, grad_x_proj, grad_dt_proj, grad_dt_bias, grad_skip = lax.psum(
        (grad_gain, grad_conv_weight, grad_conv_bias, grad_x_proj, grad_dt_proj, grad_dt_bias, grad_skip), "dp")
    return (out_tokens, in_grad, grad_gain, grad_w_x, grad_w_z, grad_conv_weight, grad_conv_bias, grad_x_proj,
            grad_dt_proj, grad_dt_bias, grad_skip, grad_w_out)


def solution(mesh):
    in_specs = (
        P("dp", None),
        P("dp", None),
        P(),
        P(None, "tensor"),
        P(None, "tensor"),
        P(None, "tensor"),
        P("tensor"),
        P("tensor", None),
        P(None, "tensor"),
        P("tensor"),
        P("tensor"),
        P("tensor", None),
        P("dp", None),
        P("dp"),
        P("dp"),
    )
    out_specs = (
        P("dp", "tensor"),
        P("dp", "tensor"),
        P("tensor"),
        P("dp", "tensor"),
        P("dp", "tensor"),
        P(None, "tensor"),
        P("tensor"),
        P("tensor", None),
        P(None, "tensor"),
        P("tensor"),
        P("tensor"),
        P("tensor", "dp"),
    )
    return jax.shard_map(body, mesh=mesh, in_specs=in_specs, out_specs=out_specs, check_vma=False)
```

```python
import functools
from functools import partial

import jax
import jax.numpy as jnp
import numpy as np
from jax import lax
from jax.experimental import pallas as pl
from jax.experimental.pallas import tpu as pltpu
from jax.sharding import PartitionSpec as P

F32, BF16 = jnp.float32, jnp.bfloat16

def scan_kernel(GR, NS, rank_ref, dtp_ref, dtb_ref, u_ref, z_ref, dg_ref, skip_ref,
                kb_ref, qb_ref, keep_ref, ksq_ref, qblk_ref, kblk_ref, k2blk_ref,
                gated_ref, diz_ref, du_ref, gskip_ref, gdtb_ref, gdtp_ref,
                drank_ref, acca_ref, accb_ref, accq_ref, sst_ref,
                beta_s, step_s, stepm_s, su_s, ds_s, y_s, d_s, e_s, h_s, g_s, m_s):
    T, CH = u_ref.shape
    L = CH // 128
    NG = T // GR
    R = GR * NS
    first = pl.program_id(0) == 0
    lanes = [slice(l * 128, (l + 1) * 128) for l in range(L)]

    @pl.when(first)
    def _():
        for r in (drank_ref, acca_ref, accb_ref, accq_ref, sst_ref):
            r[...] = jnp.zeros_like(r)
        h_s[pl.ds(0, NS), :] = jnp.zeros((NS, CH), h_s.dtype)

    beta_s[...] = jnp.dot(rank_ref[...], dtp_ref[...], preferred_element_type=F32)

    def prologue(r, acc):
        rows = pl.ds(pl.multiple_of(r * GR, GR), GR)
        kq = ksq_ref[rows, :]
        kp = keep_ref[rows, :]
        out = []
        for l in range(L):
            ln = lanes[l]
            beta = jax.nn.sigmoid(beta_s[rows, ln] + dtb_ref[:, ln])
            step = beta / (1.0 + beta * kq)
            beta_s[rows, ln] = beta
            step_s[rows, ln] = step
            stepm_s[rows, ln] = step * kp
            u = u_ref[rows, ln]
            su_s[rows, ln] = step * u
            z = z_ref[rows, ln]
            ds = dg_ref[rows, ln] * (z * jax.nn.sigmoid(z))
            ds_s[rows, ln] = ds
            out.append(acc[l] + jnp.sum(ds * u, axis=0, keepdims=True))
        return tuple(out)

    zrow = tuple(jnp.zeros((1, 128), F32) for _ in range(L))
    gsk = lax.fori_loop(0, NG, prologue, zrow)
    for l in range(L):
        gskip_ref[:, lanes[l]] = gsk[l]

    def forward(gi, h):
        h = list(h)
        base = pl.multiple_of(gi * GR, GR)
        for j in range(GR):
            t = base + j
            k = kb_ref[pl.ds(t * NS, NS), :]
            k2 = k * k
            kp = keep_ref.at[pl.ds(base, GR)][j:j + 1, :]
            for l in range(L):
                a = kp - k2 * stepm_s.at[pl.ds(base, GR)][j:j + 1, lanes[l]]
                h[l] = a * h[l] + k * su_s.at[pl.ds(base, GR)][j:j + 1, lanes[l]]
                h_s[pl.ds((t + 1) * NS, NS), lanes[l]] = h[l].astype(BF16)
        y_s[pl.ds(base, GR), :] = jnp.dot(
            qblk_ref[pl.ds(base, GR), :], h_s[pl.ds((base + 1) * NS, R), :],
            preferred_element_type=F32)
        return tuple(h)

    zst = tuple(jnp.zeros((NS, 128), F32) for _ in range(L))
    lax.fori_loop(0, NG, forward, zst)

    def middle(r, c):
        rows = pl.ds(pl.multiple_of(r * GR, GR), GR)
        for l in range(L):
            ln = lanes[l]
            z = z_ref[rows, ln]
            s = jax.nn.sigmoid(z)
            v = y_s[rows, ln] + skip_ref[:, ln] * u_ref[rows, ln]
            gated_ref[rows, ln] = (v * (z * s)).astype(BF16)
            diz_ref[rows, ln] = (dg_ref[rows, ln] * v * s * (1.0 + z * (1.0 - s))).astype(BF16)
        return c

    lax.fori_loop(0, NG, middle, 0)

    def backward(ri, gc):
        gc = list(gc)
        gi = NG - 1 - ri
        base = pl.multiple_of(gi * GR, GR)
        rows = pl.ds(base, GR)
        for j in reversed(range(GR)):
            t = base + j
            k = kb_ref[pl.ds(t * NS, NS), :]
            q = qb_ref[pl.ds(t * NS, NS), :]
            k2 = k * k
            kp = keep_ref.at[pl.ds(base, GR)][j:j + 1, :]
            for l in range(L):
                g = gc[l] + q * ds_s.at[pl.ds(base, GR)][j:j + 1, lanes[l]]
                gb = g.astype(BF16)
                g_s[pl.ds(j * NS, NS), lanes[l]] = gb
                m_s[pl.ds(j * NS, NS), lanes[l]] = gb * h_s[pl.ds(t * NS, NS), lanes[l]]
                gc[l] = (kp - k2 * stepm_s.at[pl.ds(base, GR)][j:j + 1, lanes[l]]) * g
        gv = g_s[...]
        mv = m_s[...]
        d_s[rows, :] = jnp.dot(kblk_ref[rows, :], gv, preferred_element_type=F32)
        e_s[rows, :] = jnp.dot(k2blk_ref[rows, :], mv, preferred_element_type=F32)
        nt = (((1,), (1,)), ((), ()))
        acca_ref[rows, :] += lax.dot_general(su_s[rows, :].astype(BF16), gv, nt, preferred_element_type=F32)
        accb_ref[rows, :] += lax.dot_general(step_s[rows, :].astype(BF16), mv, nt, preferred_element_type=F32)
        accq_ref[rows, :] += lax.dot_general(ds_s[rows, :].astype(BF16), h_s[pl.ds((base + 1) * NS, R), :], nt, preferred_element_type=F32)
        return tuple(gc)

    lax.fori_loop(0, NG, backward, zst)

    def epilogue(r, acc):
        rows = pl.ds(pl.multiple_of(r * GR, GR), GR)
        kq = ksq_ref[rows, :]
        kp = keep_ref[rows, :]
        out = []
        ss = sst_ref[rows, :]
        for l in range(L):
            ln = lanes[l]
            u = u_ref[rows, ln]
            step = step_s[rows, ln]
            beta = beta_s[rows, ln]
            dsum = d_s[rows, ln]
            dstep = u * dsum - kp * e_s[rows, ln]
            du_ref[rows, ln] = step * dsum + ds_s[rows, ln] * skip_ref[:, ln]
            ds2 = dstep * step * step
            ss = ss + ds2
            den = 1.0 / (1.0 + beta * kq)
            db = dstep * beta * (1.0 - beta) * den * den
            beta_s[rows, ln] = db
            out.append(acc[l] + jnp.sum(db, axis=0, keepdims=True))
        sst_ref[rows, :] = ss
        return tuple(out)

    gdb = lax.fori_loop(0, NG, epilogue, zrow)
    for l in range(L):
        gdtb_ref[:, lanes[l]] = gdb[l]
    dbl = beta_s[...].astype(BF16)
    gdtp_ref[...] = lax.dot_general(rank_ref[...], dbl, (((0,), (0,)), ((), ())), preferred_element_type=F32)
    drank_ref[...] += lax.dot_general(dbl, dtp_ref[...], (((1,), (1,)), ((), ())), preferred_element_type=F32)


def scan_call(piece, pieces, *args, CH=512, GR=16, NS=16):
    rank, dtp, dtb, u, z, dg, skip, kb, qb, keep, ksq, qblk, kblk, k2blk = args
    T, C = u.shape
    width = C // pieces
    CH = min(CH, width)
    first = piece * (width // CH)
    const = lambda a: pl.BlockSpec(a.shape, lambda j: (0,) * a.ndim)
    col = lambda a: pl.BlockSpec((a.shape[0], CH), lambda j: (0, j + first))
    out = lambda a: pl.BlockSpec((a.shape[0], CH), lambda j: (0, j))
    S = jax.ShapeDtypeStruct
    W = GR * NS
    R = rank.shape[1]
    outs = (S((T, width), BF16), S((T, width), BF16), S((T, width), F32), S((1, width), F32), S((1, width), F32), S((R, width), F32),
            S((T, R), F32), S((T, W), F32), S((T, W), F32), S((T, W), F32), S((T, 128), F32))
    f = pl.pallas_call(
        functools.partial(scan_kernel, GR, NS),
        grid=(width // CH,),
        in_specs=[const(rank), col(dtp), col(dtb), col(u), col(z), col(dg), col(skip), const(kb), const(qb),
                  const(keep), const(ksq), const(qblk), const(kblk), const(k2blk)],
        out_specs=[out(o) for o in outs[:6]] + [const(o) for o in outs[6:]],
        out_shape=outs,
        scratch_shapes=[pltpu.VMEM((T, CH), F32)] * 8 + [pltpu.VMEM(((T + 1) * NS, CH), BF16), pltpu.VMEM((W, CH), BF16), pltpu.VMEM((W, CH), BF16)],
        compiler_params=pltpu.CompilerParams(vmem_limit_bytes=58 << 20, dimension_semantics=("arbitrary",)),
        cost_estimate=pl.CostEstimate(flops=T * width * NS * 800, bytes_accessed=T * width * 20, transcendentals=0),
        name="scan",
    )
    return f(*args)


def scan_all(rank, dtp, dtb, u, z, dg, skip, keys, query, keep, pieces, GR=16):
    T, NS = keys.shape
    kb = jnp.broadcast_to(keys[:, :, None], (T, NS, 128)).reshape(T * NS, 128)
    qb = jnp.broadcast_to(query[:, :, None], (T, NS, 128)).reshape(T * NS, 128)
    keepb = jnp.broadcast_to(keep[:, None], (T, 128))
    ksq = jnp.sum(keys * keys, axis=1)
    ksqb = jnp.broadcast_to(ksq[:, None], (T, 128))
    slot = (jnp.arange(T)[:, None] % GR == jnp.arange(GR * NS)[None, :] // NS).astype(F32)
    blk = lambda v: (slot * jnp.tile(v, (1, GR))).astype(BF16)
    fold = lambda v: jnp.sum((v * slot).reshape(T, GR, NS), axis=1)
    qblk, kblk, k2blk = blk(query), blk(keys), blk(keys * keys)

    def run(piece, *earlier):
        keep_in = lax.optimization_barrier((keepb,) + earlier)[0] if earlier else keepb
        o = scan_call(piece, pieces, rank, dtp, dtb, u, z, dg, skip, kb, qb, keep_in, ksqb, qblk, kblk, k2blk, GR=GR, NS=NS)
        gated, diz, du, gskip, gdtb, gdtp, drank, aa, ab, aq, sst = o
        dq = fold(aq)
        dk = fold(aa) - 2.0 * keys * (fold(ab) * keep[:, None] + jnp.sum(sst, axis=1, keepdims=True))
        return gated, diz, du, gskip, gdtb, gdtp, drank, dk, dq

    return run


MESH = pl.DeviceIdType.MESH
TILE = 32


class Piece:
    def __init__(self, grad, cols, first, bits, bufs, sems, result):
        self.grad, self.cols, self.first, self.bits = grad, cols, first, bits
        self.own, self.r1, self.r2, self.r3 = bufs
        self.local, self.send, self.recv = sems
        self.result = result
        self.second = "near" if first == "y" else "y"

    def block(self, mine):
        at = mine if self.first == "y" else None
        view = self.grad
        if self.first == "y":
            return view.at[:, :, mine, :, self.cols]
        return view.at[:, mine, :, :, self.cols]

    def peer(self, name):
        me = lax.axis_index("dp")
        stride = {"y": 2, "near": 4, "far": 8}[name]
        return me + stride * (1 - 2 * self.bits[name])

    def remote(self, src, dst, step, name):
        copy = pltpu.make_async_remote_copy(
            src_ref=src, dst_ref=dst, send_sem=self.send.at[step], recv_sem=self.recv.at[step],
            device_id={"dp": self.peer(name)}, device_id_type=MESH)
        copy.start()
        return copy

    def step1(self):
        mine = self.bits[self.first]
        self.c1 = self.remote(self.block(1 - mine), self.r1, 0, self.first)
        self.l1 = pltpu.make_async_copy(self.block(mine), self.own, self.local)
        self.l1.start()

    def add(self, dst, src, out=None):
        rows = src.shape[0]

        def body(i, c):
            at = pl.ds(pl.multiple_of(i * TILE, TILE), TILE)
            total = dst[at, :].astype(F32) + src[at, :].astype(F32)
            if out is None:
                dst[at, :] = total.astype(BF16)
            else:
                out[at, :] = total
            return c

        lax.fori_loop(0, rows // TILE, body, 0)

    def step2(self):
        self.l1.wait()
        self.c1.wait_recv()
        s = self.bits[self.second]
        for far in range(2):
            self.add(self.own.at[far, 1 - s], self.r1.at[far, 1 - s])
        self.c2 = self.remote(self.own.at[:, 1 - s], self.r2, 1, self.second)
        for far in range(2):
            self.add(self.own.at[far, s], self.r1.at[far, s])

    def step3(self):
        self.c2.wait_recv()
        s, f = self.bits[self.second], self.bits["far"]
        self.add(self.own.at[1 - f, s], self.r2.at[1 - f])
        self.c3 = self.remote(self.own.at[1 - f, s], self.r3, 2, "far")
        self.add(self.own.at[f, s], self.r2.at[f])

    def finish(self):
        self.c3.wait_recv()
        s, f = self.bits[self.second], self.bits["far"]
        self.add(self.own.at[f, s], self.r3, self.result)
        self.c1.wait_send()
        self.c2.wait_send()
        self.c3.wait_send()


class Total:
    NAMES = ("core", "y", "near", "far")

    def __init__(self, acc, got, out, bits, sems):
        self.acc, self.got, self.out, self.bits, self.sems = acc, got, out, bits, sems
        self.at, self.copy, self.all = 0, None, []

    def go(self, src, dst, name):
        stride = {"core": 1, "y": 2, "near": 4, "far": 8}[name]
        self.copy = pltpu.make_async_remote_copy(
            src_ref=src, dst_ref=dst, send_sem=self.sems[0].at[self.at], recv_sem=self.sems[1].at[self.at],
            device_id={"dp": lax.axis_index("dp") + stride * (1 - 2 * self.bits[name])}, device_id_type=MESH)
        self.copy.start()
        self.all.append(self.copy)
        self.at += 1

    def path(self, depth):
        return tuple(self.bits[n] for n in self.NAMES[:depth])

    def step(self):
        i = self.at
        if self.copy is not None:
            self.copy.wait_recv()
        if 0 < i <= 4:
            self.fold(self.acc.at[self.path(i)], self.got[i - 1])
        if i < 4:
            self.go(self.acc.at[self.path(i) + (1 - self.bits[self.NAMES[i]],)], self.got[i], self.NAMES[i])
        elif i < 8:
            depth = 8 - i
            if i == 4:
                self.out[self.path(4)] = self.acc[self.path(4)]
            here = self.out.at[self.path(depth)]
            self.go(here, here, self.NAMES[depth - 1])

    def fold(self, dst, src):
        lead = src.shape[:-2]
        for flat in range(int(np.prod(lead, dtype=int))):
            index = tuple(int(v) for v in np.unravel_index(flat, lead)) if lead else ()
            d, s = (dst.at[index], src.at[index]) if lead else (dst, src)

            def body(i, c):
                at = pl.ds(pl.multiple_of(i * 16, 16), 16)
                d[at, :] = (d[at, :].astype(F32) + s[at, :].astype(F32)).astype(BF16)
                return c

            lax.fori_loop(0, src.shape[-2] // 16, body, 0)


def tail_kernel(orders, gout_ref, gz_ref, gx_ref, dn_ref, mx_ref, x_ref, dy_ref, small_ref, gain_ref, scale_ref, settle_ref, deal_ref,
                out_ref, in_ref, gg_ref, sum_ref, wout_ref, wz_ref, wx_ref,
                own, r1, r2, r3, p_local, p_send, p_recv,
                dn_own, dn_got, mx_own, mx_got, x_half, dy_half, du, rs_own, rs_got, gg_all, low,
                y_send, y_got, d_send, d_got, sem, x_send, x_recv, a_send, a_recv, g_send, g_recv,
                s_acc, s_got0, s_got1, s_got2, s_got3, s_out, s_send, s_recv):
    me, ten = lax.axis_index("dp"), lax.axis_index("tensor")
    count = lax.axis_size("dp")
    T, W = x_half.shape
    L = W // 128
    per = T // count
    barrier = pltpu.get_barrier_semaphore()
    for p in range(1, count):
        pl.semaphore_signal(barrier, inc=1, device_id={"dp": (me + p) % count}, device_id_type=MESH)
    pl.semaphore_signal(barrier, inc=1, device_id={"tensor": 1 - ten}, device_id_type=MESH)
    mine = pl.ds(pl.multiple_of(ten * W, 128), W)
    other = pl.ds(pl.multiple_of((1 - ten) * W, 128), W)
    loads = []
    for n, (src, dst) in enumerate(((dn_ref, dn_own), (mx_ref, mx_own), (x_ref, x_half), (dy_ref, dy_half), (small_ref, s_acc))):
        copy = pltpu.make_async_copy(src if n == 4 else src.at[:, mine], dst, sem.at[n])
        copy.start()
        loads.append(copy)
    pl.semaphore_wait(barrier, count)

    def swap(src, dst, n):
        copy = pltpu.make_async_remote_copy(
            src_ref=src, dst_ref=dst, send_sem=x_send.at[n], recv_sem=x_recv.at[n],
            device_id={"tensor": 1 - ten}, device_id_type=MESH)
        copy.start()
        return copy

    dn_copy = swap(dn_ref.at[:, other], dn_got, 0)
    bits = {"core": me % 2, "y": me // 2 % 2, "near": me // 4 % 2, "far": me // 8}
    grads, results = (gout_ref, gz_ref, gx_ref), (wout_ref, wz_ref, wx_ref)
    half = own.shape[-1]
    pieces = []
    for i, (g, h, first) in enumerate(orders):
        cols = slice(h * half, (h + 1) * half)
        pieces.append(Piece(grads[g], cols, first, bits, (own.at[i], r1.at[i], r2.at[i], r3.at[i]),
                            (p_local.at[i], p_send.at[i], p_recv.at[i]), results[g].at[:, cols]))
    for n in (0, 1, 2, 4):
        pieces[n].step1()
    mx_copy = swap(mx_ref.at[:, other], mx_got, 1)
    for copy in loads:
        copy.wait()
    total = Total(s_acc, (s_got0, s_got1, s_got2, s_got3), s_out, bits, (s_send, s_recv))
    total.step()

    def tiles(body, init):
        def step(i, c):
            return body(pl.ds(pl.multiple_of(i * 16, 16), 16), c)
        return lax.fori_loop(0, T // 16, step, init)

    dn_copy.wait_recv()
    gain = gain_ref[:, mine]

    def share(at, acc):
        scale = scale_ref[at, :]
        total = None
        out = []
        for l in range(L):
            ln = slice(l * 128, (l + 1) * 128)
            d = dn_own[at, ln].astype(F32) + dn_got[at, ln].astype(F32)
            unit = x_half[at, ln].astype(F32) * scale
            d_unit = d * gain[:, ln]
            du[at, ln] = d_unit
            out.append(acc[l] + jnp.sum(d * unit, axis=0, keepdims=True))
            total = d_unit * unit if total is None else total + d_unit * unit
        rs_own[at, :] = total
        return tuple(out)

    acc = tiles(share, tuple(jnp.zeros((1, 128), F32) for _ in range(L)))
    rs_copy = swap(rs_own, rs_got, 2)
    for l in range(L):
        gg_all[pl.ds(me, 1), 0:1, l * 128 : (l + 1) * 128] = acc[l][None]
    gains = []
    for p in range(1, count):
        copy = pltpu.make_async_remote_copy(
            src_ref=gg_all.at[me], dst_ref=gg_all.at[me], send_sem=g_send.at[p], recv_sem=g_recv.at[p],
            device_id={"dp": (me + p) % count}, device_id_type=MESH)
        copy.start()
        gains.append(copy)

    def deal_out(rows, send, got, n):
        sent = jnp.dot(settle_ref[...], rows[...], preferred_element_type=F32).astype(BF16)
        send[...] = sent.reshape(send.shape)
        got[me] = send[me]
        copies = []
        for p in range(1, count):
            to = (me + p) % count
            copy = pltpu.make_async_remote_copy(
                src_ref=send.at[to], dst_ref=got.at[me], send_sem=a_send.at[n, p], recv_sem=a_recv.at[n, p],
                device_id={"dp": to}, device_id_type=MESH)
            copy.start()
            copies.append(copy)
        return copies

    def take_in(copies, got, out):
        for copy in copies:
            copy.wait_recv()
        out[...] = jnp.dot(deal_ref[...], got[...].reshape(T, W), preferred_element_type=F32).astype(BF16)
        for copy in copies:
            copy.wait_send()

    total.step()
    pieces[0].step2()
    pieces[3].step1()
    rs_copy.wait_recv()

    def norm_back(at, c):
        scale = scale_ref[at, :]
        total = jnp.sum(rs_own[at, :] + rs_got[at, :], axis=1, keepdims=True) * (0.5 / W)
        for l in range(L):
            ln = slice(l * 128, (l + 1) * 128)
            unit = x_half[at, ln].astype(F32) * scale
            low[at, ln] = (dy_half[at, ln].astype(F32) + scale * (du[at, ln] - unit * total)).astype(BF16)
        return c

    tiles(norm_back, 0)
    d_copies = deal_out(low, d_send, d_got, 0)
    total.step()
    pieces[1].step2()
    mx_copy.wait_recv()

    def add_resid(at, c):
        for l in range(L):
            ln = slice(l * 128, (l + 1) * 128)
            total = mx_own[at, ln].astype(F32) + mx_got[at, ln].astype(F32)
            mx_own[at, ln] = (x_half[at, ln].astype(F32) + total).astype(BF16)
        return c

    tiles(add_resid, 0)
    y_copies = deal_out(mx_own, y_send, y_got, 1)
    total.step()
    pieces[2].step2()
    pieces[5].step1()
    pieces[0].step3()
    total.step()
    pieces[4].step2()
    pieces[1].step3()
    take_in(d_copies, d_got, in_ref)
    total.step()
    pieces[3].step2()
    pieces[0].finish()
    pieces[2].step3()
    total.step()
    pieces[4].step3()
    pieces[1].finish()
    pieces[5].step2()
    pieces[3].step3()
    total.step()
    pieces[2].finish()
    for copy in gains:
        copy.wait_recv()
    gg_ref[...] = jnp.sum(gg_all[...], axis=0)
    total.step()
    sum_ref[...] = s_out[...]
    pieces[5].step3()
    take_in(y_copies, y_got, out_ref)
    pieces[4].finish()
    pieces[3].finish()
    pieces[5].finish()
    for copy in total.all:
        copy.wait_send()
    for copy in gains + [dn_copy, mx_copy, rs_copy]:
        copy.wait_send()


def tail_call(gout, gz, gx, dn, mx, x, dy, small, gain, scale, settle_t, deal):
    T, D = x.shape
    W = D // 2
    n, half = 128, gx.shape[-1] // 2
    count = lax.axis_size("dp")
    n = gx.shape[3]
    orders = ((0, 0, "y"), (1, 0, "near"), (0, 1, "y"), (2, 0, "y"), (2, 1, "near"), (1, 1, "y"))
    S = jax.ShapeDtypeStruct
    full = 2 * half
    outs = (S((T, W), BF16), S((T, W), BF16), S((1, W), F32), S(small.shape, BF16), S((n, full), F32), S((n, full), F32), S((n, full), F32))
    anyspace = pl.BlockSpec(memory_space=pl.ANY)
    vmem = pl.BlockSpec(memory_space=pltpu.VMEM)
    V, DMA = pltpu.VMEM, pltpu.SemaphoreType.DMA
    k = len(orders)
    return pl.pallas_call(
        functools.partial(tail_kernel, orders),
        out_shape=outs,
        in_specs=[anyspace] * 8 + [vmem] * 4,
        out_specs=[vmem] * 7,
        scratch_shapes=[
            V((k, 2, 2, n, half), BF16), V((k, 2, 2, n, half), BF16), V((k, 2, n, half), BF16), V((k, n, half), BF16),
            DMA((k,)), DMA((k, 3)), DMA((k, 3)),
            V((T, W), BF16), V((T, W), BF16), V((T, W), BF16), V((T, W), BF16), V((T, W), BF16), V((T, W), BF16),
            V((T, W), F32), V((T, 128), F32), V((T, 128), F32), V((count, 1, W), F32), V((T, W), BF16),
            V((count, T // count, W), BF16), V((count, T // count, W), BF16),
            V((count, T // count, W), BF16), V((count, T // count, W), BF16),
            DMA((5,)), DMA((3,)), DMA((3,)), DMA((2, count)), DMA((2, count)), DMA((count,)), DMA((count,)),
            V(small.shape, BF16)] + [V(small.shape[i:], BF16) for i in range(1, 5)] + [V(small.shape, BF16), DMA((8,)), DMA((8,)),
        ],
        compiler_params=pltpu.CompilerParams(collective_id=1, has_side_effects=True, vmem_limit_bytes=58 << 20),
        cost_estimate=pl.CostEstimate(flops=T * T * D * 4, bytes_accessed=64 << 20, transcendentals=0),
        name="tail",
    )(gout, gz, gx, dn, mx, x, dy, small, gain, scale, settle_t, deal)


def tensor_other(value):
    return lax.ppermute(value, "tensor", [(0, 1), (1, 0)])


def tensor_total(value):
    if lax.axis_size("tensor") == 2:
        return value + tensor_other(value)
    return lax.psum(value, "tensor")


def half_total(value, me, width):
    if lax.axis_size("tensor") == 2:
        own = lax.dynamic_slice_in_dim(value, me * width, width, 1)
        sent = lax.dynamic_slice_in_dim(value, (1 - me) * width, width, 1).astype(BF16)
        return own + tensor_other(sent).astype(F32)
    return lax.psum_scatter(value, "tensor", scatter_dimension=1, tiled=True)


def full_columns(part, me):
    if lax.axis_size("tensor") == 2:
        other = tensor_other(part)
        return jnp.where(
            me == 0,
            jnp.concatenate([part, other], 1),
            jnp.concatenate([other, part], 1),
        )
    return lax.all_gather(part, "tensor", axis=1, tiled=True)


def pair_up(value, stride):
    count = lax.axis_size("dp")
    return lax.ppermute(value, "dp", [(i, i ^ stride) for i in range(count)])


def pick_dim(value, index, dim):
    return lax.dynamic_index_in_dim(value, index, dim, keepdims=False)


class Halves:
    def __init__(self, value, blocks):
        rows, width = value.shape
        core = lax.axis_index("dp") % 2
        split = value.reshape(rows, blocks // 2, 2, width // blocks)
        self.own = pick_dim(split, core, 2).reshape(rows, width // 2)
        self.other = pair_up(pick_dim(split, 1 - core, 2).reshape(rows, width // 2), 1)


def pair_gradient(left, right):
    return (contract_rows(left.own, right) + contract_rows(left.other, pair_up(right, 1))).astype(BF16)


def after(value, *earlier):
    return lax.optimization_barrier((value,) + earlier)[0]


def flatten(values):
    return jnp.concatenate([v.reshape(-1) for v in values])


def cut(flat, values):
    out, at = [], 0
    for v in values:
        out.append(flat[at : at + v.size].reshape(v.shape))
        at += v.size
    return out


def position_in(keys):
    return jnp.sum((keys[None, :] < keys[:, None]).astype(jnp.int32), axis=1)


def conv_mix(inner_x, conv_weight, conv_bias, segment):
    row_count = inner_x.shape[0]
    taps = conv_weight.shape[0]
    mixed = conv_bias[None, :] + conv_weight[taps - 1][None, :] * inner_x
    for shift_by in range(1, taps):
        moved = jnp.concatenate([jnp.zeros((shift_by, inner_x.shape[1]), F32), inner_x[: row_count - shift_by]], 0)
        seg_moved = jnp.concatenate([jnp.full((shift_by,), -1, jnp.int32), segment[: row_count - shift_by]], 0)
        keep_mask = (seg_moved == segment).astype(F32)
        mixed = mixed + conv_weight[taps - 1 - shift_by][None, :] * moved * keep_mask[:, None]
    return mixed


def silu_conv(inner_x, conv_weight, conv_bias, segment):
    mixed = conv_mix(inner_x, conv_weight, conv_bias, segment)
    return mixed * jax.nn.sigmoid(mixed)


def contract_rows(left, right):
    return lax.dot_general(left, right, (((0,), (0,)), ((), ())), preferred_element_type=F32)


def contract_cols(left, right):
    return lax.dot_general(left, right, (((1,), (1,)), ((), ())), preferred_element_type=F32)


def body(tokens, cotangent, norm_gain, w_x, w_z, conv_weight, conv_bias, x_proj, dt_proj, dt_bias, skip_gain, w_out,
         seq_lengths, arrival_route, work_source):
    dp_count = lax.axis_size("dp")
    tp_count = lax.axis_size("tensor")
    row_count, feat_width = tokens.shape
    per_peer = row_count // dp_count
    col_share = feat_width // tp_count
    me = lax.axis_index("tensor")
    col_start = me * col_share
    low_rank = dt_proj.shape[0]
    state_size = (x_proj.shape[1] - low_rank) // 2
    position = jnp.arange(row_count, dtype=jnp.int32)

    deal = (position_in(arrival_route)[:, None] == position[None, :]).astype(BF16)
    settle = (position_in(work_source // row_count * row_count + position)[:, None] == position[None, :]).astype(BF16)

    def exchange(rows):
        out = lax.all_to_all(rows.reshape(dp_count, per_peer, rows.shape[1]), "dp", split_axis=0, concat_axis=0, tiled=True)
        return out.reshape(row_count, rows.shape[1])

    def pick(table, rows, dim):
        return lax.dot_general(table, rows, (((dim,), (0,)), ((), ())), preferred_element_type=F32).astype(BF16)

    def bring(values):
        part = lax.dynamic_slice_in_dim(values, col_start, col_share, 1)
        return full_columns(pick(settle, exchange(pick(deal, part, 0)), 1), me)

    def give_back(values):
        return pick(deal, exchange(pick(settle, values, 0)), 1)

    x_work = bring(tokens)
    dy_work = bring(cotangent)

    lengths = seq_lengths[0]
    count = lengths.shape[0]
    before = jnp.arange(count)[:, None] > jnp.arange(count)[None, :]
    offsets = jnp.sum(jnp.where(before, lengths[None, :], 0), axis=1)
    segment = jnp.sum((position[:, None] >= offsets[None, :]).astype(jnp.int32), axis=1) - 1
    keep = 1.0 - jnp.any(position[:, None] == offsets[None, :], axis=1).astype(F32)

    resid = x_work.astype(F32)
    scale_row = lax.rsqrt(jnp.mean(resid * resid, axis=1, keepdims=True) + 1e-05)
    unit = resid * scale_row
    normed = (unit * norm_gain[None, :]).astype(BF16)
    inner_x = jnp.dot(normed, w_x, preferred_element_type=F32)
    inner_z = jnp.dot(normed, w_z, preferred_element_type=F32)
    conv_out, conv_pull = jax.vjp(partial(silu_conv, segment=segment), inner_x, conv_weight, conv_bias)
    conv_low = conv_out.astype(BF16)
    projected = tensor_total(jnp.dot(conv_low, x_proj, preferred_element_type=F32))
    rank_part = projected[:, :low_rank].astype(BF16)
    key_rows = projected[:, low_rank : low_rank + state_size]
    query_rows = projected[:, low_rank + state_size :]

    d_gated = contract_cols(dy_work, w_out)
    paired = dp_count == 16 and tp_count == 2
    scans = [scan_all(rank_part, dt_proj, dt_bias[None, :], conv_out, inner_z, d_gated, skip_gain[None, :], key_rows,
                      query_rows, keep, 1)(0)]
    gated_low, d_inner_z_low, d_conv_out, grad_skip, grad_dt_bias, grad_dt_proj, d_rank, d_keys, d_query = scans[0]
    grad_skip, grad_dt_bias = grad_skip[0], grad_dt_bias[0]
    d_proj = tensor_total(jnp.concatenate([d_rank, d_keys, d_query], axis=1))
    mixed = jnp.dot(gated_low, w_out, preferred_element_type=F32)
    if paired:
        mixed = mixed.astype(BF16)
        normed_halves, dy_halves = Halves(normed, dp_count), Halves(dy_work, dp_count)
        blocks = lambda g: g.reshape(2, 2, 2, g.shape[0] // 8, g.shape[1])
        g_out = blocks(pair_gradient(dy_halves, gated_low))
        g_z = blocks(pair_gradient(normed_halves, d_inner_z_low))
        d_proj = after(d_proj, g_out, g_z, mixed)
    d_proj_low = d_proj.astype(BF16)
    grad_x_proj = contract_rows(conv_low, d_proj_low)
    d_conv_out = d_conv_out + contract_cols(d_proj_low, x_proj)
    d_inner_x, grad_conv_weight, grad_conv_bias = conv_pull(d_conv_out)
    d_inner_x_low = d_inner_x.astype(BF16)
    d_normed = contract_cols(d_inner_x_low, w_x) + contract_cols(d_inner_z_low, w_z)
    small = (grad_x_proj, grad_dt_proj, grad_dt_bias, grad_skip, grad_conv_weight, grad_conv_bias)
    if paired:
        g_x = blocks(pair_gradient(normed_halves, d_inner_x_low))
        flat = jnp.concatenate([v.astype(BF16).reshape(-1, 128) for v in small])
        deep = -(-flat.shape[0] // 256) * 16
        flat = jnp.pad(flat, ((0, 16 * deep - flat.shape[0]), (0, 0))).reshape(2, 2, 2, 2, deep, 128)
        out_tokens, in_grad, grad_gain, flat, grad_w_out, grad_w_z, grad_w_x = tail_call(
            g_out, g_z, g_x, d_normed.astype(BF16), mixed, x_work, dy_work, flat, norm_gain[None, :],
            jnp.broadcast_to(scale_row, (row_count, 128)), settle.T, deal)
        grad_gain, grad_w_out = grad_gain[0], grad_w_out.T
        small = cut(flat.astype(F32).reshape(-1), small)
    else:
        unit_cols = lax.dynamic_slice_in_dim(unit, col_start, col_share, 1)
        gain_cols = lax.dynamic_slice_in_dim(norm_gain, col_start, col_share, 0)
        dy_cols = lax.dynamic_slice_in_dim(dy_work, col_start, col_share, 1).astype(F32)
        d_share = half_total(d_normed, me, col_share)
        d_unit_cols = d_share * gain_cols[None, :]
        row_total = tensor_total(jnp.sum(d_unit_cols * unit_cols, axis=1, keepdims=True))
        grad_gain = jnp.sum(d_share * unit_cols, axis=0)
        d_resid = dy_cols + scale_row * (d_unit_cols - unit_cols * (row_total / feat_width))
        mixed_share = half_total(mixed, me, col_share)
        out_cols = (lax.dynamic_slice_in_dim(resid, col_start, col_share, 1) + mixed_share).astype(BF16)
        out_tokens, in_grad = give_back(out_cols), give_back(d_resid.astype(BF16))
        grad_w_out, grad_w_z, grad_w_x = (
            lax.psum_scatter(g.astype(BF16), "dp", scatter_dimension=dim, tiled=True).astype(F32)
            for g, dim in ((contract_rows(gated_low, dy_work), 1), (contract_rows(normed, d_inner_z_low), 0),
                           (contract_rows(normed, d_inner_x_low), 0)))
        small += (grad_gain,)
        *small, grad_gain = cut(lax.psum(flatten(small), "dp"), small)
    grad_x_proj, grad_dt_proj, grad_dt_bias, grad_skip, grad_conv_weight, grad_conv_bias = small
    return (out_tokens, in_grad, grad_gain, grad_w_x, grad_w_z, grad_conv_weight, grad_conv_bias, grad_x_proj,
            grad_dt_proj, grad_dt_bias, grad_skip, grad_w_out)


def solution(mesh):
    in_specs = (
        P("dp", None),
        P("dp", None),
        P(),
        P(None, "tensor"),
        P(None, "tensor"),
        P(None, "tensor"),
        P("tensor"),
        P("tensor", None),
        P(None, "tensor"),
        P("tensor"),
        P("tensor"),
        P("tensor", None),
        P("dp", None),
        P("dp"),
        P("dp"),
    )
    out_specs = (
        P("dp", "tensor"),
        P("dp", "tensor"),
        P("tensor"),
        P("dp", "tensor"),
        P("dp", "tensor"),
        P(None, "tensor"),
        P("tensor"),
        P("tensor", None),
        P(None, "tensor"),
        P("tensor"),
        P("tensor"),
        P("tensor", "dp"),
    )
    return jax.shard_map(body, mesh=mesh, in_specs=in_specs, out_specs=out_specs, check_vma=False)
```

```python
import functools
from functools import partial

import jax
import jax.numpy as jnp
import numpy as np
from jax import lax
from jax.experimental import pallas as pl
from jax.experimental.pallas import tpu as pltpu
from jax.sharding import PartitionSpec as P

F32, BF16 = jnp.float32, jnp.bfloat16
MESH = pl.DeviceIdType.MESH
TILE = 32
STRIDE = {"core": 1, "y": 2, "near": 4, "far": 8}


class Piece:
    def __init__(self, grad, first, bufs, sems, result):
        self.grad, self.first, self.result = grad, first, result
        self.own, self.r1, self.r2, self.r3 = bufs
        self.local, self.send, self.recv = sems
        self.second = "near" if first == "y" else "y"

    def bit(self, name):
        return lax.axis_index("dp") // STRIDE[name] % 2

    def block(self, mine):
        return self.grad.at[:, :, mine] if self.first == "y" else self.grad.at[:, mine]

    def remote(self, step):
        s, f = self.bit(self.second), self.bit("far")
        name, src, dst = (
            (self.first, lambda: self.block(1 - self.bit(self.first)), self.r1),
            (self.second, lambda: self.own.at[:, 1 - s], self.r2),
            ("far", lambda: self.own.at[1 - f, s], self.r3),
        )[step]
        to = lax.axis_index("dp") + STRIDE[name] * (1 - 2 * self.bit(name))
        return pltpu.make_async_remote_copy(
            src_ref=src(), dst_ref=dst, send_sem=self.send.at[step], recv_sem=self.recv.at[step],
            device_id={"dp": to}, device_id_type=MESH)

    def load(self):
        return pltpu.make_async_copy(self.block(self.bit(self.first)), self.own, self.local)

    def step1(self):
        self.remote(0).start()
        self.load().start()

    def add(self, dst, src, out=None):
        def body(i, c):
            at = pl.ds(pl.multiple_of(i * TILE, TILE), TILE)
            total = dst[at, :].astype(F32) + src[at, :].astype(F32)
            if out is None:
                dst[at, :] = total.astype(BF16)
            else:
                out[at, :] = total
            return c

        lax.fori_loop(0, src.shape[0] // TILE, body, 0)

    def step2(self):
        self.load().wait()
        self.remote(0).wait_recv()
        s = self.bit(self.second)
        for far in range(2):
            self.add(self.own.at[far, 1 - s], self.r1.at[far, 1 - s])
        self.remote(1).start()
        for far in range(2):
            self.add(self.own.at[far, s], self.r1.at[far, s])

    def step3(self):
        self.remote(1).wait_recv()
        s, f = self.bit(self.second), self.bit("far")
        self.add(self.own.at[1 - f, s], self.r2.at[1 - f])
        self.remote(2).start()
        self.add(self.own.at[f, s], self.r2.at[f])

    def finish(self):
        self.remote(2).wait_recv()
        self.add(self.own.at[self.bit("far"), self.bit(self.second)], self.r3, self.result)
        for step in range(3):
            self.remote(step).wait_send()


def piece_scratch(k, n, w):
    V, DMA = pltpu.VMEM, pltpu.SemaphoreType.DMA
    return [V((k, 2, 2, n, w), BF16), V((k, 2, 2, n, w), BF16), V((k, 2, n, w), BF16), V((k, n, w), BF16),
            DMA((k,)), DMA((k, 3)), DMA((k, 3))]


def piece_of(i, grad, first, scratch, result):
    return Piece(grad, first, tuple(r.at[i] for r in scratch[:4]), tuple(r.at[i] for r in scratch[4:]), result)


def greet_dp(peers):
    for p in peers:
        pl.semaphore_signal(pltpu.get_barrier_semaphore(), inc=1, device_id={"dp": p}, device_id_type=MESH)
    return len(peers)


class Total:
    NAMES = ("core", "y", "near", "far")

    def __init__(self, acc, got, out, bits, sems):
        self.acc, self.got, self.out, self.bits, self.sems = acc, got, out, bits, sems
        self.at, self.copy, self.all = 0, None, []

    def go(self, src, dst, name):
        stride = STRIDE[name]
        self.copy = pltpu.make_async_remote_copy(
            src_ref=src, dst_ref=dst, send_sem=self.sems[0].at[self.at], recv_sem=self.sems[1].at[self.at],
            device_id={"dp": lax.axis_index("dp") + stride * (1 - 2 * self.bits[name])}, device_id_type=MESH)
        self.copy.start()
        self.all.append(self.copy)
        self.at += 1

    def path(self, depth):
        return tuple(self.bits[n] for n in self.NAMES[:depth])

    def step(self):
        i = self.at
        if self.copy is not None:
            self.copy.wait_recv()
        if 0 < i <= 4:
            self.fold(self.acc.at[self.path(i)], self.got[i - 1])
        if i < 4:
            self.go(self.acc.at[self.path(i) + (1 - self.bits[self.NAMES[i]],)], self.got[i], self.NAMES[i])
        elif i < 8:
            depth = 8 - i
            if i == 4:
                self.out[self.path(4)] = self.acc[self.path(4)]
            here = self.out.at[self.path(depth)]
            self.go(here, here, self.NAMES[depth - 1])

    def fold(self, dst, src):
        lead = src.shape[:-2]
        for flat in range(int(np.prod(lead, dtype=int))):
            index = tuple(int(v) for v in np.unravel_index(flat, lead)) if lead else ()
            d, s = (dst.at[index], src.at[index]) if lead else (dst, src)

            def body(i, c):
                at = pl.ds(pl.multiple_of(i * 16, 16), 16)
                d[at, :] = (d[at, :].astype(F32) + s[at, :].astype(F32)).astype(BF16)
                return c

            lax.fori_loop(0, src.shape[-2] // 16, body, 0)


def tail_kernel(gout_ref, gz_ref, gx_ref, dn_ref, mx_ref, x_ref, dy_ref, small_ref, gain_ref, scale_ref, settle_ref, deal_ref,
                out_ref, in_ref, gg_ref, sum_ref, wout_ref, wz_ref, wx_ref,
                p0, p1, p2, p3, p4, p5, p6,
                dn_own, dn_got, mx_own, mx_got, x_half, dy_half, du, rs_own, rs_got, gg_all, low,
                y_send, y_got, d_send, d_got, sem, x_send, x_recv, a_send, a_recv, g_send, g_recv,
                s_acc, s_got0, s_got1, s_got2, s_got3, s_out, s_send, s_recv):
    me, ten = lax.axis_index("dp"), lax.axis_index("tensor")
    count = lax.axis_size("dp")
    T, W = x_half.shape
    L = W // 128
    per = T // count
    barrier = pltpu.get_barrier_semaphore()
    for p in range(1, count):
        pl.semaphore_signal(barrier, inc=1, device_id={"dp": (me + p) % count}, device_id_type=MESH)
    pl.semaphore_signal(barrier, inc=1, device_id={"tensor": 1 - ten}, device_id_type=MESH)
    mine = pl.ds(pl.multiple_of(ten * W, 128), W)
    other = pl.ds(pl.multiple_of((1 - ten) * W, 128), W)
    loads = []
    for n, (src, dst) in enumerate(((dn_ref, dn_own), (mx_ref, mx_own), (x_ref, x_half), (dy_ref, dy_half), (small_ref, s_acc))):
        copy = pltpu.make_async_copy(src if n in (2, 4) else src.at[:, mine], dst, sem.at[n])
        copy.start()
        loads.append(copy)
    pl.semaphore_wait(barrier, count)

    def swap(src, dst, n):
        copy = pltpu.make_async_remote_copy(
            src_ref=src, dst_ref=dst, send_sem=x_send.at[n], recv_sem=x_recv.at[n],
            device_id={"tensor": 1 - ten}, device_id_type=MESH)
        copy.start()
        return copy

    dn_copy = swap(dn_ref.at[:, other], dn_got, 0)
    bits = {"core": me % 2, "y": me // 2 % 2, "near": me // 4 % 2, "far": me // 8}
    half = gout_ref.shape[-1]
    scratch = (p0, p1, p2, p3, p4, p5, p6)
    x_cols = [slice(0, half), slice(half, 2 * half)]
    pieces = [
        piece_of(0, gout_ref, "y", scratch, wout_ref), piece_of(1, gz_ref, "near", scratch, wz_ref),
        piece_of(2, gx_ref.at[:, :, :, :, x_cols[0]], "y", scratch, wx_ref.at[:, x_cols[0]]),
        piece_of(3, gx_ref.at[:, :, :, :, x_cols[1]], "near", scratch, wx_ref.at[:, x_cols[1]]),
    ]
    pieces[0].step1()
    pieces[1].step1()
    mx_copy = swap(mx_ref.at[:, other], mx_got, 1)
    for copy in loads:
        copy.wait()
    total = Total(s_acc, (s_got0, s_got1, s_got2, s_got3), s_out, bits, (s_send, s_recv))
    total.step()

    def tiles(body, init):
        def step(i, c):
            return body(pl.ds(pl.multiple_of(i * 16, 16), 16), c)
        return lax.fori_loop(0, T // 16, step, init)

    dn_copy.wait_recv()
    gain = gain_ref[:, mine]

    def share(at, acc):
        scale = scale_ref[at, :]
        total = None
        out = []
        for l in range(L):
            ln = slice(l * 128, (l + 1) * 128)
            d = dn_own[at, ln].astype(F32) + dn_got[at, ln].astype(F32)
            unit = x_half[at, ln].astype(F32) * scale
            d_unit = d * gain[:, ln]
            du[at, ln] = d_unit
            out.append(acc[l] + jnp.sum(d * unit, axis=0, keepdims=True))
            total = d_unit * unit if total is None else total + d_unit * unit
        rs_own[at, :] = total
        return tuple(out)

    acc = tiles(share, tuple(jnp.zeros((1, 128), F32) for _ in range(L)))
    rs_copy = swap(rs_own, rs_got, 2)
    for l in range(L):
        gg_all[pl.ds(me, 1), 0:1, l * 128 : (l + 1) * 128] = acc[l][None]
    gains = []
    for p in range(1, count):
        copy = pltpu.make_async_remote_copy(
            src_ref=gg_all.at[me], dst_ref=gg_all.at[me], send_sem=g_send.at[p], recv_sem=g_recv.at[p],
            device_id={"dp": (me + p) % count}, device_id_type=MESH)
        copy.start()
        gains.append(copy)

    def deal_out(rows, send, got, n):
        sent = jnp.dot(settle_ref[...], rows[...], preferred_element_type=F32).astype(BF16)
        send[...] = sent.reshape(send.shape)
        got[me] = send[me]
        copies = []
        for p in range(1, count):
            to = (me + p) % count
            copy = pltpu.make_async_remote_copy(
                src_ref=send.at[to], dst_ref=got.at[me], send_sem=a_send.at[n, p], recv_sem=a_recv.at[n, p],
                device_id={"dp": to}, device_id_type=MESH)
            copy.start()
            copies.append(copy)
        return copies

    def take_in(copies, got, out):
        for copy in copies:
            copy.wait_recv()
        out[...] = jnp.dot(deal_ref[...], got[...].reshape(T, W), preferred_element_type=F32).astype(BF16)
        for copy in copies:
            copy.wait_send()

    pieces[2].step1()
    pieces[3].step1()
    total.step()
    pieces[0].step2()
    pieces[1].step2()
    rs_copy.wait_recv()

    def norm_back(at, c):
        scale = scale_ref[at, :]
        total = jnp.sum(rs_own[at, :] + rs_got[at, :], axis=1, keepdims=True) * (0.5 / W)
        for l in range(L):
            ln = slice(l * 128, (l + 1) * 128)
            unit = x_half[at, ln].astype(F32) * scale
            low[at, ln] = (dy_half[at, ln].astype(F32) + scale * (du[at, ln] - unit * total)).astype(BF16)
        return c

    tiles(norm_back, 0)
    d_copies = deal_out(low, d_send, d_got, 0)
    total.step()
    mx_copy.wait_recv()

    def add_resid(at, c):
        for l in range(L):
            ln = slice(l * 128, (l + 1) * 128)
            total = mx_own[at, ln].astype(F32) + mx_got[at, ln].astype(F32)
            mx_own[at, ln] = (x_half[at, ln].astype(F32) + total).astype(BF16)
        return c

    tiles(add_resid, 0)
    y_copies = deal_out(mx_own, y_send, y_got, 1)
    total.step()
    pieces[2].step2()
    pieces[3].step2()
    total.step()
    pieces[0].step3()
    pieces[1].step3()
    total.step()
    take_in(d_copies, d_got, in_ref)
    total.step()
    pieces[2].step3()
    pieces[3].step3()
    total.step()
    for copy in gains:
        copy.wait_recv()
    gg_ref[...] = jnp.sum(gg_all[...], axis=0)
    pieces[0].finish()
    pieces[1].finish()
    total.step()
    sum_ref[...] = s_out[...]
    take_in(y_copies, y_got, out_ref)
    pieces[2].finish()
    pieces[3].finish()
    for copy in total.all:
        copy.wait_send()
    for copy in gains + [dn_copy, mx_copy, rs_copy]:
        copy.wait_send()


def tail_call(gout, gz, gx, dn, mx, x, dy, small, gain, scale, settle_t, deal):
    T, W = x.shape
    D = 2 * W
    n, half = gout.shape[3:]
    count = lax.axis_size("dp")
    S = jax.ShapeDtypeStruct
    full = 2 * half
    outs = (S((T, W), BF16), S((T, W), BF16), S((1, W), F32), S(small.shape, BF16), S((n, half), F32), S((n, half), F32), S((n, full), F32))
    anyspace = pl.BlockSpec(memory_space=pl.ANY)
    vmem = pl.BlockSpec(memory_space=pltpu.VMEM)
    V, DMA = pltpu.VMEM, pltpu.SemaphoreType.DMA
    return pl.pallas_call(
        tail_kernel,
        out_shape=outs,
        in_specs=[anyspace] * 8 + [vmem] * 4,
        out_specs=[vmem] * 7,
        scratch_shapes=[
            *piece_scratch(4, n, half),
            V((T, W), BF16), V((T, W), BF16), V((T, W), BF16), V((T, W), BF16), V((T, W), BF16), V((T, W), BF16),
            V((T, W), F32), V((T, 128), F32), V((T, 128), F32), V((count, 1, W), F32), V((T, W), BF16),
            V((count, T // count, W), BF16), V((count, T // count, W), BF16),
            V((count, T // count, W), BF16), V((count, T // count, W), BF16),
            DMA((5,)), DMA((3,)), DMA((3,)), DMA((2, count)), DMA((2, count)), DMA((count,)), DMA((count,)),
            V(small.shape, BF16)] + [V(small.shape[i:], BF16) for i in range(1, 5)] + [V(small.shape, BF16), DMA((8,)), DMA((8,)),
        ],
        compiler_params=pltpu.CompilerParams(collective_id=1, has_side_effects=True, vmem_limit_bytes=58 << 20),
        cost_estimate=pl.CostEstimate(flops=T * T * D * 4, bytes_accessed=64 << 20, transcendentals=0),
        name="tail",
    )(gout, gz, gx, dn, mx, x, dy, small, gain, scale, settle_t, deal)


def head_kernel(tok_ref, cot_ref, gain_ref, deal_ref, settle_ref,
                half_ref, normed_ref, dy_ref, scale_ref, n_own_ref, n_other_ref, d_own_ref, d_other_ref,
                part, send, got, across, n_send, d_send, load, a_send, a_recv, x_send, x_recv, c_send, c_recv):
    me, ten = lax.axis_index("dp"), lax.axis_index("tensor")
    count = lax.axis_size("dp")
    T, W = half_ref.shape
    per = T // count
    L = W // 128
    barrier = pltpu.get_barrier_semaphore()
    greet_dp([(me + p) % count for p in range(1, count)])
    pl.semaphore_signal(barrier, inc=1, device_id={"tensor": 1 - ten}, device_id_type=MESH)
    start = pl.multiple_of(ten * W, 128)
    loads = [pltpu.make_async_copy(src.at[:, pl.ds(start, W)], part.at[n], load.at[n]) for n, src in enumerate((tok_ref, cot_ref))]
    for copy in loads:
        copy.start()

    def deal(n):
        loads[n].wait()
        rows = jnp.dot(deal_ref[...], part[n], preferred_element_type=F32).astype(BF16)
        send[n] = rows.reshape(count, per, W)

    def out(n, p):
        to = (me + p) % count
        return pltpu.make_async_remote_copy(
            src_ref=send.at[n, to], dst_ref=got.at[n, me], send_sem=a_send.at[n, p], recv_sem=a_recv.at[n, p],
            device_id={"dp": to}, device_id_type=MESH)

    def over(n, p):
        at = (me + count - p) % count
        return pltpu.make_async_remote_copy(
            src_ref=(send if p == 0 else got).at[n, at], dst_ref=across.at[n, at], send_sem=x_send.at[n, p],
            recv_sem=x_recv.at[n, p], device_id={"tensor": 1 - ten}, device_id_type=MESH)

    def launch(n):
        for p in range(1, count):
            out(n, p).start()
        over(n, 0).start()
        got[n, me] = send[n, me]

    def forward(n):
        for p in range(1, count):
            out(n, p).wait_recv()
            over(n, p).start()

    def settle(n, source, at):
        rows = jnp.dot(settle_ref[...], source[n].reshape(T, W), preferred_element_type=F32)
        return rows.astype(BF16)

    deal(0)
    pl.semaphore_wait(barrier, count)
    launch(0)
    deal(1)
    forward(0)
    launch(1)
    half_ref[...] = settle(0, got, ten)
    for p in range(count):
        over(0, p).wait_recv()
    part[0] = settle(0, across, 1 - ten)
    core = me % 2

    def norm(i, c):
        at = pl.ds(pl.multiple_of(i * 16, 16), 16)
        mine, other = half_ref[at, :].astype(F32), part[0, at, :].astype(F32)
        square = jnp.sum(mine * mine + other * other, axis=1, keepdims=True)
        scale = lax.rsqrt(square * (0.5 / W) + 1e-05)
        scale_ref[at, :] = jnp.broadcast_to(scale, (16, 128))
        for value, begin in ((mine, start), (other, pl.multiple_of((1 - ten) * W, 128))):
            cols = pl.ds(begin, W)
            normed_ref[at, cols] = (value * scale * gain_ref[:, cols]).astype(BF16)
        return c

    lax.fori_loop(0, T // 16, norm, 0)

    def halves(source, own, other):
        def body(b, c):
            for into, k in ((own, core), (other, 1 - core)):
                into[:, pl.ds(pl.multiple_of(b * 128, 128), 128)] = source[:, pl.ds(pl.multiple_of((2 * b + k) * 128, 128), 128)]
            return c

        lax.fori_loop(0, W // 128, body, 0)

    def swap(n, source, into):
        return pltpu.make_async_remote_copy(
            src_ref=source, dst_ref=into, send_sem=c_send.at[n], recv_sem=c_recv.at[n],
            device_id={"dp": me + 1 - 2 * core}, device_id_type=MESH)

    halves(normed_ref, n_own_ref, n_send)
    first = swap(0, n_send, n_other_ref)
    first.start()
    forward(1)
    dy_ref[:, pl.ds(start, W)] = settle(1, got, ten)
    for p in range(count):
        over(1, p).wait_recv()
    dy_ref[:, pl.ds(pl.multiple_of((1 - ten) * W, 128), W)] = settle(1, across, 1 - ten)
    halves(dy_ref, d_own_ref, d_send)
    second = swap(1, d_send, d_other_ref)
    second.start()
    for copy in (first, second):
        copy.wait_recv()
        copy.wait_send()
    for n in range(2):
        for p in range(count):
            over(n, p).wait_send()
            if p:
                out(n, p).wait_send()


def head_call(tokens, cotangent, gain, deal_t, settle):
    T, D = tokens.shape
    W = D // 2
    count = lax.axis_size("dp")
    S = jax.ShapeDtypeStruct
    V, DMA = pltpu.VMEM, pltpu.SemaphoreType.DMA
    outs = (S((T, W), BF16), S((T, D), BF16), S((T, D), BF16), S((T, 128), F32)) + (S((T, W), BF16),) * 4
    block = V((2, count, T // count, W), BF16)
    vmem = pl.BlockSpec(memory_space=pltpu.VMEM)
    return pl.pallas_call(
        head_kernel,
        out_shape=outs,
        in_specs=[pl.BlockSpec(memory_space=pl.ANY)] * 2 + [vmem] * 3,
        out_specs=[vmem] * len(outs),
        scratch_shapes=[V((2, T, W), BF16), block, block, block, V((T, W), BF16), V((T, W), BF16), DMA((2,)),
                        DMA((2, count)), DMA((2, count)), DMA((2, count)), DMA((2, count)), DMA((2,)), DMA((2,))],
        compiler_params=pltpu.CompilerParams(collective_id=3, has_side_effects=True, vmem_limit_bytes=50 << 20),
        cost_estimate=pl.CostEstimate(flops=T * T * D * 4, bytes_accessed=24 << 20, transcendentals=0),
        name="head",
    )(tokens, cotangent, gain, deal_t, settle)


NT = (((1,), (1,)), ((), ()))
PR = 64


def scan_kernel(GR, NS, hosted, *refs):
    if not hosted:
        return scan_body(GR, NS, lambda at: None, *refs)
    ins, outs, own = 14, 10, 18
    refs = list(refs)
    g_refs = [refs.pop(ins), refs.pop(ins)]
    r_refs = [refs.pop(ins + outs), refs.pop(ins + outs)]
    scratch, refs = refs[-7:], refs[:-7]
    pieces = [piece_of(0, g_refs[0], "y", scratch, r_refs[0]), piece_of(1, g_refs[1], "near", scratch, r_refs[1])]
    steps = pl.num_programs(0)
    plan = {(0, "start"): 0, (0, "end"): 1, (1, "middle"): 2, (1, "end"): 3}

    def host(at):
        for (step, place), stage in plan.items():
            if place != at:
                continue

            @pl.when(pl.program_id(0) == step)
            def _(stage=stage):
                if stage == 0:
                    me = lax.axis_index("dp")
                    peers = [me + STRIDE[n] * (1 - 2 * (me // STRIDE[n] % 2)) for n in ("y", "near", "far")]
                    pl.semaphore_wait(pltpu.get_barrier_semaphore(), greet_dp(peers))
                for piece in pieces:
                    (piece.step1, piece.step2, piece.step3, piece.finish)[stage]()

    return scan_body(GR, NS, host, *refs)


def scan_body(GR, NS, host, rank_ref, dtp_ref, dtb_ref, u_ref, z_ref, dg_ref, skip_ref,
                kb_ref, qb_ref, keep_ref, ksq_ref, qblk_ref, kblk_ref, k2blk_ref,
                gated_ref, diz_ref, du_ref, gskip_ref, gdtb_ref, gdtp_ref,
                drank_ref, sst_ref, dk_ref, dq_ref,
                den_s, step_s, su_s, ds_s, sz_s, y_s, d_s, e_s, h0_s, h1_s, ga_s, gb_s, ma_s, mb_s, dk_s, dq_s):
    T, CH = u_ref.shape
    L = CH // 128
    NG = T // GR
    R = GR * NS
    first, last = pl.program_id(0) == 0, pl.program_id(0) == pl.num_programs(0) - 1
    lanes = [slice(l * 128, (l + 1) * 128) for l in range(L)]
    hist = (h0_s, h1_s)

    @pl.when(first)
    def _():
        for r in (drank_ref, sst_ref, dk_s, dq_s):
            r[...] = jnp.zeros_like(r)
        h1_s[pl.ds(0, R), :] = jnp.zeros((R, CH), BF16)
        gb_s[...] = jnp.zeros_like(gb_s)
        mb_s[...] = jnp.zeros_like(mb_s)

    host("start")
    y_s[...] = jnp.dot(rank_ref[...], dtp_ref[...], preferred_element_type=F32)

    def prologue(r, acc):
        rows = pl.ds(pl.multiple_of(r * PR, PR), PR)
        kq = ksq_ref[rows, :]
        out = []
        for l in range(L):
            ln = lanes[l]
            beta = jax.nn.sigmoid(y_s[rows, ln] + dtb_ref[:, ln])
            den = 1.0 / (1.0 + beta * kq)
            step = beta * den
            den_s[rows, ln] = den
            step_s[rows, ln] = step
            u = u_ref[rows, ln]
            su_s[rows, ln] = step * u
            z = z_ref[rows, ln]
            s = jax.nn.sigmoid(z)
            sz_s[rows, ln] = s
            ds = dg_ref[rows, ln] * (z * s)
            ds_s[rows, ln] = ds
            out.append(acc[l] + jnp.sum(ds * u, axis=0, keepdims=True))
        return tuple(out)

    zrow = tuple(jnp.zeros((1, 128), F32) for _ in range(L))
    gsk = lax.fori_loop(0, T // PR, prologue, zrow)
    for l in range(L):
        gskip_ref[:, lanes[l]] = gsk[l]

    def rows_of(gi):
        return pl.ds(pl.multiple_of(gi * GR, GR), GR)

    def fill(gi, half, h, dst):
        h = list(h)
        base = pl.multiple_of(gi * GR, GR)
        rows = rows_of(gi)
        hb = pl.multiple_of(half * R, R)
        for j in range(GR):
            k = kb_ref[pl.ds(base * NS + j * NS, NS), :]
            kp = keep_ref.at[rows][j:j + 1, :]
            k2 = k * k * kp
            for l in range(L):
                a = kp - k2 * step_s.at[rows][j:j + 1, lanes[l]]
                h[l] = a * h[l] + k * su_s.at[rows][j:j + 1, lanes[l]]
                dst[pl.ds(hb + j * NS, NS), lanes[l]] = h[l].astype(BF16)
        return tuple(h)

    def read(gi, half, src):
        y_s[rows_of(gi), :] = jnp.dot(qblk_ref[rows_of(gi), :], src[pl.ds(pl.multiple_of(half * R, R), R), :],
                                      preferred_element_type=F32)

    def forward(i, h):
        before = jnp.maximum(i - 1, 0)
        read(2 * before + 1, before, h1_s)
        h = fill(2 * i, i, h, h0_s)
        read(2 * i, i, h0_s)
        return fill(2 * i + 1, i, h, h1_s)

    zst = tuple(jnp.zeros((NS, 128), F32) for _ in range(L))
    lax.fori_loop(0, NG // 2, forward, zst)
    read(NG - 1, NG // 2 - 1, h1_s)

    host("middle")

    def middle(r, c):
        rows = pl.ds(pl.multiple_of(r * PR, PR), PR)
        for l in range(L):
            ln = lanes[l]
            z = z_ref[rows, ln]
            s = sz_s[rows, ln]
            v = y_s[rows, ln] + skip_ref[:, ln] * u_ref[rows, ln]
            gated_ref[rows, ln] = (v * (z * s)).astype(BF16)
            diz_ref[rows, ln] = (dg_ref[rows, ln] * v * s * (1.0 + z * (1.0 - s))).astype(BF16)
        return c

    lax.fori_loop(0, T // PR, middle, 0)

    def back(gi, half, gc, own, before, before_at, g_dst, m_dst):
        gc = list(gc)
        base = pl.multiple_of(gi * GR, GR)
        rows = rows_of(gi)
        hb = pl.multiple_of(half * R, R)
        nows = [own[pl.ds(hb + (GR - 1) * NS, NS), ln] for ln in lanes]
        for j in reversed(range(GR)):
            at = pl.ds(base * NS + j * NS, NS)
            k = kb_ref[at, :]
            q = qb_ref[at, :]
            kp = keep_ref.at[rows][j:j + 1, :]
            k2 = k * k * kp
            a_sum = b_sum = q_sum = None
            for l in range(L):
                ln = lanes[l]
                ds = ds_s.at[rows][j:j + 1, ln]
                g = gc[l] + q * ds
                gb = g.astype(BF16)
                step = step_s.at[rows][j:j + 1, ln]
                now = nows[l]
                if j:
                    prev = own[pl.ds(hb + (j - 1) * NS, NS), ln]
                else:
                    prev = before[pl.ds(before_at + (GR - 1) * NS, NS), ln]
                nows[l] = prev
                m = gb * prev
                g_dst[j * NS:(j + 1) * NS, ln] = gb
                m_dst[j * NS:(j + 1) * NS, ln] = m
                wide = lambda v: jnp.broadcast_to(v, (NS, 128)).astype(BF16)
                pa = gb * wide(su_s.at[rows][j:j + 1, ln])
                pb = m * wide(step)
                pq = now * wide(ds)
                a_sum = pa if a_sum is None else a_sum + pa
                b_sum = pb if b_sum is None else b_sum + pb
                q_sum = pq if q_sum is None else q_sum + pq
                gc[l] = (kp - k2 * step) * g
            dk_s[at, :] += a_sum.astype(F32) - (2.0 * k * kp) * b_sum.astype(F32)
            dq_s[at, :] += q_sum.astype(F32)
        return tuple(gc)

    def sums(gi, g_src, m_src):
        rows = rows_of(gi)
        d_s[rows, :] = jnp.dot(kblk_ref[rows, :], g_src[...], preferred_element_type=F32)
        e_s[rows, :] = jnp.dot(k2blk_ref[rows, :], m_src[...], preferred_element_type=F32)

    def backward(i, gc):
        half = NG // 2 - 1 - i
        hi, lo = 2 * half + 1, 2 * half
        sums(jnp.minimum(hi + 1, NG - 1), gb_s, mb_s)
        gc = back(hi, half, gc, h1_s, h0_s, pl.multiple_of(half * R, R), ga_s, ma_s)
        sums(hi, ga_s, ma_s)
        return back(lo, half, gc, h0_s, h1_s, pl.multiple_of(jnp.maximum(half - 1, 0) * R, R), gb_s, mb_s)

    lax.fori_loop(0, NG // 2, backward, zst)
    sums(0, gb_s, mb_s)

    def epilogue(r, acc):
        rows = pl.ds(pl.multiple_of(r * PR, PR), PR)
        kp = keep_ref[rows, :]
        out = []
        ss = sst_ref[rows, :]
        for l in range(L):
            ln = lanes[l]
            step = step_s[rows, ln]
            dsum = d_s[rows, ln]
            dstep = u_ref[rows, ln] * dsum - kp * e_s[rows, ln]
            du_ref[rows, ln] = step * dsum + ds_s[rows, ln] * skip_ref[:, ln]
            t = dstep * step
            ss = ss + t * step
            db = t * (den_s[rows, ln] - step)
            y_s[rows, ln] = db
            out.append(acc[l] + jnp.sum(db, axis=0, keepdims=True))
        sst_ref[rows, :] = ss
        return tuple(out)

    gdb = lax.fori_loop(0, T // PR, epilogue, zrow)
    for l in range(L):
        gdtb_ref[:, lanes[l]] = gdb[l]
    dbl = y_s[...].astype(BF16)
    gdtp_ref[...] = lax.dot_general(rank_ref[...], dbl, (((0,), (0,)), ((), ())), preferred_element_type=F32)
    drank_ref[...] += lax.dot_general(dbl, dtp_ref[...], NT, preferred_element_type=F32)

    host("end")

    @pl.when(last)
    def _():
        ones = jnp.ones((8, 128), BF16)
        for src, dst in ((dk_s, dk_ref), (dq_s, dq_ref)):
            for c in range(0, T * NS, 1024):
                dst[:, c:c + 1024] = lax.dot_general(ones, src[c:c + 1024, :].astype(BF16), NT, preferred_element_type=F32)


def scan_call(piece, pieces, hosted, *args, CH=512, GR=16, NS=16):
    rank, dtp, dtb, u, z, dg, skip, kb, qb, keep, ksq, qblk, kblk, k2blk = args
    T, C = u.shape
    width = C // pieces
    CH = min(CH, width)
    first = piece * (width // CH)
    const = lambda a: pl.BlockSpec(a.shape, lambda j: (0,) * a.ndim, pipeline_mode=pl.Buffered(1))
    oconst = lambda a: pl.BlockSpec(a.shape, lambda j: (0,) * a.ndim)
    col = lambda a: pl.BlockSpec((a.shape[0], CH), lambda j: (0, j + first))
    out = lambda a: pl.BlockSpec((a.shape[0], CH), lambda j: (0, j))
    S = jax.ShapeDtypeStruct
    W = GR * NS
    R = rank.shape[1]
    outs = (S((T, width), BF16), S((T, width), BF16), S((T, width), F32), S((1, width), F32), S((1, width), F32), S((R, width), F32),
            S((T, R), F32), S((T, 128), F32), S((8, T * NS), F32), S((8, T * NS), F32))
    outs += tuple(S(g.shape[3:], F32) for g in hosted)
    V = pltpu.VMEM
    f = pl.pallas_call(
        functools.partial(scan_kernel, GR, NS, bool(hosted)),
        grid=(width // CH,),
        in_specs=[const(rank), col(dtp), col(dtb), col(u), col(z), col(dg), col(skip), const(kb), const(qb),
                  const(keep), const(ksq), const(qblk), const(kblk), const(k2blk)] + [pl.BlockSpec(memory_space=pl.ANY)] * len(hosted),
        out_specs=[out(o) for o in outs[:6]] + [oconst(o) for o in outs[6:]],
        out_shape=outs,
        scratch_shapes=[V((T, CH), F32)] * 8 + [V((T * NS // 2, CH), BF16)] * 2 + [V((W, CH), BF16)] * 4 + [V((T * NS, 128), F32)] * 2
        + (piece_scratch(2, *hosted[0].shape[3:]) if hosted else []),
        compiler_params=pltpu.CompilerParams(vmem_limit_bytes=60 << 20, dimension_semantics=("arbitrary",),
                                             **(dict(collective_id=2, has_side_effects=True) if hosted else {})),
        cost_estimate=pl.CostEstimate(flops=T * width * NS * 800, bytes_accessed=T * width * 20, transcendentals=0),
        name="scan_reduce" if hosted else "scan",
    )
    return f(*args, *hosted)


def scan_all(rank, dtp, dtb, u, z, dg, skip, keys, query, keep, pieces, GR=16, **kw):
    T, NS = keys.shape
    kb = jnp.broadcast_to(keys[:, :, None], (T, NS, 128)).reshape(T * NS, 128)
    qb = jnp.broadcast_to(query[:, :, None], (T, NS, 128)).reshape(T * NS, 128)
    keepb = jnp.broadcast_to(keep[:, None], (T, 128))
    ksq = jnp.sum(keys * keys, axis=1)
    ksqb = jnp.broadcast_to(ksq[:, None], (T, 128))
    slot = (jnp.arange(T)[:, None] % GR == jnp.arange(GR * NS)[None, :] // NS).astype(F32)
    blk = lambda v: (slot * jnp.tile(v, (1, GR))).astype(BF16)
    qblk, kblk, k2blk = blk(query), blk(keys), blk(keys * keys)

    def run(piece, *hosted):
        o = scan_call(piece, pieces, hosted, rank, dtp, dtb, u, z, dg, skip, kb, qb, keepb, ksqb, qblk, kblk, k2blk, GR=GR, NS=NS, **kw)
        gated, diz, du, gskip, gdtb, gdtp, drank, sst, dk, dq, *summed = o
        dq = dq[0].reshape(T, NS)
        dk = dk[0].reshape(T, NS) - 2.0 * keys * jnp.sum(sst, axis=1, keepdims=True)
        return gated, diz, du, gskip, gdtb, gdtp, drank, dk, dq, summed

    return run


def tensor_other(value):
    return lax.ppermute(value, "tensor", [(0, 1), (1, 0)])


def tensor_total(value):
    if lax.axis_size("tensor") == 2:
        return value + tensor_other(value)
    return lax.psum(value, "tensor")


def half_total(value, me, width):
    if lax.axis_size("tensor") == 2:
        own = lax.dynamic_slice_in_dim(value, me * width, width, 1)
        sent = lax.dynamic_slice_in_dim(value, (1 - me) * width, width, 1).astype(BF16)
        return own + tensor_other(sent).astype(F32)
    return lax.psum_scatter(value, "tensor", scatter_dimension=1, tiled=True)


def full_columns(part, me):
    if lax.axis_size("tensor") == 2:
        other = tensor_other(part)
        return jnp.where(
            me == 0,
            jnp.concatenate([part, other], 1),
            jnp.concatenate([other, part], 1),
        )
    return lax.all_gather(part, "tensor", axis=1, tiled=True)


def pair_up(value, stride):
    count = lax.axis_size("dp")
    return lax.ppermute(value, "dp", [(i, i ^ stride) for i in range(count)])


def pair_gradient(own, other, right):
    return (contract_rows(own, right) + contract_rows(other, pair_up(right, 1))).astype(BF16)


def after(value, *earlier):
    return lax.optimization_barrier((value,) + earlier)[0]


def flatten(values):
    return jnp.concatenate([v.reshape(-1) for v in values])


def cut(flat, values):
    out, at = [], 0
    for v in values:
        out.append(flat[at : at + v.size].reshape(v.shape))
        at += v.size
    return out


def position_in(keys):
    return jnp.sum((keys[None, :] < keys[:, None]).astype(jnp.int32), axis=1)


def conv_mix(inner_x, conv_weight, conv_bias, segment):
    row_count = inner_x.shape[0]
    taps = conv_weight.shape[0]
    mixed = conv_bias[None, :] + conv_weight[taps - 1][None, :] * inner_x
    for shift_by in range(1, taps):
        moved = jnp.concatenate([jnp.zeros((shift_by, inner_x.shape[1]), F32), inner_x[: row_count - shift_by]], 0)
        seg_moved = jnp.concatenate([jnp.full((shift_by,), -1, jnp.int32), segment[: row_count - shift_by]], 0)
        keep_mask = (seg_moved == segment).astype(F32)
        mixed = mixed + conv_weight[taps - 1 - shift_by][None, :] * moved * keep_mask[:, None]
    return mixed


def silu_conv(inner_x, conv_weight, conv_bias, segment):
    mixed = conv_mix(inner_x, conv_weight, conv_bias, segment)
    return mixed * jax.nn.sigmoid(mixed)


def contract_rows(left, right):
    return lax.dot_general(left, right, (((0,), (0,)), ((), ())), preferred_element_type=F32)


def contract_cols(left, right):
    return lax.dot_general(left, right, (((1,), (1,)), ((), ())), preferred_element_type=F32)


def body(tokens, cotangent, norm_gain, w_x, w_z, conv_weight, conv_bias, x_proj, dt_proj, dt_bias, skip_gain, w_out,
         seq_lengths, arrival_route, work_source):
    dp_count = lax.axis_size("dp")
    tp_count = lax.axis_size("tensor")
    row_count, feat_width = tokens.shape
    per_peer = row_count // dp_count
    col_share = feat_width // tp_count
    me = lax.axis_index("tensor")
    col_start = me * col_share
    low_rank = dt_proj.shape[0]
    state_size = (x_proj.shape[1] - low_rank) // 2
    position = jnp.arange(row_count, dtype=jnp.int32)

    deal = (position_in(arrival_route)[:, None] == position[None, :]).astype(BF16)
    settle = (position_in(work_source // row_count * row_count + position)[:, None] == position[None, :]).astype(BF16)

    def exchange(rows):
        out = lax.all_to_all(rows.reshape(dp_count, per_peer, rows.shape[1]), "dp", split_axis=0, concat_axis=0, tiled=True)
        return out.reshape(row_count, rows.shape[1])

    def pick(table, rows, dim):
        return lax.dot_general(table, rows, (((dim,), (0,)), ((), ())), preferred_element_type=F32).astype(BF16)

    def bring(values):
        part = lax.dynamic_slice_in_dim(values, col_start, col_share, 1)
        return full_columns(pick(settle, exchange(pick(deal, part, 0)), 1), me)

    def give_back(values):
        return pick(deal, exchange(pick(settle, values, 0)), 1)

    paired = dp_count == 16 and tp_count == 2
    if paired:
        x_half, normed, dy_work, scale_wide, normed_own, normed_other, dy_own, dy_other = head_call(
            tokens, cotangent, norm_gain[None, :], deal.T, settle)
    else:
        x_work = bring(tokens)
        dy_work = bring(cotangent)
        resid = x_work.astype(F32)
        scale_row = lax.rsqrt(jnp.mean(resid * resid, axis=1, keepdims=True) + 1e-05)
        unit = resid * scale_row
        normed = (unit * norm_gain[None, :]).astype(BF16)

    lengths = seq_lengths[0]
    count = lengths.shape[0]
    before = jnp.arange(count)[:, None] > jnp.arange(count)[None, :]
    offsets = jnp.sum(jnp.where(before, lengths[None, :], 0), axis=1)
    segment = jnp.sum((position[:, None] >= offsets[None, :]).astype(jnp.int32), axis=1) - 1
    keep = 1.0 - jnp.any(position[:, None] == offsets[None, :], axis=1).astype(F32)

    inner_x = jnp.dot(normed, w_x, preferred_element_type=F32)
    inner_z = jnp.dot(normed, w_z, preferred_element_type=F32)
    conv_out, conv_pull = jax.vjp(partial(silu_conv, segment=segment), inner_x, conv_weight, conv_bias)
    conv_low = conv_out.astype(BF16)
    projected = tensor_total(jnp.dot(conv_low, x_proj, preferred_element_type=F32))
    rank_part = projected[:, :low_rank].astype(BF16)
    key_rows = projected[:, low_rank : low_rank + state_size]
    query_rows = projected[:, low_rank + state_size :]

    d_gated = contract_cols(dy_work, w_out)
    pieces = 2 if paired else 1
    scan = scan_all(rank_part, dt_proj, dt_bias[None, :], conv_out, inner_z, d_gated, skip_gain[None, :], key_rows,
                    query_rows, keep, pieces)
    scans = [scan(0)]
    if paired:
        blocks = lambda g: g.reshape(2, 2, 2, g.shape[0] // 8, g.shape[1])
        outer = lambda part: (blocks(pair_gradient(dy_own, dy_other, part[0])),
                              blocks(pair_gradient(normed_own, normed_other, part[1])))
        scans.append(scan(1, *outer(scans[0])))
    wide = lambda index: jnp.concatenate([part[index] for part in scans], axis=1) if paired else scans[0][index]
    d_conv_out, grad_dt_proj = wide(2), wide(5)
    grad_skip, grad_dt_bias = wide(3)[0], wide(4)[0]
    d_rank, d_keys, d_query = (sum(part[index] for part in scans) for index in (6, 7, 8))
    gated_low, d_inner_z_low = wide(0), wide(1)
    d_proj = tensor_total(jnp.concatenate([d_rank, d_keys, d_query], axis=1))
    mixed = jnp.dot(gated_low, w_out, preferred_element_type=F32)
    if paired:
        mixed = mixed.astype(BF16)
        g_out, g_z = outer(scans[1])
        d_proj = after(d_proj, g_out, g_z, mixed)
    d_proj_low = d_proj.astype(BF16)
    grad_x_proj = contract_rows(conv_low, d_proj_low)
    d_conv_out = d_conv_out + contract_cols(d_proj_low, x_proj)
    d_inner_x, grad_conv_weight, grad_conv_bias = conv_pull(d_conv_out)
    d_inner_x_low = d_inner_x.astype(BF16)
    d_normed = contract_cols(d_inner_x_low, w_x) + contract_cols(d_inner_z_low, w_z)
    small = (grad_x_proj, grad_dt_proj, grad_dt_bias, grad_skip, grad_conv_weight, grad_conv_bias)
    if paired:
        g_x = blocks(pair_gradient(normed_own, normed_other, d_inner_x_low))
        flat = jnp.concatenate([v.astype(BF16).reshape(-1, 128) for v in small])
        deep = -(-flat.shape[0] // 256) * 16
        flat = jnp.pad(flat, ((0, 16 * deep - flat.shape[0]), (0, 0))).reshape(2, 2, 2, 2, deep, 128)
        out_tokens, in_grad, grad_gain, flat, grad_w_out, grad_w_z, grad_w_x = tail_call(
            g_out, g_z, g_x, d_normed.astype(BF16), mixed, x_half, dy_work, flat, norm_gain[None, :],
            scale_wide, settle.T, deal)
        grad_gain = grad_gain[0]
        early_out, early_z = scans[1][9]
        grad_w_out = jnp.concatenate([early_out, grad_w_out], axis=1).T
        grad_w_z = jnp.concatenate([early_z, grad_w_z], axis=1)
        small = cut(flat.astype(F32).reshape(-1), small)
    else:
        unit_cols = lax.dynamic_slice_in_dim(unit, col_start, col_share, 1)
        gain_cols = lax.dynamic_slice_in_dim(norm_gain, col_start, col_share, 0)
        dy_cols = lax.dynamic_slice_in_dim(dy_work, col_start, col_share, 1).astype(F32)
        d_share = half_total(d_normed, me, col_share)
        d_unit_cols = d_share * gain_cols[None, :]
        row_total = tensor_total(jnp.sum(d_unit_cols * unit_cols, axis=1, keepdims=True))
        grad_gain = jnp.sum(d_share * unit_cols, axis=0)
        d_resid = dy_cols + scale_row * (d_unit_cols - unit_cols * (row_total / feat_width))
        mixed_share = half_total(mixed, me, col_share)
        out_cols = (lax.dynamic_slice_in_dim(resid, col_start, col_share, 1) + mixed_share).astype(BF16)
        out_tokens, in_grad = give_back(out_cols), give_back(d_resid.astype(BF16))
        grad_w_out, grad_w_z, grad_w_x = (
            lax.psum_scatter(g.astype(BF16), "dp", scatter_dimension=dim, tiled=True).astype(F32)
            for g, dim in ((contract_rows(gated_low, dy_work), 1), (contract_rows(normed, d_inner_z_low), 0),
                           (contract_rows(normed, d_inner_x_low), 0)))
        small += (grad_gain,)
        *small, grad_gain = cut(lax.psum(flatten(small), "dp"), small)
    grad_x_proj, grad_dt_proj, grad_dt_bias, grad_skip, grad_conv_weight, grad_conv_bias = small
    return (out_tokens, in_grad, grad_gain, grad_w_x, grad_w_z, grad_conv_weight, grad_conv_bias, grad_x_proj,
            grad_dt_proj, grad_dt_bias, grad_skip, grad_w_out)


def solution(mesh):
    in_specs = (
        P("dp", None),
        P("dp", None),
        P(),
        P(None, "tensor"),
        P(None, "tensor"),
        P(None, "tensor"),
        P("tensor"),
        P("tensor", None),
        P(None, "tensor"),
        P("tensor"),
        P("tensor"),
        P("tensor", None),
        P("dp", None),
        P("dp"),
        P("dp"),
    )
    out_specs = (
        P("dp", "tensor"),
        P("dp", "tensor"),
        P("tensor"),
        P("dp", "tensor"),
        P("dp", "tensor"),
        P(None, "tensor"),
        P("tensor"),
        P("tensor", None),
        P(None, "tensor"),
        P("tensor"),
        P("tensor"),
        P("tensor", "dp"),
    )
    return jax.shard_map(body, mesh=mesh, in_specs=in_specs, out_specs=out_specs, check_vma=False)
```

```python
import functools
from functools import partial

import jax
import jax.numpy as jnp
import numpy as np
from jax import lax
from jax.experimental import pallas as pl
from jax.experimental.pallas import tpu as pltpu
from jax.sharding import PartitionSpec as P

F32, BF16 = jnp.float32, jnp.bfloat16
MESH = pl.DeviceIdType.MESH
TILE = 32
STRIDE = {"core": 1, "y": 2, "near": 4, "far": 8}


class Piece:
    def __init__(self, grad, first, bufs, sems, result, came=None):
        self.grad, self.first, self.result, self.came = grad, first, result, came
        self.own, self.r1, self.r2, self.r3 = bufs
        self.local, self.send, self.recv = sems
        self.second = "near" if first == "y" else "y"

    def bit(self, name):
        return lax.axis_index("dp") // STRIDE[name] % 2

    def block(self, mine):
        return self.grad.at[:, :, mine] if self.first == "y" else self.grad.at[:, mine]

    def remote(self, step):
        s, f = self.bit(self.second), self.bit("far")
        name, src, dst = (
            (self.first, lambda: self.block(1 - self.bit(self.first)), self.r1),
            (self.second, lambda: self.own.at[:, 1 - s], self.r2),
            ("far", lambda: self.own.at[1 - f, s], self.r3),
        )[step]
        to = lax.axis_index("dp") + STRIDE[name] * (1 - 2 * self.bit(name))
        return pltpu.make_async_remote_copy(
            src_ref=src(), dst_ref=dst, send_sem=self.send.at[step], recv_sem=self.recv.at[step],
            device_id={"dp": to}, device_id_type=MESH)

    def load(self):
        return pltpu.make_async_copy(self.block(self.bit(self.first)), self.own, self.local)

    def bring(self):
        if self.came is None:
            return self.remote(0)
        return pltpu.make_async_copy(self.came, self.r1, self.recv.at[0])

    def step1(self):
        self.bring().start()
        self.load().start()

    def add(self, dst, src, out=None):
        def body(i, c):
            at = pl.ds(pl.multiple_of(i * TILE, TILE), TILE)
            total = dst[at, :].astype(F32) + src[at, :].astype(F32)
            if out is None:
                dst[at, :] = total.astype(BF16)
            else:
                out[at, :] = total.astype(out.dtype)
            return c

        lax.fori_loop(0, src.shape[0] // TILE, body, 0)

    def step2(self):
        self.load().wait()
        if self.came is None:
            self.remote(0).wait_recv()
        else:
            self.bring().wait()
        s = self.bit(self.second)
        for far in range(2):
            self.add(self.own.at[far, 1 - s], self.r1.at[far, 1 - s])
        self.remote(1).start()
        for far in range(2):
            self.add(self.own.at[far, s], self.r1.at[far, s])

    def step3(self):
        self.remote(1).wait_recv()
        s, f = self.bit(self.second), self.bit("far")
        self.add(self.own.at[1 - f, s], self.r2.at[1 - f])
        self.remote(2).start()
        self.add(self.own.at[f, s], self.r2.at[f])

    def stop(self):
        self.remote(1).wait_recv()
        for far in range(2):
            self.add(self.own.at[far, self.bit(self.second)], self.r2.at[far], self.result.at[far])
        for step in range(2):
            self.remote(step).wait_send()

    def finish(self):
        self.remote(2).wait_recv()
        self.add(self.own.at[self.bit("far"), self.bit(self.second)], self.r3, self.result)
        for step in range(0 if self.came is None else 1, 3):
            self.remote(step).wait_send()


def piece_scratch(k, n, w):
    V, DMA = pltpu.VMEM, pltpu.SemaphoreType.DMA
    return [V((k, 2, 2, n, w), BF16), V((k, 2, 2, n, w), BF16), V((k, 2, n, w), BF16), V((k, n, w), BF16),
            DMA((k,)), DMA((k, 3)), DMA((k, 3))]


def piece_of(i, grad, first, scratch, result, came=None):
    return Piece(grad, first, tuple(r.at[i] for r in scratch[:4]), tuple(r.at[i] for r in scratch[4:]), result, came)


def greet_dp(peers):
    for p in peers:
        pl.semaphore_signal(pltpu.get_barrier_semaphore(), inc=1, device_id={"dp": p}, device_id_type=MESH)
    return len(peers)


class Total:
    NAMES = ("core", "y", "near", "far")

    def __init__(self, acc, got, out, bits, sems):
        self.acc, self.got, self.out, self.bits, self.sems = acc, got, out, bits, sems
        self.at, self.copy, self.all = 0, None, []

    def go(self, src, dst, name):
        stride = STRIDE[name]
        self.copy = pltpu.make_async_remote_copy(
            src_ref=src, dst_ref=dst, send_sem=self.sems[0].at[self.at], recv_sem=self.sems[1].at[self.at],
            device_id={"dp": lax.axis_index("dp") + stride * (1 - 2 * self.bits[name])}, device_id_type=MESH)
        self.copy.start()
        self.all.append(self.copy)
        self.at += 1

    def path(self, depth):
        return tuple(self.bits[n] for n in self.NAMES[:depth])

    def step(self):
        i = self.at
        if self.copy is not None:
            self.copy.wait_recv()
        if 0 < i <= 4:
            self.fold(self.acc.at[self.path(i)], self.got[i - 1])
        if i < 4:
            self.go(self.acc.at[self.path(i) + (1 - self.bits[self.NAMES[i]],)], self.got[i], self.NAMES[i])
        elif i < 8:
            depth = 8 - i
            if i == 4:
                self.out[self.path(4)] = self.acc[self.path(4)]
            here = self.out.at[self.path(depth)]
            self.go(here, here, self.NAMES[depth - 1])

    def fold(self, dst, src):
        lead = src.shape[:-2]
        for flat in range(int(np.prod(lead, dtype=int))):
            index = tuple(int(v) for v in np.unravel_index(flat, lead)) if lead else ()
            d, s = (dst.at[index], src.at[index]) if lead else (dst, src)

            def body(i, c):
                at = pl.ds(pl.multiple_of(i * 16, 16), 16)
                d[at, :] = (d[at, :].astype(F32) + s[at, :].astype(F32)).astype(BF16)
                return c

            lax.fori_loop(0, src.shape[-2] // 16, body, 0)


def tail_kernel(gout_ref, gz_ref, gx_ref, cout_ref, cz_ref, dn_ref, mx_ref, other_ref, x_ref, dy_ref, small_ref, gain_ref, scale_ref, settle_ref, deal_ref,
                out_ref, in_ref, gg_ref, sum_ref, wout_ref, wz_ref, wx_ref,
                p0, p1, p2, p3, p4, p5, p6,
                dn_own, dn_got, mx_own, mx_got, x_half, dy_half, du, rs_own, rs_got, gg_all, low,
                y_send, y_got, d_send, d_got, sem, x_send, x_recv, a_send, a_recv, g_send, g_recv,
                s_acc, s_got0, s_got1, s_got2, s_got3, s_out, s_send, s_recv):
    me, ten = lax.axis_index("dp"), lax.axis_index("tensor")
    count = lax.axis_size("dp")
    T, W = x_half.shape
    L = W // 128
    per = T // count
    barrier = pltpu.get_barrier_semaphore()
    for p in range(1, count):
        pl.semaphore_signal(barrier, inc=1, device_id={"dp": (me + p) % count}, device_id_type=MESH)
    pl.semaphore_signal(barrier, inc=1, device_id={"tensor": 1 - ten}, device_id_type=MESH)
    mine = pl.ds(pl.multiple_of(ten * W, 128), W)
    other = pl.ds(pl.multiple_of((1 - ten) * W, 128), W)
    loads = []
    for n, (src, dst) in enumerate(((dn_ref, dn_own), (mx_ref, mx_own), (x_ref, x_half), (dy_ref, dy_half), (small_ref, s_acc), (other_ref, mx_got))):
        copy = pltpu.make_async_copy(src if n in (2, 4, 5) else src.at[:, mine], dst, sem.at[n])
        copy.start()
        loads.append(copy)
    pl.semaphore_wait(barrier, count)

    def swap(src, dst, n):
        copy = pltpu.make_async_remote_copy(
            src_ref=src, dst_ref=dst, send_sem=x_send.at[n], recv_sem=x_recv.at[n],
            device_id={"tensor": 1 - ten}, device_id_type=MESH)
        copy.start()
        return copy

    dn_copy = swap(dn_ref.at[:, other], dn_got, 0)
    bits = {"core": me % 2, "y": me // 2 % 2, "near": me // 4 % 2, "far": me // 8}
    half = gout_ref.shape[-1]
    scratch = (p0, p1, p2, p3, p4, p5, p6)
    x_cols = [slice(0, half), slice(half, 2 * half)]
    pieces = [
        piece_of(0, gout_ref, "y", scratch, wout_ref, cout_ref),
        piece_of(1, gz_ref, "near", scratch, wz_ref, cz_ref),
        piece_of(2, gx_ref.at[:, :, :, :, x_cols[0]], "y", scratch, wx_ref.at[:, x_cols[0]]),
        piece_of(3, gx_ref.at[:, :, :, :, x_cols[1]], "near", scratch, wx_ref.at[:, x_cols[1]]),
    ]
    for piece in pieces:
        piece.step1()
    for copy in loads:
        copy.wait()
    total = Total(s_acc, (s_got0, s_got1, s_got2, s_got3), s_out, bits, (s_send, s_recv))
    total.step()

    def tiles(body, init):
        def step(i, c):
            return body(pl.ds(pl.multiple_of(i * 16, 16), 16), c)
        return lax.fori_loop(0, T // 16, step, init)

    def add_resid(at, c):
        for l in range(L):
            ln = slice(l * 128, (l + 1) * 128)
            both = mx_own[at, ln].astype(F32) + mx_got[at, ln].astype(F32)
            mx_own[at, ln] = (x_half[at, ln].astype(F32) + both).astype(BF16)
        return c

    def deal_out(rows, send, got, n):
        sent = jnp.dot(settle_ref[...], rows[...], preferred_element_type=F32).astype(BF16)
        send[...] = sent.reshape(send.shape)
        got[me] = send[me]
        copies = []
        for p in range(1, count):
            to = (me + p) % count
            copy = pltpu.make_async_remote_copy(
                src_ref=send.at[to], dst_ref=got.at[me], send_sem=a_send.at[n, p], recv_sem=a_recv.at[n, p],
                device_id={"dp": to}, device_id_type=MESH)
            copy.start()
            copies.append(copy)
        return copies

    def take_in(copies, got, out):
        for copy in copies:
            copy.wait_recv()
        out[...] = jnp.dot(deal_ref[...], got[...].reshape(T, W), preferred_element_type=F32).astype(BF16)
        for copy in copies:
            copy.wait_send()

    pieces[0].step2()
    pieces[1].step2()
    tiles(add_resid, 0)
    y_copies = deal_out(mx_own, y_send, y_got, 1)
    total.step()

    dn_copy.wait_recv()
    gain = gain_ref[:, mine]

    def share(at, acc):
        scale = scale_ref[at, :]
        total = None
        out = []
        for l in range(L):
            ln = slice(l * 128, (l + 1) * 128)
            d = dn_own[at, ln].astype(F32) + dn_got[at, ln].astype(F32)
            unit = x_half[at, ln].astype(F32) * scale
            d_unit = d * gain[:, ln]
            du[at, ln] = d_unit
            out.append(acc[l] + jnp.sum(d * unit, axis=0, keepdims=True))
            total = d_unit * unit if total is None else total + d_unit * unit
        rs_own[at, :] = total
        return tuple(out)

    acc = tiles(share, tuple(jnp.zeros((1, 128), F32) for _ in range(L)))
    rs_copy = swap(rs_own, rs_got, 2)
    for l in range(L):
        gg_all[pl.ds(me, 1), 0:1, l * 128 : (l + 1) * 128] = acc[l][None]
    gains = []
    for p in range(1, count):
        copy = pltpu.make_async_remote_copy(
            src_ref=gg_all.at[me], dst_ref=gg_all.at[me], send_sem=g_send.at[p], recv_sem=g_recv.at[p],
            device_id={"dp": (me + p) % count}, device_id_type=MESH)
        copy.start()
        gains.append(copy)

    total.step()
    pieces[0].step3()
    pieces[1].step3()
    rs_copy.wait_recv()

    def norm_back(at, c):
        scale = scale_ref[at, :]
        total = jnp.sum(rs_own[at, :] + rs_got[at, :], axis=1, keepdims=True) * (0.5 / W)
        for l in range(L):
            ln = slice(l * 128, (l + 1) * 128)
            unit = x_half[at, ln].astype(F32) * scale
            low[at, ln] = (dy_half[at, ln].astype(F32) + scale * (du[at, ln] - unit * total)).astype(BF16)
        return c

    tiles(norm_back, 0)
    d_copies = deal_out(low, d_send, d_got, 0)
    total.step()
    pieces[2].step2()
    pieces[3].step2()
    total.step()
    take_in(y_copies, y_got, out_ref)
    pieces[0].finish()
    pieces[1].finish()
    total.step()
    pieces[2].step3()
    pieces[3].step3()
    total.step()
    for copy in gains:
        copy.wait_recv()
    gg_ref[...] = jnp.sum(gg_all[...], axis=0)
    total.step()
    take_in(d_copies, d_got, in_ref)
    total.step()
    sum_ref[...] = s_out[...]
    pieces[2].finish()
    pieces[3].finish()
    for copy in total.all:
        copy.wait_send()
    for copy in gains + [dn_copy, rs_copy]:
        copy.wait_send()


def tail_call(gout, gz, gx, cout, cz, dn, mx, other, x, dy, small, gain, scale, settle_t, deal):
    T, W = x.shape
    D = 2 * W
    n, half = gout.shape[3:]
    count = lax.axis_size("dp")
    S = jax.ShapeDtypeStruct
    full = 2 * half
    outs = (S((T, W), BF16), S((T, W), BF16), S((1, W), F32), S(small.shape, BF16), S((n, half), F32), S((n, half), F32), S((n, full), F32))
    anyspace = pl.BlockSpec(memory_space=pl.ANY)
    vmem = pl.BlockSpec(memory_space=pltpu.VMEM)
    V, DMA = pltpu.VMEM, pltpu.SemaphoreType.DMA
    return pl.pallas_call(
        tail_kernel,
        out_shape=outs,
        in_specs=[anyspace] * 11 + [vmem] * 4,
        out_specs=[vmem] * 7,
        scratch_shapes=[
            *piece_scratch(4, n, half),
            V((T, W), BF16), V((T, W), BF16), V((T, W), BF16), V((T, W), BF16), V((T, W), BF16), V((T, W), BF16),
            V((T, W), F32), V((T, 128), F32), V((T, 128), F32), V((count, 1, W), F32), V((T, W), BF16),
            V((count, T // count, W), BF16), V((count, T // count, W), BF16),
            V((count, T // count, W), BF16), V((count, T // count, W), BF16),
            DMA((6,)), DMA((3,)), DMA((3,)), DMA((2, count)), DMA((2, count)), DMA((count,)), DMA((count,)),
            V(small.shape, BF16)] + [V(small.shape[i:], BF16) for i in range(1, 5)] + [V(small.shape, BF16), DMA((8,)), DMA((8,)),
        ],
        compiler_params=pltpu.CompilerParams(collective_id=1, has_side_effects=True, vmem_limit_bytes=58 << 20),
        cost_estimate=pl.CostEstimate(flops=T * T * D * 4, bytes_accessed=64 << 20, transcendentals=0),
        name="tail",
    )(gout, gz, gx, cout, cz, dn, mx, other, x, dy, small, gain, scale, settle_t, deal)


def head_kernel(tok_ref, cot_ref, gain_ref, deal_ref, settle_ref,
                half_ref, normed_ref, dy_ref, scale_ref, n_own_ref, n_other_ref, d_own_ref, d_other_ref,
                part, send, got, across, n_send, d_send, load, a_send, a_recv, x_send, x_recv, c_send, c_recv):
    me, ten = lax.axis_index("dp"), lax.axis_index("tensor")
    count = lax.axis_size("dp")
    T, W = half_ref.shape
    per = T // count
    L = W // 128
    barrier = pltpu.get_barrier_semaphore()
    greet_dp([(me + p) % count for p in range(1, count)])
    pl.semaphore_signal(barrier, inc=1, device_id={"tensor": 1 - ten}, device_id_type=MESH)
    start = pl.multiple_of(ten * W, 128)
    loads = [pltpu.make_async_copy(src.at[:, pl.ds(start, W)], part.at[n], load.at[n]) for n, src in enumerate((tok_ref, cot_ref))]
    for copy in loads:
        copy.start()

    def deal(n):
        loads[n].wait()
        rows = jnp.dot(deal_ref[...], part[n], preferred_element_type=F32).astype(BF16)
        send[n] = rows.reshape(count, per, W)

    def out(n, p):
        to = (me + p) % count
        return pltpu.make_async_remote_copy(
            src_ref=send.at[n, to], dst_ref=got.at[n, me], send_sem=a_send.at[n, p], recv_sem=a_recv.at[n, p],
            device_id={"dp": to}, device_id_type=MESH)

    def over(n, p):
        at = (me + count - p) % count
        return pltpu.make_async_remote_copy(
            src_ref=(send if p == 0 else got).at[n, at], dst_ref=across.at[n, at], send_sem=x_send.at[n, p],
            recv_sem=x_recv.at[n, p], device_id={"tensor": 1 - ten}, device_id_type=MESH)

    def launch(n):
        for p in range(1, count):
            out(n, p).start()
        over(n, 0).start()
        got[n, me] = send[n, me]

    def forward(n):
        for p in range(1, count):
            out(n, p).wait_recv()
            over(n, p).start()

    def settle(n, source, at):
        rows = jnp.dot(settle_ref[...], source[n].reshape(T, W), preferred_element_type=F32)
        return rows.astype(BF16)

    deal(0)
    pl.semaphore_wait(barrier, count)
    launch(0)
    deal(1)
    forward(0)
    launch(1)
    half_ref[...] = settle(0, got, ten)
    for p in range(count):
        over(0, p).wait_recv()
    part[0] = settle(0, across, 1 - ten)
    core = me % 2

    def norm(i, c):
        at = pl.ds(pl.multiple_of(i * 16, 16), 16)
        mine, other = half_ref[at, :].astype(F32), part[0, at, :].astype(F32)
        square = jnp.sum(mine * mine + other * other, axis=1, keepdims=True)
        scale = lax.rsqrt(square * (0.5 / W) + 1e-05)
        scale_ref[at, :] = jnp.broadcast_to(scale, (16, 128))
        for value, begin in ((mine, start), (other, pl.multiple_of((1 - ten) * W, 128))):
            cols = pl.ds(begin, W)
            normed_ref[at, cols] = (value * scale * gain_ref[:, cols]).astype(BF16)
        return c

    lax.fori_loop(0, T // 16, norm, 0)

    def halves(source, own, other):
        def body(b, c):
            for into, k in ((own, core), (other, 1 - core)):
                into[:, pl.ds(pl.multiple_of(b * 128, 128), 128)] = source[:, pl.ds(pl.multiple_of((2 * b + k) * 128, 128), 128)]
            return c

        lax.fori_loop(0, W // 128, body, 0)

    def swap(n, source, into):
        return pltpu.make_async_remote_copy(
            src_ref=source, dst_ref=into, send_sem=c_send.at[n], recv_sem=c_recv.at[n],
            device_id={"dp": me + 1 - 2 * core}, device_id_type=MESH)

    halves(normed_ref, n_own_ref, n_send)
    first = swap(0, n_send, n_other_ref)
    first.start()
    forward(1)
    dy_ref[:, pl.ds(start, W)] = settle(1, got, ten)
    for p in range(count):
        over(1, p).wait_recv()
    dy_ref[:, pl.ds(pl.multiple_of((1 - ten) * W, 128), W)] = settle(1, across, 1 - ten)
    halves(dy_ref, d_own_ref, d_send)
    second = swap(1, d_send, d_other_ref)
    second.start()
    for copy in (first, second):
        copy.wait_recv()
        copy.wait_send()
    for n in range(2):
        for p in range(count):
            over(n, p).wait_send()
            if p:
                out(n, p).wait_send()


def head_call(tokens, cotangent, gain, deal_t, settle):
    T, D = tokens.shape
    W = D // 2
    count = lax.axis_size("dp")
    S = jax.ShapeDtypeStruct
    V, DMA = pltpu.VMEM, pltpu.SemaphoreType.DMA
    outs = (S((T, W), BF16), S((T, D), BF16), S((T, D), BF16), S((T, 128), F32)) + (S((T, W), BF16),) * 4
    block = V((2, count, T // count, W), BF16)
    vmem = pl.BlockSpec(memory_space=pltpu.VMEM)
    return pl.pallas_call(
        head_kernel,
        out_shape=outs,
        in_specs=[pl.BlockSpec(memory_space=pl.ANY)] * 2 + [vmem] * 3,
        out_specs=[vmem] * len(outs),
        scratch_shapes=[V((2, T, W), BF16), block, block, block, V((T, W), BF16), V((T, W), BF16), DMA((2,)),
                        DMA((2, count)), DMA((2, count)), DMA((2, count)), DMA((2, count)), DMA((2,)), DMA((2,))],
        compiler_params=pltpu.CompilerParams(collective_id=3, has_side_effects=True, vmem_limit_bytes=50 << 20),
        cost_estimate=pl.CostEstimate(flops=T * T * D * 4, bytes_accessed=24 << 20, transcendentals=0),
        name="head",
    )(tokens, cotangent, gain, deal_t, settle)


def mid_kernel(taps, halves, *refs):
    (dproj_ref, mask_ref, own_ref, other_ref, x_ref, wx_ref, wz_ref, xp_ref, cw_ref, cb_ref) = refs[:10]
    du_refs, dz_refs = refs[10:10 + halves], refs[10 + halves:10 + 2 * halves]
    (mixed_ref, gout_ref, gz_ref, eout_ref, ez_ref, dn_ref, gx_ref, gxp_ref, gcw_ref, gcb_ref, mgot_ref, cout_ref, cz_ref,
     fout_ref, fz_ref,
     acc, dconv, low, mixed_s, dix, sib, sends, recvs, core_send, core_recv) = refs[10 + 2 * halves:]
    j, steps = pl.program_id(0), pl.num_programs(0)
    me, ten = lax.axis_index("dp"), lax.axis_index("tensor")
    T, CH = x_ref.shape
    W = mgot_ref.shape[1]
    bit = {name: me // stride % 2 for name, stride in STRIDE.items()}
    peer = {name: me + stride * (1 - 2 * bit[name]) for name, stride in STRIDE.items()}
    per = steps // halves

    def swaps():
        far = pl.ds(pl.multiple_of((1 - ten) * W, 128), W)
        for n, (src, dst, to) in enumerate((
                (mixed_ref.at[:, far], mgot_ref, {"tensor": 1 - ten}),
                (gout_ref.at[:, :, 1 - bit["y"]], cout_ref, {"dp": peer["y"]}),
                (gz_ref.at[:, 1 - bit["near"]], cz_ref, {"dp": peer["near"]}),
                (eout_ref.at[1 - bit["far"]], fout_ref, {"dp": peer["far"]}),
                (ez_ref.at[1 - bit["far"]], fz_ref, {"dp": peer["far"]}))):
            yield pltpu.make_async_remote_copy(src_ref=src, dst_ref=dst, send_sem=sends.at[n], recv_sem=recvs.at[n],
                                               device_id=to, device_id_type=MESH)

    @pl.when(j == 0)
    def _():
        barrier = pltpu.get_barrier_semaphore()
        count = greet_dp([peer[name] for name in STRIDE])
        pl.semaphore_signal(barrier, inc=1, device_id={"tensor": 1 - ten}, device_id_type=MESH)
        pl.semaphore_wait(barrier, count + 1)
        for copy in swaps():
            copy.start()
        acc[...] = jnp.zeros_like(acc)

    dconv[...] = lax.dot_general(dproj_ref[...], xp_ref[...], NT, preferred_element_type=F32)
    for h in range(halves):
        @pl.when(j // per == h)
        def _(h=h):
            acc[...] += lax.dot_general(dz_refs[h][...], wz_ref[...], NT, preferred_element_type=F32)
            dconv[...] += du_refs[h][...]

    def conv(i, c):
        ln = pl.ds(pl.multiple_of(i * 128, 128), 128)
        weight = [cw_ref[taps - 1 - s:taps - s, ln] for s in range(taps)]
        x = x_ref[:, ln]
        mixed = cb_ref[:, ln] + weight[0] * x
        for s in range(1, taps):
            mixed = mixed + weight[s] * (pltpu.roll(x, s, 0) * mask_ref[s - 1])
        gate = jax.nn.sigmoid(mixed)
        low[:, ln] = (mixed * gate).astype(BF16)
        d = dconv[:, ln] * (gate * (1.0 + mixed * (1.0 - gate)))
        gcb_ref[:, ln] = jnp.sum(d, axis=0, keepdims=True)
        gcw_ref[taps - 1:taps, ln] = jnp.sum(d * x, axis=0, keepdims=True)
        back = weight[0] * d
        for s in range(1, taps):
            masked = d * mask_ref[s - 1]
            gcw_ref[taps - 1 - s:taps - s, ln] = jnp.sum(masked * pltpu.roll(x, s, 0), axis=0, keepdims=True)
            back = back + weight[s] * pltpu.roll(masked, T - s, 0)
        dix[j, :, ln] = back.astype(BF16)
        return c

    lax.fori_loop(0, CH // 128, conv, 0)
    over = pltpu.make_async_remote_copy(src_ref=dix.at[j], dst_ref=sib.at[j], send_sem=core_send.at[j],
                                        recv_sem=core_recv.at[j], device_id={"dp": peer["core"]}, device_id_type=MESH)
    over.start()
    acc[...] += lax.dot_general(dix[j], wx_ref[...], NT, preferred_element_type=F32)
    rows = (((0,), (0,)), ((), ()))
    gxp_ref[...] = lax.dot_general(low[...], dproj_ref[...], rows, preferred_element_type=F32)
    over.wait_recv()
    gx_ref[...] = (lax.dot_general(own_ref[...], dix[j], rows, preferred_element_type=F32)
                   + lax.dot_general(other_ref[...], sib[j], rows, preferred_element_type=F32)).astype(BF16)
    over.wait_send()

    @pl.when(j == steps - 1)
    def _():
        dn_ref[...] = acc[...].astype(BF16)
        for copy in swaps():
            copy.wait_recv()
            copy.wait_send()


def mid_call(dproj, masks, own, other, inner_x, w_x, w_z, x_proj, conv_weight, conv_bias, du, dz, mixed, gout, gz, early, CH=512):
    T, C = inner_x.shape
    D = w_x.shape[0]
    W = mixed.shape[1] // 2
    halves = len(du)
    taps = conv_weight.shape[0]
    P_ = dproj.shape[1]
    steps = C // CH
    per = steps // halves
    S = jax.ShapeDtypeStruct
    V, DMA = pltpu.VMEM, pltpu.SemaphoreType.DMA
    const = lambda a: pl.BlockSpec(a.shape, lambda j: (0,) * a.ndim, pipeline_mode=pl.Buffered(1))
    col = lambda a: pl.BlockSpec((a.shape[0], CH), lambda j: (0, j))
    row = lambda a: pl.BlockSpec((CH, a.shape[1]), lambda j: (j, 0))
    part = lambda h: pl.BlockSpec((T, CH), lambda j: (0, jnp.clip(j - h * per, 0, per - 1)))
    anyspace = pl.BlockSpec(memory_space=pl.ANY)
    outs = (S((T, D), BF16), S((own.shape[1], C), BF16), S((C, P_), F32), S((taps, C), F32), S((1, C), F32),
            S((T, W), BF16), S((2, 2) + gout.shape[3:], BF16), S((2, 2) + gz.shape[3:], BF16),
            S(early[0].shape[1:], BF16), S(early[1].shape[1:], BF16))
    return pl.pallas_call(
        functools.partial(mid_kernel, taps, halves),
        grid=(steps,),
        in_specs=[const(dproj), const(masks), const(own), const(other), col(inner_x), col(w_x), col(w_z), row(x_proj),
                  col(conv_weight), col(conv_bias)] + [part(h) for h in range(halves)] * 2 + [anyspace] * 5,
        out_specs=[pl.BlockSpec((T, D), lambda j: (0, 0)), col(outs[1]), row(outs[2]), col(outs[3]), col(outs[4])] + [anyspace] * 5,
        out_shape=outs,
        scratch_shapes=[V((T, D), F32), V((T, CH), F32), V((T, CH), BF16), V((8, 128), F32), V((steps, T, CH), BF16),
                        V((steps, T, CH), BF16), DMA((5,)), DMA((5,)), DMA((steps,)), DMA((steps,))],
        compiler_params=pltpu.CompilerParams(collective_id=4, has_side_effects=True, vmem_limit_bytes=58 << 20,
                                             dimension_semantics=("arbitrary",)),
        cost_estimate=pl.CostEstimate(flops=6 * T * D * C, bytes_accessed=40 << 20, transcendentals=0),
        name="mid",
    )(dproj, masks, own, other, inner_x, w_x, w_z, x_proj, conv_weight, conv_bias, *du, *dz, mixed, gout, gz, *early)


NT = (((1,), (1,)), ((), ()))
PR = 64


def scan_kernel(GR, NS, hosted, *refs):
    if not hosted:
        return scan_body(GR, NS, lambda at: None, *refs)
    ins, outs, own = 14, 10, 18
    refs = list(refs)
    g_refs = [refs.pop(ins), refs.pop(ins)]
    r_refs = [refs.pop(ins + outs), refs.pop(ins + outs)]
    scratch, refs = refs[-7:], refs[:-7]
    pieces = [piece_of(0, g_refs[0], "y", scratch, r_refs[0]), piece_of(1, g_refs[1], "near", scratch, r_refs[1])]
    steps = pl.num_programs(0)
    plan = {(0, "start"): 0, (0, "end"): 1, (1, "end"): 2}

    def host(at):
        for (step, place), stage in plan.items():
            if place != at:
                continue

            @pl.when(pl.program_id(0) == step)
            def _(stage=stage):
                if stage == 0:
                    me = lax.axis_index("dp")
                    peers = [me + STRIDE[n] * (1 - 2 * (me // STRIDE[n] % 2)) for n in ("y", "near", "far")]
                    pl.semaphore_wait(pltpu.get_barrier_semaphore(), greet_dp(peers))
                for piece in pieces:
                    (piece.step1, piece.step2, piece.stop)[stage]()

    return scan_body(GR, NS, host, *refs)


def scan_body(GR, NS, host, rank_ref, dtp_ref, dtb_ref, u_ref, z_ref, dg_ref, skip_ref,
                kb_ref, qb_ref, keep_ref, ksq_ref, qblk_ref, kblk_ref, k2blk_ref,
                gated_ref, diz_ref, du_ref, gskip_ref, gdtb_ref, gdtp_ref,
                drank_ref, sst_ref, dk_ref, dq_ref,
                den_s, step_s, su_s, ds_s, sz_s, y_s, d_s, e_s, h0_s, h1_s, ga_s, gb_s, ma_s, mb_s, dk_s, dq_s):
    T, CH = u_ref.shape
    L = CH // 128
    NG = T // GR
    R = GR * NS
    first, last = pl.program_id(0) == 0, pl.program_id(0) == pl.num_programs(0) - 1
    lanes = [slice(l * 128, (l + 1) * 128) for l in range(L)]
    hist = (h0_s, h1_s)

    @pl.when(first)
    def _():
        for r in (drank_ref, sst_ref, dk_s, dq_s):
            r[...] = jnp.zeros_like(r)
        h1_s[pl.ds(0, R), :] = jnp.zeros((R, CH), BF16)
        gb_s[...] = jnp.zeros_like(gb_s)
        mb_s[...] = jnp.zeros_like(mb_s)

    host("start")
    y_s[...] = jnp.dot(rank_ref[...], dtp_ref[...], preferred_element_type=F32)

    def prologue(r, acc):
        rows = pl.ds(pl.multiple_of(r * PR, PR), PR)
        kq = ksq_ref[rows, :]
        out = []
        for l in range(L):
            ln = lanes[l]
            beta = jax.nn.sigmoid(y_s[rows, ln] + dtb_ref[:, ln])
            den = 1.0 / (1.0 + beta * kq)
            step = beta * den
            den_s[rows, ln] = den
            step_s[rows, ln] = step
            u = u_ref[rows, ln]
            su_s[rows, ln] = step * u
            z = z_ref[rows, ln]
            s = jax.nn.sigmoid(z)
            sz_s[rows, ln] = s
            ds = dg_ref[rows, ln] * (z * s)
            ds_s[rows, ln] = ds
            out.append(acc[l] + jnp.sum(ds * u, axis=0, keepdims=True))
        return tuple(out)

    zrow = tuple(jnp.zeros((1, 128), F32) for _ in range(L))
    gsk = lax.fori_loop(0, T // PR, prologue, zrow)
    for l in range(L):
        gskip_ref[:, lanes[l]] = gsk[l]

    def rows_of(gi):
        return pl.ds(pl.multiple_of(gi * GR, GR), GR)

    def fill(gi, half, h, dst):
        h = list(h)
        base = pl.multiple_of(gi * GR, GR)
        rows = rows_of(gi)
        hb = pl.multiple_of(half * R, R)
        for j in range(GR):
            k = kb_ref[pl.ds(base * NS + j * NS, NS), :]
            kp = keep_ref.at[rows][j:j + 1, :]
            k2 = k * k * kp
            for l in range(L):
                a = kp - k2 * step_s.at[rows][j:j + 1, lanes[l]]
                h[l] = a * h[l] + k * su_s.at[rows][j:j + 1, lanes[l]]
                dst[pl.ds(hb + j * NS, NS), lanes[l]] = h[l].astype(BF16)
        return tuple(h)

    def read(gi, half, src):
        y_s[rows_of(gi), :] = jnp.dot(qblk_ref[rows_of(gi), :], src[pl.ds(pl.multiple_of(half * R, R), R), :],
                                      preferred_element_type=F32)

    def forward(i, h):
        before = jnp.maximum(i - 1, 0)
        read(2 * before + 1, before, h1_s)
        h = fill(2 * i, i, h, h0_s)
        read(2 * i, i, h0_s)
        return fill(2 * i + 1, i, h, h1_s)

    zst = tuple(jnp.zeros((NS, 128), F32) for _ in range(L))
    lax.fori_loop(0, NG // 2, forward, zst)
    read(NG - 1, NG // 2 - 1, h1_s)

    host("middle")

    def middle(r, c):
        rows = pl.ds(pl.multiple_of(r * PR, PR), PR)
        for l in range(L):
            ln = lanes[l]
            z = z_ref[rows, ln]
            s = sz_s[rows, ln]
            v = y_s[rows, ln] + skip_ref[:, ln] * u_ref[rows, ln]
            gated_ref[rows, ln] = (v * (z * s)).astype(BF16)
            diz_ref[rows, ln] = (dg_ref[rows, ln] * v * s * (1.0 + z * (1.0 - s))).astype(BF16)
        return c

    lax.fori_loop(0, T // PR, middle, 0)

    def back(gi, half, gc, own, before, before_at, g_dst, m_dst):
        gc = list(gc)
        base = pl.multiple_of(gi * GR, GR)
        rows = rows_of(gi)
        hb = pl.multiple_of(half * R, R)
        nows = [own[pl.ds(hb + (GR - 1) * NS, NS), ln] for ln in lanes]
        for j in reversed(range(GR)):
            at = pl.ds(base * NS + j * NS, NS)
            k = kb_ref[at, :]
            q = qb_ref[at, :]
            kp = keep_ref.at[rows][j:j + 1, :]
            k2 = k * k * kp
            a_sum = b_sum = q_sum = None
            for l in range(L):
                ln = lanes[l]
                ds = ds_s.at[rows][j:j + 1, ln]
                g = gc[l] + q * ds
                gb = g.astype(BF16)
                step = step_s.at[rows][j:j + 1, ln]
                now = nows[l]
                if j:
                    prev = own[pl.ds(hb + (j - 1) * NS, NS), ln]
                else:
                    prev = before[pl.ds(before_at + (GR - 1) * NS, NS), ln]
                nows[l] = prev
                m = gb * prev
                g_dst[j * NS:(j + 1) * NS, ln] = gb
                m_dst[j * NS:(j + 1) * NS, ln] = m
                wide = lambda v: jnp.broadcast_to(v, (NS, 128)).astype(BF16)
                pa = gb * wide(su_s.at[rows][j:j + 1, ln])
                pb = m * wide(step)
                pq = now * wide(ds)
                a_sum = pa if a_sum is None else a_sum + pa
                b_sum = pb if b_sum is None else b_sum + pb
                q_sum = pq if q_sum is None else q_sum + pq
                gc[l] = (kp - k2 * step) * g
            dk_s[at, :] += a_sum.astype(F32) - (2.0 * k * kp) * b_sum.astype(F32)
            dq_s[at, :] += q_sum.astype(F32)
        return tuple(gc)

    def sums(gi, g_src, m_src):
        rows = rows_of(gi)
        d_s[rows, :] = jnp.dot(kblk_ref[rows, :], g_src[...], preferred_element_type=F32)
        e_s[rows, :] = jnp.dot(k2blk_ref[rows, :], m_src[...], preferred_element_type=F32)

    def backward(i, gc):
        half = NG // 2 - 1 - i
        hi, lo = 2 * half + 1, 2 * half
        sums(jnp.minimum(hi + 1, NG - 1), gb_s, mb_s)
        gc = back(hi, half, gc, h1_s, h0_s, pl.multiple_of(half * R, R), ga_s, ma_s)
        sums(hi, ga_s, ma_s)
        return back(lo, half, gc, h0_s, h1_s, pl.multiple_of(jnp.maximum(half - 1, 0) * R, R), gb_s, mb_s)

    lax.fori_loop(0, NG // 2, backward, zst)
    sums(0, gb_s, mb_s)

    def epilogue(r, acc):
        rows = pl.ds(pl.multiple_of(r * PR, PR), PR)
        kp = keep_ref[rows, :]
        out = []
        ss = sst_ref[rows, :]
        for l in range(L):
            ln = lanes[l]
            step = step_s[rows, ln]
            dsum = d_s[rows, ln]
            dstep = u_ref[rows, ln] * dsum - kp * e_s[rows, ln]
            du_ref[rows, ln] = step * dsum + ds_s[rows, ln] * skip_ref[:, ln]
            t = dstep * step
            ss = ss + t * step
            db = t * (den_s[rows, ln] - step)
            y_s[rows, ln] = db
            out.append(acc[l] + jnp.sum(db, axis=0, keepdims=True))
        sst_ref[rows, :] = ss
        return tuple(out)

    gdb = lax.fori_loop(0, T // PR, epilogue, zrow)
    for l in range(L):
        gdtb_ref[:, lanes[l]] = gdb[l]
    dbl = y_s[...].astype(BF16)
    gdtp_ref[...] = lax.dot_general(rank_ref[...], dbl, (((0,), (0,)), ((), ())), preferred_element_type=F32)
    drank_ref[...] += lax.dot_general(dbl, dtp_ref[...], NT, preferred_element_type=F32)

    host("end")

    @pl.when(last)
    def _():
        ones = jnp.ones((8, 128), BF16)
        for src, dst in ((dk_s, dk_ref), (dq_s, dq_ref)):
            for c in range(0, T * NS, 1024):
                dst[:, c:c + 1024] = lax.dot_general(ones, src[c:c + 1024, :].astype(BF16), NT, preferred_element_type=F32)


def scan_call(piece, pieces, hosted, *args, CH=512, GR=16, NS=16):
    rank, dtp, dtb, u, z, dg, skip, kb, qb, keep, ksq, qblk, kblk, k2blk = args
    T, C = u.shape
    width = C // pieces
    CH = min(CH, width)
    first = piece * (width // CH)
    const = lambda a: pl.BlockSpec(a.shape, lambda j: (0,) * a.ndim, pipeline_mode=pl.Buffered(1))
    oconst = lambda a: pl.BlockSpec(a.shape, lambda j: (0,) * a.ndim)
    col = lambda a: pl.BlockSpec((a.shape[0], CH), lambda j: (0, j + first))
    out = lambda a: pl.BlockSpec((a.shape[0], CH), lambda j: (0, j))
    S = jax.ShapeDtypeStruct
    W = GR * NS
    R = rank.shape[1]
    outs = (S((T, width), BF16), S((T, width), BF16), S((T, width), F32), S((1, width), F32), S((1, width), F32), S((R, width), F32),
            S((T, R), F32), S((T, 128), F32), S((8, T * NS), F32), S((8, T * NS), F32))
    outs += tuple(S((2,) + g.shape[3:], BF16) for g in hosted)
    V = pltpu.VMEM
    f = pl.pallas_call(
        functools.partial(scan_kernel, GR, NS, bool(hosted)),
        grid=(width // CH,),
        in_specs=[const(rank), col(dtp), col(dtb), col(u), col(z), col(dg), col(skip), const(kb), const(qb),
                  const(keep), const(ksq), const(qblk), const(kblk), const(k2blk)] + [pl.BlockSpec(memory_space=pl.ANY)] * len(hosted),
        out_specs=[out(o) for o in outs[:6]] + [oconst(o) for o in outs[6:]],
        out_shape=outs,
        scratch_shapes=[V((T, CH), F32)] * 8 + [V((T * NS // 2, CH), BF16)] * 2 + [V((W, CH), BF16)] * 4 + [V((T * NS, 128), F32)] * 2
        + (piece_scratch(2, *hosted[0].shape[3:]) if hosted else []),
        compiler_params=pltpu.CompilerParams(vmem_limit_bytes=60 << 20, dimension_semantics=("arbitrary",),
                                             **(dict(collective_id=2, has_side_effects=True) if hosted else {})),
        cost_estimate=pl.CostEstimate(flops=T * width * NS * 800, bytes_accessed=T * width * 20, transcendentals=0),
        name="scan_reduce" if hosted else "scan",
    )
    return f(*args, *hosted)


def scan_all(rank, dtp, dtb, u, z, dg, skip, keys, query, keep, pieces, GR=16, **kw):
    T, NS = keys.shape
    kb = jnp.broadcast_to(keys[:, :, None], (T, NS, 128)).reshape(T * NS, 128)
    qb = jnp.broadcast_to(query[:, :, None], (T, NS, 128)).reshape(T * NS, 128)
    keepb = jnp.broadcast_to(keep[:, None], (T, 128))
    ksq = jnp.sum(keys * keys, axis=1)
    ksqb = jnp.broadcast_to(ksq[:, None], (T, 128))
    slot = (jnp.arange(T)[:, None] % GR == jnp.arange(GR * NS)[None, :] // NS).astype(F32)
    blk = lambda v: (slot * jnp.tile(v, (1, GR))).astype(BF16)
    qblk, kblk, k2blk = blk(query), blk(keys), blk(keys * keys)

    def run(piece, *hosted):
        o = scan_call(piece, pieces, hosted, rank, dtp, dtb, u, z, dg, skip, kb, qb, keepb, ksqb, qblk, kblk, k2blk, GR=GR, NS=NS, **kw)
        gated, diz, du, gskip, gdtb, gdtp, drank, sst, dk, dq, *summed = o
        dq = dq[0].reshape(T, NS)
        dk = dk[0].reshape(T, NS) - 2.0 * keys * jnp.sum(sst, axis=1, keepdims=True)
        return gated, diz, du, gskip, gdtb, gdtp, drank, dk, dq, summed

    return run


def tensor_other(value):
    return lax.ppermute(value, "tensor", [(0, 1), (1, 0)])


def tensor_total(value):
    if lax.axis_size("tensor") == 2:
        return value + tensor_other(value)
    return lax.psum(value, "tensor")


def half_total(value, me, width):
    if lax.axis_size("tensor") == 2:
        own = lax.dynamic_slice_in_dim(value, me * width, width, 1)
        sent = lax.dynamic_slice_in_dim(value, (1 - me) * width, width, 1).astype(BF16)
        return own + tensor_other(sent).astype(F32)
    return lax.psum_scatter(value, "tensor", scatter_dimension=1, tiled=True)


def full_columns(part, me):
    if lax.axis_size("tensor") == 2:
        other = tensor_other(part)
        return jnp.where(
            me == 0,
            jnp.concatenate([part, other], 1),
            jnp.concatenate([other, part], 1),
        )
    return lax.all_gather(part, "tensor", axis=1, tiled=True)


def pair_up(value, stride):
    count = lax.axis_size("dp")
    return lax.ppermute(value, "dp", [(i, i ^ stride) for i in range(count)])


def pick_dim(value, index, dim):
    return lax.dynamic_index_in_dim(value, index, dim, keepdims=False)


def pair_gradient(own, other, right):
    return (contract_rows(own, right) + contract_rows(other, pair_up(right, 1))).astype(BF16)


def after(value, *earlier):
    return lax.optimization_barrier((value,) + earlier)[0]


def flatten(values):
    return jnp.concatenate([v.reshape(-1) for v in values])


def cut(flat, values):
    out, at = [], 0
    for v in values:
        out.append(flat[at : at + v.size].reshape(v.shape))
        at += v.size
    return out


def position_in(keys):
    return jnp.sum((keys[None, :] < keys[:, None]).astype(jnp.int32), axis=1)


def conv_mix(inner_x, conv_weight, conv_bias, segment):
    row_count = inner_x.shape[0]
    taps = conv_weight.shape[0]
    mixed = conv_bias[None, :] + conv_weight[taps - 1][None, :] * inner_x
    for shift_by in range(1, taps):
        moved = jnp.concatenate([jnp.zeros((shift_by, inner_x.shape[1]), F32), inner_x[: row_count - shift_by]], 0)
        seg_moved = jnp.concatenate([jnp.full((shift_by,), -1, jnp.int32), segment[: row_count - shift_by]], 0)
        keep_mask = (seg_moved == segment).astype(F32)
        mixed = mixed + conv_weight[taps - 1 - shift_by][None, :] * moved * keep_mask[:, None]
    return mixed


def silu_conv(inner_x, conv_weight, conv_bias, segment):
    mixed = conv_mix(inner_x, conv_weight, conv_bias, segment)
    return mixed * jax.nn.sigmoid(mixed)


def contract_rows(left, right):
    return lax.dot_general(left, right, (((0,), (0,)), ((), ())), preferred_element_type=F32)


def contract_cols(left, right):
    return lax.dot_general(left, right, (((1,), (1,)), ((), ())), preferred_element_type=F32)


def body(tokens, cotangent, norm_gain, w_x, w_z, conv_weight, conv_bias, x_proj, dt_proj, dt_bias, skip_gain, w_out,
         seq_lengths, arrival_route, work_source):
    dp_count = lax.axis_size("dp")
    tp_count = lax.axis_size("tensor")
    row_count, feat_width = tokens.shape
    per_peer = row_count // dp_count
    col_share = feat_width // tp_count
    me = lax.axis_index("tensor")
    col_start = me * col_share
    low_rank = dt_proj.shape[0]
    state_size = (x_proj.shape[1] - low_rank) // 2
    position = jnp.arange(row_count, dtype=jnp.int32)

    deal = (position_in(arrival_route)[:, None] == position[None, :]).astype(BF16)
    settle = (position_in(work_source // row_count * row_count + position)[:, None] == position[None, :]).astype(BF16)

    def exchange(rows):
        out = lax.all_to_all(rows.reshape(dp_count, per_peer, rows.shape[1]), "dp", split_axis=0, concat_axis=0, tiled=True)
        return out.reshape(row_count, rows.shape[1])

    def pick(table, rows, dim):
        return lax.dot_general(table, rows, (((dim,), (0,)), ((), ())), preferred_element_type=F32).astype(BF16)

    def bring(values):
        part = lax.dynamic_slice_in_dim(values, col_start, col_share, 1)
        return full_columns(pick(settle, exchange(pick(deal, part, 0)), 1), me)

    def give_back(values):
        return pick(deal, exchange(pick(settle, values, 0)), 1)

    paired = dp_count == 16 and tp_count == 2
    if paired:
        x_half, normed, dy_work, scale_wide, normed_own, normed_other, dy_own, dy_other = head_call(
            tokens, cotangent, norm_gain[None, :], deal.T, settle)
    else:
        x_work = bring(tokens)
        dy_work = bring(cotangent)
        resid = x_work.astype(F32)
        scale_row = lax.rsqrt(jnp.mean(resid * resid, axis=1, keepdims=True) + 1e-05)
        unit = resid * scale_row
        normed = (unit * norm_gain[None, :]).astype(BF16)

    lengths = seq_lengths[0]
    count = lengths.shape[0]
    before = jnp.arange(count)[:, None] > jnp.arange(count)[None, :]
    offsets = jnp.sum(jnp.where(before, lengths[None, :], 0), axis=1)
    segment = jnp.sum((position[:, None] >= offsets[None, :]).astype(jnp.int32), axis=1) - 1
    keep = 1.0 - jnp.any(position[:, None] == offsets[None, :], axis=1).astype(F32)

    inner_x = jnp.dot(normed, w_x, preferred_element_type=F32)
    inner_z = jnp.dot(normed, w_z, preferred_element_type=F32)
    conv_out, conv_pull = jax.vjp(partial(silu_conv, segment=segment), inner_x, conv_weight, conv_bias)
    conv_low = conv_out.astype(BF16)
    projected = tensor_total(jnp.dot(conv_low, x_proj, preferred_element_type=F32))
    rank_part = projected[:, :low_rank].astype(BF16)
    key_rows = projected[:, low_rank : low_rank + state_size]
    query_rows = projected[:, low_rank + state_size :]

    d_gated = contract_cols(dy_work, w_out)
    pieces = 2 if paired else 1
    scan = scan_all(rank_part, dt_proj, dt_bias[None, :], conv_out, inner_z, d_gated, skip_gain[None, :], key_rows,
                    query_rows, keep, pieces)
    scans = [scan(0)]
    if paired:
        blocks = lambda g: g.reshape(2, 2, 2, g.shape[0] // 8, g.shape[1])
        outer = lambda part: (blocks(pair_gradient(dy_own, dy_other, part[0])),
                              blocks(pair_gradient(normed_own, normed_other, part[1])))
        scans.append(scan(1, *outer(scans[0])))
    wide = lambda index: jnp.concatenate([part[index] for part in scans], axis=1) if paired else scans[0][index]
    grad_dt_proj = wide(5)
    grad_skip, grad_dt_bias = wide(3)[0], wide(4)[0]
    d_rank, d_keys, d_query = (sum(part[index] for part in scans) for index in (6, 7, 8))
    gated_low, d_inner_z_low = wide(0), wide(1)
    d_proj = tensor_total(jnp.concatenate([d_rank, d_keys, d_query], axis=1))
    mixed = jnp.dot(gated_low, w_out, preferred_element_type=F32)
    if paired:
        mixed = mixed.astype(BF16)
        g_out, g_z = outer(scans[1])
        bit = {name: lax.axis_index("dp") // stride % 2 for name, stride in STRIDE.items()}
        d_proj = after(d_proj, g_out, g_z, mixed)
        taps = conv_weight.shape[0]
        pre = [jnp.concatenate([jnp.full((s,), -1, jnp.int32), segment[: row_count - s]]) for s in range(1, taps)]
        masks = jnp.stack([jnp.broadcast_to((p == segment).astype(F32)[:, None], (row_count, 128)) for p in pre])
        d_normed, g_x, grad_x_proj, grad_conv_weight, grad_conv_bias, mixed_other, came_out, came_z, *far = mid_call(
            d_proj.astype(BF16), masks, normed_own, normed_other, inner_x, w_x, w_z, x_proj, conv_weight,
            conv_bias[None, :], [part[2] for part in scans], [part[1] for part in scans], mixed, g_out, g_z,
            scans[1][9])
        grad_conv_bias = grad_conv_bias[0]
        early = [pick_dim(v, bit["far"], 0).astype(F32) + came.astype(F32) for v, came in zip(scans[1][9], far)]
    else:
        d_proj_low = d_proj.astype(BF16)
        grad_x_proj = contract_rows(conv_low, d_proj_low)
        d_conv_out = scans[0][2] + contract_cols(d_proj_low, x_proj)
        d_inner_x, grad_conv_weight, grad_conv_bias = conv_pull(d_conv_out)
        d_inner_x_low = d_inner_x.astype(BF16)
        d_normed = contract_cols(d_inner_x_low, w_x) + contract_cols(d_inner_z_low, w_z)
    small = (grad_x_proj, grad_dt_proj, grad_dt_bias, grad_skip, grad_conv_weight, grad_conv_bias)
    if paired:
        g_x = blocks(g_x)
        flat = jnp.concatenate([v.astype(BF16).reshape(-1, 128) for v in small])
        deep = -(-flat.shape[0] // 256) * 16
        flat = jnp.pad(flat, ((0, 16 * deep - flat.shape[0]), (0, 0))).reshape(2, 2, 2, 2, deep, 128)
        out_tokens, in_grad, grad_gain, flat, grad_w_out, grad_w_z, grad_w_x = tail_call(
            g_out, g_z, g_x, came_out, came_z, d_normed, mixed, mixed_other, x_half, dy_work, flat, norm_gain[None, :],
            scale_wide, settle.T, deal)
        grad_gain = grad_gain[0]
        early_out, early_z = early
        grad_w_out = jnp.concatenate([early_out, grad_w_out], axis=1).T
        grad_w_z = jnp.concatenate([early_z, grad_w_z], axis=1)
        small = cut(flat.astype(F32).reshape(-1), small)
    else:
        unit_cols = lax.dynamic_slice_in_dim(unit, col_start, col_share, 1)
        gain_cols = lax.dynamic_slice_in_dim(norm_gain, col_start, col_share, 0)
        dy_cols = lax.dynamic_slice_in_dim(dy_work, col_start, col_share, 1).astype(F32)
        d_share = half_total(d_normed, me, col_share)
        d_unit_cols = d_share * gain_cols[None, :]
        row_total = tensor_total(jnp.sum(d_unit_cols * unit_cols, axis=1, keepdims=True))
        grad_gain = jnp.sum(d_share * unit_cols, axis=0)
        d_resid = dy_cols + scale_row * (d_unit_cols - unit_cols * (row_total / feat_width))
        mixed_share = half_total(mixed, me, col_share)
        out_cols = (lax.dynamic_slice_in_dim(resid, col_start, col_share, 1) + mixed_share).astype(BF16)
        out_tokens, in_grad = give_back(out_cols), give_back(d_resid.astype(BF16))
        grad_w_out, grad_w_z, grad_w_x = (
            lax.psum_scatter(g.astype(BF16), "dp", scatter_dimension=dim, tiled=True).astype(F32)
            for g, dim in ((contract_rows(gated_low, dy_work), 1), (contract_rows(normed, d_inner_z_low), 0),
                           (contract_rows(normed, d_inner_x_low), 0)))
        small += (grad_gain,)
        *small, grad_gain = cut(lax.psum(flatten(small), "dp"), small)
    grad_x_proj, grad_dt_proj, grad_dt_bias, grad_skip, grad_conv_weight, grad_conv_bias = small
    return (out_tokens, in_grad, grad_gain, grad_w_x, grad_w_z, grad_conv_weight, grad_conv_bias, grad_x_proj,
            grad_dt_proj, grad_dt_bias, grad_skip, grad_w_out)


def solution(mesh):
    in_specs = (
        P("dp", None),
        P("dp", None),
        P(),
        P(None, "tensor"),
        P(None, "tensor"),
        P(None, "tensor"),
        P("tensor"),
        P("tensor", None),
        P(None, "tensor"),
        P("tensor"),
        P("tensor"),
        P("tensor", None),
        P("dp", None),
        P("dp"),
        P("dp"),
    )
    out_specs = (
        P("dp", "tensor"),
        P("dp", "tensor"),
        P("tensor"),
        P("dp", "tensor"),
        P("dp", "tensor"),
        P(None, "tensor"),
        P("tensor"),
        P("tensor", None),
        P(None, "tensor"),
        P("tensor"),
        P("tensor"),
        P("tensor", "dp"),
    )
    return jax.shard_map(body, mesh=mesh, in_specs=in_specs, out_specs=out_specs, check_vma=False)
```

```python
import functools
from functools import partial

import jax
import jax.numpy as jnp
import numpy as np
from jax import lax
from jax.experimental import pallas as pl
from jax.experimental.pallas import tpu as pltpu
from jax.sharding import PartitionSpec as P

F32, BF16 = jnp.float32, jnp.bfloat16
MESH = pl.DeviceIdType.MESH
TILE = 32
GAIN_ROW = 5
STRIDE = {"core": 1, "y": 2, "near": 4, "far": 8}


class Piece:
    def __init__(self, grad, first, bufs, sems, result):
        self.grad, self.first, self.result = grad, first, result
        self.own, self.r1, self.r2, self.r3 = bufs
        self.local, self.send, self.recv = sems
        self.second = "near" if first == "y" else "y"

    def bit(self, name):
        return lax.axis_index("dp") // STRIDE[name] % 2

    def block(self, mine):
        return self.grad.at[:, :, mine] if self.first == "y" else self.grad.at[:, mine]

    def remote(self, step):
        s, f = self.bit(self.second), self.bit("far")
        name, src, dst = (
            (self.first, lambda: self.block(1 - self.bit(self.first)), self.r1),
            (self.second, lambda: self.own.at[:, 1 - s], self.r2),
            ("far", lambda: self.own.at[1 - f, s], self.r3),
        )[step]
        to = lax.axis_index("dp") + STRIDE[name] * (1 - 2 * self.bit(name))
        return pltpu.make_async_remote_copy(
            src_ref=src(), dst_ref=dst, send_sem=self.send.at[step], recv_sem=self.recv.at[step],
            device_id={"dp": to}, device_id_type=MESH)

    def load(self):
        return pltpu.make_async_copy(self.block(self.bit(self.first)), self.own, self.local)

    def step1(self):
        self.remote(0).start()
        self.load().start()

    def add(self, dst, src, out=None):
        def body(i, c):
            at = pl.ds(pl.multiple_of(i * TILE, TILE), TILE)
            total = dst[at, :].astype(F32) + src[at, :].astype(F32)
            if out is None:
                dst[at, :] = total.astype(BF16)
            else:
                out[at, :] = total.astype(out.dtype)
            return c

        lax.fori_loop(0, src.shape[0] // TILE, body, 0)

    def step2(self):
        self.load().wait()
        self.remote(0).wait_recv()
        s = self.bit(self.second)
        for far in range(2):
            self.add(self.own.at[far, 1 - s], self.r1.at[far, 1 - s])
        self.remote(1).start()
        for far in range(2):
            self.add(self.own.at[far, s], self.r1.at[far, s])

    def step3(self):
        self.remote(1).wait_recv()
        s, f = self.bit(self.second), self.bit("far")
        self.add(self.own.at[1 - f, s], self.r2.at[1 - f])
        self.remote(2).start()
        self.add(self.own.at[f, s], self.r2.at[f])

    def stop(self):
        self.remote(1).wait_recv()
        for far in range(2):
            self.add(self.own.at[far, self.bit(self.second)], self.r2.at[far], self.result.at[far])
        for step in range(2):
            self.remote(step).wait_send()

    def finish(self):
        self.remote(2).wait_recv()
        self.add(self.own.at[self.bit("far"), self.bit(self.second)], self.r3, self.result)
        for step in range(3):
            self.remote(step).wait_send()


class FarPiece(Piece):
    def __init__(self, grad, bufs, sems, result):
        self.grad, self.result = grad, result
        self.own, self.r3 = bufs
        self.local, self.send, self.recv = sems

    def remote(self, step):
        f = self.bit("far")
        return pltpu.make_async_remote_copy(
            src_ref=self.grad.at[1 - f], dst_ref=self.r3, send_sem=self.send, recv_sem=self.recv,
            device_id={"dp": lax.axis_index("dp") + STRIDE["far"] * (1 - 2 * f)}, device_id_type=MESH)

    def load(self):
        return pltpu.make_async_copy(self.grad.at[self.bit("far")], self.own, self.local)

    def finish(self):
        self.load().wait()
        self.remote(0).wait_recv()
        self.add(self.own, self.r3, self.result)
        self.remote(0).wait_send()


def piece_scratch(k, n, w):
    V, DMA = pltpu.VMEM, pltpu.SemaphoreType.DMA
    return [V((k, 2, 2, n, w), BF16), V((k, 2, 2, n, w), BF16), V((k, 2, n, w), BF16), V((k, n, w), BF16),
            DMA((k,)), DMA((k, 3)), DMA((k, 3))]


def piece_of(i, grad, first, scratch, result):
    return Piece(grad, first, tuple(r.at[i] for r in scratch[:4]), tuple(r.at[i] for r in scratch[4:]), result)


def greet_dp(peers):
    for p in peers:
        pl.semaphore_signal(pltpu.get_barrier_semaphore(), inc=1, device_id={"dp": p}, device_id_type=MESH)
    return len(peers)


class Total:
    NAMES = ("y", "near", "far")

    def __init__(self, acc, half, got, out, sems):
        self.acc, self.half, self.got, self.out, self.sems = acc, half, got, out, sems
        self.me = lax.axis_index("dp")
        self.bits = {name: self.me // stride % 2 for name, stride in STRIDE.items()}

    def flip(self, q):
        path, to = [self.bits["core"]], self.me
        for n, name in enumerate(self.NAMES):
            bit, turn = self.bits[name], q >> n & 1
            path.append(1 - bit if turn else bit)
            if turn:
                to = to + STRIDE[name] * (1 - 2 * bit)
        return tuple(path), to

    def copies(self, stage):
        mine, core = self.flip(0)[0], self.bits["core"]
        other = self.me + 1 - 2 * core
        if stage == 0:
            jobs = [(0, self.acc.at[1 - core], self.half, other)]
        elif stage == 1:
            jobs = [(q, self.acc.at[self.flip(q)[0]], self.got.at[q], self.flip(q)[1]) for q in range(1, 8)]
        elif stage == 2:
            jobs = [(q, self.out.at[mine], self.out.at[mine], self.flip(q)[1]) for q in range(1, 8)]
        else:
            jobs = [(0, self.out.at[core], self.out.at[core], other)]
        return [pltpu.make_async_remote_copy(
            src_ref=src, dst_ref=dst, send_sem=self.sems[0].at[stage, q], recv_sem=self.sems[1].at[stage, q],
            device_id={"dp": to}, device_id_type=MESH) for q, src, dst, to in jobs]

    def step(self, i):
        if i:
            for copy in self.copies(i - 1):
                copy.wait_recv()
        if i == 1:
            for b in range(8):
                at = (b // 4, b // 2 % 2, b % 2)
                here = self.acc.at[(self.bits["core"],) + at]
                here[...] = (here[...].astype(F32) + self.half[at].astype(F32)).astype(BF16)
        if i == 2:
            mine = self.flip(0)[0]
            total = self.acc[mine].astype(F32)
            for q in range(1, 8):
                total = total + self.got[q].astype(F32)
            self.out[mine] = total.astype(BF16)
        if i < 4:
            for copy in self.copies(i):
                copy.start()
        else:
            for stage in range(4):
                for copy in self.copies(stage):
                    copy.wait_send()


def sixteenth(b):
    return b // 8, b // 4 % 2, b // 2 % 2, b % 2


def total_scratch(rows):
    V, DMA = pltpu.VMEM, pltpu.SemaphoreType.DMA
    full = (2, 2, 2, 2, rows, 128)
    return [V(full, BF16), V(full[1:], BF16), V((8, rows, 128), BF16), V(full, BF16), DMA((4, 8)), DMA((4, 8)), DMA((16,))]


def tail_kernel(gout_ref, gz_ref, gx_ref, dn_ref, mx_ref, other_ref, x_ref, dy_ref, conv_ref, gain_ref, scale_ref, settle_ref, deal_ref,
                out_ref, in_ref, gg_ref, csum_ref, wout_ref, wz_ref, wx_ref,
                p0, p1, p2, p3, p4, p5, p6,
                dn_own, dn_got, mx_own, mx_got, x_half, dy_half, du, rs_own, rs_got, low,
                y_send, y_got, d_send, d_got, sem, x_send, x_recv, a_send, a_recv,
                m_part, m_got, m_out, m_send, m_recv,
                f_own, f_got, f_sem):
    me, ten = lax.axis_index("dp"), lax.axis_index("tensor")
    count = lax.axis_size("dp")
    T, W = x_half.shape
    L = W // 128
    per = T // count
    barrier = pltpu.get_barrier_semaphore()
    for p in range(1, count):
        pl.semaphore_signal(barrier, inc=1, device_id={"dp": (me + p) % count}, device_id_type=MESH)
    pl.semaphore_signal(barrier, inc=1, device_id={"tensor": 1 - ten}, device_id_type=MESH)
    mine = pl.ds(pl.multiple_of(ten * W, 128), W)
    other = pl.ds(pl.multiple_of((1 - ten) * W, 128), W)
    loads = []
    jobs = [(mx_ref.at[:, mine], mx_own), (other_ref, mx_got), (x_ref, x_half), (dn_ref.at[:, mine], dn_own),
            (dy_ref.at[:, mine], dy_half)]
    for b in range(count):
        jobs.append((conv_ref.at[:, b * 128 : (b + 1) * 128], m_part.at[b]))
    for n, (src, dst) in enumerate(jobs):
        copy = pltpu.make_async_copy(src, dst, sem.at[n])
        copy.start()
        loads.append(copy)
    pl.semaphore_wait(barrier, count)

    def swap(src, dst, n):
        copy = pltpu.make_async_remote_copy(
            src_ref=src, dst_ref=dst, send_sem=x_send.at[n], recv_sem=x_recv.at[n],
            device_id={"tensor": 1 - ten}, device_id_type=MESH)
        copy.start()
        return copy

    dn_copy = swap(dn_ref.at[:, other], dn_got, 0)
    bits = {"core": me % 2, "y": me // 2 % 2, "near": me // 4 % 2, "far": me // 8}
    half = gout_ref.shape[-1]
    scratch = (p0, p1, p2, p3, p4, p5, p6)
    x_cols = [slice(0, half), slice(half, 2 * half)]
    pieces = [
        FarPiece(gout_ref, (f_own.at[0], f_got.at[0]), tuple(f_sem.at[0, n] for n in range(3)), wout_ref),
        FarPiece(gz_ref, (f_own.at[1], f_got.at[1]), tuple(f_sem.at[1, n] for n in range(3)), wz_ref),
        piece_of(0, gx_ref.at[:, :, :, :, x_cols[0]], "y", scratch, wx_ref.at[:, x_cols[0]]),
        piece_of(1, gx_ref.at[:, :, :, :, x_cols[1]], "near", scratch, wx_ref.at[:, x_cols[1]]),
    ]
    for piece in (pieces[2], pieces[3], pieces[0], pieces[1]):
        piece.step1()
    for copy in loads:
        copy.wait()
    def small(stage, p):
        to = (me + p) % count
        src, dst = ((m_part.at[to], m_got.at[me]), (m_out.at[me], m_out.at[me]))[stage]
        return pltpu.make_async_remote_copy(
            src_ref=src, dst_ref=dst, send_sem=m_send.at[stage, p], recv_sem=m_recv.at[stage, p],
            device_id={"dp": to}, device_id_type=MESH)

    def tiles(body, init):
        def step(i, c):
            return body(pl.ds(pl.multiple_of(i * 16, 16), 16), c)
        return lax.fori_loop(0, T // 16, step, init)

    def add_resid(at, c):
        for l in range(L):
            ln = slice(l * 128, (l + 1) * 128)
            both = mx_own[at, ln].astype(F32) + mx_got[at, ln].astype(F32)
            mx_own[at, ln] = (x_half[at, ln].astype(F32) + both).astype(BF16)
        return c

    def deal_out(rows, send, got, n):
        sent = jnp.dot(settle_ref[...], rows[...], preferred_element_type=F32).astype(BF16)
        send[...] = sent.reshape(send.shape)
        got[me] = send[me]
        copies = []
        for p in range(1, count):
            to = (me + p) % count
            copy = pltpu.make_async_remote_copy(
                src_ref=send.at[to], dst_ref=got.at[me], send_sem=a_send.at[n, p], recv_sem=a_recv.at[n, p],
                device_id={"dp": to}, device_id_type=MESH)
            copy.start()
            copies.append(copy)
        return copies

    def take_in(copies, got, out):
        for copy in copies:
            copy.wait_recv()
        out[...] = jnp.dot(deal_ref[...], got[...].reshape(T, W), preferred_element_type=F32).astype(BF16)
        for copy in copies:
            copy.wait_send()

    tiles(add_resid, 0)
    y_copies = deal_out(mx_own, y_send, y_got, 1)

    dn_copy.wait_recv()
    gain = gain_ref[:, mine]

    def share(at, acc):
        scale = scale_ref[at, :]
        total = None
        out = []
        for l in range(L):
            ln = slice(l * 128, (l + 1) * 128)
            d = dn_own[at, ln].astype(F32) + dn_got[at, ln].astype(F32)
            unit = x_half[at, ln].astype(F32) * scale
            d_unit = d * gain[:, ln]
            du[at, ln] = d_unit
            out.append(acc[l] + jnp.sum(d * unit, axis=0, keepdims=True))
            total = d_unit * unit if total is None else total + d_unit * unit
        rs_own[at, :] = total
        return tuple(out)

    acc = tiles(share, tuple(jnp.zeros((1, 128), F32) for _ in range(L)))
    rs_copy = swap(rs_own, rs_got, 2)
    for l in range(L):
        m_part[l, GAIN_ROW : GAIN_ROW + 1, :] = acc[l]
    for p in range(1, count):
        small(0, p).start()
    m_got[me] = m_part[me]
    pieces[2].step2()
    pieces[3].step2()
    rs_copy.wait_recv()

    def norm_back(at, c):
        scale = scale_ref[at, :]
        total = jnp.sum(rs_own[at, :] + rs_got[at, :], axis=1, keepdims=True) * (0.5 / W)
        for l in range(L):
            ln = slice(l * 128, (l + 1) * 128)
            unit = x_half[at, ln].astype(F32) * scale
            low[at, ln] = (dy_half[at, ln].astype(F32) + scale * (du[at, ln] - unit * total)).astype(BF16)
        return c

    tiles(norm_back, 0)
    d_copies = deal_out(low, d_send, d_got, 0)
    for p in range(1, count):
        small(0, p).wait_recv()
    m_out[me] = jnp.sum(m_got[...], axis=0)
    for p in range(1, count):
        small(1, p).start()
    pieces[2].step3()
    pieces[3].step3()
    pieces[0].finish()
    pieces[1].finish()
    take_in(y_copies, y_got, out_ref)
    for p in range(1, count):
        small(1, p).wait_recv()
    for b in range(count):
        csum_ref[:, b * 128 : (b + 1) * 128] = m_out[b]
    for l in range(L):
        gg_ref[:, l * 128 : (l + 1) * 128] = m_out[l, GAIN_ROW : GAIN_ROW + 1, :]
    take_in(d_copies, d_got, in_ref)
    pieces[2].finish()
    pieces[3].finish()
    for copy in (dn_copy, rs_copy):
        copy.wait_send()
    for stage in range(2):
        for p in range(1, count):
            small(stage, p).wait_send()


def tail_call(gout, gz, gx, dn, mx, other, x, dy, conv, gain, scale, settle_t, deal):
    T, W = x.shape
    D = 2 * W
    n, half = gout.shape[1:]
    count = lax.axis_size("dp")
    S = jax.ShapeDtypeStruct
    full = 2 * half
    outs = (S((T, W), BF16), S((T, W), BF16), S((1, W), F32), S(conv.shape, F32), S((n, half), F32), S((n, half), F32), S((n, full), F32))
    anyspace = pl.BlockSpec(memory_space=pl.ANY)
    vmem = pl.BlockSpec(memory_space=pltpu.VMEM)
    V, DMA = pltpu.VMEM, pltpu.SemaphoreType.DMA
    return pl.pallas_call(
        tail_kernel,
        out_shape=outs,
        in_specs=[anyspace] * 9 + [vmem] * 4,
        out_specs=[vmem] * 7,
        scratch_shapes=[
            *piece_scratch(2, n, half),
            V((T, W), BF16), V((T, W), BF16), V((T, W), BF16), V((T, W), BF16), V((T, W), BF16), V((T, W), BF16),
            V((T, W), F32), V((T, 128), F32), V((T, 128), F32), V((T, W), BF16),
            V((count, T // count, W), BF16), V((count, T // count, W), BF16),
            V((count, T // count, W), BF16), V((count, T // count, W), BF16),
            DMA((5 + count,)), DMA((3,)), DMA((3,)), DMA((2, count)), DMA((2, count)),
            V((count, 8, 128), F32), V((count, 8, 128), F32), V((count, 8, 128), F32), DMA((2, count)), DMA((2, count)),
            V((2, n, half), BF16), V((2, n, half), BF16), DMA((2, 3)),
        ],
        compiler_params=pltpu.CompilerParams(collective_id=1, has_side_effects=True, vmem_limit_bytes=58 << 20),
        cost_estimate=pl.CostEstimate(flops=T * T * D * 4, bytes_accessed=64 << 20, transcendentals=0),
        name="tail",
    )(gout, gz, gx, dn, mx, other, x, dy, conv, gain, scale, settle_t, deal)


def head_kernel(tok_ref, cot_ref, gain_ref, deal_ref, settle_ref,
                half_ref, normed_ref, dy_ref, scale_ref, n_own_ref, n_other_ref, d_own_ref, d_other_ref,
                part, send, got, across, n_send, d_send, load, a_send, a_recv, x_send, x_recv, c_send, c_recv):
    me, ten = lax.axis_index("dp"), lax.axis_index("tensor")
    count = lax.axis_size("dp")
    T, W = half_ref.shape
    per = T // count
    L = W // 128
    barrier = pltpu.get_barrier_semaphore()
    greet_dp([(me + p) % count for p in range(1, count)])
    pl.semaphore_signal(barrier, inc=1, device_id={"tensor": 1 - ten}, device_id_type=MESH)
    start = pl.multiple_of(ten * W, 128)
    loads = [pltpu.make_async_copy(src.at[:, pl.ds(start, W)], part.at[n], load.at[n]) for n, src in enumerate((tok_ref, cot_ref))]
    for copy in loads:
        copy.start()

    def deal(n):
        loads[n].wait()
        rows = jnp.dot(deal_ref[...], part[n], preferred_element_type=F32).astype(BF16)
        send[n] = rows.reshape(count, per, W)

    def out(n, p):
        to = (me + p) % count
        return pltpu.make_async_remote_copy(
            src_ref=send.at[n, to], dst_ref=got.at[n, me], send_sem=a_send.at[n, p], recv_sem=a_recv.at[n, p],
            device_id={"dp": to}, device_id_type=MESH)

    def over(n, p):
        at = (me + count - p) % count
        return pltpu.make_async_remote_copy(
            src_ref=(send if p == 0 else got).at[n, at], dst_ref=across.at[n, at], send_sem=x_send.at[n, p],
            recv_sem=x_recv.at[n, p], device_id={"tensor": 1 - ten}, device_id_type=MESH)

    def launch(n):
        for p in range(1, count):
            out(n, p).start()
        over(n, 0).start()
        got[n, me] = send[n, me]

    def forward(n):
        for p in range(1, count):
            out(n, p).wait_recv()
            over(n, p).start()

    def settle(n, source, at):
        rows = jnp.dot(settle_ref[...], source[n].reshape(T, W), preferred_element_type=F32)
        return rows.astype(BF16)

    deal(0)
    pl.semaphore_wait(barrier, count)
    launch(0)
    deal(1)
    forward(0)
    launch(1)
    half_ref[...] = settle(0, got, ten)
    for p in range(count):
        over(0, p).wait_recv()
    part[0] = settle(0, across, 1 - ten)
    core = me % 2

    def norm(i, c):
        at = pl.ds(pl.multiple_of(i * 16, 16), 16)
        mine, other = half_ref[at, :].astype(F32), part[0, at, :].astype(F32)
        square = jnp.sum(mine * mine + other * other, axis=1, keepdims=True)
        scale = lax.rsqrt(square * (0.5 / W) + 1e-05)
        scale_ref[at, :] = jnp.broadcast_to(scale, (16, 128))
        for value, begin in ((mine, start), (other, pl.multiple_of((1 - ten) * W, 128))):
            cols = pl.ds(begin, W)
            normed_ref[at, cols] = (value * scale * gain_ref[:, cols]).astype(BF16)
        return c

    lax.fori_loop(0, T // 16, norm, 0)

    def halves(source, own, other):
        def body(b, c):
            for into, k in ((own, core), (other, 1 - core)):
                into[:, pl.ds(pl.multiple_of(b * 128, 128), 128)] = source[:, pl.ds(pl.multiple_of((2 * b + k) * 128, 128), 128)]
            return c

        lax.fori_loop(0, W // 128, body, 0)

    def swap(n, source, into):
        return pltpu.make_async_remote_copy(
            src_ref=source, dst_ref=into, send_sem=c_send.at[n], recv_sem=c_recv.at[n],
            device_id={"dp": me + 1 - 2 * core}, device_id_type=MESH)

    halves(normed_ref, n_own_ref, n_send)
    first = swap(0, n_send, n_other_ref)
    first.start()
    forward(1)
    dy_ref[:, pl.ds(start, W)] = settle(1, got, ten)
    for p in range(count):
        over(1, p).wait_recv()
    dy_ref[:, pl.ds(pl.multiple_of((1 - ten) * W, 128), W)] = settle(1, across, 1 - ten)
    halves(dy_ref, d_own_ref, d_send)
    second = swap(1, d_send, d_other_ref)
    second.start()
    for copy in (first, second):
        copy.wait_recv()
        copy.wait_send()
    for n in range(2):
        for p in range(count):
            over(n, p).wait_send()
            if p:
                out(n, p).wait_send()


def head_call(tokens, cotangent, gain, deal_t, settle):
    T, D = tokens.shape
    W = D // 2
    count = lax.axis_size("dp")
    S = jax.ShapeDtypeStruct
    V, DMA = pltpu.VMEM, pltpu.SemaphoreType.DMA
    outs = (S((T, W), BF16), S((T, D), BF16), S((T, D), BF16), S((T, 128), F32)) + (S((T, W), BF16),) * 4
    block = V((2, count, T // count, W), BF16)
    vmem = pl.BlockSpec(memory_space=pltpu.VMEM)
    return pl.pallas_call(
        head_kernel,
        out_shape=outs,
        in_specs=[pl.BlockSpec(memory_space=pl.ANY)] * 2 + [vmem] * 3,
        out_specs=[vmem] * len(outs),
        scratch_shapes=[V((2, T, W), BF16), block, block, block, V((T, W), BF16), V((T, W), BF16), DMA((2,)),
                        DMA((2, count)), DMA((2, count)), DMA((2, count)), DMA((2, count)), DMA((2,)), DMA((2,))],
        compiler_params=pltpu.CompilerParams(collective_id=3, has_side_effects=True, vmem_limit_bytes=50 << 20),
        cost_estimate=pl.CostEstimate(flops=T * T * D * 4, bytes_accessed=24 << 20, transcendentals=0),
        name="head",
    )(tokens, cotangent, gain, deal_t, settle)


def mid_kernel(taps, halves, count_steps, *refs):
    (dproj_ref, mask_ref, own_ref, other_ref, x_ref, wx_ref, wz_ref, xp_ref, cw_ref, cb_ref) = refs[:10]
    du_refs, dz_refs = refs[10:10 + halves], refs[10 + halves:10 + 2 * halves]
    (mixed_ref, gout_ref, gz_ref, small_ref, dn_ref, gx_ref, sum_ref, gcw_ref, gcb_ref, mgot_ref, cout_ref, cz_ref,
     acc, dconv, dix, sib, sends, recvs, core_send, core_recv, *scratch) = refs[10 + 2 * halves:]
    j, steps = pl.program_id(0), pl.num_programs(0)
    me, ten = lax.axis_index("dp"), lax.axis_index("tensor")
    T, CH = x_ref.shape
    W = mgot_ref.shape[1]
    bit = {name: me // stride % 2 for name, stride in STRIDE.items()}
    peer = {name: me + stride * (1 - 2 * bit[name]) for name, stride in STRIDE.items()}
    per = steps // halves
    s_acc, s_half, s_got, s_out, s_send, s_recv, s_load = scratch[7:]
    total = Total(s_acc, s_half, s_got, s_out, (s_send, s_recv))
    scratch = scratch[:7]
    pieces = [piece_of(0, gout_ref, "y", scratch, cout_ref), piece_of(1, gz_ref, "near", scratch, cz_ref)]

    def swap():
        far = pl.ds(pl.multiple_of((1 - ten) * W, 128), W)
        return pltpu.make_async_remote_copy(src_ref=mixed_ref.at[:, far], dst_ref=mgot_ref, send_sem=sends, recv_sem=recvs,
                                            device_id={"tensor": 1 - ten}, device_id_type=MESH)

    def small(*at):
        return [functools.partial(total.step, i) for i in at]

    final = count_steps - 1
    program = {
        (0, "start"): small(0) + [pieces[0].step1, pieces[1].step1],
        (0, "dots"): small(1),
        (1, "end"): small(2),
        (2, "dots"): [pieces[0].step2, pieces[1].step2],
        (2, "end"): small(3),
        (3, "end"): small(4) + [pieces[0].stop, pieces[1].stop],
    }

    def point(place):
        for (step, at), actions in program.items():
            if at == place:
                @pl.when(j == min(step, final))
                def _(actions=actions):
                    for act in actions:
                        act()

    @pl.when(j == 0)
    def _():
        loads = [pltpu.make_async_copy(small_ref.at[:, b * 128:(b + 1) * 128], s_acc.at[sixteenth(b)], s_load.at[b])
                 for b in range(16)]
        for copy in loads:
            copy.start()
        barrier = pltpu.get_barrier_semaphore()
        count = greet_dp([peer["core"]] + [total.flip(q)[1] for q in range(1, 8)])
        pl.semaphore_signal(barrier, inc=1, device_id={"tensor": 1 - ten}, device_id_type=MESH)
        pl.semaphore_wait(barrier, count + 1)
        swap().start()
        acc[...] = jnp.zeros_like(acc)
        for copy in loads:
            copy.wait()

    point("start")

    dconv[...] = lax.dot_general(dproj_ref[...], xp_ref[...], NT, preferred_element_type=F32)
    for h in range(halves):
        @pl.when(j // per == h)
        def _(h=h):
            acc[...] += lax.dot_general(dz_refs[h][...], wz_ref[...], NT, preferred_element_type=F32)
            dconv[...] += du_refs[h][...]

    point("dots")

    def conv(i, c):
        ln = pl.ds(pl.multiple_of(i * 128, 128), 128)
        weight = [cw_ref[taps - 1 - s:taps - s, ln] for s in range(taps)]
        x = x_ref[:, ln]
        mixed = cb_ref[:, ln] + weight[0] * x
        for s in range(1, taps):
            mixed = mixed + weight[s] * (pltpu.roll(x, s, 0) * mask_ref[s - 1])
        gate = jax.nn.sigmoid(mixed)
        d = dconv[:, ln] * (gate * (1.0 + mixed * (1.0 - gate)))
        gcb_ref[:, ln] = jnp.sum(d, axis=0, keepdims=True)
        gcw_ref[taps - 1:taps, ln] = jnp.sum(d * x, axis=0, keepdims=True)
        back = weight[0] * d
        for s in range(1, taps):
            masked = d * mask_ref[s - 1]
            gcw_ref[taps - 1 - s:taps - s, ln] = jnp.sum(masked * pltpu.roll(x, s, 0), axis=0, keepdims=True)
            back = back + weight[s] * pltpu.roll(masked, T - s, 0)
        dix[j, :, ln] = back.astype(BF16)
        return c

    lax.fori_loop(0, CH // 128, conv, 0)
    over = pltpu.make_async_remote_copy(src_ref=dix.at[j], dst_ref=sib.at[j], send_sem=core_send.at[j],
                                        recv_sem=core_recv.at[j], device_id={"dp": peer["core"]}, device_id_type=MESH)
    over.start()
    acc[...] += lax.dot_general(dix[j], wx_ref[...], NT, preferred_element_type=F32)
    rows = (((0,), (0,)), ((), ()))
    over.wait_recv()
    gx_ref[...] = (lax.dot_general(own_ref[...], dix[j], rows, preferred_element_type=F32)
                   + lax.dot_general(other_ref[...], sib[j], rows, preferred_element_type=F32)).astype(BF16)
    over.wait_send()

    point("end")

    @pl.when(j == steps - 1)
    def _():
        for b in range(16):
            sum_ref[:, b * 128:(b + 1) * 128] = s_out[sixteenth(b)].astype(F32)
        dn_ref[...] = acc[...].astype(BF16)
        swap().wait_recv()
        swap().wait_send()


def mid_call(dproj, masks, own, other, inner_x, w_x, w_z, x_proj, conv_weight, conv_bias, du, dz, mixed, gout, gz, small, CH=512):
    T, C = inner_x.shape
    D = w_x.shape[0]
    W = mixed.shape[1] // 2
    halves = len(du)
    taps = conv_weight.shape[0]
    steps = C // CH
    per = steps // halves
    S = jax.ShapeDtypeStruct
    V, DMA = pltpu.VMEM, pltpu.SemaphoreType.DMA
    const = lambda a: pl.BlockSpec(a.shape, lambda j: (0,) * a.ndim, pipeline_mode=pl.Buffered(1))
    col = lambda a: pl.BlockSpec((a.shape[0], CH), lambda j: (0, j))
    row = lambda a: pl.BlockSpec((CH, a.shape[1]), lambda j: (j, 0))
    part = lambda h: pl.BlockSpec((T, CH), lambda j: (0, jnp.clip(j - h * per, 0, per - 1)))
    anyspace = pl.BlockSpec(memory_space=pl.ANY)
    outs = (S((T, D), BF16), S((own.shape[1], C), BF16), S(small.shape, F32), S((taps, C), F32), S((1, C), F32),
            S((T, W), BF16),
            S((2,) + gout.shape[3:], BF16), S((2,) + gz.shape[3:], BF16))
    return pl.pallas_call(
        functools.partial(mid_kernel, taps, halves, steps),
        grid=(steps,),
        in_specs=[const(dproj), const(masks), const(own), const(other), col(inner_x), col(w_x), col(w_z), row(x_proj),
                  col(conv_weight), col(conv_bias)] + [part(h) for h in range(halves)] * 2 + [anyspace] * 4,
        out_specs=[pl.BlockSpec((T, D), lambda j: (0, 0)), col(outs[1]), pl.BlockSpec(small.shape, lambda j: (0, 0)), col(outs[3]), col(outs[4])] + [anyspace]
        + [pl.BlockSpec(o.shape, lambda j: (0, 0, 0)) for o in outs[6:]],
        out_shape=outs,
        scratch_shapes=[V((T, D), F32), V((T, CH), F32), V((steps, T, CH), BF16),
                        V((steps, T, CH), BF16), DMA, DMA, DMA((steps,)), DMA((steps,)),
                        *piece_scratch(2, *gout.shape[3:]), *total_scratch(small.shape[0])],
        compiler_params=pltpu.CompilerParams(collective_id=4, has_side_effects=True, vmem_limit_bytes=58 << 20,
                                             dimension_semantics=("arbitrary",)),
        cost_estimate=pl.CostEstimate(flops=6 * T * D * C, bytes_accessed=40 << 20, transcendentals=0),
        name="mid",
    )(dproj, masks, own, other, inner_x, w_x, w_z, x_proj, conv_weight, conv_bias, *du, *dz, mixed, gout, gz, small)


NT = (((1,), (1,)), ((), ()))
PR = 64


def scan_kernel(GR, NS, hosted, *refs):
    if not hosted:
        return scan_body(GR, NS, lambda at: None, *refs)
    ins, outs, own = 14, 10, 18
    refs = list(refs)
    g_refs = [refs.pop(ins), refs.pop(ins)]
    r_refs = [refs.pop(ins + outs), refs.pop(ins + outs)]
    scratch, refs = refs[-7:], refs[:-7]
    pieces = [piece_of(0, g_refs[0], "y", scratch, r_refs[0]), piece_of(1, g_refs[1], "near", scratch, r_refs[1])]
    steps = pl.num_programs(0)
    plan = {(0, "start"): 0, (0, "end"): 1, (1, "end"): 2}

    def host(at):
        for (step, place), stage in plan.items():
            if place != at:
                continue

            @pl.when(pl.program_id(0) == step)
            def _(stage=stage):
                if stage == 0:
                    me = lax.axis_index("dp")
                    peers = [me + STRIDE[n] * (1 - 2 * (me // STRIDE[n] % 2)) for n in ("y", "near", "far")]
                    pl.semaphore_wait(pltpu.get_barrier_semaphore(), greet_dp(peers))
                for piece in pieces:
                    (piece.step1, piece.step2, piece.stop)[stage]()

    return scan_body(GR, NS, host, *refs)


def scan_body(GR, NS, host, rank_ref, dtp_ref, dtb_ref, u_ref, z_ref, dg_ref, skip_ref,
                kb_ref, qb_ref, keep_ref, ksq_ref, qblk_ref, kblk_ref, k2blk_ref,
                gated_ref, diz_ref, du_ref, gskip_ref, gdtb_ref, gdtp_ref,
                drank_ref, sst_ref, dk_ref, dq_ref,
                den_s, step_s, su_s, ds_s, sz_s, y_s, d_s, e_s, h0_s, h1_s, ga_s, gb_s, ma_s, mb_s, dk_s, dq_s):
    T, CH = u_ref.shape
    L = CH // 128
    NG = T // GR
    R = GR * NS
    first, last = pl.program_id(0) == 0, pl.program_id(0) == pl.num_programs(0) - 1
    lanes = [slice(l * 128, (l + 1) * 128) for l in range(L)]
    hist = (h0_s, h1_s)

    @pl.when(first)
    def _():
        for r in (drank_ref, sst_ref, dk_s, dq_s):
            r[...] = jnp.zeros_like(r)
        h1_s[pl.ds(0, R), :] = jnp.zeros((R, CH), BF16)
        gb_s[...] = jnp.zeros_like(gb_s)
        mb_s[...] = jnp.zeros_like(mb_s)

    host("start")
    y_s[...] = jnp.dot(rank_ref[...], dtp_ref[...], preferred_element_type=F32)

    def prologue(r, acc):
        rows = pl.ds(pl.multiple_of(r * PR, PR), PR)
        kq = ksq_ref[rows, :]
        out = []
        for l in range(L):
            ln = lanes[l]
            beta = jax.nn.sigmoid(y_s[rows, ln] + dtb_ref[:, ln])
            den = 1.0 / (1.0 + beta * kq)
            step = beta * den
            den_s[rows, ln] = den
            step_s[rows, ln] = step
            u = u_ref[rows, ln]
            su_s[rows, ln] = step * u
            z = z_ref[rows, ln]
            s = jax.nn.sigmoid(z)
            sz_s[rows, ln] = s
            ds = dg_ref[rows, ln] * (z * s)
            ds_s[rows, ln] = ds
            out.append(acc[l] + jnp.sum(ds * u, axis=0, keepdims=True))
        return tuple(out)

    zrow = tuple(jnp.zeros((1, 128), F32) for _ in range(L))
    gsk = lax.fori_loop(0, T // PR, prologue, zrow)
    for l in range(L):
        gskip_ref[:, lanes[l]] = gsk[l]

    def rows_of(gi):
        return pl.ds(pl.multiple_of(gi * GR, GR), GR)

    def fill(gi, half, h, dst):
        h = list(h)
        base = pl.multiple_of(gi * GR, GR)
        rows = rows_of(gi)
        hb = pl.multiple_of(half * R, R)
        for j in range(GR):
            k = kb_ref[pl.ds(base * NS + j * NS, NS), :]
            kp = keep_ref.at[rows][j:j + 1, :]
            k2 = k * k * kp
            for l in range(L):
                a = kp - k2 * step_s.at[rows][j:j + 1, lanes[l]]
                h[l] = a * h[l] + k * su_s.at[rows][j:j + 1, lanes[l]]
                dst[pl.ds(hb + j * NS, NS), lanes[l]] = h[l].astype(BF16)
        return tuple(h)

    def read(gi, half, src):
        y_s[rows_of(gi), :] = jnp.dot(qblk_ref[rows_of(gi), :], src[pl.ds(pl.multiple_of(half * R, R), R), :],
                                      preferred_element_type=F32)

    def forward(i, h):
        before = jnp.maximum(i - 1, 0)
        read(2 * before + 1, before, h1_s)
        h = fill(2 * i, i, h, h0_s)
        read(2 * i, i, h0_s)
        return fill(2 * i + 1, i, h, h1_s)

    zst = tuple(jnp.zeros((NS, 128), F32) for _ in range(L))
    lax.fori_loop(0, NG // 2, forward, zst)
    read(NG - 1, NG // 2 - 1, h1_s)

    host("middle")

    def middle(r, c):
        rows = pl.ds(pl.multiple_of(r * PR, PR), PR)
        for l in range(L):
            ln = lanes[l]
            z = z_ref[rows, ln]
            s = sz_s[rows, ln]
            v = y_s[rows, ln] + skip_ref[:, ln] * u_ref[rows, ln]
            gated_ref[rows, ln] = (v * (z * s)).astype(BF16)
            diz_ref[rows, ln] = (dg_ref[rows, ln] * v * s * (1.0 + z * (1.0 - s))).astype(BF16)
        return c

    lax.fori_loop(0, T // PR, middle, 0)

    def back(gi, half, gc, own, before, before_at, g_dst, m_dst):
        gc = list(gc)
        base = pl.multiple_of(gi * GR, GR)
        rows = rows_of(gi)
        hb = pl.multiple_of(half * R, R)
        nows = [own[pl.ds(hb + (GR - 1) * NS, NS), ln] for ln in lanes]
        for j in reversed(range(GR)):
            at = pl.ds(base * NS + j * NS, NS)
            k = kb_ref[at, :]
            q = qb_ref[at, :]
            kp = keep_ref.at[rows][j:j + 1, :]
            k2 = k * k * kp
            a_sum = b_sum = q_sum = None
            for l in range(L):
                ln = lanes[l]
                ds = ds_s.at[rows][j:j + 1, ln]
                g = gc[l] + q * ds
                gb = g.astype(BF16)
                step = step_s.at[rows][j:j + 1, ln]
                now = nows[l]
                if j:
                    prev = own[pl.ds(hb + (j - 1) * NS, NS), ln]
                else:
                    prev = before[pl.ds(before_at + (GR - 1) * NS, NS), ln]
                nows[l] = prev
                m = gb * prev
                g_dst[j * NS:(j + 1) * NS, ln] = gb
                m_dst[j * NS:(j + 1) * NS, ln] = m
                wide = lambda v: jnp.broadcast_to(v, (NS, 128)).astype(BF16)
                pa = gb * wide(su_s.at[rows][j:j + 1, ln])
                pb = m * wide(step)
                pq = now * wide(ds)
                a_sum = pa if a_sum is None else a_sum + pa
                b_sum = pb if b_sum is None else b_sum + pb
                q_sum = pq if q_sum is None else q_sum + pq
                gc[l] = (kp - k2 * step) * g
            dk_s[at, :] += a_sum.astype(F32) - (2.0 * k * kp) * b_sum.astype(F32)
            dq_s[at, :] += q_sum.astype(F32)
        return tuple(gc)

    def sums(gi, g_src, m_src):
        rows = rows_of(gi)
        d_s[rows, :] = jnp.dot(kblk_ref[rows, :], g_src[...], preferred_element_type=F32)
        e_s[rows, :] = jnp.dot(k2blk_ref[rows, :], m_src[...], preferred_element_type=F32)

    def backward(i, gc):
        half = NG // 2 - 1 - i
        hi, lo = 2 * half + 1, 2 * half
        sums(jnp.minimum(hi + 1, NG - 1), gb_s, mb_s)
        gc = back(hi, half, gc, h1_s, h0_s, pl.multiple_of(half * R, R), ga_s, ma_s)
        sums(hi, ga_s, ma_s)
        return back(lo, half, gc, h0_s, h1_s, pl.multiple_of(jnp.maximum(half - 1, 0) * R, R), gb_s, mb_s)

    lax.fori_loop(0, NG // 2, backward, zst)
    sums(0, gb_s, mb_s)

    def epilogue(r, acc):
        rows = pl.ds(pl.multiple_of(r * PR, PR), PR)
        kp = keep_ref[rows, :]
        out = []
        ss = sst_ref[rows, :]
        for l in range(L):
            ln = lanes[l]
            step = step_s[rows, ln]
            dsum = d_s[rows, ln]
            dstep = u_ref[rows, ln] * dsum - kp * e_s[rows, ln]
            du_ref[rows, ln] = step * dsum + ds_s[rows, ln] * skip_ref[:, ln]
            t = dstep * step
            ss = ss + t * step
            db = t * (den_s[rows, ln] - step)
            y_s[rows, ln] = db
            out.append(acc[l] + jnp.sum(db, axis=0, keepdims=True))
        sst_ref[rows, :] = ss
        return tuple(out)

    gdb = lax.fori_loop(0, T // PR, epilogue, zrow)
    for l in range(L):
        gdtb_ref[:, lanes[l]] = gdb[l]
    dbl = y_s[...].astype(BF16)
    gdtp_ref[...] = lax.dot_general(rank_ref[...], dbl, (((0,), (0,)), ((), ())), preferred_element_type=F32)
    drank_ref[...] += lax.dot_general(dbl, dtp_ref[...], NT, preferred_element_type=F32)

    host("end")

    @pl.when(last)
    def _():
        ones = jnp.ones((8, 128), BF16)
        for src, dst in ((dk_s, dk_ref), (dq_s, dq_ref)):
            for c in range(0, T * NS, 1024):
                dst[:, c:c + 1024] = lax.dot_general(ones, src[c:c + 1024, :].astype(BF16), NT, preferred_element_type=F32)


def scan_call(piece, pieces, hosted, *args, CH=512, GR=16, NS=16):
    rank, dtp, dtb, u, z, dg, skip, kb, qb, keep, ksq, qblk, kblk, k2blk = args
    T, C = u.shape
    width = C // pieces
    CH = min(CH, width)
    first = piece * (width // CH)
    const = lambda a: pl.BlockSpec(a.shape, lambda j: (0,) * a.ndim, pipeline_mode=pl.Buffered(1))
    oconst = lambda a: pl.BlockSpec(a.shape, lambda j: (0,) * a.ndim)
    col = lambda a: pl.BlockSpec((a.shape[0], CH), lambda j: (0, j + first))
    out = lambda a: pl.BlockSpec((a.shape[0], CH), lambda j: (0, j))
    S = jax.ShapeDtypeStruct
    W = GR * NS
    R = rank.shape[1]
    outs = (S((T, width), BF16), S((T, width), BF16), S((T, width), F32), S((1, width), F32), S((1, width), F32), S((R, width), F32),
            S((T, R), F32), S((T, 128), F32), S((8, T * NS), F32), S((8, T * NS), F32))
    outs += tuple(S((2,) + g.shape[3:], BF16) for g in hosted)
    V = pltpu.VMEM
    f = pl.pallas_call(
        functools.partial(scan_kernel, GR, NS, bool(hosted)),
        grid=(width // CH,),
        in_specs=[const(rank), col(dtp), col(dtb), col(u), col(z), col(dg), col(skip), const(kb), const(qb),
                  const(keep), const(ksq), const(qblk), const(kblk), const(k2blk)] + [pl.BlockSpec(memory_space=pl.ANY)] * len(hosted),
        out_specs=[out(o) for o in outs[:6]] + [oconst(o) for o in outs[6:]],
        out_shape=outs,
        scratch_shapes=[V((T, CH), F32)] * 8 + [V((T * NS // 2, CH), BF16)] * 2 + [V((W, CH), BF16)] * 4 + [V((T * NS, 128), F32)] * 2
        + (piece_scratch(2, *hosted[0].shape[3:]) if hosted else []),
        compiler_params=pltpu.CompilerParams(vmem_limit_bytes=60 << 20, dimension_semantics=("arbitrary",),
                                             **(dict(collective_id=2, has_side_effects=True) if hosted else {})),
        cost_estimate=pl.CostEstimate(flops=T * width * NS * 800, bytes_accessed=T * width * 20, transcendentals=0),
        name="scan_reduce" if hosted else "scan",
    )
    return f(*args, *hosted)


def scan_all(rank, dtp, dtb, u, z, dg, skip, keys, query, keep, pieces, GR=16, **kw):
    T, NS = keys.shape
    kb = jnp.broadcast_to(keys[:, :, None], (T, NS, 128)).reshape(T * NS, 128)
    qb = jnp.broadcast_to(query[:, :, None], (T, NS, 128)).reshape(T * NS, 128)
    keepb = jnp.broadcast_to(keep[:, None], (T, 128))
    ksq = jnp.sum(keys * keys, axis=1)
    ksqb = jnp.broadcast_to(ksq[:, None], (T, 128))
    slot = (jnp.arange(T)[:, None] % GR == jnp.arange(GR * NS)[None, :] // NS).astype(F32)
    blk = lambda v: (slot * jnp.tile(v, (1, GR))).astype(BF16)
    qblk, kblk, k2blk = blk(query), blk(keys), blk(keys * keys)

    def run(piece, *hosted):
        o = scan_call(piece, pieces, hosted, rank, dtp, dtb, u, z, dg, skip, kb, qb, keepb, ksqb, qblk, kblk, k2blk, GR=GR, NS=NS, **kw)
        gated, diz, du, gskip, gdtb, gdtp, drank, sst, dk, dq, *summed = o
        dq = dq[0].reshape(T, NS)
        dk = dk[0].reshape(T, NS) - 2.0 * keys * jnp.sum(sst, axis=1, keepdims=True)
        return gated, diz, du, gskip, gdtb, gdtp, drank, dk, dq, summed

    return run


def tensor_other(value):
    return lax.ppermute(value, "tensor", [(0, 1), (1, 0)])


def tensor_total(value):
    if lax.axis_size("tensor") == 2:
        return value + tensor_other(value)
    return lax.psum(value, "tensor")


def half_total(value, me, width):
    if lax.axis_size("tensor") == 2:
        own = lax.dynamic_slice_in_dim(value, me * width, width, 1)
        sent = lax.dynamic_slice_in_dim(value, (1 - me) * width, width, 1).astype(BF16)
        return own + tensor_other(sent).astype(F32)
    return lax.psum_scatter(value, "tensor", scatter_dimension=1, tiled=True)


def full_columns(part, me):
    if lax.axis_size("tensor") == 2:
        other = tensor_other(part)
        return jnp.where(
            me == 0,
            jnp.concatenate([part, other], 1),
            jnp.concatenate([other, part], 1),
        )
    return lax.all_gather(part, "tensor", axis=1, tiled=True)


def pair_up(value, stride):
    count = lax.axis_size("dp")
    return lax.ppermute(value, "dp", [(i, i ^ stride) for i in range(count)])


def pick_dim(value, index, dim):
    return lax.dynamic_index_in_dim(value, index, dim, keepdims=False)


def pair_gradient(own, other, right):
    return (contract_rows(own, right) + contract_rows(other, pair_up(right, 1))).astype(BF16)


def after(value, *earlier):
    return lax.optimization_barrier((value,) + earlier)[0]


def flatten(values):
    return jnp.concatenate([v.reshape(-1) for v in values])


def cut(flat, values):
    out, at = [], 0
    for v in values:
        out.append(flat[at : at + v.size].reshape(v.shape))
        at += v.size
    return out


def position_in(keys):
    return jnp.sum((keys[None, :] < keys[:, None]).astype(jnp.int32), axis=1)


def conv_mix(inner_x, conv_weight, conv_bias, segment):
    row_count = inner_x.shape[0]
    taps = conv_weight.shape[0]
    mixed = conv_bias[None, :] + conv_weight[taps - 1][None, :] * inner_x
    for shift_by in range(1, taps):
        moved = jnp.concatenate([jnp.zeros((shift_by, inner_x.shape[1]), F32), inner_x[: row_count - shift_by]], 0)
        seg_moved = jnp.concatenate([jnp.full((shift_by,), -1, jnp.int32), segment[: row_count - shift_by]], 0)
        keep_mask = (seg_moved == segment).astype(F32)
        mixed = mixed + conv_weight[taps - 1 - shift_by][None, :] * moved * keep_mask[:, None]
    return mixed


def silu_conv(inner_x, conv_weight, conv_bias, segment):
    mixed = conv_mix(inner_x, conv_weight, conv_bias, segment)
    return mixed * jax.nn.sigmoid(mixed)


def contract_rows(left, right):
    return lax.dot_general(left, right, (((0,), (0,)), ((), ())), preferred_element_type=F32)


def contract_cols(left, right):
    return lax.dot_general(left, right, (((1,), (1,)), ((), ())), preferred_element_type=F32)


def body(tokens, cotangent, norm_gain, w_x, w_z, conv_weight, conv_bias, x_proj, dt_proj, dt_bias, skip_gain, w_out,
         seq_lengths, arrival_route, work_source):
    dp_count = lax.axis_size("dp")
    tp_count = lax.axis_size("tensor")
    row_count, feat_width = tokens.shape
    per_peer = row_count // dp_count
    col_share = feat_width // tp_count
    me = lax.axis_index("tensor")
    col_start = me * col_share
    low_rank = dt_proj.shape[0]
    state_size = (x_proj.shape[1] - low_rank) // 2
    position = jnp.arange(row_count, dtype=jnp.int32)

    deal = (position_in(arrival_route)[:, None] == position[None, :]).astype(BF16)
    settle = (position_in(work_source // row_count * row_count + position)[:, None] == position[None, :]).astype(BF16)

    def exchange(rows):
        out = lax.all_to_all(rows.reshape(dp_count, per_peer, rows.shape[1]), "dp", split_axis=0, concat_axis=0, tiled=True)
        return out.reshape(row_count, rows.shape[1])

    def pick(table, rows, dim):
        return lax.dot_general(table, rows, (((dim,), (0,)), ((), ())), preferred_element_type=F32).astype(BF16)

    def bring(values):
        part = lax.dynamic_slice_in_dim(values, col_start, col_share, 1)
        return full_columns(pick(settle, exchange(pick(deal, part, 0)), 1), me)

    def give_back(values):
        return pick(deal, exchange(pick(settle, values, 0)), 1)

    paired = dp_count == 16 and tp_count == 2
    if paired:
        x_half, normed, dy_work, scale_wide, normed_own, normed_other, dy_own, dy_other = head_call(
            tokens, cotangent, norm_gain[None, :], deal.T, settle)
    else:
        x_work = bring(tokens)
        dy_work = bring(cotangent)
        resid = x_work.astype(F32)
        scale_row = lax.rsqrt(jnp.mean(resid * resid, axis=1, keepdims=True) + 1e-05)
        unit = resid * scale_row
        normed = (unit * norm_gain[None, :]).astype(BF16)

    lengths = seq_lengths[0]
    count = lengths.shape[0]
    before = jnp.arange(count)[:, None] > jnp.arange(count)[None, :]
    offsets = jnp.sum(jnp.where(before, lengths[None, :], 0), axis=1)
    segment = jnp.sum((position[:, None] >= offsets[None, :]).astype(jnp.int32), axis=1) - 1
    keep = 1.0 - jnp.any(position[:, None] == offsets[None, :], axis=1).astype(F32)

    inner_x = jnp.dot(normed, w_x, preferred_element_type=F32)
    inner_z = jnp.dot(normed, w_z, preferred_element_type=F32)
    conv_out, conv_pull = jax.vjp(partial(silu_conv, segment=segment), inner_x, conv_weight, conv_bias)
    conv_low = conv_out.astype(BF16)
    projected = tensor_total(jnp.dot(conv_low, x_proj, preferred_element_type=F32))
    rank_part = projected[:, :low_rank].astype(BF16)
    key_rows = projected[:, low_rank : low_rank + state_size]
    query_rows = projected[:, low_rank + state_size :]

    d_gated = contract_cols(dy_work, w_out)
    pieces = 2 if paired else 1
    scan = scan_all(rank_part, dt_proj, dt_bias[None, :], conv_out, inner_z, d_gated, skip_gain[None, :], key_rows,
                    query_rows, keep, pieces)
    scans = [scan(0)]
    if paired:
        blocks = lambda g: g.reshape(2, 2, 2, g.shape[0] // 8, g.shape[1])
        outer = lambda part: (blocks(pair_gradient(dy_own, dy_other, part[0])),
                              blocks(pair_gradient(normed_own, normed_other, part[1])))
        scans.append(scan(1, *outer(scans[0])))
    wide = lambda index: jnp.concatenate([part[index] for part in scans], axis=1) if paired else scans[0][index]
    grad_dt_proj = wide(5)
    grad_skip, grad_dt_bias = wide(3)[0], wide(4)[0]
    d_rank, d_keys, d_query = (sum(part[index] for part in scans) for index in (6, 7, 8))
    gated_low, d_inner_z_low = wide(0), wide(1)
    d_proj = tensor_total(jnp.concatenate([d_rank, d_keys, d_query], axis=1))
    mixed = jnp.dot(gated_low, w_out, preferred_element_type=F32)
    if paired:
        mixed = mixed.astype(BF16)
        g_out, g_z = outer(scans[1])
        bit = {name: lax.axis_index("dp") // stride % 2 for name, stride in STRIDE.items()}
        far = [pair_up(pick_dim(v, 1 - bit["far"], 0), STRIDE["far"]) for v in scans[1][9]]
        d_proj = after(d_proj, g_out, g_z, mixed)
        taps = conv_weight.shape[0]
        pre = [jnp.concatenate([jnp.full((s,), -1, jnp.int32), segment[: row_count - s]]) for s in range(1, taps)]
        masks = jnp.stack([jnp.broadcast_to((p == segment).astype(F32)[:, None], (row_count, 128)) for p in pre])
        d_proj_low = d_proj.astype(BF16)
        rows = (contract_rows(d_proj_low, conv_low), grad_dt_proj, grad_dt_bias[None, :], grad_skip[None, :])
        stack = jnp.concatenate(rows).astype(BF16)
        stack = jnp.pad(stack, ((0, -stack.shape[0] % 16), (0, 0)))
        d_normed, g_x, stack, grad_conv_weight, grad_conv_bias, mixed_other, left_out, left_z = mid_call(
            d_proj_low, masks, normed_own, normed_other, inner_x, w_x, w_z, x_proj, conv_weight,
            conv_bias[None, :], [part[2] for part in scans], [part[1] for part in scans], mixed, g_out, g_z,
            stack)
        early = [pick_dim(v, bit["far"], 0).astype(F32) + after(came, d_normed).astype(F32)
                 for v, came in zip(scans[1][9], far)]
    else:
        d_proj_low = d_proj.astype(BF16)
        grad_x_proj = contract_rows(conv_low, d_proj_low)
        d_conv_out = scans[0][2] + contract_cols(d_proj_low, x_proj)
        d_inner_x, grad_conv_weight, grad_conv_bias = conv_pull(d_conv_out)
        d_inner_x_low = d_inner_x.astype(BF16)
        d_normed = contract_cols(d_inner_x_low, w_x) + contract_cols(d_inner_z_low, w_z)
    if paired:
        conv = jnp.concatenate([grad_conv_weight, grad_conv_bias])
        conv = jnp.pad(conv, ((0, 8 - conv.shape[0]), (0, 0)))
        out_tokens, in_grad, grad_gain, conv, grad_w_out, grad_w_z, grad_w_x = tail_call(
            left_out, left_z, blocks(g_x), d_normed, mixed, mixed_other, x_half, dy_work, conv, norm_gain[None, :],
            scale_wide, settle.T, deal)
        split = x_proj.shape[1]
        grad_x_proj, grad_dt_proj = stack[:split].T, stack[split : split + low_rank]
        grad_dt_bias, grad_skip = stack[split + low_rank], stack[split + low_rank + 1]
        grad_conv_weight, grad_conv_bias = conv[:taps], conv[taps]
        grad_gain = grad_gain[0]
        early_out, early_z = early
        grad_w_out = jnp.concatenate([early_out, grad_w_out], axis=1).T
        grad_w_z = jnp.concatenate([early_z, grad_w_z], axis=1)
    else:
        small = (grad_x_proj, grad_dt_proj, grad_conv_weight, grad_conv_bias, grad_dt_bias, grad_skip)
        unit_cols = lax.dynamic_slice_in_dim(unit, col_start, col_share, 1)
        gain_cols = lax.dynamic_slice_in_dim(norm_gain, col_start, col_share, 0)
        dy_cols = lax.dynamic_slice_in_dim(dy_work, col_start, col_share, 1).astype(F32)
        d_share = half_total(d_normed, me, col_share)
        d_unit_cols = d_share * gain_cols[None, :]
        row_total = tensor_total(jnp.sum(d_unit_cols * unit_cols, axis=1, keepdims=True))
        grad_gain = jnp.sum(d_share * unit_cols, axis=0)
        d_resid = dy_cols + scale_row * (d_unit_cols - unit_cols * (row_total / feat_width))
        mixed_share = half_total(mixed, me, col_share)
        out_cols = (lax.dynamic_slice_in_dim(resid, col_start, col_share, 1) + mixed_share).astype(BF16)
        out_tokens, in_grad = give_back(out_cols), give_back(d_resid.astype(BF16))
        grad_w_out, grad_w_z, grad_w_x = (
            lax.psum_scatter(g.astype(BF16), "dp", scatter_dimension=dim, tiled=True).astype(F32)
            for g, dim in ((contract_rows(gated_low, dy_work), 1), (contract_rows(normed, d_inner_z_low), 0),
                           (contract_rows(normed, d_inner_x_low), 0)))
        small += (grad_gain,)
        (grad_x_proj, grad_dt_proj, grad_conv_weight, grad_conv_bias, grad_dt_bias, grad_skip, grad_gain) = cut(
            lax.psum(flatten(small), "dp"), small)
    return (out_tokens, in_grad, grad_gain, grad_w_x, grad_w_z, grad_conv_weight, grad_conv_bias, grad_x_proj,
            grad_dt_proj, grad_dt_bias, grad_skip, grad_w_out)


def solution(mesh):
    in_specs = (
        P("dp", None),
        P("dp", None),
        P(),
        P(None, "tensor"),
        P(None, "tensor"),
        P(None, "tensor"),
        P("tensor"),
        P("tensor", None),
        P(None, "tensor"),
        P("tensor"),
        P("tensor"),
        P("tensor", None),
        P("dp", None),
        P("dp"),
        P("dp"),
    )
    out_specs = (
        P("dp", "tensor"),
        P("dp", "tensor"),
        P("tensor"),
        P("dp", "tensor"),
        P("dp", "tensor"),
        P(None, "tensor"),
        P("tensor"),
        P("tensor", None),
        P(None, "tensor"),
        P("tensor"),
        P("tensor"),
        P("tensor", "dp"),
    )
    return jax.shard_map(body, mesh=mesh, in_specs=in_specs, out_specs=out_specs, check_vma=False)
```

```python
import functools
from functools import partial

import jax
import jax.numpy as jnp
import numpy as np
from jax import lax
from jax.experimental import pallas as pl
from jax.experimental.pallas import tpu as pltpu
from jax.sharding import PartitionSpec as P

F32, BF16 = jnp.float32, jnp.bfloat16
MESH = pl.DeviceIdType.MESH
TILE = 32
GAIN_ROW = 5
STRIDE = {"core": 1, "y": 2, "near": 4, "far": 8}


class Piece:
    def __init__(self, grad, first, bufs, sems, result):
        self.grad, self.first, self.result = grad, first, result
        self.own, self.r1, self.r2, self.r3 = bufs
        self.local, self.send, self.recv = sems
        self.second = "near" if first == "y" else "y"

    def bit(self, name):
        return lax.axis_index("dp") // STRIDE[name] % 2

    def block(self, mine):
        return self.grad.at[:, :, mine] if self.first == "y" else self.grad.at[:, mine]

    def remote(self, step):
        s, f = self.bit(self.second), self.bit("far")
        name, src, dst = (
            (self.first, lambda: self.block(1 - self.bit(self.first)), self.r1),
            (self.second, lambda: self.own.at[:, 1 - s], self.r2),
            ("far", lambda: self.own.at[1 - f, s], self.r3),
        )[step]
        to = lax.axis_index("dp") + STRIDE[name] * (1 - 2 * self.bit(name))
        return pltpu.make_async_remote_copy(
            src_ref=src(), dst_ref=dst, send_sem=self.send.at[step], recv_sem=self.recv.at[step],
            device_id={"dp": to}, device_id_type=MESH)

    def load(self):
        return pltpu.make_async_copy(self.block(self.bit(self.first)), self.own, self.local)

    def step1(self):
        self.remote(0).start()
        self.load().start()

    def add(self, dst, src, out=None):
        def body(i, c):
            at = pl.ds(pl.multiple_of(i * TILE, TILE), TILE)
            total = dst[at, :].astype(F32) + src[at, :].astype(F32)
            if out is None:
                dst[at, :] = total.astype(BF16)
            else:
                out[at, :] = total.astype(out.dtype)
            return c

        lax.fori_loop(0, src.shape[0] // TILE, body, 0)

    def step2(self):
        self.load().wait()
        self.remote(0).wait_recv()
        s = self.bit(self.second)
        for far in range(2):
            self.add(self.own.at[far, 1 - s], self.r1.at[far, 1 - s])
        self.remote(1).start()
        for far in range(2):
            self.add(self.own.at[far, s], self.r1.at[far, s])

    def step3(self):
        self.remote(1).wait_recv()
        s, f = self.bit(self.second), self.bit("far")
        self.add(self.own.at[1 - f, s], self.r2.at[1 - f])
        self.remote(2).start()
        self.add(self.own.at[f, s], self.r2.at[f])

    def stop(self):
        self.remote(1).wait_recv()
        for far in range(2):
            self.add(self.own.at[far, self.bit(self.second)], self.r2.at[far], self.result.at[far])
        for step in range(2):
            self.remote(step).wait_send()

    def finish(self):
        self.remote(2).wait_recv()
        self.add(self.own.at[self.bit("far"), self.bit(self.second)], self.r3, self.result)
        for step in range(3):
            self.remote(step).wait_send()


class FarPiece(Piece):
    def __init__(self, grad, bufs, sems, result):
        self.grad, self.result = grad, result
        self.own, self.r3 = bufs
        self.local, self.send, self.recv = sems

    def remote(self, step):
        f = self.bit("far")
        return pltpu.make_async_remote_copy(
            src_ref=self.grad.at[1 - f], dst_ref=self.r3, send_sem=self.send, recv_sem=self.recv,
            device_id={"dp": lax.axis_index("dp") + STRIDE["far"] * (1 - 2 * f)}, device_id_type=MESH)

    def load(self):
        return pltpu.make_async_copy(self.grad.at[self.bit("far")], self.own, self.local)

    def finish(self):
        self.load().wait()
        self.remote(0).wait_recv()
        self.add(self.own, self.r3, self.result)
        self.remote(0).wait_send()


def piece_scratch(k, n, w):
    V, DMA = pltpu.VMEM, pltpu.SemaphoreType.DMA
    return [V((k, 2, 2, n, w), BF16), V((k, 2, 2, n, w), BF16), V((k, 2, n, w), BF16), V((k, n, w), BF16),
            DMA((k,)), DMA((k, 3)), DMA((k, 3))]


def piece_of(i, grad, first, scratch, result):
    return Piece(grad, first, tuple(r.at[i] for r in scratch[:4]), tuple(r.at[i] for r in scratch[4:]), result)


def greet_dp(peers):
    for p in peers:
        pl.semaphore_signal(pltpu.get_barrier_semaphore(), inc=1, device_id={"dp": p}, device_id_type=MESH)
    return len(peers)


class Total:
    NAMES = ("y", "near", "far")

    def __init__(self, acc, half, got, out, sems):
        self.acc, self.half, self.got, self.out, self.sems = acc, half, got, out, sems
        self.me = lax.axis_index("dp")
        self.bits = {name: self.me // stride % 2 for name, stride in STRIDE.items()}

    def flip(self, q):
        path, to = [self.bits["core"]], self.me
        for n, name in enumerate(self.NAMES):
            bit, turn = self.bits[name], q >> n & 1
            path.append(1 - bit if turn else bit)
            if turn:
                to = to + STRIDE[name] * (1 - 2 * bit)
        return tuple(path), to

    def copies(self, stage):
        mine, core = self.flip(0)[0], self.bits["core"]
        other = self.me + 1 - 2 * core
        if stage == 0:
            jobs = [(0, self.acc.at[1 - core], self.half, other)]
        elif stage == 1:
            jobs = [(q, self.acc.at[self.flip(q)[0]], self.got.at[q], self.flip(q)[1]) for q in range(1, 8)]
        elif stage == 2:
            jobs = [(q, self.out.at[mine], self.out.at[mine], self.flip(q)[1]) for q in range(1, 8)]
        else:
            jobs = [(0, self.out.at[core], self.out.at[core], other)]
        return [pltpu.make_async_remote_copy(
            src_ref=src, dst_ref=dst, send_sem=self.sems[0].at[stage, q], recv_sem=self.sems[1].at[stage, q],
            device_id={"dp": to}, device_id_type=MESH) for q, src, dst, to in jobs]

    def step(self, i):
        if i:
            for copy in self.copies(i - 1):
                copy.wait_recv()
        if i == 1:
            for b in range(8):
                at = (b // 4, b // 2 % 2, b % 2)
                here = self.acc.at[(self.bits["core"],) + at]
                here[...] = (here[...].astype(F32) + self.half[at].astype(F32)).astype(BF16)
        if i == 2:
            mine = self.flip(0)[0]
            total = self.acc[mine].astype(F32)
            for q in range(1, 8):
                total = total + self.got[q].astype(F32)
            self.out[mine] = total.astype(BF16)
        if i < 4:
            for copy in self.copies(i):
                copy.start()
        else:
            for stage in range(4):
                for copy in self.copies(stage):
                    copy.wait_send()


def sixteenth(b):
    return b // 8, b // 4 % 2, b // 2 % 2, b % 2


def total_scratch(rows):
    V, DMA = pltpu.VMEM, pltpu.SemaphoreType.DMA
    full = (2, 2, 2, 2, rows, 128)
    return [V(full, BF16), V(full[1:], BF16), V((8, rows, 128), BF16), V(full, BF16), DMA((4, 8)), DMA((4, 8)), DMA((16,))]


def tail_kernel(gout_ref, gz_ref, gx_ref, dn_ref, mx_ref, other_ref, x_ref, dy_ref, conv_ref, gain_ref, scale_ref, settle_ref, deal_ref,
                out_ref, in_ref, gg_ref, csum_ref, wout_ref, wz_ref, wx_ref,
                p0, p1, p2, p3, p4, p5, p6,
                dn_own, dn_got, mx_own, mx_got, x_half, dy_half, du, rs_own, rs_got, low,
                y_send, y_got, d_send, d_got, sem, x_send, x_recv, a_send, a_recv,
                m_part, m_got, m_out, m_send, m_recv,
                f_own, f_got, f_sem):
    me, ten = lax.axis_index("dp"), lax.axis_index("tensor")
    count = lax.axis_size("dp")
    T, W = x_half.shape
    L = W // 128
    per = T // count
    barrier = pltpu.get_barrier_semaphore()
    for p in range(1, count):
        pl.semaphore_signal(barrier, inc=1, device_id={"dp": (me + p) % count}, device_id_type=MESH)
    pl.semaphore_signal(barrier, inc=1, device_id={"tensor": 1 - ten}, device_id_type=MESH)
    mine = pl.ds(pl.multiple_of(ten * W, 128), W)
    other = pl.ds(pl.multiple_of((1 - ten) * W, 128), W)
    loads = []
    jobs = [(mx_ref.at[:, mine], mx_own), (other_ref, mx_got), (x_ref, x_half), (dn_ref.at[:, mine], dn_own),
            (dy_ref.at[:, mine], dy_half)]
    for b in range(count):
        jobs.append((conv_ref.at[:, b * 128 : (b + 1) * 128], m_part.at[b]))
    for n, (src, dst) in enumerate(jobs):
        copy = pltpu.make_async_copy(src, dst, sem.at[n])
        copy.start()
        loads.append(copy)
    pl.semaphore_wait(barrier, count)

    def swap(src, dst, n):
        copy = pltpu.make_async_remote_copy(
            src_ref=src, dst_ref=dst, send_sem=x_send.at[n], recv_sem=x_recv.at[n],
            device_id={"tensor": 1 - ten}, device_id_type=MESH)
        copy.start()
        return copy

    dn_copy = swap(dn_ref.at[:, other], dn_got, 0)
    bits = {"core": me % 2, "y": me // 2 % 2, "near": me // 4 % 2, "far": me // 8}
    half = gout_ref.shape[-1]
    scratch = (p0, p1, p2, p3, p4, p5, p6)
    x_cols = [slice(0, half), slice(half, 2 * half)]
    pieces = [
        FarPiece(gout_ref, (f_own.at[0], f_got.at[0]), tuple(f_sem.at[0, n] for n in range(3)), wout_ref),
        FarPiece(gz_ref, (f_own.at[1], f_got.at[1]), tuple(f_sem.at[1, n] for n in range(3)), wz_ref),
        piece_of(0, gx_ref.at[:, :, :, :, x_cols[0]], "y", scratch, wx_ref.at[:, x_cols[0]]),
        piece_of(1, gx_ref.at[:, :, :, :, x_cols[1]], "near", scratch, wx_ref.at[:, x_cols[1]]),
    ]
    for piece in (pieces[2], pieces[3], pieces[0], pieces[1]):
        piece.step1()
    for copy in loads:
        copy.wait()
    def small(stage, p):
        to = (me + p) % count
        src, dst = ((m_part.at[to], m_got.at[me]), (m_out.at[me], m_out.at[me]))[stage]
        return pltpu.make_async_remote_copy(
            src_ref=src, dst_ref=dst, send_sem=m_send.at[stage, p], recv_sem=m_recv.at[stage, p],
            device_id={"dp": to}, device_id_type=MESH)

    def tiles(body, init):
        def step(i, c):
            return body(pl.ds(pl.multiple_of(i * 16, 16), 16), c)
        return lax.fori_loop(0, T // 16, step, init)

    def add_resid(at, c):
        for l in range(L):
            ln = slice(l * 128, (l + 1) * 128)
            both = mx_own[at, ln].astype(F32) + mx_got[at, ln].astype(F32)
            mx_own[at, ln] = (x_half[at, ln].astype(F32) + both).astype(BF16)
        return c

    def deal_out(rows, send, got, n):
        sent = jnp.dot(settle_ref[...], rows[...], preferred_element_type=F32).astype(BF16)
        send[...] = sent.reshape(send.shape)
        got[me] = send[me]
        copies = []
        for p in range(1, count):
            to = (me + p) % count
            copy = pltpu.make_async_remote_copy(
                src_ref=send.at[to], dst_ref=got.at[me], send_sem=a_send.at[n, p], recv_sem=a_recv.at[n, p],
                device_id={"dp": to}, device_id_type=MESH)
            copy.start()
            copies.append(copy)
        return copies

    def take_in(copies, got, out):
        for copy in copies:
            copy.wait_recv()
        out[...] = jnp.dot(deal_ref[...], got[...].reshape(T, W), preferred_element_type=F32).astype(BF16)
        for copy in copies:
            copy.wait_send()

    tiles(add_resid, 0)
    y_copies = deal_out(mx_own, y_send, y_got, 1)

    dn_copy.wait_recv()
    gain = gain_ref[:, mine]

    def share(at, acc):
        scale = scale_ref[at, :]
        total = None
        out = []
        for l in range(L):
            ln = slice(l * 128, (l + 1) * 128)
            d = dn_own[at, ln].astype(F32) + dn_got[at, ln].astype(F32)
            unit = x_half[at, ln].astype(F32) * scale
            d_unit = d * gain[:, ln]
            du[at, ln] = d_unit
            out.append(acc[l] + jnp.sum(d * unit, axis=0, keepdims=True))
            total = d_unit * unit if total is None else total + d_unit * unit
        rs_own[at, :] = total
        return tuple(out)

    acc = tiles(share, tuple(jnp.zeros((1, 128), F32) for _ in range(L)))
    rs_copy = swap(rs_own, rs_got, 2)
    for l in range(L):
        m_part[l, GAIN_ROW : GAIN_ROW + 1, :] = acc[l]
    for p in range(1, count):
        small(0, p).start()
    m_got[me] = m_part[me]
    pieces[2].step2()
    pieces[3].step2()
    rs_copy.wait_recv()

    def norm_back(at, c):
        scale = scale_ref[at, :]
        total = jnp.sum(rs_own[at, :] + rs_got[at, :], axis=1, keepdims=True) * (0.5 / W)
        for l in range(L):
            ln = slice(l * 128, (l + 1) * 128)
            unit = x_half[at, ln].astype(F32) * scale
            low[at, ln] = (dy_half[at, ln].astype(F32) + scale * (du[at, ln] - unit * total)).astype(BF16)
        return c

    tiles(norm_back, 0)
    d_copies = deal_out(low, d_send, d_got, 0)
    for p in range(1, count):
        small(0, p).wait_recv()
    m_out[me] = jnp.sum(m_got[...], axis=0)
    for p in range(1, count):
        small(1, p).start()
    pieces[2].step3()
    pieces[3].step3()
    pieces[0].finish()
    pieces[1].finish()
    take_in(y_copies, y_got, out_ref)
    for p in range(1, count):
        small(1, p).wait_recv()
    for b in range(count):
        csum_ref[:, b * 128 : (b + 1) * 128] = m_out[b]
    for l in range(L):
        gg_ref[:, l * 128 : (l + 1) * 128] = m_out[l, GAIN_ROW : GAIN_ROW + 1, :]
    take_in(d_copies, d_got, in_ref)
    pieces[2].finish()
    pieces[3].finish()
    for copy in (dn_copy, rs_copy):
        copy.wait_send()
    for stage in range(2):
        for p in range(1, count):
            small(stage, p).wait_send()


def tail_call(gout, gz, gx, dn, mx, other, x, dy, conv, gain, scale, settle_t, deal):
    T, W = x.shape
    D = 2 * W
    n, half = gout.shape[1:]
    count = lax.axis_size("dp")
    S = jax.ShapeDtypeStruct
    full = 2 * half
    outs = (S((T, W), BF16), S((T, W), BF16), S((1, W), F32), S(conv.shape, F32), S((n, half), F32), S((n, half), F32), S((n, full), F32))
    anyspace = pl.BlockSpec(memory_space=pl.ANY)
    vmem = pl.BlockSpec(memory_space=pltpu.VMEM)
    V, DMA = pltpu.VMEM, pltpu.SemaphoreType.DMA
    return pl.pallas_call(
        tail_kernel,
        out_shape=outs,
        in_specs=[anyspace] * 9 + [vmem] * 4,
        out_specs=[vmem] * 7,
        scratch_shapes=[
            *piece_scratch(2, n, half),
            V((T, W), BF16), V((T, W), BF16), V((T, W), BF16), V((T, W), BF16), V((T, W), BF16), V((T, W), BF16),
            V((T, W), F32), V((T, 128), F32), V((T, 128), F32), V((T, W), BF16),
            V((count, T // count, W), BF16), V((count, T // count, W), BF16),
            V((count, T // count, W), BF16), V((count, T // count, W), BF16),
            DMA((5 + count,)), DMA((3,)), DMA((3,)), DMA((2, count)), DMA((2, count)),
            V((count, 8, 128), F32), V((count, 8, 128), F32), V((count, 8, 128), F32), DMA((2, count)), DMA((2, count)),
            V((2, n, half), BF16), V((2, n, half), BF16), DMA((2, 3)),
        ],
        compiler_params=pltpu.CompilerParams(collective_id=1, has_side_effects=True, vmem_limit_bytes=58 << 20),
        cost_estimate=pl.CostEstimate(flops=T * T * D * 4, bytes_accessed=64 << 20, transcendentals=0),
        name="tail",
    )(gout, gz, gx, dn, mx, other, x, dy, conv, gain, scale, settle_t, deal)


NT = (((1,), (1,)), ((), ()))


def head_kernel(taps, tok_ref, cot_ref, w_ref, wz_ref, wo_ref, gain_ref, deal_ref, settle_ref, mask_ref, cw_ref, cb_ref, xp_ref,
                half_ref, normed_ref, dy_ref, scale_ref, n_own_ref, n_other_ref, d_own_ref, d_other_ref,
                inner_ref, conv_ref, low_ref, proj_ref, z_ref, dg_ref,
                part, send, got, across, n_send, d_send, w_s, p_own, p_got, load, w_load, p_send, p_recv, a_send, a_recv, x_send, x_recv, c_send, c_recv):
    me, ten = lax.axis_index("dp"), lax.axis_index("tensor")
    count = lax.axis_size("dp")
    T, W = half_ref.shape
    chunks, per, WC = send.shape[1], send.shape[3], send.shape[4]
    barrier = pltpu.get_barrier_semaphore()
    greet_dp([(me + p) % count for p in range(1, count)])
    pl.semaphore_signal(barrier, inc=1, device_id={"tensor": 1 - ten}, device_id_type=MESH)
    start = pl.multiple_of(ten * W, 128)
    away = pl.multiple_of((1 - ten) * W, 128)
    loads = [pltpu.make_async_copy(src.at[:, pl.ds(start, W)], part.at[n], load.at[n]) for n, src in enumerate((tok_ref, cot_ref))]
    weights = [pltpu.make_async_copy(w, w_s, w_load.at[n]) for n, w in enumerate((w_ref, wz_ref, wo_ref))]
    for copy in loads:
        copy.start()
    weights[0].start()

    def deal(n):
        loads[n].wait()
        rows = jnp.dot(deal_ref[...], part[n], preferred_element_type=F32).astype(BF16)
        for c in range(chunks):
            send[n, c] = rows[:, c * WC : (c + 1) * WC].reshape(count, per, WC)

    def out(n, c, p):
        to = (me + p) % count
        return pltpu.make_async_remote_copy(
            src_ref=send.at[n, c, to], dst_ref=got.at[n, c, me], send_sem=a_send.at[n, c, p], recv_sem=a_recv.at[n, c, p],
            device_id={"dp": to}, device_id_type=MESH)

    def over(n, c, p):
        at = (me + count - p) % count
        return pltpu.make_async_remote_copy(
            src_ref=(send if p == 0 else got).at[n, c, at], dst_ref=across.at[n, c, at], send_sem=x_send.at[n, c, p],
            recv_sem=x_recv.at[n, c, p], device_id={"tensor": 1 - ten}, device_id_type=MESH)

    def launch(n, c):
        for p in range(1, count):
            out(n, c, p).start()
        over(n, c, 0).start()
        got[n, c, me] = send[n, c, me]

    def forward(n, c):
        for p in range(1, count):
            out(n, c, p).wait_recv()
            over(n, c, p).start()

    def settle(n, c, source, into, begin):
        rows = jnp.dot(settle_ref[...], source[n, c].reshape(T, WC), preferred_element_type=F32)
        into[:, pl.ds(pl.multiple_of(begin + c * WC, 128), WC)] = rows.astype(BF16)

    order = [(n, c) for n in range(2) for c in range(chunks)]
    deal(0)
    pl.semaphore_wait(barrier, count)
    launch(0, 0)
    deal(1)
    for at in range(chunks):
        forward(*order[at])
        launch(*order[at + 1])
        settle(0, at, got, half_ref, 0)
    for c in range(chunks):
        for p in range(count):
            over(0, c, p).wait_recv()
        if c == chunks - 1:
            forward(1, 0)
            launch(1, 1)
        settle(0, c, across, part.at[0], 0)
    core = me % 2

    def norm(i, c):
        at = pl.ds(pl.multiple_of(i * 16, 16), 16)
        mine, other = half_ref[at, :].astype(F32), part[0, at, :].astype(F32)
        square = jnp.sum(mine * mine + other * other, axis=1, keepdims=True)
        scale = lax.rsqrt(square * (0.5 / W) + 1e-05)
        scale_ref[at, :] = jnp.broadcast_to(scale, (16, 128))
        for value, begin in ((mine, start), (other, away)):
            cols = pl.ds(begin, W)
            normed_ref[at, cols] = (value * scale * gain_ref[:, cols]).astype(BF16)
        return c

    lax.fori_loop(0, T // 16, norm, 0)

    def halves(source, own, other):
        def body(b, c):
            for into, k in ((own, core), (other, 1 - core)):
                into[:, pl.ds(pl.multiple_of(b * 128, 128), 128)] = source[:, pl.ds(pl.multiple_of((2 * b + k) * 128, 128), 128)]
            return c

        lax.fori_loop(0, W // 128, body, 0)

    def swap(n, source, into):
        return pltpu.make_async_remote_copy(
            src_ref=source, dst_ref=into, send_sem=c_send.at[n], recv_sem=c_recv.at[n],
            device_id={"dp": me + 1 - 2 * core}, device_id_type=MESH)

    halves(normed_ref, n_own_ref, n_send)
    first = swap(0, n_send, n_other_ref)
    first.start()
    CH = 512
    wide = range(0, inner_ref.shape[1], CH)
    weights[0].wait()
    for c in wide:
        inner_ref[:, c : c + CH] = jnp.dot(normed_ref[...], w_s[:, c : c + CH], preferred_element_type=F32)
    weights[1].start()
    for c in range(1, chunks):
        forward(1, c)
        if c + 1 < chunks:
            launch(1, c + 1)

    def conv(i, c):
        ln = pl.ds(pl.multiple_of(i * 128, 128), 128)
        x = inner_ref[:, ln]
        mixed = cb_ref[:, ln] + cw_ref[taps - 1 : taps, ln] * x
        for s in range(1, taps):
            mixed = mixed + cw_ref[taps - 1 - s : taps - s, ln] * (pltpu.roll(x, s, 0) * mask_ref[s - 1])
        value = mixed * jax.nn.sigmoid(mixed)
        conv_ref[:, ln] = value
        low_ref[:, ln] = value.astype(BF16)
        return c

    lax.fori_loop(0, inner_ref.shape[1] // 128, conv, 0)
    p_own[...] = jnp.dot(low_ref[...], xp_ref[...], preferred_element_type=F32)
    share = pltpu.make_async_remote_copy(src_ref=p_own, dst_ref=p_got, send_sem=p_send, recv_sem=p_recv,
                                         device_id={"tensor": 1 - ten}, device_id_type=MESH)
    share.start()
    weights[1].wait()
    for c in wide:
        z_ref[:, c : c + CH] = jnp.dot(normed_ref[...], w_s[:, c : c + CH], preferred_element_type=F32)
    weights[2].start()
    for c in range(chunks):
        settle(1, c, got, dy_ref, start)
    for c in range(chunks):
        for p in range(count):
            over(1, c, p).wait_recv()
        settle(1, c, across, dy_ref, away)
    halves(dy_ref, d_own_ref, d_send)
    second = swap(1, d_send, d_other_ref)
    second.start()
    weights[2].wait()
    for c in wide:
        dg_ref[:, c : c + CH] = lax.dot_general(dy_ref[...], w_s[c : c + CH, :], NT, preferred_element_type=F32)
    share.wait_recv()
    proj_ref[...] = p_own[...] + p_got[...]
    share.wait_send()
    for copy in (first, second):
        copy.wait_recv()
        copy.wait_send()
    for n, c in order:
        for p in range(count):
            over(n, c, p).wait_send()
            if p:
                out(n, c, p).wait_send()


def head_call(tokens, cotangent, w_x, w_z, w_out, gain, deal_t, settle, masks, conv_weight, conv_bias, x_proj, chunks=2):
    T, D = tokens.shape
    W = D // 2
    count = lax.axis_size("dp")
    S = jax.ShapeDtypeStruct
    V, DMA = pltpu.VMEM, pltpu.SemaphoreType.DMA
    outs = (S((T, W), BF16), S((T, D), BF16), S((T, D), BF16), S((T, 128), F32)) + (S((T, W), BF16),) * 4
    C = w_x.shape[1]
    outs += (S((T, C), F32), S((T, C), F32), S((T, C), BF16), S((T, x_proj.shape[1]), F32),
             S((T, C), F32), S((T, C), F32))
    block = V((2, chunks, count, T // count, W // chunks), BF16)
    vmem = pl.BlockSpec(memory_space=pltpu.VMEM)
    return pl.pallas_call(
        functools.partial(head_kernel, conv_weight.shape[0]),
        out_shape=outs,
        in_specs=[pl.BlockSpec(memory_space=pl.ANY)] * 5 + [vmem] * 7,
        out_specs=[vmem] * len(outs),
        scratch_shapes=[V((2, T, W), BF16), block, block, block, V((T, W), BF16), V((T, W), BF16), V(w_x.shape, BF16),
                        V((T, x_proj.shape[1]), F32), V((T, x_proj.shape[1]), F32), DMA((2,)), DMA((3,)), DMA, DMA] + [DMA((2, chunks, count))] * 4 + [ DMA((2,)), DMA((2,))],
        compiler_params=pltpu.CompilerParams(collective_id=3, has_side_effects=True, vmem_limit_bytes=58 << 20),
        cost_estimate=pl.CostEstimate(flops=T * T * D * 4, bytes_accessed=48 << 20, transcendentals=0),
        name="head",
    )(tokens, cotangent, w_x, w_z, w_out, gain, deal_t, settle, masks, conv_weight, conv_bias, x_proj)


def mid_kernel(taps, halves, count_steps, *refs):
    (dproj_ref, mask_ref, own_ref, other_ref, x_ref, wx_ref, wz_ref, xp_ref, cw_ref, cb_ref) = refs[:10]
    du_refs, dz_refs = refs[10:10 + halves], refs[10 + halves:10 + 2 * halves]
    (mixed_ref, gout_ref, gz_ref, small_ref, dn_ref, gx_ref, sum_ref, gcw_ref, gcb_ref, mgot_ref, cout_ref, cz_ref,
     acc, dconv, dix, sib, sends, recvs, core_send, core_recv, *scratch) = refs[10 + 2 * halves:]
    j, steps = pl.program_id(0), pl.num_programs(0)
    me, ten = lax.axis_index("dp"), lax.axis_index("tensor")
    T, CH = x_ref.shape
    W = mgot_ref.shape[1]
    bit = {name: me // stride % 2 for name, stride in STRIDE.items()}
    peer = {name: me + stride * (1 - 2 * bit[name]) for name, stride in STRIDE.items()}
    per = steps // halves
    s_acc, s_half, s_got, s_out, s_send, s_recv, s_load = scratch[7:]
    total = Total(s_acc, s_half, s_got, s_out, (s_send, s_recv))
    scratch = scratch[:7]
    pieces = [piece_of(0, gout_ref, "y", scratch, cout_ref), piece_of(1, gz_ref, "near", scratch, cz_ref)]

    def swap():
        far = pl.ds(pl.multiple_of((1 - ten) * W, 128), W)
        return pltpu.make_async_remote_copy(src_ref=mixed_ref.at[:, far], dst_ref=mgot_ref, send_sem=sends, recv_sem=recvs,
                                            device_id={"tensor": 1 - ten}, device_id_type=MESH)

    def small(*at):
        return [functools.partial(total.step, i) for i in at]

    final = count_steps - 1
    program = {
        (0, "start"): small(0) + [pieces[0].step1, pieces[1].step1],
        (0, "dots"): small(1),
        (1, "end"): small(2),
        (2, "dots"): [pieces[0].step2, pieces[1].step2],
        (2, "end"): small(3),
        (3, "end"): small(4) + [pieces[0].stop, pieces[1].stop],
    }

    def point(place):
        for (step, at), actions in program.items():
            if at == place:
                @pl.when(j == min(step, final))
                def _(actions=actions):
                    for act in actions:
                        act()

    @pl.when(j == 0)
    def _():
        loads = [pltpu.make_async_copy(small_ref.at[:, b * 128:(b + 1) * 128], s_acc.at[sixteenth(b)], s_load.at[b])
                 for b in range(16)]
        for copy in loads:
            copy.start()
        barrier = pltpu.get_barrier_semaphore()
        count = greet_dp([peer["core"]] + [total.flip(q)[1] for q in range(1, 8)])
        pl.semaphore_signal(barrier, inc=1, device_id={"tensor": 1 - ten}, device_id_type=MESH)
        pl.semaphore_wait(barrier, count + 1)
        swap().start()
        acc[...] = jnp.zeros_like(acc)
        for copy in loads:
            copy.wait()

    point("start")

    dconv[...] = lax.dot_general(dproj_ref[...], xp_ref[...], NT, preferred_element_type=F32)
    for h in range(halves):
        @pl.when(j // per == h)
        def _(h=h):
            acc[...] += lax.dot_general(dz_refs[h][...], wz_ref[...], NT, preferred_element_type=F32)
            dconv[...] += du_refs[h][...]

    point("dots")

    def conv(i, c):
        ln = pl.ds(pl.multiple_of(i * 128, 128), 128)
        weight = [cw_ref[taps - 1 - s:taps - s, ln] for s in range(taps)]
        x = x_ref[:, ln]
        mixed = cb_ref[:, ln] + weight[0] * x
        for s in range(1, taps):
            mixed = mixed + weight[s] * (pltpu.roll(x, s, 0) * mask_ref[s - 1])
        gate = jax.nn.sigmoid(mixed)
        d = dconv[:, ln] * (gate * (1.0 + mixed * (1.0 - gate)))
        gcb_ref[:, ln] = jnp.sum(d, axis=0, keepdims=True)
        gcw_ref[taps - 1:taps, ln] = jnp.sum(d * x, axis=0, keepdims=True)
        back = weight[0] * d
        for s in range(1, taps):
            masked = d * mask_ref[s - 1]
            gcw_ref[taps - 1 - s:taps - s, ln] = jnp.sum(masked * pltpu.roll(x, s, 0), axis=0, keepdims=True)
            back = back + weight[s] * pltpu.roll(masked, T - s, 0)
        dix[j, :, ln] = back.astype(BF16)
        return c

    lax.fori_loop(0, CH // 128, conv, 0)
    over = pltpu.make_async_remote_copy(src_ref=dix.at[j], dst_ref=sib.at[j], send_sem=core_send.at[j],
                                        recv_sem=core_recv.at[j], device_id={"dp": peer["core"]}, device_id_type=MESH)
    over.start()
    acc[...] += lax.dot_general(dix[j], wx_ref[...], NT, preferred_element_type=F32)
    rows = (((0,), (0,)), ((), ()))
    over.wait_recv()
    gx_ref[...] = (lax.dot_general(own_ref[...], dix[j], rows, preferred_element_type=F32)
                   + lax.dot_general(other_ref[...], sib[j], rows, preferred_element_type=F32)).astype(BF16)
    over.wait_send()

    point("end")

    @pl.when(j == steps - 1)
    def _():
        for b in range(16):
            sum_ref[:, b * 128:(b + 1) * 128] = s_out[sixteenth(b)].astype(F32)
        dn_ref[...] = acc[...].astype(BF16)
        swap().wait_recv()
        swap().wait_send()


def mid_call(dproj, masks, own, other, inner_x, w_x, w_z, x_proj, conv_weight, conv_bias, du, dz, mixed, gout, gz, small, CH=512):
    T, C = inner_x.shape
    D = w_x.shape[0]
    W = mixed.shape[1] // 2
    halves = len(du)
    taps = conv_weight.shape[0]
    steps = C // CH
    per = steps // halves
    S = jax.ShapeDtypeStruct
    V, DMA = pltpu.VMEM, pltpu.SemaphoreType.DMA
    const = lambda a: pl.BlockSpec(a.shape, lambda j: (0,) * a.ndim, pipeline_mode=pl.Buffered(1))
    col = lambda a: pl.BlockSpec((a.shape[0], CH), lambda j: (0, j))
    row = lambda a: pl.BlockSpec((CH, a.shape[1]), lambda j: (j, 0))
    part = lambda h: pl.BlockSpec((T, CH), lambda j: (0, jnp.clip(j - h * per, 0, per - 1)))
    anyspace = pl.BlockSpec(memory_space=pl.ANY)
    outs = (S((T, D), BF16), S((own.shape[1], C), BF16), S(small.shape, F32), S((taps, C), F32), S((1, C), F32),
            S((T, W), BF16),
            S((2,) + gout.shape[3:], BF16), S((2,) + gz.shape[3:], BF16))
    return pl.pallas_call(
        functools.partial(mid_kernel, taps, halves, steps),
        grid=(steps,),
        in_specs=[const(dproj), const(masks), const(own), const(other), col(inner_x), col(w_x), col(w_z), row(x_proj),
                  col(conv_weight), col(conv_bias)] + [part(h) for h in range(halves)] * 2 + [anyspace] * 4,
        out_specs=[pl.BlockSpec((T, D), lambda j: (0, 0)), col(outs[1]), pl.BlockSpec(small.shape, lambda j: (0, 0)), col(outs[3]), col(outs[4])] + [anyspace]
        + [pl.BlockSpec(o.shape, lambda j: (0, 0, 0)) for o in outs[6:]],
        out_shape=outs,
        scratch_shapes=[V((T, D), F32), V((T, CH), F32), V((steps, T, CH), BF16),
                        V((steps, T, CH), BF16), DMA, DMA, DMA((steps,)), DMA((steps,)),
                        *piece_scratch(2, *gout.shape[3:]), *total_scratch(small.shape[0])],
        compiler_params=pltpu.CompilerParams(collective_id=4, has_side_effects=True, vmem_limit_bytes=58 << 20,
                                             dimension_semantics=("arbitrary",)),
        cost_estimate=pl.CostEstimate(flops=6 * T * D * C, bytes_accessed=40 << 20, transcendentals=0),
        name="mid",
    )(dproj, masks, own, other, inner_x, w_x, w_z, x_proj, conv_weight, conv_bias, *du, *dz, mixed, gout, gz, small)


NT = (((1,), (1,)), ((), ()))
PR = 64


def scan_kernel(GR, NS, hosted, *refs):
    if not hosted:
        return scan_body(GR, NS, lambda at: None, *refs)
    ins, outs, own = 14, 10, 18
    refs = list(refs)
    g_refs = [refs.pop(ins), refs.pop(ins)]
    r_refs = [refs.pop(ins + outs), refs.pop(ins + outs)]
    scratch, refs = refs[-7:], refs[:-7]
    pieces = [piece_of(0, g_refs[0], "y", scratch, r_refs[0]), piece_of(1, g_refs[1], "near", scratch, r_refs[1])]
    steps = pl.num_programs(0)
    plan = {(0, "start"): 0, (0, "end"): 1, (1, "end"): 2}

    def host(at):
        for (step, place), stage in plan.items():
            if place != at:
                continue

            @pl.when(pl.program_id(0) == step)
            def _(stage=stage):
                if stage == 0:
                    me = lax.axis_index("dp")
                    peers = [me + STRIDE[n] * (1 - 2 * (me // STRIDE[n] % 2)) for n in ("y", "near", "far")]
                    pl.semaphore_wait(pltpu.get_barrier_semaphore(), greet_dp(peers))
                for piece in pieces:
                    (piece.step1, piece.step2, piece.stop)[stage]()

    return scan_body(GR, NS, host, *refs)


def scan_body(GR, NS, host, rank_ref, dtp_ref, dtb_ref, u_ref, z_ref, dg_ref, skip_ref,
                kb_ref, qb_ref, keep_ref, ksq_ref, qblk_ref, kblk_ref, k2blk_ref,
                gated_ref, diz_ref, du_ref, gskip_ref, gdtb_ref, gdtp_ref,
                drank_ref, sst_ref, dk_ref, dq_ref,
                den_s, step_s, su_s, ds_s, sz_s, y_s, d_s, e_s, h0_s, h1_s, ga_s, gb_s, ma_s, mb_s, dk_s, dq_s):
    T, CH = u_ref.shape
    L = CH // 128
    NG = T // GR
    R = GR * NS
    first, last = pl.program_id(0) == 0, pl.program_id(0) == pl.num_programs(0) - 1
    lanes = [slice(l * 128, (l + 1) * 128) for l in range(L)]
    hist = (h0_s, h1_s)

    @pl.when(first)
    def _():
        for r in (drank_ref, sst_ref, dk_s, dq_s):
            r[...] = jnp.zeros_like(r)
        h1_s[pl.ds(0, R), :] = jnp.zeros((R, CH), BF16)
        gb_s[...] = jnp.zeros_like(gb_s)
        mb_s[...] = jnp.zeros_like(mb_s)

    host("start")
    y_s[...] = jnp.dot(rank_ref[...], dtp_ref[...], preferred_element_type=F32)

    def prologue(r, acc):
        rows = pl.ds(pl.multiple_of(r * PR, PR), PR)
        kq = ksq_ref[rows, :]
        out = []
        for l in range(L):
            ln = lanes[l]
            beta = jax.nn.sigmoid(y_s[rows, ln] + dtb_ref[:, ln])
            den = 1.0 / (1.0 + beta * kq)
            step = beta * den
            den_s[rows, ln] = den
            step_s[rows, ln] = step
            u = u_ref[rows, ln]
            su_s[rows, ln] = step * u
            z = z_ref[rows, ln]
            s = jax.nn.sigmoid(z)
            sz_s[rows, ln] = s
            ds = dg_ref[rows, ln] * (z * s)
            ds_s[rows, ln] = ds
            out.append(acc[l] + jnp.sum(ds * u, axis=0, keepdims=True))
        return tuple(out)

    zrow = tuple(jnp.zeros((1, 128), F32) for _ in range(L))
    gsk = lax.fori_loop(0, T // PR, prologue, zrow)
    for l in range(L):
        gskip_ref[:, lanes[l]] = gsk[l]

    def rows_of(gi):
        return pl.ds(pl.multiple_of(gi * GR, GR), GR)

    def fill(gi, half, h, dst):
        h = list(h)
        base = pl.multiple_of(gi * GR, GR)
        rows = rows_of(gi)
        hb = pl.multiple_of(half * R, R)
        for j in range(GR):
            k = kb_ref[pl.ds(base * NS + j * NS, NS), :]
            kp = keep_ref.at[rows][j:j + 1, :]
            k2 = k * k * kp
            for l in range(L):
                a = kp - k2 * step_s.at[rows][j:j + 1, lanes[l]]
                h[l] = a * h[l] + k * su_s.at[rows][j:j + 1, lanes[l]]
                dst[pl.ds(hb + j * NS, NS), lanes[l]] = h[l].astype(BF16)
        return tuple(h)

    def read(gi, half, src):
        y_s[rows_of(gi), :] = jnp.dot(qblk_ref[rows_of(gi), :], src[pl.ds(pl.multiple_of(half * R, R), R), :],
                                      preferred_element_type=F32)

    def forward(i, h):
        before = jnp.maximum(i - 1, 0)
        read(2 * before + 1, before, h1_s)
        h = fill(2 * i, i, h, h0_s)
        read(2 * i, i, h0_s)
        return fill(2 * i + 1, i, h, h1_s)

    zst = tuple(jnp.zeros((NS, 128), F32) for _ in range(L))
    lax.fori_loop(0, NG // 2, forward, zst)
    read(NG - 1, NG // 2 - 1, h1_s)

    host("middle")

    def middle(r, c):
        rows = pl.ds(pl.multiple_of(r * PR, PR), PR)
        for l in range(L):
            ln = lanes[l]
            z = z_ref[rows, ln]
            s = sz_s[rows, ln]
            v = y_s[rows, ln] + skip_ref[:, ln] * u_ref[rows, ln]
            gated_ref[rows, ln] = (v * (z * s)).astype(BF16)
            diz_ref[rows, ln] = (dg_ref[rows, ln] * v * s * (1.0 + z * (1.0 - s))).astype(BF16)
        return c

    lax.fori_loop(0, T // PR, middle, 0)

    def back(gi, half, gc, own, before, before_at, g_dst, m_dst):
        gc = list(gc)
        base = pl.multiple_of(gi * GR, GR)
        rows = rows_of(gi)
        hb = pl.multiple_of(half * R, R)
        nows = [own[pl.ds(hb + (GR - 1) * NS, NS), ln] for ln in lanes]
        for j in reversed(range(GR)):
            at = pl.ds(base * NS + j * NS, NS)
            k = kb_ref[at, :]
            q = qb_ref[at, :]
            kp = keep_ref.at[rows][j:j + 1, :]
            k2 = k * k * kp
            a_sum = b_sum = q_sum = None
            for l in range(L):
                ln = lanes[l]
                ds = ds_s.at[rows][j:j + 1, ln]
                g = gc[l] + q * ds
                gb = g.astype(BF16)
                step = step_s.at[rows][j:j + 1, ln]
                now = nows[l]
                if j:
                    prev = own[pl.ds(hb + (j - 1) * NS, NS), ln]
                else:
                    prev = before[pl.ds(before_at + (GR - 1) * NS, NS), ln]
                nows[l] = prev
                m = gb * prev
                g_dst[j * NS:(j + 1) * NS, ln] = gb
                m_dst[j * NS:(j + 1) * NS, ln] = m
                wide = lambda v: jnp.broadcast_to(v, (NS, 128)).astype(BF16)
                pa = gb * wide(su_s.at[rows][j:j + 1, ln])
                pb = m * wide(step)
                pq = now * wide(ds)
                a_sum = pa if a_sum is None else a_sum + pa
                b_sum = pb if b_sum is None else b_sum + pb
                q_sum = pq if q_sum is None else q_sum + pq
                gc[l] = (kp - k2 * step) * g
            dk_s[at, :] += a_sum.astype(F32) - (2.0 * k * kp) * b_sum.astype(F32)
            dq_s[at, :] += q_sum.astype(F32)
        return tuple(gc)

    def sums(gi, g_src, m_src):
        rows = rows_of(gi)
        d_s[rows, :] = jnp.dot(kblk_ref[rows, :], g_src[...], preferred_element_type=F32)
        e_s[rows, :] = jnp.dot(k2blk_ref[rows, :], m_src[...], preferred_element_type=F32)

    def backward(i, gc):
        half = NG // 2 - 1 - i
        hi, lo = 2 * half + 1, 2 * half
        sums(jnp.minimum(hi + 1, NG - 1), gb_s, mb_s)
        gc = back(hi, half, gc, h1_s, h0_s, pl.multiple_of(half * R, R), ga_s, ma_s)
        sums(hi, ga_s, ma_s)
        return back(lo, half, gc, h0_s, h1_s, pl.multiple_of(jnp.maximum(half - 1, 0) * R, R), gb_s, mb_s)

    lax.fori_loop(0, NG // 2, backward, zst)
    sums(0, gb_s, mb_s)

    def epilogue(r, acc):
        rows = pl.ds(pl.multiple_of(r * PR, PR), PR)
        kp = keep_ref[rows, :]
        out = []
        ss = sst_ref[rows, :]
        for l in range(L):
            ln = lanes[l]
            step = step_s[rows, ln]
            dsum = d_s[rows, ln]
            dstep = u_ref[rows, ln] * dsum - kp * e_s[rows, ln]
            du_ref[rows, ln] = step * dsum + ds_s[rows, ln] * skip_ref[:, ln]
            t = dstep * step
            ss = ss + t * step
            db = t * (den_s[rows, ln] - step)
            y_s[rows, ln] = db
            out.append(acc[l] + jnp.sum(db, axis=0, keepdims=True))
        sst_ref[rows, :] = ss
        return tuple(out)

    gdb = lax.fori_loop(0, T // PR, epilogue, zrow)
    for l in range(L):
        gdtb_ref[:, lanes[l]] = gdb[l]
    dbl = y_s[...].astype(BF16)
    gdtp_ref[...] = lax.dot_general(rank_ref[...], dbl, (((0,), (0,)), ((), ())), preferred_element_type=F32)
    drank_ref[...] += lax.dot_general(dbl, dtp_ref[...], NT, preferred_element_type=F32)

    host("end")

    @pl.when(last)
    def _():
        ones = jnp.ones((8, 128), BF16)
        for src, dst in ((dk_s, dk_ref), (dq_s, dq_ref)):
            for c in range(0, T * NS, 1024):
                dst[:, c:c + 1024] = lax.dot_general(ones, src[c:c + 1024, :].astype(BF16), NT, preferred_element_type=F32)


def scan_call(piece, pieces, hosted, *args, CH=512, GR=16, NS=16):
    rank, dtp, dtb, u, z, dg, skip, kb, qb, keep, ksq, qblk, kblk, k2blk = args
    T, C = u.shape
    width = C // pieces
    CH = min(CH, width)
    first = piece * (width // CH)
    const = lambda a: pl.BlockSpec(a.shape, lambda j: (0,) * a.ndim, pipeline_mode=pl.Buffered(1))
    oconst = lambda a: pl.BlockSpec(a.shape, lambda j: (0,) * a.ndim)
    col = lambda a: pl.BlockSpec((a.shape[0], CH), lambda j: (0, j + first))
    out = lambda a: pl.BlockSpec((a.shape[0], CH), lambda j: (0, j))
    S = jax.ShapeDtypeStruct
    W = GR * NS
    R = rank.shape[1]
    outs = (S((T, width), BF16), S((T, width), BF16), S((T, width), F32), S((1, width), F32), S((1, width), F32), S((R, width), F32),
            S((T, R), F32), S((T, 128), F32), S((8, T * NS), F32), S((8, T * NS), F32))
    outs += tuple(S((2,) + g.shape[3:], BF16) for g in hosted)
    V = pltpu.VMEM
    f = pl.pallas_call(
        functools.partial(scan_kernel, GR, NS, bool(hosted)),
        grid=(width // CH,),
        in_specs=[const(rank), col(dtp), col(dtb), col(u), col(z), col(dg), col(skip), const(kb), const(qb),
                  const(keep), const(ksq), const(qblk), const(kblk), const(k2blk)] + [pl.BlockSpec(memory_space=pl.ANY)] * len(hosted),
        out_specs=[out(o) for o in outs[:6]] + [oconst(o) for o in outs[6:]],
        out_shape=outs,
        scratch_shapes=[V((T, CH), F32)] * 8 + [V((T * NS // 2, CH), BF16)] * 2 + [V((W, CH), BF16)] * 4 + [V((T * NS, 128), F32)] * 2
        + (piece_scratch(2, *hosted[0].shape[3:]) if hosted else []),
        compiler_params=pltpu.CompilerParams(vmem_limit_bytes=60 << 20, dimension_semantics=("arbitrary",),
                                             **(dict(collective_id=2, has_side_effects=True) if hosted else {})),
        cost_estimate=pl.CostEstimate(flops=T * width * NS * 800, bytes_accessed=T * width * 20, transcendentals=0),
        name="scan_reduce" if hosted else "scan",
    )
    return f(*args, *hosted)


def scan_all(rank, dtp, dtb, u, z, dg, skip, keys, query, keep, pieces, GR=16, **kw):
    T, NS = keys.shape
    kb = jnp.broadcast_to(keys[:, :, None], (T, NS, 128)).reshape(T * NS, 128)
    qb = jnp.broadcast_to(query[:, :, None], (T, NS, 128)).reshape(T * NS, 128)
    keepb = jnp.broadcast_to(keep[:, None], (T, 128))
    ksq = jnp.sum(keys * keys, axis=1)
    ksqb = jnp.broadcast_to(ksq[:, None], (T, 128))
    slot = (jnp.arange(T)[:, None] % GR == jnp.arange(GR * NS)[None, :] // NS).astype(F32)
    blk = lambda v: (slot * jnp.tile(v, (1, GR))).astype(BF16)
    qblk, kblk, k2blk = blk(query), blk(keys), blk(keys * keys)

    def run(piece, *hosted):
        o = scan_call(piece, pieces, hosted, rank, dtp, dtb, u, z, dg, skip, kb, qb, keepb, ksqb, qblk, kblk, k2blk, GR=GR, NS=NS, **kw)
        gated, diz, du, gskip, gdtb, gdtp, drank, sst, dk, dq, *summed = o
        dq = dq[0].reshape(T, NS)
        dk = dk[0].reshape(T, NS) - 2.0 * keys * jnp.sum(sst, axis=1, keepdims=True)
        return gated, diz, du, gskip, gdtb, gdtp, drank, dk, dq, summed

    return run


def tensor_other(value):
    return lax.ppermute(value, "tensor", [(0, 1), (1, 0)])


def tensor_total(value):
    if lax.axis_size("tensor") == 2:
        return value + tensor_other(value)
    return lax.psum(value, "tensor")


def half_total(value, me, width):
    if lax.axis_size("tensor") == 2:
        own = lax.dynamic_slice_in_dim(value, me * width, width, 1)
        sent = lax.dynamic_slice_in_dim(value, (1 - me) * width, width, 1).astype(BF16)
        return own + tensor_other(sent).astype(F32)
    return lax.psum_scatter(value, "tensor", scatter_dimension=1, tiled=True)


def full_columns(part, me):
    if lax.axis_size("tensor") == 2:
        other = tensor_other(part)
        return jnp.where(
            me == 0,
            jnp.concatenate([part, other], 1),
            jnp.concatenate([other, part], 1),
        )
    return lax.all_gather(part, "tensor", axis=1, tiled=True)


def pair_up(value, stride):
    count = lax.axis_size("dp")
    return lax.ppermute(value, "dp", [(i, i ^ stride) for i in range(count)])


def pick_dim(value, index, dim):
    return lax.dynamic_index_in_dim(value, index, dim, keepdims=False)


def pair_gradient(own, other, right):
    return (contract_rows(own, right) + contract_rows(other, pair_up(right, 1))).astype(BF16)


def after(value, *earlier):
    return lax.optimization_barrier((value,) + earlier)[0]


def flatten(values):
    return jnp.concatenate([v.reshape(-1) for v in values])


def cut(flat, values):
    out, at = [], 0
    for v in values:
        out.append(flat[at : at + v.size].reshape(v.shape))
        at += v.size
    return out


def position_in(keys):
    return jnp.sum((keys[None, :] < keys[:, None]).astype(jnp.int32), axis=1)


def conv_mix(inner_x, conv_weight, conv_bias, segment):
    row_count = inner_x.shape[0]
    taps = conv_weight.shape[0]
    mixed = conv_bias[None, :] + conv_weight[taps - 1][None, :] * inner_x
    for shift_by in range(1, taps):
        moved = jnp.concatenate([jnp.zeros((shift_by, inner_x.shape[1]), F32), inner_x[: row_count - shift_by]], 0)
        seg_moved = jnp.concatenate([jnp.full((shift_by,), -1, jnp.int32), segment[: row_count - shift_by]], 0)
        keep_mask = (seg_moved == segment).astype(F32)
        mixed = mixed + conv_weight[taps - 1 - shift_by][None, :] * moved * keep_mask[:, None]
    return mixed


def silu_conv(inner_x, conv_weight, conv_bias, segment):
    mixed = conv_mix(inner_x, conv_weight, conv_bias, segment)
    return mixed * jax.nn.sigmoid(mixed)


def contract_rows(left, right):
    return lax.dot_general(left, right, (((0,), (0,)), ((), ())), preferred_element_type=F32)


def contract_cols(left, right):
    return lax.dot_general(left, right, (((1,), (1,)), ((), ())), preferred_element_type=F32)


def body(tokens, cotangent, norm_gain, w_x, w_z, conv_weight, conv_bias, x_proj, dt_proj, dt_bias, skip_gain, w_out,
         seq_lengths, arrival_route, work_source):
    dp_count = lax.axis_size("dp")
    tp_count = lax.axis_size("tensor")
    row_count, feat_width = tokens.shape
    per_peer = row_count // dp_count
    col_share = feat_width // tp_count
    me = lax.axis_index("tensor")
    col_start = me * col_share
    low_rank = dt_proj.shape[0]
    state_size = (x_proj.shape[1] - low_rank) // 2
    position = jnp.arange(row_count, dtype=jnp.int32)

    deal = (position_in(arrival_route)[:, None] == position[None, :]).astype(BF16)
    settle = (position_in(work_source // row_count * row_count + position)[:, None] == position[None, :]).astype(BF16)

    def exchange(rows):
        out = lax.all_to_all(rows.reshape(dp_count, per_peer, rows.shape[1]), "dp", split_axis=0, concat_axis=0, tiled=True)
        return out.reshape(row_count, rows.shape[1])

    def pick(table, rows, dim):
        return lax.dot_general(table, rows, (((dim,), (0,)), ((), ())), preferred_element_type=F32).astype(BF16)

    def bring(values):
        part = lax.dynamic_slice_in_dim(values, col_start, col_share, 1)
        return full_columns(pick(settle, exchange(pick(deal, part, 0)), 1), me)

    def give_back(values):
        return pick(deal, exchange(pick(settle, values, 0)), 1)

    lengths = seq_lengths[0]
    count = lengths.shape[0]
    before = jnp.arange(count)[:, None] > jnp.arange(count)[None, :]
    offsets = jnp.sum(jnp.where(before, lengths[None, :], 0), axis=1)
    segment = jnp.sum((position[:, None] >= offsets[None, :]).astype(jnp.int32), axis=1) - 1
    keep = 1.0 - jnp.any(position[:, None] == offsets[None, :], axis=1).astype(F32)

    paired = dp_count == 16 and tp_count == 2
    if paired:
        taps = conv_weight.shape[0]
        pre = [jnp.concatenate([jnp.full((s,), -1, jnp.int32), segment[: row_count - s]]) for s in range(1, taps)]
        masks = jnp.stack([jnp.broadcast_to((p == segment).astype(F32)[:, None], (row_count, 128)) for p in pre])
        (x_half, normed, dy_work, scale_wide, normed_own, normed_other, dy_own, dy_other,
         inner_x, conv_out, conv_low, projected, inner_z, d_gated) = head_call(
            tokens, cotangent, w_x, w_z, w_out, norm_gain[None, :], deal.T, settle, masks, conv_weight, conv_bias[None, :], x_proj)
    else:
        x_work = bring(tokens)
        dy_work = bring(cotangent)
        resid = x_work.astype(F32)
        scale_row = lax.rsqrt(jnp.mean(resid * resid, axis=1, keepdims=True) + 1e-05)
        unit = resid * scale_row
        normed = (unit * norm_gain[None, :]).astype(BF16)
        inner_x = jnp.dot(normed, w_x, preferred_element_type=F32)
        conv_out, conv_pull = jax.vjp(partial(silu_conv, segment=segment), inner_x, conv_weight, conv_bias)
        conv_low = conv_out.astype(BF16)
        projected = tensor_total(jnp.dot(conv_low, x_proj, preferred_element_type=F32))
        inner_z = jnp.dot(normed, w_z, preferred_element_type=F32)
        d_gated = contract_cols(dy_work, w_out)
    rank_part = projected[:, :low_rank].astype(BF16)
    key_rows = projected[:, low_rank : low_rank + state_size]
    query_rows = projected[:, low_rank + state_size :]

    pieces = 2 if paired else 1
    scan = scan_all(rank_part, dt_proj, dt_bias[None, :], conv_out, inner_z, d_gated, skip_gain[None, :], key_rows,
                    query_rows, keep, pieces)
    scans = [scan(0)]
    if paired:
        blocks = lambda g: g.reshape(2, 2, 2, g.shape[0] // 8, g.shape[1])
        outer = lambda part: (blocks(pair_gradient(dy_own, dy_other, part[0])),
                              blocks(pair_gradient(normed_own, normed_other, part[1])))
        scans.append(scan(1, *outer(scans[0])))
    wide = lambda index: jnp.concatenate([part[index] for part in scans], axis=1) if paired else scans[0][index]
    grad_dt_proj = wide(5)
    grad_skip, grad_dt_bias = wide(3)[0], wide(4)[0]
    d_rank, d_keys, d_query = (sum(part[index] for part in scans) for index in (6, 7, 8))
    gated_low, d_inner_z_low = wide(0), wide(1)
    d_proj = tensor_total(jnp.concatenate([d_rank, d_keys, d_query], axis=1))
    mixed = jnp.dot(gated_low, w_out, preferred_element_type=F32)
    if paired:
        mixed = mixed.astype(BF16)
        g_out, g_z = outer(scans[1])
        bit = {name: lax.axis_index("dp") // stride % 2 for name, stride in STRIDE.items()}
        far = [pair_up(pick_dim(v, 1 - bit["far"], 0), STRIDE["far"]) for v in scans[1][9]]
        d_proj = after(d_proj, g_out, g_z, mixed)
        d_proj_low = d_proj.astype(BF16)
        rows = (contract_rows(d_proj_low, conv_low), grad_dt_proj, grad_dt_bias[None, :], grad_skip[None, :])
        stack = jnp.concatenate(rows).astype(BF16)
        stack = jnp.pad(stack, ((0, -stack.shape[0] % 16), (0, 0)))
        d_normed, g_x, stack, grad_conv_weight, grad_conv_bias, mixed_other, left_out, left_z = mid_call(
            d_proj_low, masks, normed_own, normed_other, inner_x, w_x, w_z, x_proj, conv_weight,
            conv_bias[None, :], [part[2] for part in scans], [part[1] for part in scans], mixed, g_out, g_z,
            stack)
        early = [pick_dim(v, bit["far"], 0).astype(F32) + after(came, d_normed).astype(F32)
                 for v, came in zip(scans[1][9], far)]
    else:
        d_proj_low = d_proj.astype(BF16)
        grad_x_proj = contract_rows(conv_low, d_proj_low)
        d_conv_out = scans[0][2] + contract_cols(d_proj_low, x_proj)
        d_inner_x, grad_conv_weight, grad_conv_bias = conv_pull(d_conv_out)
        d_inner_x_low = d_inner_x.astype(BF16)
        d_normed = contract_cols(d_inner_x_low, w_x) + contract_cols(d_inner_z_low, w_z)
    if paired:
        conv = jnp.concatenate([grad_conv_weight, grad_conv_bias])
        conv = jnp.pad(conv, ((0, 8 - conv.shape[0]), (0, 0)))
        out_tokens, in_grad, grad_gain, conv, grad_w_out, grad_w_z, grad_w_x = tail_call(
            left_out, left_z, blocks(g_x), d_normed, mixed, mixed_other, x_half, dy_work, conv, norm_gain[None, :],
            scale_wide, settle.T, deal)
        split = x_proj.shape[1]
        grad_x_proj, grad_dt_proj = stack[:split].T, stack[split : split + low_rank]
        grad_dt_bias, grad_skip = stack[split + low_rank], stack[split + low_rank + 1]
        grad_conv_weight, grad_conv_bias = conv[:taps], conv[taps]
        grad_gain = grad_gain[0]
        early_out, early_z = early
        grad_w_out = jnp.concatenate([early_out, grad_w_out], axis=1).T
        grad_w_z = jnp.concatenate([early_z, grad_w_z], axis=1)
    else:
        small = (grad_x_proj, grad_dt_proj, grad_conv_weight, grad_conv_bias, grad_dt_bias, grad_skip)
        unit_cols = lax.dynamic_slice_in_dim(unit, col_start, col_share, 1)
        gain_cols = lax.dynamic_slice_in_dim(norm_gain, col_start, col_share, 0)
        dy_cols = lax.dynamic_slice_in_dim(dy_work, col_start, col_share, 1).astype(F32)
        d_share = half_total(d_normed, me, col_share)
        d_unit_cols = d_share * gain_cols[None, :]
        row_total = tensor_total(jnp.sum(d_unit_cols * unit_cols, axis=1, keepdims=True))
        grad_gain = jnp.sum(d_share * unit_cols, axis=0)
        d_resid = dy_cols + scale_row * (d_unit_cols - unit_cols * (row_total / feat_width))
        mixed_share = half_total(mixed, me, col_share)
        out_cols = (lax.dynamic_slice_in_dim(resid, col_start, col_share, 1) + mixed_share).astype(BF16)
        out_tokens, in_grad = give_back(out_cols), give_back(d_resid.astype(BF16))
        grad_w_out, grad_w_z, grad_w_x = (
            lax.psum_scatter(g.astype(BF16), "dp", scatter_dimension=dim, tiled=True).astype(F32)
            for g, dim in ((contract_rows(gated_low, dy_work), 1), (contract_rows(normed, d_inner_z_low), 0),
                           (contract_rows(normed, d_inner_x_low), 0)))
        small += (grad_gain,)
        (grad_x_proj, grad_dt_proj, grad_conv_weight, grad_conv_bias, grad_dt_bias, grad_skip, grad_gain) = cut(
            lax.psum(flatten(small), "dp"), small)
    return (out_tokens, in_grad, grad_gain, grad_w_x, grad_w_z, grad_conv_weight, grad_conv_bias, grad_x_proj,
            grad_dt_proj, grad_dt_bias, grad_skip, grad_w_out)


def solution(mesh):
    in_specs = (
        P("dp", None),
        P("dp", None),
        P(),
        P(None, "tensor"),
        P(None, "tensor"),
        P(None, "tensor"),
        P("tensor"),
        P("tensor", None),
        P(None, "tensor"),
        P("tensor"),
        P("tensor"),
        P("tensor", None),
        P("dp", None),
        P("dp"),
        P("dp"),
    )
    out_specs = (
        P("dp", "tensor"),
        P("dp", "tensor"),
        P("tensor"),
        P("dp", "tensor"),
        P("dp", "tensor"),
        P(None, "tensor"),
        P("tensor"),
        P("tensor", None),
        P(None, "tensor"),
        P("tensor"),
        P("tensor"),
        P("tensor", "dp"),
    )
    return jax.shard_map(body, mesh=mesh, in_specs=in_specs, out_specs=out_specs, check_vma=False)
```

```python
import functools
from functools import partial

import jax
import jax.numpy as jnp
import numpy as np
from jax import lax
from jax.experimental import pallas as pl
from jax.experimental.pallas import tpu as pltpu
from jax.sharding import PartitionSpec as P

F32, BF16 = jnp.float32, jnp.bfloat16
MESH = pl.DeviceIdType.MESH
TILE = 32
GAIN_ROW = 5
STRIDE = {"core": 1, "y": 2, "near": 4, "far": 8}


class Piece:
    def __init__(self, grad, first, bufs, sems, result):
        self.grad, self.first, self.result = grad, first, result
        self.own, self.r1, self.r2, self.r3 = bufs
        self.local, self.send, self.recv = sems
        self.second = "near" if first == "y" else "y"

    def bit(self, name):
        return lax.axis_index("dp") // STRIDE[name] % 2

    def block(self, mine):
        return self.grad.at[:, :, mine] if self.first == "y" else self.grad.at[:, mine]

    def remote(self, step):
        s, f = self.bit(self.second), self.bit("far")
        name, src, dst = (
            (self.first, lambda: self.block(1 - self.bit(self.first)), self.r1),
            (self.second, lambda: self.own.at[:, 1 - s], self.r2),
            ("far", lambda: self.own.at[1 - f, s], self.r3),
        )[step]
        to = lax.axis_index("dp") + STRIDE[name] * (1 - 2 * self.bit(name))
        return pltpu.make_async_remote_copy(
            src_ref=src(), dst_ref=dst, send_sem=self.send.at[step], recv_sem=self.recv.at[step],
            device_id={"dp": to}, device_id_type=MESH)

    def load(self):
        return pltpu.make_async_copy(self.block(self.bit(self.first)), self.own, self.local)

    def step1(self):
        self.remote(0).start()
        self.load().start()

    def add(self, dst, src, out=None):
        def body(i, c):
            at = pl.ds(pl.multiple_of(i * TILE, TILE), TILE)
            total = dst[at, :].astype(F32) + src[at, :].astype(F32)
            if out is None:
                dst[at, :] = total.astype(BF16)
            else:
                out[at, :] = total.astype(out.dtype)
            return c

        lax.fori_loop(0, src.shape[0] // TILE, body, 0)

    def step2(self):
        self.load().wait()
        self.remote(0).wait_recv()
        s = self.bit(self.second)
        for far in range(2):
            self.add(self.own.at[far, 1 - s], self.r1.at[far, 1 - s])
        self.remote(1).start()
        for far in range(2):
            self.add(self.own.at[far, s], self.r1.at[far, s])

    def step3(self):
        self.remote(1).wait_recv()
        s, f = self.bit(self.second), self.bit("far")
        self.add(self.own.at[1 - f, s], self.r2.at[1 - f])
        self.remote(2).start()
        self.add(self.own.at[f, s], self.r2.at[f])

    def stop(self):
        self.remote(1).wait_recv()
        for far in range(2):
            place = far + self.bit("far") * (1 - 2 * far)
            self.add(self.own.at[far, self.bit(self.second)], self.r2.at[far], self.result.at[place])
        for step in range(2):
            self.remote(step).wait_send()

    def finish(self):
        self.remote(2).wait_recv()
        self.add(self.own.at[self.bit("far"), self.bit(self.second)], self.r3, self.result)
        for step in range(3):
            self.remote(step).wait_send()


class FarPiece(Piece):
    def __init__(self, grad, bufs, sems, result):
        self.grad, self.result = grad, result
        self.own, self.r3 = bufs
        self.local, self.send, self.recv = sems

    def remote(self, step):
        f = self.bit("far")
        return pltpu.make_async_remote_copy(
            src_ref=self.grad.at[1], dst_ref=self.r3, send_sem=self.send, recv_sem=self.recv,
            device_id={"dp": lax.axis_index("dp") + STRIDE["far"] * (1 - 2 * f)}, device_id_type=MESH)

    def load(self):
        return pltpu.make_async_copy(self.grad.at[0], self.own, self.local)

    def finish(self):
        self.load().wait()
        self.remote(0).wait_recv()
        self.add(self.own, self.r3, self.result)
        self.remote(0).wait_send()


def piece_scratch(k, n, w):
    V, DMA = pltpu.VMEM, pltpu.SemaphoreType.DMA
    return [V((k, 2, 2, n, w), BF16), V((k, 2, 2, n, w), BF16), V((k, 2, n, w), BF16), V((k, n, w), BF16),
            DMA((k,)), DMA((k, 3)), DMA((k, 3))]


def piece_of(i, grad, first, scratch, result):
    return Piece(grad, first, tuple(r.at[i] for r in scratch[:4]), tuple(r.at[i] for r in scratch[4:]), result)


def greet_dp(peers):
    for p in peers:
        pl.semaphore_signal(pltpu.get_barrier_semaphore(), inc=1, device_id={"dp": p}, device_id_type=MESH)
    return len(peers)


class Total:
    NAMES = ("y", "near", "far")

    def __init__(self, acc, half, got, out, sems):
        self.acc, self.half, self.got, self.out, self.sems = acc, half, got, out, sems
        self.me = lax.axis_index("dp")
        self.bits = {name: self.me // stride % 2 for name, stride in STRIDE.items()}

    def flip(self, q):
        path, to = [self.bits["core"]], self.me
        for n, name in enumerate(self.NAMES):
            bit, turn = self.bits[name], q >> n & 1
            path.append(1 - bit if turn else bit)
            if turn:
                to = to + STRIDE[name] * (1 - 2 * bit)
        return tuple(path), to

    def copies(self, stage):
        mine, core = self.flip(0)[0], self.bits["core"]
        other = self.me + 1 - 2 * core
        if stage == 0:
            jobs = [(0, self.acc.at[1 - core], self.half, other)]
        elif stage == 1:
            jobs = [(q, self.acc.at[self.flip(q)[0]], self.got.at[q], self.flip(q)[1]) for q in range(1, 8)]
        elif stage == 2:
            jobs = [(q, self.out.at[mine], self.out.at[mine], self.flip(q)[1]) for q in range(1, 8)]
        else:
            jobs = [(0, self.out.at[core], self.out.at[core], other)]
        return [pltpu.make_async_remote_copy(
            src_ref=src, dst_ref=dst, send_sem=self.sems[0].at[stage, q], recv_sem=self.sems[1].at[stage, q],
            device_id={"dp": to}, device_id_type=MESH) for q, src, dst, to in jobs]

    def step(self, i):
        if i:
            for copy in self.copies(i - 1):
                copy.wait_recv()
        if i == 1:
            for b in range(8):
                at = (b // 4, b // 2 % 2, b % 2)
                here = self.acc.at[(self.bits["core"],) + at]
                here[...] = (here[...].astype(F32) + self.half[at].astype(F32)).astype(BF16)
        if i == 2:
            mine = self.flip(0)[0]
            total = self.acc[mine].astype(F32)
            for q in range(1, 8):
                total = total + self.got[q].astype(F32)
            self.out[mine] = total.astype(BF16)
        if i < 4:
            for copy in self.copies(i):
                copy.start()
        else:
            for stage in range(4):
                for copy in self.copies(stage):
                    copy.wait_send()


def sixteenth(b):
    return b // 8, b // 4 % 2, b // 2 % 2, b % 2


def total_scratch(rows):
    V, DMA = pltpu.VMEM, pltpu.SemaphoreType.DMA
    full = (2, 2, 2, 2, rows, 128)
    return [V(full, BF16), V(full[1:], BF16), V((8, rows, 128), BF16), V(full, BF16), DMA((4, 8)), DMA((4, 8)), DMA((16,))]


def tail_kernel(gout_ref, gz_ref, kout_ref, kz_ref, fout_ref, fz_ref, gx_ref, dn_ref, mx_ref, other_ref, x_ref, dy_ref, conv_ref, gain_ref, scale_ref, settle_ref, deal_ref,
                out_ref, in_ref, gg_ref, csum_ref, wout_ref, wz_ref, wx_ref,
                p0, p1, p2, p3, p4, p5, p6,
                dn_own, dn_got, mx_own, mx_got, x_half, dy_half, du, rs_own, rs_got, low,
                y_send, y_got, d_send, d_got, sem, x_send, x_recv, a_send, a_recv,
                m_part, m_got, m_out, m_send, m_recv,
                f_own, f_got, f_sem, early, wout_s):
    me, ten = lax.axis_index("dp"), lax.axis_index("tensor")
    count = lax.axis_size("dp")
    T, W = x_half.shape
    L = W // 128
    per = T // count
    barrier = pltpu.get_barrier_semaphore()
    for p in range(1, count):
        pl.semaphore_signal(barrier, inc=1, device_id={"dp": (me + p) % count}, device_id_type=MESH)
    pl.semaphore_signal(barrier, inc=1, device_id={"tensor": 1 - ten}, device_id_type=MESH)
    mine = pl.ds(pl.multiple_of(ten * W, 128), W)
    other = pl.ds(pl.multiple_of((1 - ten) * W, 128), W)
    loads = []
    jobs = [(mx_ref.at[:, mine], mx_own), (other_ref, mx_got), (x_ref, x_half), (dn_ref.at[:, mine], dn_own),
            (dy_ref.at[:, mine], dy_half)]
    jobs += [(kout_ref.at[0], early.at[0]), (fout_ref, early.at[1]), (kz_ref.at[0], early.at[2]), (fz_ref, early.at[3])]
    for b in range(count):
        jobs.append((conv_ref.at[:, b * 128 : (b + 1) * 128], m_part.at[b]))
    for n, (src, dst) in enumerate(jobs):
        copy = pltpu.make_async_copy(src, dst, sem.at[n])
        copy.start()
        loads.append(copy)
    pl.semaphore_wait(barrier, count)

    def swap(src, dst, n):
        copy = pltpu.make_async_remote_copy(
            src_ref=src, dst_ref=dst, send_sem=x_send.at[n], recv_sem=x_recv.at[n],
            device_id={"tensor": 1 - ten}, device_id_type=MESH)
        copy.start()
        return copy

    dn_copy = swap(dn_ref.at[:, other], dn_got, 0)
    bits = {"core": me % 2, "y": me // 2 % 2, "near": me // 4 % 2, "far": me // 8}
    half = gout_ref.shape[-1]
    scratch = (p0, p1, p2, p3, p4, p5, p6)
    x_cols = [slice(0, half), slice(half, 2 * half)]
    pieces = [
        FarPiece(gout_ref, (f_own.at[0], f_got.at[0]), tuple(f_sem.at[0, n] for n in range(3)), wout_s.at[:, x_cols[1]]),
        FarPiece(gz_ref, (f_own.at[1], f_got.at[1]), tuple(f_sem.at[1, n] for n in range(3)), wz_ref.at[:, x_cols[1]]),
        piece_of(0, gx_ref.at[:, :, :, :, x_cols[0]], "y", scratch, wx_ref.at[:, x_cols[0]]),
        piece_of(1, gx_ref.at[:, :, :, :, x_cols[1]], "near", scratch, wx_ref.at[:, x_cols[1]]),
    ]
    for piece in (pieces[2], pieces[3], pieces[0], pieces[1]):
        piece.step1()
    for copy in loads:
        copy.wait()
    def small(stage, p):
        to = (me + p) % count
        src, dst = ((m_part.at[to], m_got.at[me]), (m_out.at[me], m_out.at[me]))[stage]
        return pltpu.make_async_remote_copy(
            src_ref=src, dst_ref=dst, send_sem=m_send.at[stage, p], recv_sem=m_recv.at[stage, p],
            device_id={"dp": to}, device_id_type=MESH)

    def tiles(body, init):
        def step(i, c):
            return body(pl.ds(pl.multiple_of(i * 16, 16), 16), c)
        return lax.fori_loop(0, T // 16, step, init)

    def add_resid(at, c):
        for l in range(L):
            ln = slice(l * 128, (l + 1) * 128)
            both = mx_own[at, ln].astype(F32) + mx_got[at, ln].astype(F32)
            mx_own[at, ln] = (x_half[at, ln].astype(F32) + both).astype(BF16)
        return c

    def deal_out(rows, send, got, n):
        sent = jnp.dot(settle_ref[...], rows[...], preferred_element_type=F32).astype(BF16)
        send[...] = sent.reshape(send.shape)
        got[me] = send[me]
        copies = []
        for p in range(1, count):
            to = (me + p) % count
            copy = pltpu.make_async_remote_copy(
                src_ref=send.at[to], dst_ref=got.at[me], send_sem=a_send.at[n, p], recv_sem=a_recv.at[n, p],
                device_id={"dp": to}, device_id_type=MESH)
            copy.start()
            copies.append(copy)
        return copies

    def take_in(copies, got, out):
        for copy in copies:
            copy.wait_recv()
        out[...] = jnp.dot(deal_ref[...], got[...].reshape(T, W), preferred_element_type=F32).astype(BF16)
        for copy in copies:
            copy.wait_send()

    tiles(add_resid, 0)
    y_copies = deal_out(mx_own, y_send, y_got, 1)

    dn_copy.wait_recv()
    gain = gain_ref[:, mine]

    def share(at, acc):
        scale = scale_ref[at, :]
        total = None
        out = []
        for l in range(L):
            ln = slice(l * 128, (l + 1) * 128)
            d = dn_own[at, ln].astype(F32) + dn_got[at, ln].astype(F32)
            unit = x_half[at, ln].astype(F32) * scale
            d_unit = d * gain[:, ln]
            du[at, ln] = d_unit
            out.append(acc[l] + jnp.sum(d * unit, axis=0, keepdims=True))
            total = d_unit * unit if total is None else total + d_unit * unit
        rs_own[at, :] = total
        return tuple(out)

    acc = tiles(share, tuple(jnp.zeros((1, 128), F32) for _ in range(L)))
    rs_copy = swap(rs_own, rs_got, 2)
    for l in range(L):
        m_part[l, GAIN_ROW : GAIN_ROW + 1, :] = acc[l]
    for p in range(1, count):
        small(0, p).start()
    m_got[me] = m_part[me]
    pieces[2].step2()
    pieces[3].step2()
    rs_copy.wait_recv()

    def norm_back(at, c):
        scale = scale_ref[at, :]
        total = jnp.sum(rs_own[at, :] + rs_got[at, :], axis=1, keepdims=True) * (0.5 / W)
        for l in range(L):
            ln = slice(l * 128, (l + 1) * 128)
            unit = x_half[at, ln].astype(F32) * scale
            low[at, ln] = (dy_half[at, ln].astype(F32) + scale * (du[at, ln] - unit * total)).astype(BF16)
        return c

    tiles(norm_back, 0)
    d_copies = deal_out(low, d_send, d_got, 0)
    for p in range(1, count):
        small(0, p).wait_recv()
    m_out[me] = jnp.sum(m_got[...], axis=0)
    for p in range(1, count):
        small(1, p).start()
    pieces[2].step3()
    pieces[3].step3()
    wout_s[:, x_cols[0]] = early[0].astype(F32) + early[1].astype(F32)
    wz_ref[:, x_cols[0]] = early[2].astype(F32) + early[3].astype(F32)
    pieces[0].finish()
    pieces[1].finish()
    wout_ref[...] = wout_s[...].T
    take_in(y_copies, y_got, out_ref)
    for p in range(1, count):
        small(1, p).wait_recv()
    for b in range(count):
        csum_ref[:, b * 128 : (b + 1) * 128] = m_out[b]
    for l in range(L):
        gg_ref[:, l * 128 : (l + 1) * 128] = m_out[l, GAIN_ROW : GAIN_ROW + 1, :]
    take_in(d_copies, d_got, in_ref)
    pieces[2].finish()
    pieces[3].finish()
    for copy in (dn_copy, rs_copy):
        copy.wait_send()
    for stage in range(2):
        for p in range(1, count):
            small(stage, p).wait_send()


def tail_call(gout, gz, kept, far, gx, dn, mx, other, x, dy, conv, gain, scale, settle_t, deal):
    T, W = x.shape
    D = 2 * W
    n, half = gout.shape[1:]
    count = lax.axis_size("dp")
    S = jax.ShapeDtypeStruct
    full = 2 * half
    outs = (S((T, W), BF16), S((T, W), BF16), S((1, W), F32), S(conv.shape, F32), S((full, n), F32), S((n, full), F32), S((n, full), F32))
    anyspace = pl.BlockSpec(memory_space=pl.ANY)
    vmem = pl.BlockSpec(memory_space=pltpu.VMEM)
    V, DMA = pltpu.VMEM, pltpu.SemaphoreType.DMA
    return pl.pallas_call(
        tail_kernel,
        out_shape=outs,
        in_specs=[anyspace] * 13 + [vmem] * 4,
        out_specs=[vmem] * 7,
        scratch_shapes=[
            *piece_scratch(2, n, half),
            V((T, W), BF16), V((T, W), BF16), V((T, W), BF16), V((T, W), BF16), V((T, W), BF16), V((T, W), BF16),
            V((T, W), F32), V((T, 128), F32), V((T, 128), F32), V((T, W), BF16),
            V((count, T // count, W), BF16), V((count, T // count, W), BF16),
            V((count, T // count, W), BF16), V((count, T // count, W), BF16),
            DMA((9 + count,)), DMA((3,)), DMA((3,)), DMA((2, count)), DMA((2, count)),
            V((count, 8, 128), F32), V((count, 8, 128), F32), V((count, 8, 128), F32), DMA((2, count)), DMA((2, count)),
            V((2, n, half), BF16), V((2, n, half), BF16), DMA((2, 3)), V((4, n, half), BF16), V((n, full), F32),
        ],
        compiler_params=pltpu.CompilerParams(collective_id=1, has_side_effects=True, vmem_limit_bytes=58 << 20),
        cost_estimate=pl.CostEstimate(flops=T * T * D * 4, bytes_accessed=64 << 20, transcendentals=0),
        name="tail",
    )(gout, gz, *kept, *far, gx, dn, mx, other, x, dy, conv, gain, scale, settle_t, deal)


NT = (((1,), (1,)), ((), ()))


def head_kernel(taps, tok_ref, cot_ref, w_ref, wz_ref, wo_ref, gain_ref, deal_ref, settle_ref, mask_ref, cw_ref, cb_ref, xp_ref,
                half_ref, normed_ref, dy_ref, scale_ref, n_own_ref, n_other_ref, d_own_ref, d_other_ref,
                inner_ref, conv_ref, low_ref, keys_ref, z_ref, dg_ref, rank_ref, ksq_ref,
                part, send, got, across, n_send, d_send, w_s, p_own, p_got, load, w_load, p_send, p_recv, a_send, a_recv, x_send, x_recv, c_send, c_recv):
    me, ten = lax.axis_index("dp"), lax.axis_index("tensor")
    count = lax.axis_size("dp")
    T, W = half_ref.shape
    chunks, per, WC = send.shape[1], send.shape[3], send.shape[4]
    barrier = pltpu.get_barrier_semaphore()
    greet_dp([(me + p) % count for p in range(1, count)])
    pl.semaphore_signal(barrier, inc=1, device_id={"tensor": 1 - ten}, device_id_type=MESH)
    start = pl.multiple_of(ten * W, 128)
    away = pl.multiple_of((1 - ten) * W, 128)
    loads = [pltpu.make_async_copy(src.at[:, pl.ds(start, W)], part.at[n], load.at[n]) for n, src in enumerate((tok_ref, cot_ref))]
    weights = [pltpu.make_async_copy(w, w_s, w_load.at[n]) for n, w in enumerate((w_ref, wz_ref, wo_ref))]
    for copy in loads:
        copy.start()
    weights[0].start()

    def deal(n):
        loads[n].wait()
        rows = jnp.dot(deal_ref[...], part[n], preferred_element_type=F32).astype(BF16)
        for c in range(chunks):
            send[n, c] = rows[:, c * WC : (c + 1) * WC].reshape(count, per, WC)

    def out(n, c, p):
        to = (me + p) % count
        return pltpu.make_async_remote_copy(
            src_ref=send.at[n, c, to], dst_ref=got.at[n, c, me], send_sem=a_send.at[n, c, p], recv_sem=a_recv.at[n, c, p],
            device_id={"dp": to}, device_id_type=MESH)

    def over(n, c, p):
        at = (me + count - p) % count
        return pltpu.make_async_remote_copy(
            src_ref=(send if p == 0 else got).at[n, c, at], dst_ref=across.at[n, c, at], send_sem=x_send.at[n, c, p],
            recv_sem=x_recv.at[n, c, p], device_id={"tensor": 1 - ten}, device_id_type=MESH)

    def launch(n, c):
        for p in range(1, count):
            out(n, c, p).start()
        over(n, c, 0).start()
        got[n, c, me] = send[n, c, me]

    def forward(n, c):
        for p in range(1, count):
            out(n, c, p).wait_recv()
            over(n, c, p).start()

    def settle(n, c, source, into, begin):
        rows = jnp.dot(settle_ref[...], source[n, c].reshape(T, WC), preferred_element_type=F32)
        into[:, pl.ds(pl.multiple_of(begin + c * WC, 128), WC)] = rows.astype(BF16)

    order = [(n, c) for n in range(2) for c in range(chunks)]
    deal(0)
    pl.semaphore_wait(barrier, count)
    launch(0, 0)
    deal(1)
    for at in range(chunks):
        forward(*order[at])
        launch(*order[at + 1])
        settle(0, at, got, half_ref, 0)
    for c in range(chunks):
        for p in range(count):
            over(0, c, p).wait_recv()
        if c == chunks - 1:
            forward(1, 0)
            launch(1, 1)
        settle(0, c, across, part.at[0], 0)
    core = me % 2

    def norm(i, c):
        at = pl.ds(pl.multiple_of(i * 16, 16), 16)
        mine, other = half_ref[at, :].astype(F32), part[0, at, :].astype(F32)
        square = jnp.sum(mine * mine + other * other, axis=1, keepdims=True)
        scale = lax.rsqrt(square * (0.5 / W) + 1e-05)
        scale_ref[at, :] = jnp.broadcast_to(scale, (16, 128))
        for value, begin in ((mine, start), (other, away)):
            cols = pl.ds(begin, W)
            normed_ref[at, cols] = (value * scale * gain_ref[:, cols]).astype(BF16)
        return c

    lax.fori_loop(0, T // 16, norm, 0)

    def halves(source, own, other):
        def body(b, c):
            for into, k in ((own, core), (other, 1 - core)):
                into[:, pl.ds(pl.multiple_of(b * 128, 128), 128)] = source[:, pl.ds(pl.multiple_of((2 * b + k) * 128, 128), 128)]
            return c

        lax.fori_loop(0, W // 128, body, 0)

    def swap(n, source, into):
        return pltpu.make_async_remote_copy(
            src_ref=source, dst_ref=into, send_sem=c_send.at[n], recv_sem=c_recv.at[n],
            device_id={"dp": me + 1 - 2 * core}, device_id_type=MESH)

    halves(normed_ref, n_own_ref, n_send)
    first = swap(0, n_send, n_other_ref)
    first.start()
    CH = 512
    wide = range(0, inner_ref.shape[1], CH)
    weights[0].wait()
    for c in wide:
        inner_ref[:, c : c + CH] = jnp.dot(normed_ref[...], w_s[:, c : c + CH], preferred_element_type=F32)
    weights[1].start()
    for c in range(1, chunks):
        forward(1, c)
        if c + 1 < chunks:
            launch(1, c + 1)

    def conv(i, c):
        ln = pl.ds(pl.multiple_of(i * 128, 128), 128)
        x = inner_ref[:, ln]
        mixed = cb_ref[:, ln] + cw_ref[taps - 1 : taps, ln] * x
        for s in range(1, taps):
            mixed = mixed + cw_ref[taps - 1 - s : taps - s, ln] * (pltpu.roll(x, s, 0) * mask_ref[s - 1])
        value = mixed * jax.nn.sigmoid(mixed)
        conv_ref[:, ln] = value
        low_ref[:, ln] = value.astype(BF16)
        return c

    lax.fori_loop(0, inner_ref.shape[1] // 128, conv, 0)
    p_own[...] = jnp.dot(low_ref[...], xp_ref[...], preferred_element_type=F32)
    share = pltpu.make_async_remote_copy(src_ref=p_own, dst_ref=p_got, send_sem=p_send, recv_sem=p_recv,
                                         device_id={"tensor": 1 - ten}, device_id_type=MESH)
    share.start()
    weights[1].wait()
    for c in wide:
        z_ref[:, c : c + CH] = jnp.dot(normed_ref[...], w_s[:, c : c + CH], preferred_element_type=F32)
    weights[2].start()
    for c in range(chunks):
        settle(1, c, got, dy_ref, start)
    for c in range(chunks):
        for p in range(count):
            over(1, c, p).wait_recv()
        settle(1, c, across, dy_ref, away)
    halves(dy_ref, d_own_ref, d_send)
    second = swap(1, d_send, d_other_ref)
    second.start()
    weights[2].wait()
    for c in wide:
        dg_ref[:, c : c + CH] = lax.dot_general(dy_ref[...], w_s[c : c + CH, :], NT, preferred_element_type=F32)
    share.wait_recv()
    rank = rank_ref.shape[1]
    state = keys_ref.shape[1] // 2

    def whole(i, c):
        at = pl.ds(pl.multiple_of(i * 32, 32), 32)
        total = p_own[at, :] + p_got[at, :]
        rank_ref[at, :] = total[:, :rank].astype(BF16)
        keys_ref[at, :] = total[:, rank:]
        keys = total[:, rank : rank + state]
        ksq_ref[at, :] = jnp.broadcast_to(jnp.sum(keys * keys, axis=1, keepdims=True), (32, 128))
        return c

    lax.fori_loop(0, T // 32, whole, 0)
    share.wait_send()
    for copy in (first, second):
        copy.wait_recv()
        copy.wait_send()
    for n, c in order:
        for p in range(count):
            over(n, c, p).wait_send()
            if p:
                out(n, c, p).wait_send()


def head_call(tokens, cotangent, w_x, w_z, w_out, gain, deal_t, settle, masks, conv_weight, conv_bias, x_proj, rank, chunks=2):
    T, D = tokens.shape
    W = D // 2
    count = lax.axis_size("dp")
    S = jax.ShapeDtypeStruct
    V, DMA = pltpu.VMEM, pltpu.SemaphoreType.DMA
    outs = (S((T, W), BF16), S((T, D), BF16), S((T, D), BF16), S((T, 128), F32)) + (S((T, W), BF16),) * 4
    C = w_x.shape[1]
    outs += (S((T, C), F32), S((T, C), F32), S((T, C), BF16), S((T, x_proj.shape[1] - rank), F32),
             S((T, C), F32), S((T, C), F32), S((T, rank), BF16), S((T, 128), F32))
    block = V((2, chunks, count, T // count, W // chunks), BF16)
    vmem = pl.BlockSpec(memory_space=pltpu.VMEM)
    return pl.pallas_call(
        functools.partial(head_kernel, conv_weight.shape[0]),
        out_shape=outs,
        in_specs=[pl.BlockSpec(memory_space=pl.ANY)] * 5 + [vmem] * 7,
        out_specs=[vmem] * len(outs),
        scratch_shapes=[V((2, T, W), BF16), block, block, block, V((T, W), BF16), V((T, W), BF16), V(w_x.shape, BF16),
                        V((T, x_proj.shape[1]), F32), V((T, x_proj.shape[1]), F32), DMA((2,)), DMA((3,)), DMA, DMA] + [DMA((2, chunks, count))] * 4 + [ DMA((2,)), DMA((2,))],
        compiler_params=pltpu.CompilerParams(collective_id=3, has_side_effects=True, vmem_limit_bytes=58 << 20),
        cost_estimate=pl.CostEstimate(flops=T * T * D * 4, bytes_accessed=48 << 20, transcendentals=0),
        name="head",
    )(tokens, cotangent, w_x, w_z, w_out, gain, deal_t, settle, masks, conv_weight, conv_bias, x_proj)


def mid_kernel(taps, halves, count_steps, *refs):
    (dproj_ref, mask_ref, own_ref, other_ref, x_ref, wx_ref, wz_ref, xp_ref, cw_ref, cb_ref) = refs[:10]
    du_refs, dz_refs = refs[10:10 + halves], refs[10 + halves:10 + 2 * halves]
    (mixed_ref, gout_ref, gz_ref, small_ref, dn_ref, gx_ref, sum_ref, gcw_ref, gcb_ref, mgot_ref, cout_ref, cz_ref,
     acc, dconv, dix, sib, sends, recvs, core_send, core_recv, *scratch) = refs[10 + 2 * halves:]
    j, steps = pl.program_id(0), pl.num_programs(0)
    me, ten = lax.axis_index("dp"), lax.axis_index("tensor")
    T, CH = x_ref.shape
    W = mgot_ref.shape[1]
    bit = {name: me // stride % 2 for name, stride in STRIDE.items()}
    peer = {name: me + stride * (1 - 2 * bit[name]) for name, stride in STRIDE.items()}
    per = steps // halves
    s_acc, s_half, s_got, s_out, s_send, s_recv, s_load = scratch[7:]
    total = Total(s_acc, s_half, s_got, s_out, (s_send, s_recv))
    scratch = scratch[:7]
    pieces = [piece_of(0, gout_ref, "y", scratch, cout_ref), piece_of(1, gz_ref, "near", scratch, cz_ref)]

    def swap():
        far = pl.ds(pl.multiple_of((1 - ten) * W, 128), W)
        return pltpu.make_async_remote_copy(src_ref=mixed_ref.at[:, far], dst_ref=mgot_ref, send_sem=sends, recv_sem=recvs,
                                            device_id={"tensor": 1 - ten}, device_id_type=MESH)

    def small(*at):
        return [functools.partial(total.step, i) for i in at]

    final = count_steps - 1
    program = {
        (0, "start"): small(0) + [pieces[0].step1, pieces[1].step1],
        (0, "dots"): small(1),
        (1, "end"): small(2),
        (2, "dots"): [pieces[0].step2, pieces[1].step2],
        (2, "end"): small(3),
        (3, "end"): small(4) + [pieces[0].stop, pieces[1].stop],
    }

    def point(place):
        for (step, at), actions in program.items():
            if at == place:
                @pl.when(j == min(step, final))
                def _(actions=actions):
                    for act in actions:
                        act()

    @pl.when(j == 0)
    def _():
        loads = [pltpu.make_async_copy(small_ref.at[:, b * 128:(b + 1) * 128], s_acc.at[sixteenth(b)], s_load.at[b])
                 for b in range(16)]
        for copy in loads:
            copy.start()
        barrier = pltpu.get_barrier_semaphore()
        count = greet_dp([peer["core"]] + [total.flip(q)[1] for q in range(1, 8)])
        pl.semaphore_signal(barrier, inc=1, device_id={"tensor": 1 - ten}, device_id_type=MESH)
        pl.semaphore_wait(barrier, count + 1)
        swap().start()
        acc[...] = jnp.zeros_like(acc)
        for copy in loads:
            copy.wait()

    point("start")

    dconv[...] = lax.dot_general(dproj_ref[...], xp_ref[...], NT, preferred_element_type=F32)
    for h in range(halves):
        @pl.when(j // per == h)
        def _(h=h):
            acc[...] += lax.dot_general(dz_refs[h][...], wz_ref[...], NT, preferred_element_type=F32)
            dconv[...] += du_refs[h][...]

    point("dots")

    def conv(i, c):
        ln = pl.ds(pl.multiple_of(i * 128, 128), 128)
        weight = [cw_ref[taps - 1 - s:taps - s, ln] for s in range(taps)]
        x = x_ref[:, ln]
        mixed = cb_ref[:, ln] + weight[0] * x
        for s in range(1, taps):
            mixed = mixed + weight[s] * (pltpu.roll(x, s, 0) * mask_ref[s - 1])
        gate = jax.nn.sigmoid(mixed)
        d = dconv[:, ln] * (gate * (1.0 + mixed * (1.0 - gate)))
        gcb_ref[:, ln] = jnp.sum(d, axis=0, keepdims=True)
        gcw_ref[taps - 1:taps, ln] = jnp.sum(d * x, axis=0, keepdims=True)
        back = weight[0] * d
        for s in range(1, taps):
            masked = d * mask_ref[s - 1]
            gcw_ref[taps - 1 - s:taps - s, ln] = jnp.sum(masked * pltpu.roll(x, s, 0), axis=0, keepdims=True)
            back = back + weight[s] * pltpu.roll(masked, T - s, 0)
        dix[j, :, ln] = back.astype(BF16)
        return c

    lax.fori_loop(0, CH // 128, conv, 0)
    over = pltpu.make_async_remote_copy(src_ref=dix.at[j], dst_ref=sib.at[j], send_sem=core_send.at[j],
                                        recv_sem=core_recv.at[j], device_id={"dp": peer["core"]}, device_id_type=MESH)
    over.start()
    acc[...] += lax.dot_general(dix[j], wx_ref[...], NT, preferred_element_type=F32)
    rows = (((0,), (0,)), ((), ()))
    over.wait_recv()
    gx_ref[...] = (lax.dot_general(own_ref[...], dix[j], rows, preferred_element_type=F32)
                   + lax.dot_general(other_ref[...], sib[j], rows, preferred_element_type=F32)).astype(BF16)
    over.wait_send()

    point("end")

    @pl.when(j == steps - 1)
    def _():
        for b in range(16):
            sum_ref[:, b * 128:(b + 1) * 128] = s_out[sixteenth(b)].astype(F32)
        dn_ref[...] = acc[...].astype(BF16)
        swap().wait_recv()
        swap().wait_send()


def mid_call(dproj, masks, own, other, inner_x, w_x, w_z, x_proj, conv_weight, conv_bias, du, dz, mixed, gout, gz, small, CH=512):
    T, C = inner_x.shape
    D = w_x.shape[0]
    W = mixed.shape[1] // 2
    halves = len(du)
    taps = conv_weight.shape[0]
    steps = C // CH
    per = steps // halves
    S = jax.ShapeDtypeStruct
    V, DMA = pltpu.VMEM, pltpu.SemaphoreType.DMA
    const = lambda a: pl.BlockSpec(a.shape, lambda j: (0,) * a.ndim, pipeline_mode=pl.Buffered(1))
    col = lambda a: pl.BlockSpec((a.shape[0], CH), lambda j: (0, j))
    row = lambda a: pl.BlockSpec((CH, a.shape[1]), lambda j: (j, 0))
    part = lambda h: pl.BlockSpec((T, CH), lambda j: (0, jnp.clip(j - h * per, 0, per - 1)))
    anyspace = pl.BlockSpec(memory_space=pl.ANY)
    outs = (S((T, D), BF16), S((own.shape[1], C), BF16), S(small.shape, F32), S((taps, C), F32), S((1, C), F32),
            S((T, W), BF16),
            S((2,) + gout.shape[3:], BF16), S((2,) + gz.shape[3:], BF16))
    return pl.pallas_call(
        functools.partial(mid_kernel, taps, halves, steps),
        grid=(steps,),
        in_specs=[const(dproj), const(masks), const(own), const(other), col(inner_x), col(w_x), col(w_z), row(x_proj),
                  col(conv_weight), col(conv_bias)] + [part(h) for h in range(halves)] * 2 + [anyspace] * 4,
        out_specs=[pl.BlockSpec((T, D), lambda j: (0, 0)), col(outs[1]), pl.BlockSpec(small.shape, lambda j: (0, 0)), col(outs[3]), col(outs[4])] + [anyspace]
        + [pl.BlockSpec(o.shape, lambda j: (0, 0, 0)) for o in outs[6:]],
        out_shape=outs,
        scratch_shapes=[V((T, D), F32), V((T, CH), F32), V((steps, T, CH), BF16),
                        V((steps, T, CH), BF16), DMA, DMA, DMA((steps,)), DMA((steps,)),
                        *piece_scratch(2, *gout.shape[3:]), *total_scratch(small.shape[0])],
        compiler_params=pltpu.CompilerParams(collective_id=4, has_side_effects=True, vmem_limit_bytes=58 << 20,
                                             dimension_semantics=("arbitrary",)),
        cost_estimate=pl.CostEstimate(flops=6 * T * D * C, bytes_accessed=40 << 20, transcendentals=0),
        name="mid",
    )(dproj, masks, own, other, inner_x, w_x, w_z, x_proj, conv_weight, conv_bias, *du, *dz, mixed, gout, gz, small)


NT = (((1,), (1,)), ((), ()))
PR = 64


def scan_kernel(GR, NS, hosted, *refs):
    if not hosted:
        return scan_body(GR, NS, lambda at: None, *refs)
    ins, outs, own = 14, 10, 18
    refs = list(refs)
    g_refs = [refs.pop(ins), refs.pop(ins)]
    r_refs = [refs.pop(ins + outs), refs.pop(ins + outs)]
    scratch, refs = refs[-7:], refs[:-7]
    pieces = [piece_of(0, g_refs[0], "y", scratch, r_refs[0]), piece_of(1, g_refs[1], "near", scratch, r_refs[1])]
    steps = pl.num_programs(0)
    plan = {(0, "start"): 0, (0, "end"): 1, (1, "end"): 2}

    def host(at):
        for (step, place), stage in plan.items():
            if place != at:
                continue

            @pl.when(pl.program_id(0) == step)
            def _(stage=stage):
                if stage == 0:
                    me = lax.axis_index("dp")
                    peers = [me + STRIDE[n] * (1 - 2 * (me // STRIDE[n] % 2)) for n in ("y", "near", "far")]
                    pl.semaphore_wait(pltpu.get_barrier_semaphore(), greet_dp(peers))
                for piece in pieces:
                    (piece.step1, piece.step2, piece.stop)[stage]()

    return scan_body(GR, NS, host, *refs)


def scan_body(GR, NS, host, rank_ref, dtp_ref, dtb_ref, u_ref, z_ref, dg_ref, skip_ref,
                kb_ref, qb_ref, keep_ref, ksq_ref, qblk_ref, kblk_ref, k2blk_ref,
                gated_ref, diz_ref, du_ref, gskip_ref, gdtb_ref, gdtp_ref,
                drank_ref, sst_ref, dk_ref, dq_ref,
                den_s, step_s, su_s, ds_s, sz_s, y_s, d_s, e_s, h0_s, h1_s, ga_s, gb_s, ma_s, mb_s, dk_s, dq_s):
    T, CH = u_ref.shape
    L = CH // 128
    NG = T // GR
    R = GR * NS
    first, last = pl.program_id(0) == 0, pl.program_id(0) == pl.num_programs(0) - 1
    lanes = [slice(l * 128, (l + 1) * 128) for l in range(L)]
    hist = (h0_s, h1_s)

    @pl.when(first)
    def _():
        for r in (drank_ref, sst_ref, dk_s, dq_s):
            r[...] = jnp.zeros_like(r)
        h1_s[pl.ds(0, R), :] = jnp.zeros((R, CH), BF16)
        gb_s[...] = jnp.zeros_like(gb_s)
        mb_s[...] = jnp.zeros_like(mb_s)

    host("start")
    y_s[...] = jnp.dot(rank_ref[...], dtp_ref[...], preferred_element_type=F32)

    def prologue(r, acc):
        rows = pl.ds(pl.multiple_of(r * PR, PR), PR)
        kq = ksq_ref[rows, :]
        out = []
        for l in range(L):
            ln = lanes[l]
            beta = jax.nn.sigmoid(y_s[rows, ln] + dtb_ref[:, ln])
            den = 1.0 / (1.0 + beta * kq)
            step = beta * den
            den_s[rows, ln] = den
            step_s[rows, ln] = step
            u = u_ref[rows, ln]
            su_s[rows, ln] = step * u
            z = z_ref[rows, ln]
            s = jax.nn.sigmoid(z)
            sz_s[rows, ln] = s
            ds = dg_ref[rows, ln] * (z * s)
            ds_s[rows, ln] = ds
            out.append(acc[l] + jnp.sum(ds * u, axis=0, keepdims=True))
        return tuple(out)

    zrow = tuple(jnp.zeros((1, 128), F32) for _ in range(L))
    gsk = lax.fori_loop(0, T // PR, prologue, zrow)
    for l in range(L):
        gskip_ref[:, lanes[l]] = gsk[l]

    def rows_of(gi):
        return pl.ds(pl.multiple_of(gi * GR, GR), GR)

    def fill(gi, half, h, dst):
        h = list(h)
        base = pl.multiple_of(gi * GR, GR)
        rows = rows_of(gi)
        hb = pl.multiple_of(half * R, R)
        for j in range(GR):
            k = kb_ref[pl.ds(base * NS + j * NS, NS), :]
            kp = keep_ref.at[rows][j:j + 1, :]
            k2 = k * k * kp
            for l in range(L):
                a = kp - k2 * step_s.at[rows][j:j + 1, lanes[l]]
                h[l] = a * h[l] + k * su_s.at[rows][j:j + 1, lanes[l]]
                dst[pl.ds(hb + j * NS, NS), lanes[l]] = h[l].astype(BF16)
        return tuple(h)

    def read(gi, half, src):
        y_s[rows_of(gi), :] = jnp.dot(qblk_ref[rows_of(gi), :], src[pl.ds(pl.multiple_of(half * R, R), R), :],
                                      preferred_element_type=F32)

    def forward(i, h):
        before = jnp.maximum(i - 1, 0)
        read(2 * before + 1, before, h1_s)
        h = fill(2 * i, i, h, h0_s)
        read(2 * i, i, h0_s)
        return fill(2 * i + 1, i, h, h1_s)

    zst = tuple(jnp.zeros((NS, 128), F32) for _ in range(L))
    lax.fori_loop(0, NG // 2, forward, zst)
    read(NG - 1, NG // 2 - 1, h1_s)

    host("middle")

    def middle(r, c):
        rows = pl.ds(pl.multiple_of(r * PR, PR), PR)
        for l in range(L):
            ln = lanes[l]
            z = z_ref[rows, ln]
            s = sz_s[rows, ln]
            v = y_s[rows, ln] + skip_ref[:, ln] * u_ref[rows, ln]
            gated_ref[rows, ln] = (v * (z * s)).astype(BF16)
            diz_ref[rows, ln] = (dg_ref[rows, ln] * v * s * (1.0 + z * (1.0 - s))).astype(BF16)
        return c

    lax.fori_loop(0, T // PR, middle, 0)

    def back(gi, half, gc, own, before, before_at, g_dst, m_dst):
        gc = list(gc)
        base = pl.multiple_of(gi * GR, GR)
        rows = rows_of(gi)
        hb = pl.multiple_of(half * R, R)
        nows = [own[pl.ds(hb + (GR - 1) * NS, NS), ln] for ln in lanes]
        for j in reversed(range(GR)):
            at = pl.ds(base * NS + j * NS, NS)
            k = kb_ref[at, :]
            q = qb_ref[at, :]
            kp = keep_ref.at[rows][j:j + 1, :]
            k2 = k * k * kp
            a_sum = b_sum = q_sum = None
            for l in range(L):
                ln = lanes[l]
                ds = ds_s.at[rows][j:j + 1, ln]
                g = gc[l] + q * ds
                gb = g.astype(BF16)
                step = step_s.at[rows][j:j + 1, ln]
                now = nows[l]
                if j:
                    prev = own[pl.ds(hb + (j - 1) * NS, NS), ln]
                else:
                    prev = before[pl.ds(before_at + (GR - 1) * NS, NS), ln]
                nows[l] = prev
                m = gb * prev
                g_dst[j * NS:(j + 1) * NS, ln] = gb
                m_dst[j * NS:(j + 1) * NS, ln] = m
                wide = lambda v: jnp.broadcast_to(v, (NS, 128)).astype(BF16)
                pa = gb * wide(su_s.at[rows][j:j + 1, ln])
                pb = m * wide(step)
                pq = now * wide(ds)
                a_sum = pa if a_sum is None else a_sum + pa
                b_sum = pb if b_sum is None else b_sum + pb
                q_sum = pq if q_sum is None else q_sum + pq
                gc[l] = (kp - k2 * step) * g
            dk_s[at, :] += a_sum.astype(F32) - (2.0 * k * kp) * b_sum.astype(F32)
            dq_s[at, :] += q_sum.astype(F32)
        return tuple(gc)

    def sums(gi, g_src, m_src):
        rows = rows_of(gi)
        d_s[rows, :] = jnp.dot(kblk_ref[rows, :], g_src[...], preferred_element_type=F32)
        e_s[rows, :] = jnp.dot(k2blk_ref[rows, :], m_src[...], preferred_element_type=F32)

    def backward(i, gc):
        half = NG // 2 - 1 - i
        hi, lo = 2 * half + 1, 2 * half
        sums(jnp.minimum(hi + 1, NG - 1), gb_s, mb_s)
        gc = back(hi, half, gc, h1_s, h0_s, pl.multiple_of(half * R, R), ga_s, ma_s)
        sums(hi, ga_s, ma_s)
        return back(lo, half, gc, h0_s, h1_s, pl.multiple_of(jnp.maximum(half - 1, 0) * R, R), gb_s, mb_s)

    lax.fori_loop(0, NG // 2, backward, zst)
    sums(0, gb_s, mb_s)

    def epilogue(r, acc):
        rows = pl.ds(pl.multiple_of(r * PR, PR), PR)
        kp = keep_ref[rows, :]
        out = []
        ss = sst_ref[rows, :]
        for l in range(L):
            ln = lanes[l]
            step = step_s[rows, ln]
            dsum = d_s[rows, ln]
            dstep = u_ref[rows, ln] * dsum - kp * e_s[rows, ln]
            du_ref[rows, ln] = step * dsum + ds_s[rows, ln] * skip_ref[:, ln]
            t = dstep * step
            ss = ss + t * step
            db = t * (den_s[rows, ln] - step)
            y_s[rows, ln] = db
            out.append(acc[l] + jnp.sum(db, axis=0, keepdims=True))
        sst_ref[rows, :] = ss
        return tuple(out)

    gdb = lax.fori_loop(0, T // PR, epilogue, zrow)
    for l in range(L):
        gdtb_ref[:, lanes[l]] = gdb[l]
    dbl = y_s[...].astype(BF16)
    gdtp_ref[...] = lax.dot_general(rank_ref[...], dbl, (((0,), (0,)), ((), ())), preferred_element_type=F32)
    drank_ref[...] += lax.dot_general(dbl, dtp_ref[...], NT, preferred_element_type=F32)

    host("end")

    @pl.when(last)
    def _():
        ones = jnp.ones((8, 128), BF16)
        for src, dst in ((dk_s, dk_ref), (dq_s, dq_ref)):
            for c in range(0, T * NS, 1024):
                dst[:, c:c + 1024] = lax.dot_general(ones, src[c:c + 1024, :].astype(BF16), NT, preferred_element_type=F32)


def scan_call(piece, pieces, hosted, *args, CH=512, GR=16, NS=16):
    rank, dtp, dtb, u, z, dg, skip, kb, qb, keep, ksq, qblk, kblk, k2blk = args
    T, C = u.shape
    width = C // pieces
    CH = min(CH, width)
    first = piece * (width // CH)
    const = lambda a: pl.BlockSpec(a.shape, lambda j: (0,) * a.ndim, pipeline_mode=pl.Buffered(1))
    oconst = lambda a: pl.BlockSpec(a.shape, lambda j: (0,) * a.ndim)
    col = lambda a: pl.BlockSpec((a.shape[0], CH), lambda j: (0, j + first))
    out = lambda a: pl.BlockSpec((a.shape[0], CH), lambda j: (0, j))
    S = jax.ShapeDtypeStruct
    W = GR * NS
    R = rank.shape[1]
    outs = (S((T, width), BF16), S((T, width), BF16), S((T, width), F32), S((1, width), F32), S((1, width), F32), S((R, width), F32),
            S((T, R), F32), S((T, 128), F32), S((8, T * NS), F32), S((8, T * NS), F32))
    outs += tuple(S((2,) + g.shape[3:], BF16) for g in hosted)
    V = pltpu.VMEM
    f = pl.pallas_call(
        functools.partial(scan_kernel, GR, NS, bool(hosted)),
        grid=(width // CH,),
        in_specs=[const(rank), col(dtp), col(dtb), col(u), col(z), col(dg), col(skip), const(kb), const(qb),
                  const(keep), const(ksq), const(qblk), const(kblk), const(k2blk)] + [pl.BlockSpec(memory_space=pl.ANY)] * len(hosted),
        out_specs=[out(o) for o in outs[:6]] + [oconst(o) for o in outs[6:]],
        out_shape=outs,
        scratch_shapes=[V((T, CH), F32)] * 8 + [V((T * NS // 2, CH), BF16)] * 2 + [V((W, CH), BF16)] * 4 + [V((T * NS, 128), F32)] * 2
        + (piece_scratch(2, *hosted[0].shape[3:]) if hosted else []),
        compiler_params=pltpu.CompilerParams(vmem_limit_bytes=60 << 20, dimension_semantics=("arbitrary",),
                                             **(dict(collective_id=2, has_side_effects=True) if hosted else {})),
        cost_estimate=pl.CostEstimate(flops=T * width * NS * 800, bytes_accessed=T * width * 20, transcendentals=0),
        name="scan_reduce" if hosted else "scan",
    )
    return f(*args, *hosted)


def scan_all(rank, dtp, dtb, u, z, dg, skip, keys, query, keep, pieces, ksqb=None, GR=16, **kw):
    T, NS = keys.shape
    kb = jnp.broadcast_to(keys[:, :, None], (T, NS, 128)).reshape(T * NS, 128)
    qb = jnp.broadcast_to(query[:, :, None], (T, NS, 128)).reshape(T * NS, 128)
    keepb = jnp.broadcast_to(keep[:, None], (T, 128))
    if ksqb is None:
        ksqb = jnp.broadcast_to(jnp.sum(keys * keys, axis=1)[:, None], (T, 128))
    slot = (jnp.arange(T)[:, None] % GR == jnp.arange(GR * NS)[None, :] // NS).astype(F32)
    blk = lambda v: (slot * jnp.tile(v, (1, GR))).astype(BF16)
    qblk, kblk, k2blk = blk(query), blk(keys), blk(keys * keys)

    def run(piece, *hosted):
        o = scan_call(piece, pieces, hosted, rank, dtp, dtb, u, z, dg, skip, kb, qb, keepb, ksqb, qblk, kblk, k2blk, GR=GR, NS=NS, **kw)
        gated, diz, du, gskip, gdtb, gdtp, drank, sst, dk, dq, *summed = o
        dq = dq[0].reshape(T, NS)
        dk = dk[0].reshape(T, NS) - 2.0 * keys * jnp.sum(sst, axis=1, keepdims=True)
        return gated, diz, du, gskip, gdtb, gdtp, drank, dk, dq, summed

    return run


def tensor_other(value):
    return lax.ppermute(value, "tensor", [(0, 1), (1, 0)])


def tensor_total(value):
    if lax.axis_size("tensor") == 2:
        return value + tensor_other(value)
    return lax.psum(value, "tensor")


def half_total(value, me, width):
    if lax.axis_size("tensor") == 2:
        own = lax.dynamic_slice_in_dim(value, me * width, width, 1)
        sent = lax.dynamic_slice_in_dim(value, (1 - me) * width, width, 1).astype(BF16)
        return own + tensor_other(sent).astype(F32)
    return lax.psum_scatter(value, "tensor", scatter_dimension=1, tiled=True)


def full_columns(part, me):
    if lax.axis_size("tensor") == 2:
        other = tensor_other(part)
        return jnp.where(
            me == 0,
            jnp.concatenate([part, other], 1),
            jnp.concatenate([other, part], 1),
        )
    return lax.all_gather(part, "tensor", axis=1, tiled=True)


def pair_up(value, stride):
    count = lax.axis_size("dp")
    return lax.ppermute(value, "dp", [(i, i ^ stride) for i in range(count)])


def pair_gradient(own, other, right):
    return (contract_rows(own, right) + contract_rows(other, pair_up(right, 1))).astype(BF16)


def after(value, *earlier):
    return lax.optimization_barrier((value,) + earlier)[0]


def flatten(values):
    return jnp.concatenate([v.reshape(-1) for v in values])


def cut(flat, values):
    out, at = [], 0
    for v in values:
        out.append(flat[at : at + v.size].reshape(v.shape))
        at += v.size
    return out


def position_in(keys):
    return jnp.sum((keys[None, :] < keys[:, None]).astype(jnp.int32), axis=1)


def conv_mix(inner_x, conv_weight, conv_bias, segment):
    row_count = inner_x.shape[0]
    taps = conv_weight.shape[0]
    mixed = conv_bias[None, :] + conv_weight[taps - 1][None, :] * inner_x
    for shift_by in range(1, taps):
        moved = jnp.concatenate([jnp.zeros((shift_by, inner_x.shape[1]), F32), inner_x[: row_count - shift_by]], 0)
        seg_moved = jnp.concatenate([jnp.full((shift_by,), -1, jnp.int32), segment[: row_count - shift_by]], 0)
        keep_mask = (seg_moved == segment).astype(F32)
        mixed = mixed + conv_weight[taps - 1 - shift_by][None, :] * moved * keep_mask[:, None]
    return mixed


def silu_conv(inner_x, conv_weight, conv_bias, segment):
    mixed = conv_mix(inner_x, conv_weight, conv_bias, segment)
    return mixed * jax.nn.sigmoid(mixed)


def contract_rows(left, right):
    return lax.dot_general(left, right, (((0,), (0,)), ((), ())), preferred_element_type=F32)


def contract_cols(left, right):
    return lax.dot_general(left, right, (((1,), (1,)), ((), ())), preferred_element_type=F32)


def body(tokens, cotangent, norm_gain, w_x, w_z, conv_weight, conv_bias, x_proj, dt_proj, dt_bias, skip_gain, w_out,
         seq_lengths, arrival_route, work_source):
    dp_count = lax.axis_size("dp")
    tp_count = lax.axis_size("tensor")
    row_count, feat_width = tokens.shape
    per_peer = row_count // dp_count
    col_share = feat_width // tp_count
    me = lax.axis_index("tensor")
    col_start = me * col_share
    low_rank = dt_proj.shape[0]
    state_size = (x_proj.shape[1] - low_rank) // 2
    position = jnp.arange(row_count, dtype=jnp.int32)

    deal = (position_in(arrival_route)[:, None] == position[None, :]).astype(BF16)
    settle = (position_in(work_source // row_count * row_count + position)[:, None] == position[None, :]).astype(BF16)

    def exchange(rows):
        out = lax.all_to_all(rows.reshape(dp_count, per_peer, rows.shape[1]), "dp", split_axis=0, concat_axis=0, tiled=True)
        return out.reshape(row_count, rows.shape[1])

    def pick(table, rows, dim):
        return lax.dot_general(table, rows, (((dim,), (0,)), ((), ())), preferred_element_type=F32).astype(BF16)

    def bring(values):
        part = lax.dynamic_slice_in_dim(values, col_start, col_share, 1)
        return full_columns(pick(settle, exchange(pick(deal, part, 0)), 1), me)

    def give_back(values):
        return pick(deal, exchange(pick(settle, values, 0)), 1)

    lengths = seq_lengths[0]
    count = lengths.shape[0]
    before = jnp.arange(count)[:, None] > jnp.arange(count)[None, :]
    offsets = jnp.sum(jnp.where(before, lengths[None, :], 0), axis=1)
    segment = jnp.sum((position[:, None] >= offsets[None, :]).astype(jnp.int32), axis=1) - 1
    keep = 1.0 - jnp.any(position[:, None] == offsets[None, :], axis=1).astype(F32)

    paired = dp_count == 16 and tp_count == 2
    if paired:
        taps = conv_weight.shape[0]
        pre = [jnp.concatenate([jnp.full((s,), -1, jnp.int32), segment[: row_count - s]]) for s in range(1, taps)]
        masks = jnp.stack([jnp.broadcast_to((p == segment).astype(F32)[:, None], (row_count, 128)) for p in pre])
        (x_half, normed, dy_work, scale_wide, normed_own, normed_other, dy_own, dy_other,
         inner_x, conv_out, conv_low, key_query, inner_z, d_gated, rank_part, key_square) = head_call(
            tokens, cotangent, w_x, w_z, w_out, norm_gain[None, :], deal.T, settle, masks, conv_weight, conv_bias[None, :], x_proj, low_rank)
    else:
        x_work = bring(tokens)
        dy_work = bring(cotangent)
        resid = x_work.astype(F32)
        scale_row = lax.rsqrt(jnp.mean(resid * resid, axis=1, keepdims=True) + 1e-05)
        unit = resid * scale_row
        normed = (unit * norm_gain[None, :]).astype(BF16)
        inner_x = jnp.dot(normed, w_x, preferred_element_type=F32)
        conv_out, conv_pull = jax.vjp(partial(silu_conv, segment=segment), inner_x, conv_weight, conv_bias)
        conv_low = conv_out.astype(BF16)
        projected = tensor_total(jnp.dot(conv_low, x_proj, preferred_element_type=F32))
        inner_z = jnp.dot(normed, w_z, preferred_element_type=F32)
        d_gated = contract_cols(dy_work, w_out)
        rank_part, key_query, key_square = projected[:, :low_rank].astype(BF16), projected[:, low_rank:], None
    key_rows, query_rows = key_query[:, :state_size], key_query[:, state_size:]
    pieces = 2 if paired else 1
    scan = scan_all(rank_part, dt_proj, dt_bias[None, :], conv_out, inner_z, d_gated, skip_gain[None, :], key_rows,
                    query_rows, keep, pieces, key_square)
    scans = [scan(0)]
    if paired:
        blocks = lambda g: g.reshape(2, 2, 2, g.shape[0] // 8, g.shape[1])
        outer = lambda part: (blocks(pair_gradient(dy_own, dy_other, part[0])),
                              blocks(pair_gradient(normed_own, normed_other, part[1])))
        scans.append(scan(1, *outer(scans[0])))
    wide = lambda index: jnp.concatenate([part[index] for part in scans], axis=1) if paired else scans[0][index]
    grad_dt_proj = wide(5)
    grad_skip, grad_dt_bias = wide(3)[0], wide(4)[0]
    d_rank, d_keys, d_query = (sum(part[index] for part in scans) for index in (6, 7, 8))
    gated_low, d_inner_z_low = wide(0), wide(1)
    d_proj = jnp.concatenate([d_rank, d_keys, d_query], axis=1)
    mixed = jnp.dot(gated_low, after(w_out, d_proj) if paired else w_out, preferred_element_type=F32)
    d_proj = tensor_total(d_proj)
    if paired:
        mixed = mixed.astype(BF16)
        g_out, g_z = outer(scans[1])
        far = [pair_up(v[1], STRIDE["far"]) for v in scans[1][9]]
        d_proj = after(d_proj, g_out, g_z, mixed)
        d_proj_low = d_proj.astype(BF16)
        rows = (contract_rows(d_proj_low, conv_low), grad_dt_proj, grad_dt_bias[None, :], grad_skip[None, :])
        stack = jnp.concatenate(rows).astype(BF16)
        stack = jnp.pad(stack, ((0, -stack.shape[0] % 16), (0, 0)))
        d_normed, g_x, stack, grad_conv_weight, grad_conv_bias, mixed_other, left_out, left_z = mid_call(
            d_proj_low, masks, normed_own, normed_other, inner_x, w_x, w_z, x_proj, conv_weight,
            conv_bias[None, :], [part[2] for part in scans], [part[1] for part in scans], mixed, g_out, g_z,
            stack)
    else:
        d_proj_low = d_proj.astype(BF16)
        grad_x_proj = contract_rows(conv_low, d_proj_low)
        d_conv_out = scans[0][2] + contract_cols(d_proj_low, x_proj)
        d_inner_x, grad_conv_weight, grad_conv_bias = conv_pull(d_conv_out)
        d_inner_x_low = d_inner_x.astype(BF16)
        d_normed = contract_cols(d_inner_x_low, w_x) + contract_cols(d_inner_z_low, w_z)
    if paired:
        conv = jnp.concatenate([grad_conv_weight, grad_conv_bias])
        conv = jnp.pad(conv, ((0, 8 - conv.shape[0]), (0, 0)))
        out_tokens, in_grad, grad_gain, conv, grad_w_out, grad_w_z, grad_w_x = tail_call(
            left_out, left_z, scans[1][9], [after(v, d_normed) for v in far], blocks(g_x), d_normed, mixed, mixed_other, x_half, dy_work, conv, norm_gain[None, :],
            scale_wide, settle.T, deal)
        split = x_proj.shape[1]
        grad_x_proj, grad_dt_proj = stack[:split].T, stack[split : split + low_rank]
        grad_dt_bias, grad_skip = stack[split + low_rank], stack[split + low_rank + 1]
        grad_conv_weight, grad_conv_bias = conv[:taps], conv[taps]
        grad_gain = grad_gain[0]
    else:
        small = (grad_x_proj, grad_dt_proj, grad_conv_weight, grad_conv_bias, grad_dt_bias, grad_skip)
        unit_cols = lax.dynamic_slice_in_dim(unit, col_start, col_share, 1)
        gain_cols = lax.dynamic_slice_in_dim(norm_gain, col_start, col_share, 0)
        dy_cols = lax.dynamic_slice_in_dim(dy_work, col_start, col_share, 1).astype(F32)
        d_share = half_total(d_normed, me, col_share)
        d_unit_cols = d_share * gain_cols[None, :]
        row_total = tensor_total(jnp.sum(d_unit_cols * unit_cols, axis=1, keepdims=True))
        grad_gain = jnp.sum(d_share * unit_cols, axis=0)
        d_resid = dy_cols + scale_row * (d_unit_cols - unit_cols * (row_total / feat_width))
        mixed_share = half_total(mixed, me, col_share)
        out_cols = (lax.dynamic_slice_in_dim(resid, col_start, col_share, 1) + mixed_share).astype(BF16)
        out_tokens, in_grad = give_back(out_cols), give_back(d_resid.astype(BF16))
        grad_w_out, grad_w_z, grad_w_x = (
            lax.psum_scatter(g.astype(BF16), "dp", scatter_dimension=dim, tiled=True).astype(F32)
            for g, dim in ((contract_rows(gated_low, dy_work), 1), (contract_rows(normed, d_inner_z_low), 0),
                           (contract_rows(normed, d_inner_x_low), 0)))
        small += (grad_gain,)
        (grad_x_proj, grad_dt_proj, grad_conv_weight, grad_conv_bias, grad_dt_bias, grad_skip, grad_gain) = cut(
            lax.psum(flatten(small), "dp"), small)
    return (out_tokens, in_grad, grad_gain, grad_w_x, grad_w_z, grad_conv_weight, grad_conv_bias, grad_x_proj,
            grad_dt_proj, grad_dt_bias, grad_skip, grad_w_out)


def solution(mesh):
    in_specs = (
        P("dp", None),
        P("dp", None),
        P(),
        P(None, "tensor"),
        P(None, "tensor"),
        P(None, "tensor"),
        P("tensor"),
        P("tensor", None),
        P(None, "tensor"),
        P("tensor"),
        P("tensor"),
        P("tensor", None),
        P("dp", None),
        P("dp"),
        P("dp"),
    )
    out_specs = (
        P("dp", "tensor"),
        P("dp", "tensor"),
        P("tensor"),
        P("dp", "tensor"),
        P("dp", "tensor"),
        P(None, "tensor"),
        P("tensor"),
        P("tensor", None),
        P(None, "tensor"),
        P("tensor"),
        P("tensor"),
        P("tensor", "dp"),
    )
    return jax.shard_map(body, mesh=mesh, in_specs=in_specs, out_specs=out_specs, check_vma=False)
```

```python
import functools
from functools import partial

import jax
import jax.numpy as jnp
import numpy as np
from jax import lax
from jax.experimental import pallas as pl
from jax.experimental.pallas import tpu as pltpu
from jax.sharding import PartitionSpec as P

F32, BF16 = jnp.float32, jnp.bfloat16
MESH = pl.DeviceIdType.MESH
TILE = 32
GAIN_ROW = 5
STRIDE = {"core": 1, "y": 2, "near": 4, "far": 8}


class Piece:
    def __init__(self, grad, first, bufs, sems, result):
        self.grad, self.first, self.result = grad, first, result
        self.own, self.r1, self.r2, self.r3 = bufs
        self.local, self.send, self.recv = sems
        self.second = "near" if first == "y" else "y"

    def bit(self, name):
        return lax.axis_index("dp") // STRIDE[name] % 2

    def block(self, mine):
        return self.grad.at[:, :, mine] if self.first == "y" else self.grad.at[:, mine]

    def remote(self, step):
        s, f = self.bit(self.second), self.bit("far")
        name, src, dst = (
            (self.first, lambda: self.block(1 - self.bit(self.first)), self.r1),
            (self.second, lambda: self.own.at[:, 1 - s], self.r2),
            ("far", lambda: self.own.at[1 - f, s], self.r3),
        )[step]
        to = lax.axis_index("dp") + STRIDE[name] * (1 - 2 * self.bit(name))
        return pltpu.make_async_remote_copy(
            src_ref=src(), dst_ref=dst, send_sem=self.send.at[step], recv_sem=self.recv.at[step],
            device_id={"dp": to}, device_id_type=MESH)

    def load(self):
        return pltpu.make_async_copy(self.block(self.bit(self.first)), self.own, self.local)

    def step1(self):
        self.remote(0).start()
        self.load().start()

    def add(self, dst, src, out=None):
        def body(i, c):
            at = pl.ds(pl.multiple_of(i * TILE, TILE), TILE)
            total = dst[at, :].astype(F32) + src[at, :].astype(F32)
            if out is None:
                dst[at, :] = total.astype(BF16)
            else:
                out[at, :] = total.astype(out.dtype)
            return c

        lax.fori_loop(0, src.shape[0] // TILE, body, 0)

    def step2(self):
        self.load().wait()
        self.remote(0).wait_recv()
        s = self.bit(self.second)
        for far in range(2):
            self.add(self.own.at[far, 1 - s], self.r1.at[far, 1 - s])
        self.remote(1).start()
        for far in range(2):
            self.add(self.own.at[far, s], self.r1.at[far, s])

    def step3(self):
        self.remote(1).wait_recv()
        s, f = self.bit(self.second), self.bit("far")
        self.add(self.own.at[1 - f, s], self.r2.at[1 - f])
        self.remote(2).start()
        self.add(self.own.at[f, s], self.r2.at[f])

    def stop(self):
        self.remote(1).wait_recv()
        for far in range(2):
            place = far + self.bit("far") * (1 - 2 * far)
            self.add(self.own.at[far, self.bit(self.second)], self.r2.at[far], self.result.at[place])
        for step in range(2):
            self.remote(step).wait_send()

    def finish(self):
        self.remote(2).wait_recv()
        self.add(self.own.at[self.bit("far"), self.bit(self.second)], self.r3, self.result)
        for step in range(3):
            self.remote(step).wait_send()


class FarPiece(Piece):
    def __init__(self, grad, bufs, sems, result):
        self.grad, self.result = grad, result
        self.own, self.r3 = bufs
        self.local, self.send, self.recv = sems

    def remote(self, step):
        f = self.bit("far")
        return pltpu.make_async_remote_copy(
            src_ref=self.grad.at[1], dst_ref=self.r3, send_sem=self.send, recv_sem=self.recv,
            device_id={"dp": lax.axis_index("dp") + STRIDE["far"] * (1 - 2 * f)}, device_id_type=MESH)

    def load(self):
        return pltpu.make_async_copy(self.grad.at[0], self.own, self.local)

    def finish(self):
        self.load().wait()
        self.remote(0).wait_recv()
        self.add(self.own, self.r3, self.result)
        self.remote(0).wait_send()


def piece_scratch(k, n, w):
    V, DMA = pltpu.VMEM, pltpu.SemaphoreType.DMA
    return [V((k, 2, 2, n, w), BF16), V((k, 2, 2, n, w), BF16), V((k, 2, n, w), BF16), V((k, n, w), BF16),
            DMA((k,)), DMA((k, 3)), DMA((k, 3))]


def piece_of(i, grad, first, scratch, result):
    return Piece(grad, first, tuple(r.at[i] for r in scratch[:4]), tuple(r.at[i] for r in scratch[4:]), result)


def greet_dp(peers):
    for p in peers:
        pl.semaphore_signal(pltpu.get_barrier_semaphore(), inc=1, device_id={"dp": p}, device_id_type=MESH)
    return len(peers)


class Total:
    NAMES = ("y", "near", "far")

    def __init__(self, acc, half, got, out, sems):
        self.acc, self.half, self.got, self.out, self.sems = acc, half, got, out, sems
        self.me = lax.axis_index("dp")
        self.bits = {name: self.me // stride % 2 for name, stride in STRIDE.items()}

    def flip(self, q):
        path, to = [self.bits["core"]], self.me
        for n, name in enumerate(self.NAMES):
            bit, turn = self.bits[name], q >> n & 1
            path.append(1 - bit if turn else bit)
            if turn:
                to = to + STRIDE[name] * (1 - 2 * bit)
        return tuple(path), to

    def copies(self, stage):
        mine, core = self.flip(0)[0], self.bits["core"]
        other = self.me + 1 - 2 * core
        if stage == 0:
            jobs = [(0, self.acc.at[1 - core], self.half, other)]
        elif stage == 1:
            jobs = [(q, self.acc.at[self.flip(q)[0]], self.got.at[q], self.flip(q)[1]) for q in range(1, 8)]
        elif stage == 2:
            jobs = [(q, self.out.at[mine], self.out.at[mine], self.flip(q)[1]) for q in range(1, 8)]
        else:
            jobs = [(0, self.out.at[core], self.out.at[core], other)]
        return [pltpu.make_async_remote_copy(
            src_ref=src, dst_ref=dst, send_sem=self.sems[0].at[stage, q], recv_sem=self.sems[1].at[stage, q],
            device_id={"dp": to}, device_id_type=MESH) for q, src, dst, to in jobs]

    def step(self, i):
        if i:
            for copy in self.copies(i - 1):
                copy.wait_recv()
        if i == 1:
            for b in range(8):
                at = (b // 4, b // 2 % 2, b % 2)
                here = self.acc.at[(self.bits["core"],) + at]
                here[...] = (here[...].astype(F32) + self.half[at].astype(F32)).astype(BF16)
        if i == 2:
            mine = self.flip(0)[0]
            total = self.acc[mine].astype(F32)
            for q in range(1, 8):
                total = total + self.got[q].astype(F32)
            self.out[mine] = total.astype(BF16)
        if i < 4:
            for copy in self.copies(i):
                copy.start()
        else:
            for stage in range(4):
                for copy in self.copies(stage):
                    copy.wait_send()


def sixteenth(b):
    return b // 8, b // 4 % 2, b // 2 % 2, b % 2


def total_scratch(rows):
    V, DMA = pltpu.VMEM, pltpu.SemaphoreType.DMA
    full = (2, 2, 2, 2, rows, 128)
    return [V(full, BF16), V(full[1:], BF16), V((8, rows, 128), BF16), V(full, BF16), DMA((4, 8)), DMA((4, 8)), DMA((16,))]


def tail_kernel(gout_ref, gz_ref, kout_ref, kz_ref, fout_ref, fz_ref, gx_ref, dn_ref, mx_ref, other_ref, x_ref, dy_ref, conv_ref, gain_ref, scale_ref, settle_ref, deal_ref,
                out_ref, in_ref, gg_ref, csum_ref, wout_ref, wz_ref, wx_ref,
                p0, p1, p2, p3, p4, p5, p6,
                dn_own, dn_got, mx_own, mx_got, x_half, dy_half, du, rs_own, rs_got, low,
                y_send, y_got, d_send, d_got, sem, x_send, x_recv, a_send, a_recv,
                m_part, m_got, m_out, m_send, m_recv,
                f_own, f_got, f_sem, early, wout_s):
    me, ten = lax.axis_index("dp"), lax.axis_index("tensor")
    count = lax.axis_size("dp")
    T, W = x_half.shape
    L = W // 128
    per = T // count
    barrier = pltpu.get_barrier_semaphore()
    for p in range(1, count):
        pl.semaphore_signal(barrier, inc=1, device_id={"dp": (me + p) % count}, device_id_type=MESH)
    pl.semaphore_signal(barrier, inc=1, device_id={"tensor": 1 - ten}, device_id_type=MESH)
    mine = pl.ds(pl.multiple_of(ten * W, 128), W)
    other = pl.ds(pl.multiple_of((1 - ten) * W, 128), W)
    loads = []
    jobs = [(mx_ref.at[:, mine], mx_own), (other_ref, mx_got), (x_ref, x_half), (dn_ref.at[:, mine], dn_own),
            (dy_ref.at[:, mine], dy_half)]
    jobs += [(kout_ref.at[0], early.at[0]), (fout_ref, early.at[1]), (kz_ref.at[0], early.at[2]), (fz_ref, early.at[3])]
    for b in range(count):
        jobs.append((conv_ref.at[:, b * 128 : (b + 1) * 128], m_part.at[b]))
    for n, (src, dst) in enumerate(jobs):
        copy = pltpu.make_async_copy(src, dst, sem.at[n])
        copy.start()
        loads.append(copy)
    pl.semaphore_wait(barrier, count)

    def swap(src, dst, n):
        copy = pltpu.make_async_remote_copy(
            src_ref=src, dst_ref=dst, send_sem=x_send.at[n], recv_sem=x_recv.at[n],
            device_id={"tensor": 1 - ten}, device_id_type=MESH)
        copy.start()
        return copy

    dn_copy = swap(dn_ref.at[:, other], dn_got, 0)
    bits = {"core": me % 2, "y": me // 2 % 2, "near": me // 4 % 2, "far": me // 8}
    half = gout_ref.shape[-1]
    scratch = (p0, p1, p2, p3, p4, p5, p6)
    x_cols = [slice(0, half), slice(half, 2 * half)]
    pieces = [
        FarPiece(gout_ref, (f_own.at[0], f_got.at[0]), tuple(f_sem.at[0, n] for n in range(3)), wout_s.at[:, x_cols[1]]),
        FarPiece(gz_ref, (f_own.at[1], f_got.at[1]), tuple(f_sem.at[1, n] for n in range(3)), wz_ref.at[:, x_cols[1]]),
        piece_of(0, gx_ref.at[:, :, :, :, x_cols[0]], "y", scratch, wx_ref.at[:, x_cols[0]]),
        piece_of(1, gx_ref.at[:, :, :, :, x_cols[1]], "near", scratch, wx_ref.at[:, x_cols[1]]),
    ]
    for piece in (pieces[2], pieces[3], pieces[0], pieces[1]):
        piece.step1()
    for copy in loads:
        copy.wait()
    def small(stage, p):
        to = (me + p) % count
        src, dst = ((m_part.at[to], m_got.at[me]), (m_out.at[me], m_out.at[me]))[stage]
        return pltpu.make_async_remote_copy(
            src_ref=src, dst_ref=dst, send_sem=m_send.at[stage, p], recv_sem=m_recv.at[stage, p],
            device_id={"dp": to}, device_id_type=MESH)

    def tiles(body, init):
        def step(i, c):
            return body(pl.ds(pl.multiple_of(i * 16, 16), 16), c)
        return lax.fori_loop(0, T // 16, step, init)

    def add_resid(at, c):
        for l in range(L):
            ln = slice(l * 128, (l + 1) * 128)
            both = mx_own[at, ln].astype(F32) + mx_got[at, ln].astype(F32)
            mx_own[at, ln] = (x_half[at, ln].astype(F32) + both).astype(BF16)
        return c

    def deal_out(rows, send, got, n):
        sent = jnp.dot(settle_ref[...], rows[...], preferred_element_type=F32).astype(BF16)
        send[...] = sent.reshape(send.shape)
        got[me] = send[me]
        copies = []
        for p in range(1, count):
            to = (me + p) % count
            copy = pltpu.make_async_remote_copy(
                src_ref=send.at[to], dst_ref=got.at[me], send_sem=a_send.at[n, p], recv_sem=a_recv.at[n, p],
                device_id={"dp": to}, device_id_type=MESH)
            copy.start()
            copies.append(copy)
        return copies

    def take_in(copies, got, out):
        for copy in copies:
            copy.wait_recv()
        out[...] = jnp.dot(deal_ref[...], got[...].reshape(T, W), preferred_element_type=F32).astype(BF16)
        for copy in copies:
            copy.wait_send()

    tiles(add_resid, 0)
    y_copies = deal_out(mx_own, y_send, y_got, 1)

    dn_copy.wait_recv()
    gain = gain_ref[:, mine]

    def share(at, acc):
        scale = scale_ref[at, :]
        total = None
        out = []
        for l in range(L):
            ln = slice(l * 128, (l + 1) * 128)
            d = dn_own[at, ln].astype(F32) + dn_got[at, ln].astype(F32)
            unit = x_half[at, ln].astype(F32) * scale
            d_unit = d * gain[:, ln]
            du[at, ln] = d_unit
            out.append(acc[l] + jnp.sum(d * unit, axis=0, keepdims=True))
            total = d_unit * unit if total is None else total + d_unit * unit
        rs_own[at, :] = total
        return tuple(out)

    acc = tiles(share, tuple(jnp.zeros((1, 128), F32) for _ in range(L)))
    rs_copy = swap(rs_own, rs_got, 2)
    for l in range(L):
        m_part[l, GAIN_ROW : GAIN_ROW + 1, :] = acc[l]
    for p in range(1, count):
        small(0, p).start()
    m_got[me] = m_part[me]
    pieces[2].step2()
    pieces[3].step2()
    rs_copy.wait_recv()

    def norm_back(at, c):
        scale = scale_ref[at, :]
        total = jnp.sum(rs_own[at, :] + rs_got[at, :], axis=1, keepdims=True) * (0.5 / W)
        for l in range(L):
            ln = slice(l * 128, (l + 1) * 128)
            unit = x_half[at, ln].astype(F32) * scale
            low[at, ln] = (dy_half[at, ln].astype(F32) + scale * (du[at, ln] - unit * total)).astype(BF16)
        return c

    tiles(norm_back, 0)
    d_copies = deal_out(low, d_send, d_got, 0)
    for p in range(1, count):
        small(0, p).wait_recv()
    m_out[me] = jnp.sum(m_got[...], axis=0)
    for p in range(1, count):
        small(1, p).start()
    pieces[2].step3()
    pieces[3].step3()
    wout_s[:, x_cols[0]] = early[0].astype(F32) + early[1].astype(F32)
    wz_ref[:, x_cols[0]] = early[2].astype(F32) + early[3].astype(F32)
    pieces[0].finish()
    pieces[1].finish()
    wout_ref[...] = wout_s[...].T
    take_in(y_copies, y_got, out_ref)
    for p in range(1, count):
        small(1, p).wait_recv()
    for b in range(count):
        csum_ref[:, b * 128 : (b + 1) * 128] = m_out[b]
    for l in range(L):
        gg_ref[:, l * 128 : (l + 1) * 128] = m_out[l, GAIN_ROW : GAIN_ROW + 1, :]
    take_in(d_copies, d_got, in_ref)
    pieces[2].finish()
    pieces[3].finish()
    for copy in (dn_copy, rs_copy):
        copy.wait_send()
    for stage in range(2):
        for p in range(1, count):
            small(stage, p).wait_send()


def tail_call(gout, gz, kept, far, gx, dn, mx, other, x, dy, conv, gain, scale, settle_t, deal):
    T, W = x.shape
    D = 2 * W
    n, half = gout.shape[1:]
    count = lax.axis_size("dp")
    S = jax.ShapeDtypeStruct
    full = 2 * half
    outs = (S((T, W), BF16), S((T, W), BF16), S((1, W), F32), S(conv.shape, F32), S((full, n), F32), S((n, full), F32), S((n, full), F32))
    anyspace = pl.BlockSpec(memory_space=pl.ANY)
    vmem = pl.BlockSpec(memory_space=pltpu.VMEM)
    V, DMA = pltpu.VMEM, pltpu.SemaphoreType.DMA
    return pl.pallas_call(
        tail_kernel,
        out_shape=outs,
        in_specs=[anyspace] * 13 + [vmem] * 4,
        out_specs=[vmem] * 7,
        scratch_shapes=[
            *piece_scratch(2, n, half),
            V((T, W), BF16), V((T, W), BF16), V((T, W), BF16), V((T, W), BF16), V((T, W), BF16), V((T, W), BF16),
            V((T, W), F32), V((T, 128), F32), V((T, 128), F32), V((T, W), BF16),
            V((count, T // count, W), BF16), V((count, T // count, W), BF16),
            V((count, T // count, W), BF16), V((count, T // count, W), BF16),
            DMA((9 + count,)), DMA((3,)), DMA((3,)), DMA((2, count)), DMA((2, count)),
            V((count, 8, 128), F32), V((count, 8, 128), F32), V((count, 8, 128), F32), DMA((2, count)), DMA((2, count)),
            V((2, n, half), BF16), V((2, n, half), BF16), DMA((2, 3)), V((4, n, half), BF16), V((n, full), F32),
        ],
        compiler_params=pltpu.CompilerParams(collective_id=1, has_side_effects=True, vmem_limit_bytes=58 << 20),
        cost_estimate=pl.CostEstimate(flops=T * T * D * 4, bytes_accessed=64 << 20, transcendentals=0),
        name="tail",
    )(gout, gz, *kept, *far, gx, dn, mx, other, x, dy, conv, gain, scale, settle_t, deal)


NT = (((1,), (1,)), ((), ()))


def head_kernel(taps, tok_ref, cot_ref, w_ref, wz_ref, wo_ref, gain_ref, deal_ref, settle_ref, mask_ref, cw_ref, cb_ref, xp_ref,
                half_ref, normed_ref, dy_ref, scale_ref, n_own_ref, n_other_ref, d_own_ref, d_other_ref,
                inner_ref, conv_ref, low_ref, keys_ref, z_ref, dg_ref, rank_ref, ksq_ref,
                part, send, got, across, n_send, d_send, w_s, p_own, p_got, load, w_load, p_send, p_recv, a_send, a_recv, x_send, x_recv, c_send, c_recv):
    me, ten = lax.axis_index("dp"), lax.axis_index("tensor")
    count = lax.axis_size("dp")
    T, W = half_ref.shape
    chunks, per, WC = send.shape[1], send.shape[3], send.shape[4]
    barrier = pltpu.get_barrier_semaphore()
    greet_dp([(me + p) % count for p in range(1, count)])
    pl.semaphore_signal(barrier, inc=1, device_id={"tensor": 1 - ten}, device_id_type=MESH)
    start = pl.multiple_of(ten * W, 128)
    away = pl.multiple_of((1 - ten) * W, 128)
    loads = [pltpu.make_async_copy(src.at[:, pl.ds(start, W)], part.at[n], load.at[n]) for n, src in enumerate((tok_ref, cot_ref))]
    weights = [pltpu.make_async_copy(w, w_s, w_load.at[n]) for n, w in enumerate((w_ref, wz_ref, wo_ref))]
    for copy in loads:
        copy.start()
    weights[0].start()

    def deal(n):
        loads[n].wait()
        rows = jnp.dot(deal_ref[...], part[n], preferred_element_type=F32).astype(BF16)
        for c in range(chunks):
            send[n, c] = rows[:, c * WC : (c + 1) * WC].reshape(count, per, WC)

    def out(n, c, p):
        to = (me + p) % count
        return pltpu.make_async_remote_copy(
            src_ref=send.at[n, c, to], dst_ref=got.at[n, c, me], send_sem=a_send.at[n, c, p], recv_sem=a_recv.at[n, c, p],
            device_id={"dp": to}, device_id_type=MESH)

    def over(n, c, p):
        at = (me + count - p) % count
        return pltpu.make_async_remote_copy(
            src_ref=(send if p == 0 else got).at[n, c, at], dst_ref=across.at[n, c, at], send_sem=x_send.at[n, c, p],
            recv_sem=x_recv.at[n, c, p], device_id={"tensor": 1 - ten}, device_id_type=MESH)

    def launch(n, c):
        for p in range(1, count):
            out(n, c, p).start()
        over(n, c, 0).start()
        got[n, c, me] = send[n, c, me]

    def forward(n, c):
        for p in range(1, count):
            out(n, c, p).wait_recv()
            over(n, c, p).start()

    def settle(n, c, source, into, begin):
        rows = jnp.dot(settle_ref[...], source[n, c].reshape(T, WC), preferred_element_type=F32)
        into[:, pl.ds(pl.multiple_of(begin + c * WC, 128), WC)] = rows.astype(BF16)

    order = [(n, c) for n in range(2) for c in range(chunks)]
    deal(0)
    pl.semaphore_wait(barrier, count)
    launch(0, 0)
    deal(1)
    for at in range(chunks):
        forward(*order[at])
        launch(*order[at + 1])
        settle(0, at, got, half_ref, 0)
    for c in range(chunks):
        for p in range(count):
            over(0, c, p).wait_recv()
        if c == chunks - 1:
            forward(1, 0)
            launch(1, 1)
        settle(0, c, across, part.at[0], 0)
    core = me % 2

    def norm(i, c):
        at = pl.ds(pl.multiple_of(i * 16, 16), 16)
        mine, other = half_ref[at, :].astype(F32), part[0, at, :].astype(F32)
        square = jnp.sum(mine * mine + other * other, axis=1, keepdims=True)
        scale = lax.rsqrt(square * (0.5 / W) + 1e-05)
        scale_ref[at, :] = jnp.broadcast_to(scale, (16, 128))
        for value, begin in ((mine, start), (other, away)):
            cols = pl.ds(begin, W)
            normed_ref[at, cols] = (value * scale * gain_ref[:, cols]).astype(BF16)
        return c

    lax.fori_loop(0, T // 16, norm, 0)

    def halves(source, own, other):
        def body(b, c):
            for into, k in ((own, core), (other, 1 - core)):
                into[:, pl.ds(pl.multiple_of(b * 128, 128), 128)] = source[:, pl.ds(pl.multiple_of((2 * b + k) * 128, 128), 128)]
            return c

        lax.fori_loop(0, W // 128, body, 0)

    def swap(n, source, into):
        return pltpu.make_async_remote_copy(
            src_ref=source, dst_ref=into, send_sem=c_send.at[n], recv_sem=c_recv.at[n],
            device_id={"dp": me + 1 - 2 * core}, device_id_type=MESH)

    halves(normed_ref, n_own_ref, n_send)
    first = swap(0, n_send, n_other_ref)
    first.start()
    CH = 512
    wide = range(0, inner_ref.shape[1], CH)
    weights[0].wait()
    for c in wide:
        inner_ref[:, c : c + CH] = jnp.dot(normed_ref[...], w_s[:, c : c + CH], preferred_element_type=F32)
    weights[1].start()
    for c in range(1, chunks):
        forward(1, c)
        if c + 1 < chunks:
            launch(1, c + 1)

    def conv(i, c):
        ln = pl.ds(pl.multiple_of(i * 128, 128), 128)
        x = inner_ref[:, ln]
        mixed = cb_ref[:, ln] + cw_ref[taps - 1 : taps, ln] * x
        for s in range(1, taps):
            mixed = mixed + cw_ref[taps - 1 - s : taps - s, ln] * (pltpu.roll(x, s, 0) * mask_ref[s - 1])
        value = mixed * jax.nn.sigmoid(mixed)
        conv_ref[:, ln] = value
        low_ref[:, ln] = value.astype(BF16)
        return c

    lax.fori_loop(0, inner_ref.shape[1] // 128, conv, 0)
    p_own[...] = jnp.dot(low_ref[...], xp_ref[...], preferred_element_type=F32)
    share = pltpu.make_async_remote_copy(src_ref=p_own, dst_ref=p_got, send_sem=p_send, recv_sem=p_recv,
                                         device_id={"tensor": 1 - ten}, device_id_type=MESH)
    share.start()
    weights[1].wait()
    for c in wide:
        z_ref[:, c : c + CH] = jnp.dot(normed_ref[...], w_s[:, c : c + CH], preferred_element_type=F32)
    weights[2].start()
    for c in range(chunks):
        settle(1, c, got, dy_ref, start)
    for c in range(chunks):
        for p in range(count):
            over(1, c, p).wait_recv()
        settle(1, c, across, dy_ref, away)
    halves(dy_ref, d_own_ref, d_send)
    second = swap(1, d_send, d_other_ref)
    second.start()
    weights[2].wait()
    for c in wide:
        dg_ref[:, c : c + CH] = lax.dot_general(dy_ref[...], w_s[c : c + CH, :], NT, preferred_element_type=F32)
    share.wait_recv()
    rank = rank_ref.shape[1]
    state = keys_ref.shape[1] // 2

    def whole(i, c):
        at = pl.ds(pl.multiple_of(i * 32, 32), 32)
        total = p_own[at, :] + p_got[at, :]
        rank_ref[at, :] = total[:, :rank].astype(BF16)
        keys_ref[at, :] = total[:, rank:]
        keys = total[:, rank : rank + state]
        ksq_ref[at, :] = jnp.broadcast_to(jnp.sum(keys * keys, axis=1, keepdims=True), (32, 128))
        return c

    lax.fori_loop(0, T // 32, whole, 0)
    share.wait_send()
    for copy in (first, second):
        copy.wait_recv()
        copy.wait_send()
    for n, c in order:
        for p in range(count):
            over(n, c, p).wait_send()
            if p:
                out(n, c, p).wait_send()


def head_call(tokens, cotangent, w_x, w_z, w_out, gain, deal_t, settle, masks, conv_weight, conv_bias, x_proj, rank, chunks=2):
    T, D = tokens.shape
    W = D // 2
    count = lax.axis_size("dp")
    S = jax.ShapeDtypeStruct
    V, DMA = pltpu.VMEM, pltpu.SemaphoreType.DMA
    outs = (S((T, W), BF16), S((T, D), BF16), S((T, D), BF16), S((T, 128), F32)) + (S((T, W), BF16),) * 4
    C = w_x.shape[1]
    outs += (S((T, C), F32), S((T, C), F32), S((T, C), BF16), S((T, x_proj.shape[1] - rank), F32),
             S((T, C), F32), S((T, C), F32), S((T, rank), BF16), S((T, 128), F32))
    block = V((2, chunks, count, T // count, W // chunks), BF16)
    vmem = pl.BlockSpec(memory_space=pltpu.VMEM)
    return pl.pallas_call(
        functools.partial(head_kernel, conv_weight.shape[0]),
        out_shape=outs,
        in_specs=[pl.BlockSpec(memory_space=pl.ANY)] * 5 + [vmem] * 7,
        out_specs=[vmem] * len(outs),
        scratch_shapes=[V((2, T, W), BF16), block, block, block, V((T, W), BF16), V((T, W), BF16), V(w_x.shape, BF16),
                        V((T, x_proj.shape[1]), F32), V((T, x_proj.shape[1]), F32), DMA((2,)), DMA((3,)), DMA, DMA] + [DMA((2, chunks, count))] * 4 + [ DMA((2,)), DMA((2,))],
        compiler_params=pltpu.CompilerParams(collective_id=3, has_side_effects=True, vmem_limit_bytes=58 << 20),
        cost_estimate=pl.CostEstimate(flops=T * T * D * 4, bytes_accessed=48 << 20, transcendentals=0),
        name="head",
    )(tokens, cotangent, w_x, w_z, w_out, gain, deal_t, settle, masks, conv_weight, conv_bias, x_proj)


def mid_kernel(taps, halves, count_steps, *refs):
    (dproj_ref, mask_ref, own_ref, other_ref, x_ref, wx_ref, wz_ref, xp_ref, cw_ref, cb_ref) = refs[:10]
    du_refs, dz_refs = refs[10:10 + halves], refs[10 + halves:10 + 2 * halves]
    (mixed_ref, gout_ref, gz_ref, small_ref, dn_ref, gx_ref, sum_ref, gcw_ref, gcb_ref, mgot_ref, cout_ref, cz_ref,
     acc, dconv, dix, sib, sends, recvs, core_send, core_recv, *scratch) = refs[10 + 2 * halves:]
    j, steps = pl.program_id(0), pl.num_programs(0)
    me, ten = lax.axis_index("dp"), lax.axis_index("tensor")
    T, CH = x_ref.shape
    W = mgot_ref.shape[1]
    bit = {name: me // stride % 2 for name, stride in STRIDE.items()}
    peer = {name: me + stride * (1 - 2 * bit[name]) for name, stride in STRIDE.items()}
    per = steps // halves
    s_acc, s_half, s_got, s_out, s_send, s_recv, s_load = scratch[7:]
    total = Total(s_acc, s_half, s_got, s_out, (s_send, s_recv))
    scratch = scratch[:7]
    pieces = [piece_of(0, gout_ref, "y", scratch, cout_ref), piece_of(1, gz_ref, "near", scratch, cz_ref)]

    def swap():
        far = pl.ds(pl.multiple_of((1 - ten) * W, 128), W)
        return pltpu.make_async_remote_copy(src_ref=mixed_ref.at[:, far], dst_ref=mgot_ref, send_sem=sends, recv_sem=recvs,
                                            device_id={"tensor": 1 - ten}, device_id_type=MESH)

    def small(*at):
        return [functools.partial(total.step, i) for i in at]

    final = count_steps - 1
    program = {
        (0, "start"): small(0) + [pieces[0].step1, pieces[1].step1],
        (0, "dots"): small(1),
        (1, "end"): small(2),
        (2, "dots"): [pieces[0].step2, pieces[1].step2],
        (2, "end"): small(3),
        (3, "end"): small(4) + [pieces[0].stop, pieces[1].stop],
    }

    def point(place):
        for (step, at), actions in program.items():
            if at == place:
                @pl.when(j == min(step, final))
                def _(actions=actions):
                    for act in actions:
                        act()

    @pl.when(j == 0)
    def _():
        loads = [pltpu.make_async_copy(small_ref.at[:, b * 128:(b + 1) * 128], s_acc.at[sixteenth(b)], s_load.at[b])
                 for b in range(16)]
        for copy in loads:
            copy.start()
        barrier = pltpu.get_barrier_semaphore()
        count = greet_dp([peer["core"]] + [total.flip(q)[1] for q in range(1, 8)])
        pl.semaphore_signal(barrier, inc=1, device_id={"tensor": 1 - ten}, device_id_type=MESH)
        pl.semaphore_wait(barrier, count + 1)
        swap().start()
        acc[...] = jnp.zeros_like(acc)
        for copy in loads:
            copy.wait()

    point("start")

    dconv[...] = lax.dot_general(dproj_ref[...], xp_ref[...], NT, preferred_element_type=F32)
    for h in range(halves):
        @pl.when(j // per == h)
        def _(h=h):
            acc[...] += lax.dot_general(dz_refs[h][...], wz_ref[...], NT, preferred_element_type=F32)
            dconv[...] += du_refs[h][...]

    point("dots")

    def conv(i, c):
        ln = pl.ds(pl.multiple_of(i * 128, 128), 128)
        weight = [cw_ref[taps - 1 - s:taps - s, ln] for s in range(taps)]
        x = x_ref[:, ln]
        mixed = cb_ref[:, ln] + weight[0] * x
        for s in range(1, taps):
            mixed = mixed + weight[s] * (pltpu.roll(x, s, 0) * mask_ref[s - 1])
        gate = jax.nn.sigmoid(mixed)
        d = dconv[:, ln] * (gate * (1.0 + mixed * (1.0 - gate)))
        gcb_ref[:, ln] = jnp.sum(d, axis=0, keepdims=True)
        gcw_ref[taps - 1:taps, ln] = jnp.sum(d * x, axis=0, keepdims=True)
        back = weight[0] * d
        for s in range(1, taps):
            masked = d * mask_ref[s - 1]
            gcw_ref[taps - 1 - s:taps - s, ln] = jnp.sum(masked * pltpu.roll(x, s, 0), axis=0, keepdims=True)
            back = back + weight[s] * pltpu.roll(masked, T - s, 0)
        dix[j, :, ln] = back.astype(BF16)
        return c

    lax.fori_loop(0, CH // 128, conv, 0)
    over = pltpu.make_async_remote_copy(src_ref=dix.at[j], dst_ref=sib.at[j], send_sem=core_send.at[j],
                                        recv_sem=core_recv.at[j], device_id={"dp": peer["core"]}, device_id_type=MESH)
    over.start()
    acc[...] += lax.dot_general(dix[j], wx_ref[...], NT, preferred_element_type=F32)
    rows = (((0,), (0,)), ((), ()))
    over.wait_recv()
    gx_ref[...] = (lax.dot_general(own_ref[...], dix[j], rows, preferred_element_type=F32)
                   + lax.dot_general(other_ref[...], sib[j], rows, preferred_element_type=F32)).astype(BF16)
    over.wait_send()

    point("end")

    @pl.when(j == steps - 1)
    def _():
        for b in range(16):
            sum_ref[:, b * 128:(b + 1) * 128] = s_out[sixteenth(b)].astype(F32)
        dn_ref[...] = acc[...].astype(BF16)
        swap().wait_recv()
        swap().wait_send()


def mid_call(dproj, masks, own, other, inner_x, w_x, w_z, x_proj, conv_weight, conv_bias, du, dz, mixed, gout, gz, small, CH=512):
    T, C = inner_x.shape
    D = w_x.shape[0]
    W = mixed.shape[1] // 2
    halves = len(du)
    taps = conv_weight.shape[0]
    steps = C // CH
    per = steps // halves
    S = jax.ShapeDtypeStruct
    V, DMA = pltpu.VMEM, pltpu.SemaphoreType.DMA
    const = lambda a: pl.BlockSpec(a.shape, lambda j: (0,) * a.ndim, pipeline_mode=pl.Buffered(1))
    col = lambda a: pl.BlockSpec((a.shape[0], CH), lambda j: (0, j))
    row = lambda a: pl.BlockSpec((CH, a.shape[1]), lambda j: (j, 0))
    part = lambda h: pl.BlockSpec((T, CH), lambda j: (0, jnp.clip(j - h * per, 0, per - 1)))
    anyspace = pl.BlockSpec(memory_space=pl.ANY)
    outs = (S((T, D), BF16), S((own.shape[1], C), BF16), S(small.shape, F32), S((taps, C), F32), S((1, C), F32),
            S((T, W), BF16),
            S((2,) + gout.shape[3:], BF16), S((2,) + gz.shape[3:], BF16))
    return pl.pallas_call(
        functools.partial(mid_kernel, taps, halves, steps),
        grid=(steps,),
        in_specs=[const(dproj), const(masks), const(own), const(other), col(inner_x), col(w_x), col(w_z), row(x_proj),
                  col(conv_weight), col(conv_bias)] + [part(h) for h in range(halves)] * 2 + [anyspace] * 4,
        out_specs=[pl.BlockSpec((T, D), lambda j: (0, 0)), col(outs[1]), pl.BlockSpec(small.shape, lambda j: (0, 0)), col(outs[3]), col(outs[4])] + [anyspace]
        + [pl.BlockSpec(o.shape, lambda j: (0, 0, 0)) for o in outs[6:]],
        out_shape=outs,
        scratch_shapes=[V((T, D), F32), V((T, CH), F32), V((steps, T, CH), BF16),
                        V((steps, T, CH), BF16), DMA, DMA, DMA((steps,)), DMA((steps,)),
                        *piece_scratch(2, *gout.shape[3:]), *total_scratch(small.shape[0])],
        compiler_params=pltpu.CompilerParams(collective_id=4, has_side_effects=True, vmem_limit_bytes=58 << 20,
                                             dimension_semantics=("arbitrary",)),
        cost_estimate=pl.CostEstimate(flops=6 * T * D * C, bytes_accessed=40 << 20, transcendentals=0),
        name="mid",
    )(dproj, masks, own, other, inner_x, w_x, w_z, x_proj, conv_weight, conv_bias, *du, *dz, mixed, gout, gz, small)


NT = (((1,), (1,)), ((), ()))
PR = 64


def scan_kernel(GR, NS, hosted, *refs):
    if not hosted:
        return scan_body(GR, NS, lambda at: None, None, *refs)
    ins, outs = 14, 10
    refs = list(refs)
    begin = [refs.pop(ins) for _ in range(4)]
    g_refs = [refs.pop(ins), refs.pop(ins)]
    r_refs = [refs.pop(ins + outs), refs.pop(ins + outs)]
    scratch, refs = refs[-7:], refs[:-7]
    pieces = [piece_of(0, g_refs[0], "y", scratch, r_refs[0]), piece_of(1, g_refs[1], "near", scratch, r_refs[1])]
    steps = pl.num_programs(0)
    plan = {(0, "start"): 0, (0, "end"): 1, (1, "end"): 2}

    def host(at):
        for (step, place), stage in plan.items():
            if place != at:
                continue

            @pl.when(pl.program_id(0) == step)
            def _(stage=stage):
                if stage == 0:
                    me = lax.axis_index("dp")
                    peers = [me + STRIDE[n] * (1 - 2 * (me // STRIDE[n] % 2)) for n in ("y", "near", "far")]
                    pl.semaphore_wait(pltpu.get_barrier_semaphore(), greet_dp(peers))
                for piece in pieces:
                    (piece.step1, piece.step2, piece.stop)[stage]()

    return scan_body(GR, NS, host, begin, *refs)


def scan_body(GR, NS, host, begin, rank_ref, dtp_ref, dtb_ref, u_ref, z_ref, dg_ref, skip_ref,
                kb_ref, qb_ref, keep_ref, ksq_ref, qblk_ref, kblk_ref, k2blk_ref,
                gated_ref, diz_ref, du_ref, gskip_ref, gdtb_ref, gdtp_ref,
                drank_ref, sst_ref, dk_ref, dq_ref,
                den_s, step_s, su_s, ds_s, sz_s, y_s, d_s, e_s, h0_s, h1_s, ga_s, gb_s, ma_s, mb_s, dk_s, dq_s):
    T, CH = u_ref.shape
    L = CH // 128
    NG = T // GR
    R = GR * NS
    first, last = pl.program_id(0) == 0, pl.program_id(0) == pl.num_programs(0) - 1
    lanes = [slice(l * 128, (l + 1) * 128) for l in range(L)]
    hist = (h0_s, h1_s)

    @pl.when(first)
    def _():
        for r in (dk_s, dq_s) + ((drank_ref, sst_ref) if begin is None else ()):
            r[...] = jnp.zeros_like(r)
        if begin is not None:
            drank_ref[...] = begin[0][...]
            sst_ref[...] = begin[1][...]
        h1_s[pl.ds(0, R), :] = jnp.zeros((R, CH), BF16)
        gb_s[...] = jnp.zeros_like(gb_s)
        mb_s[...] = jnp.zeros_like(mb_s)

    host("start")
    y_s[...] = jnp.dot(rank_ref[...], dtp_ref[...], preferred_element_type=F32)

    def prologue(r, acc):
        rows = pl.ds(pl.multiple_of(r * PR, PR), PR)
        kq = ksq_ref[rows, :]
        out = []
        for l in range(L):
            ln = lanes[l]
            beta = jax.nn.sigmoid(y_s[rows, ln] + dtb_ref[:, ln])
            den = 1.0 / (1.0 + beta * kq)
            step = beta * den
            den_s[rows, ln] = den
            step_s[rows, ln] = step
            u = u_ref[rows, ln]
            su_s[rows, ln] = step * u
            z = z_ref[rows, ln]
            s = jax.nn.sigmoid(z)
            sz_s[rows, ln] = s
            ds = dg_ref[rows, ln] * (z * s)
            ds_s[rows, ln] = ds
            out.append(acc[l] + jnp.sum(ds * u, axis=0, keepdims=True))
        return tuple(out)

    zrow = tuple(jnp.zeros((1, 128), F32) for _ in range(L))
    gsk = lax.fori_loop(0, T // PR, prologue, zrow)
    for l in range(L):
        gskip_ref[:, lanes[l]] = gsk[l]

    def rows_of(gi):
        return pl.ds(pl.multiple_of(gi * GR, GR), GR)

    def fill(gi, half, h, dst):
        h = list(h)
        base = pl.multiple_of(gi * GR, GR)
        rows = rows_of(gi)
        hb = pl.multiple_of(half * R, R)
        for j in range(GR):
            k = kb_ref[pl.ds(base * NS + j * NS, NS), :]
            kp = keep_ref.at[rows][j:j + 1, :]
            k2 = k * k * kp
            for l in range(L):
                a = kp - k2 * step_s.at[rows][j:j + 1, lanes[l]]
                h[l] = a * h[l] + k * su_s.at[rows][j:j + 1, lanes[l]]
                dst[pl.ds(hb + j * NS, NS), lanes[l]] = h[l].astype(BF16)
        return tuple(h)

    def read(gi, half, src):
        y_s[rows_of(gi), :] = jnp.dot(qblk_ref[rows_of(gi), :], src[pl.ds(pl.multiple_of(half * R, R), R), :],
                                      preferred_element_type=F32)

    def forward(i, h):
        before = jnp.maximum(i - 1, 0)
        read(2 * before + 1, before, h1_s)
        h = fill(2 * i, i, h, h0_s)
        read(2 * i, i, h0_s)
        return fill(2 * i + 1, i, h, h1_s)

    zst = tuple(jnp.zeros((NS, 128), F32) for _ in range(L))
    lax.fori_loop(0, NG // 2, forward, zst)
    read(NG - 1, NG // 2 - 1, h1_s)

    host("middle")

    def middle(r, c):
        rows = pl.ds(pl.multiple_of(r * PR, PR), PR)
        for l in range(L):
            ln = lanes[l]
            z = z_ref[rows, ln]
            s = sz_s[rows, ln]
            v = y_s[rows, ln] + skip_ref[:, ln] * u_ref[rows, ln]
            gated_ref[rows, ln] = (v * (z * s)).astype(BF16)
            diz_ref[rows, ln] = (dg_ref[rows, ln] * v * s * (1.0 + z * (1.0 - s))).astype(BF16)
        return c

    lax.fori_loop(0, T // PR, middle, 0)

    def back(gi, half, gc, own, before, before_at, g_dst, m_dst):
        gc = list(gc)
        base = pl.multiple_of(gi * GR, GR)
        rows = rows_of(gi)
        hb = pl.multiple_of(half * R, R)
        nows = [own[pl.ds(hb + (GR - 1) * NS, NS), ln] for ln in lanes]
        for j in reversed(range(GR)):
            at = pl.ds(base * NS + j * NS, NS)
            k = kb_ref[at, :]
            q = qb_ref[at, :]
            kp = keep_ref.at[rows][j:j + 1, :]
            k2 = k * k * kp
            a_sum = b_sum = q_sum = None
            for l in range(L):
                ln = lanes[l]
                ds = ds_s.at[rows][j:j + 1, ln]
                g = gc[l] + q * ds
                gb = g.astype(BF16)
                step = step_s.at[rows][j:j + 1, ln]
                now = nows[l]
                if j:
                    prev = own[pl.ds(hb + (j - 1) * NS, NS), ln]
                else:
                    prev = before[pl.ds(before_at + (GR - 1) * NS, NS), ln]
                nows[l] = prev
                m = gb * prev
                g_dst[j * NS:(j + 1) * NS, ln] = gb
                m_dst[j * NS:(j + 1) * NS, ln] = m
                wide = lambda v: jnp.broadcast_to(v, (NS, 128)).astype(BF16)
                pa = gb * wide(su_s.at[rows][j:j + 1, ln])
                pb = m * wide(step)
                pq = now * wide(ds)
                a_sum = pa if a_sum is None else a_sum + pa
                b_sum = pb if b_sum is None else b_sum + pb
                q_sum = pq if q_sum is None else q_sum + pq
                gc[l] = (kp - k2 * step) * g
            dk_s[at, :] += a_sum.astype(F32) - (2.0 * k * kp) * b_sum.astype(F32)
            dq_s[at, :] += q_sum.astype(F32)
        return tuple(gc)

    def sums(gi, g_src, m_src):
        rows = rows_of(gi)
        d_s[rows, :] = jnp.dot(kblk_ref[rows, :], g_src[...], preferred_element_type=F32)
        e_s[rows, :] = jnp.dot(k2blk_ref[rows, :], m_src[...], preferred_element_type=F32)

    def backward(i, gc):
        half = NG // 2 - 1 - i
        hi, lo = 2 * half + 1, 2 * half
        sums(jnp.minimum(hi + 1, NG - 1), gb_s, mb_s)
        gc = back(hi, half, gc, h1_s, h0_s, pl.multiple_of(half * R, R), ga_s, ma_s)
        sums(hi, ga_s, ma_s)
        return back(lo, half, gc, h0_s, h1_s, pl.multiple_of(jnp.maximum(half - 1, 0) * R, R), gb_s, mb_s)

    lax.fori_loop(0, NG // 2, backward, zst)
    sums(0, gb_s, mb_s)

    def epilogue(r, acc):
        rows = pl.ds(pl.multiple_of(r * PR, PR), PR)
        kp = keep_ref[rows, :]
        out = []
        ss = sst_ref[rows, :]
        for l in range(L):
            ln = lanes[l]
            step = step_s[rows, ln]
            dsum = d_s[rows, ln]
            dstep = u_ref[rows, ln] * dsum - kp * e_s[rows, ln]
            du_ref[rows, ln] = step * dsum + ds_s[rows, ln] * skip_ref[:, ln]
            t = dstep * step
            ss = ss + t * step
            db = t * (den_s[rows, ln] - step)
            y_s[rows, ln] = db
            out.append(acc[l] + jnp.sum(db, axis=0, keepdims=True))
        sst_ref[rows, :] = ss
        return tuple(out)

    gdb = lax.fori_loop(0, T // PR, epilogue, zrow)
    for l in range(L):
        gdtb_ref[:, lanes[l]] = gdb[l]
    dbl = y_s[...].astype(BF16)
    gdtp_ref[...] = lax.dot_general(rank_ref[...], dbl, (((0,), (0,)), ((), ())), preferred_element_type=F32)
    drank_ref[...] += lax.dot_general(dbl, dtp_ref[...], NT, preferred_element_type=F32)

    host("end")

    @pl.when(last)
    def _():
        ones = jnp.ones((8, 128), BF16)
        for n, (src, dst) in enumerate(((dk_s, dk_ref), (dq_s, dq_ref))):
            for c in range(0, T * NS, 1024):
                part = lax.dot_general(ones, src[c:c + 1024, :].astype(BF16), NT, preferred_element_type=F32)
                dst[:, c:c + 1024] = part if begin is None else part + begin[2 + n][:, c:c + 1024]


def scan_call(piece, pieces, begin, hosted, *args, CH=512, GR=16, NS=16):
    rank, dtp, dtb, u, z, dg, skip, kb, qb, keep, ksq, qblk, kblk, k2blk = args
    T, C = u.shape
    width = C // pieces
    CH = min(CH, width)
    first = piece * (width // CH)
    const = lambda a: pl.BlockSpec(a.shape, lambda j: (0,) * a.ndim, pipeline_mode=pl.Buffered(1))
    oconst = lambda a: pl.BlockSpec(a.shape, lambda j: (0,) * a.ndim)
    col = lambda a: pl.BlockSpec((a.shape[0], CH), lambda j: (0, j + first))
    out = lambda a: pl.BlockSpec((a.shape[0], CH), lambda j: (0, j))
    S = jax.ShapeDtypeStruct
    W = GR * NS
    R = rank.shape[1]
    outs = (S((T, width), BF16), S((T, width), BF16), S((T, width), F32), S((1, width), F32), S((1, width), F32), S((R, width), F32),
            S((T, R), F32), S((T, 128), F32), S((8, T * NS), F32), S((8, T * NS), F32))
    outs += tuple(S((2,) + g.shape[3:], BF16) for g in hosted)
    V = pltpu.VMEM
    f = pl.pallas_call(
        functools.partial(scan_kernel, GR, NS, bool(hosted)),
        grid=(width // CH,),
        in_specs=[const(rank), col(dtp), col(dtb), col(u), col(z), col(dg), col(skip), const(kb), const(qb),
                  const(keep), const(ksq), const(qblk), const(kblk), const(k2blk)] + [const(v) for v in begin] + [pl.BlockSpec(memory_space=pl.ANY)] * len(hosted),
        out_specs=[out(o) for o in outs[:6]] + [oconst(o) for o in outs[6:]],
        out_shape=outs,
        scratch_shapes=[V((T, CH), F32)] * 8 + [V((T * NS // 2, CH), BF16)] * 2 + [V((W, CH), BF16)] * 4 + [V((T * NS, 128), F32)] * 2
        + (piece_scratch(2, *hosted[0].shape[3:]) if hosted else []),
        compiler_params=pltpu.CompilerParams(vmem_limit_bytes=60 << 20, dimension_semantics=("arbitrary",),
                                             **(dict(collective_id=2, has_side_effects=True) if hosted else {})),
        cost_estimate=pl.CostEstimate(flops=T * width * NS * 800, bytes_accessed=T * width * 20, transcendentals=0),
        name="scan_reduce" if hosted else "scan",
    )
    return f(*args, *begin, *hosted)


def scan_all(rank, dtp, dtb, u, z, dg, skip, keys, query, keep, pieces, ksqb=None, GR=16, **kw):
    T, NS = keys.shape
    kb = jnp.broadcast_to(keys[:, :, None], (T, NS, 128)).reshape(T * NS, 128)
    qb = jnp.broadcast_to(query[:, :, None], (T, NS, 128)).reshape(T * NS, 128)
    keepb = jnp.broadcast_to(keep[:, None], (T, 128))
    if ksqb is None:
        ksqb = jnp.broadcast_to(jnp.sum(keys * keys, axis=1)[:, None], (T, 128))
    slot = (jnp.arange(T)[:, None] % GR == jnp.arange(GR * NS)[None, :] // NS).astype(F32)
    blk = lambda v: (slot * jnp.tile(v, (1, GR))).astype(BF16)
    qblk, kblk, k2blk = blk(query), blk(keys), blk(keys * keys)

    def run(piece, begin=(), hosted=()):
        o = scan_call(piece, pieces, begin, hosted, rank, dtp, dtb, u, z, dg, skip, kb, qb, keepb, ksqb, qblk, kblk, k2blk, GR=GR, NS=NS, **kw)
        return o[:6], o[6:10], o[10:]

    def finish(drank, sst, dk, dq):
        dq = dq[0].reshape(T, NS)
        dk = dk[0].reshape(T, NS) - 2.0 * keys * jnp.sum(sst, axis=1, keepdims=True)
        return jnp.concatenate([drank, dk, dq], axis=1)

    return run, finish


def tensor_other(value):
    return lax.ppermute(value, "tensor", [(0, 1), (1, 0)])


def tensor_total(value):
    if lax.axis_size("tensor") == 2:
        return value + tensor_other(value)
    return lax.psum(value, "tensor")


def half_total(value, me, width):
    if lax.axis_size("tensor") == 2:
        own = lax.dynamic_slice_in_dim(value, me * width, width, 1)
        sent = lax.dynamic_slice_in_dim(value, (1 - me) * width, width, 1).astype(BF16)
        return own + tensor_other(sent).astype(F32)
    return lax.psum_scatter(value, "tensor", scatter_dimension=1, tiled=True)


def full_columns(part, me):
    if lax.axis_size("tensor") == 2:
        other = tensor_other(part)
        return jnp.where(
            me == 0,
            jnp.concatenate([part, other], 1),
            jnp.concatenate([other, part], 1),
        )
    return lax.all_gather(part, "tensor", axis=1, tiled=True)


def pair_up(value, stride):
    count = lax.axis_size("dp")
    return lax.ppermute(value, "dp", [(i, i ^ stride) for i in range(count)])


def pair_gradient(own, other, right):
    return (contract_rows(own, right) + contract_rows(other, pair_up(right, 1))).astype(BF16)


def after(value, *earlier):
    return lax.optimization_barrier((value,) + earlier)[0]


def flatten(values):
    return jnp.concatenate([v.reshape(-1) for v in values])


def cut(flat, values):
    out, at = [], 0
    for v in values:
        out.append(flat[at : at + v.size].reshape(v.shape))
        at += v.size
    return out


def position_in(keys):
    return jnp.sum((keys[None, :] < keys[:, None]).astype(jnp.int32), axis=1)


def conv_mix(inner_x, conv_weight, conv_bias, segment):
    row_count = inner_x.shape[0]
    taps = conv_weight.shape[0]
    mixed = conv_bias[None, :] + conv_weight[taps - 1][None, :] * inner_x
    for shift_by in range(1, taps):
        moved = jnp.concatenate([jnp.zeros((shift_by, inner_x.shape[1]), F32), inner_x[: row_count - shift_by]], 0)
        seg_moved = jnp.concatenate([jnp.full((shift_by,), -1, jnp.int32), segment[: row_count - shift_by]], 0)
        keep_mask = (seg_moved == segment).astype(F32)
        mixed = mixed + conv_weight[taps - 1 - shift_by][None, :] * moved * keep_mask[:, None]
    return mixed


def silu_conv(inner_x, conv_weight, conv_bias, segment):
    mixed = conv_mix(inner_x, conv_weight, conv_bias, segment)
    return mixed * jax.nn.sigmoid(mixed)


def contract_rows(left, right):
    return lax.dot_general(left, right, (((0,), (0,)), ((), ())), preferred_element_type=F32)


def contract_cols(left, right):
    return lax.dot_general(left, right, (((1,), (1,)), ((), ())), preferred_element_type=F32)


def body(tokens, cotangent, norm_gain, w_x, w_z, conv_weight, conv_bias, x_proj, dt_proj, dt_bias, skip_gain, w_out,
         seq_lengths, arrival_route, work_source):
    dp_count = lax.axis_size("dp")
    tp_count = lax.axis_size("tensor")
    row_count, feat_width = tokens.shape
    per_peer = row_count // dp_count
    col_share = feat_width // tp_count
    me = lax.axis_index("tensor")
    col_start = me * col_share
    low_rank = dt_proj.shape[0]
    state_size = (x_proj.shape[1] - low_rank) // 2
    position = jnp.arange(row_count, dtype=jnp.int32)

    deal = (position_in(arrival_route)[:, None] == position[None, :]).astype(BF16)
    settle = (position_in(work_source // row_count * row_count + position)[:, None] == position[None, :]).astype(BF16)

    def exchange(rows):
        out = lax.all_to_all(rows.reshape(dp_count, per_peer, rows.shape[1]), "dp", split_axis=0, concat_axis=0, tiled=True)
        return out.reshape(row_count, rows.shape[1])

    def pick(table, rows, dim):
        return lax.dot_general(table, rows, (((dim,), (0,)), ((), ())), preferred_element_type=F32).astype(BF16)

    def bring(values):
        part = lax.dynamic_slice_in_dim(values, col_start, col_share, 1)
        return full_columns(pick(settle, exchange(pick(deal, part, 0)), 1), me)

    def give_back(values):
        return pick(deal, exchange(pick(settle, values, 0)), 1)

    lengths = seq_lengths[0]
    count = lengths.shape[0]
    before = jnp.arange(count)[:, None] > jnp.arange(count)[None, :]
    offsets = jnp.sum(jnp.where(before, lengths[None, :], 0), axis=1)
    segment = jnp.sum((position[:, None] >= offsets[None, :]).astype(jnp.int32), axis=1) - 1
    keep = 1.0 - jnp.any(position[:, None] == offsets[None, :], axis=1).astype(F32)

    paired = dp_count == 16 and tp_count == 2
    if paired:
        taps = conv_weight.shape[0]
        pre = [jnp.concatenate([jnp.full((s,), -1, jnp.int32), segment[: row_count - s]]) for s in range(1, taps)]
        masks = jnp.stack([jnp.broadcast_to((p == segment).astype(F32)[:, None], (row_count, 128)) for p in pre])
        (x_half, normed, dy_work, scale_wide, normed_own, normed_other, dy_own, dy_other,
         inner_x, conv_out, conv_low, key_query, inner_z, d_gated, rank_part, key_square) = head_call(
            tokens, cotangent, w_x, w_z, w_out, norm_gain[None, :], deal.T, settle, masks, conv_weight, conv_bias[None, :], x_proj, low_rank)
    else:
        x_work = bring(tokens)
        dy_work = bring(cotangent)
        resid = x_work.astype(F32)
        scale_row = lax.rsqrt(jnp.mean(resid * resid, axis=1, keepdims=True) + 1e-05)
        unit = resid * scale_row
        normed = (unit * norm_gain[None, :]).astype(BF16)
        inner_x = jnp.dot(normed, w_x, preferred_element_type=F32)
        conv_out, conv_pull = jax.vjp(partial(silu_conv, segment=segment), inner_x, conv_weight, conv_bias)
        conv_low = conv_out.astype(BF16)
        projected = tensor_total(jnp.dot(conv_low, x_proj, preferred_element_type=F32))
        inner_z = jnp.dot(normed, w_z, preferred_element_type=F32)
        d_gated = contract_cols(dy_work, w_out)
        rank_part, key_query, key_square = projected[:, :low_rank].astype(BF16), projected[:, low_rank:], None
    key_rows, query_rows = key_query[:, :state_size], key_query[:, state_size:]
    pieces = 2 if paired else 1
    scan, finish = scan_all(rank_part, dt_proj, dt_bias[None, :], conv_out, inner_z, d_gated, skip_gain[None, :], key_rows,
                    query_rows, keep, pieces, key_square)
    first, raw, _ = scan(0)
    scans = [first]
    if paired:
        blocks = lambda g: g.reshape(2, 2, 2, g.shape[0] // 8, g.shape[1])
        outer = lambda part: (blocks(pair_gradient(dy_own, dy_other, part[0])),
                              blocks(pair_gradient(normed_own, normed_other, part[1])))
        second, raw, early = scan(1, raw, outer(first))
        scans.append(second)
    wide = lambda index: jnp.concatenate([part[index] for part in scans], axis=1) if paired else scans[0][index]
    grad_dt_proj = wide(5)
    grad_skip, grad_dt_bias = wide(3)[0], wide(4)[0]
    gated_low, d_inner_z_low = wide(0), wide(1)
    d_proj = finish(*raw)
    mixed = jnp.dot(gated_low, after(w_out, d_proj) if paired else w_out, preferred_element_type=F32)
    d_proj = tensor_total(d_proj)
    if paired:
        mixed = mixed.astype(BF16)
        g_out, g_z = outer(scans[1])
        far = [pair_up(v[1], STRIDE["far"]) for v in early]
        d_proj = after(d_proj, g_out, g_z, mixed)
        d_proj_low = d_proj.astype(BF16)
        rows = (contract_rows(d_proj_low, conv_low), grad_dt_proj, grad_dt_bias[None, :], grad_skip[None, :])
        stack = jnp.concatenate(rows).astype(BF16)
        stack = jnp.pad(stack, ((0, -stack.shape[0] % 16), (0, 0)))
        d_normed, g_x, stack, grad_conv_weight, grad_conv_bias, mixed_other, left_out, left_z = mid_call(
            d_proj_low, masks, normed_own, normed_other, inner_x, w_x, w_z, x_proj, conv_weight,
            conv_bias[None, :], [part[2] for part in scans], [part[1] for part in scans], mixed, g_out, g_z,
            stack)
    else:
        d_proj_low = d_proj.astype(BF16)
        grad_x_proj = contract_rows(conv_low, d_proj_low)
        d_conv_out = scans[0][2] + contract_cols(d_proj_low, x_proj)
        d_inner_x, grad_conv_weight, grad_conv_bias = conv_pull(d_conv_out)
        d_inner_x_low = d_inner_x.astype(BF16)
        d_normed = contract_cols(d_inner_x_low, w_x) + contract_cols(d_inner_z_low, w_z)
    if paired:
        conv = jnp.concatenate([grad_conv_weight, grad_conv_bias])
        conv = jnp.pad(conv, ((0, 8 - conv.shape[0]), (0, 0)))
        out_tokens, in_grad, grad_gain, conv, grad_w_out, grad_w_z, grad_w_x = tail_call(
            left_out, left_z, early, [after(v, d_normed) for v in far], blocks(g_x), d_normed, mixed, mixed_other, x_half, dy_work, conv, norm_gain[None, :],
            scale_wide, settle.T, deal)
        split = x_proj.shape[1]
        grad_x_proj, grad_dt_proj = stack[:split].T, stack[split : split + low_rank]
        grad_dt_bias, grad_skip = stack[split + low_rank], stack[split + low_rank + 1]
        grad_conv_weight, grad_conv_bias = conv[:taps], conv[taps]
        grad_gain = grad_gain[0]
    else:
        small = (grad_x_proj, grad_dt_proj, grad_conv_weight, grad_conv_bias, grad_dt_bias, grad_skip)
        unit_cols = lax.dynamic_slice_in_dim(unit, col_start, col_share, 1)
        gain_cols = lax.dynamic_slice_in_dim(norm_gain, col_start, col_share, 0)
        dy_cols = lax.dynamic_slice_in_dim(dy_work, col_start, col_share, 1).astype(F32)
        d_share = half_total(d_normed, me, col_share)
        d_unit_cols = d_share * gain_cols[None, :]
        row_total = tensor_total(jnp.sum(d_unit_cols * unit_cols, axis=1, keepdims=True))
        grad_gain = jnp.sum(d_share * unit_cols, axis=0)
        d_resid = dy_cols + scale_row * (d_unit_cols - unit_cols * (row_total / feat_width))
        mixed_share = half_total(mixed, me, col_share)
        out_cols = (lax.dynamic_slice_in_dim(resid, col_start, col_share, 1) + mixed_share).astype(BF16)
        out_tokens, in_grad = give_back(out_cols), give_back(d_resid.astype(BF16))
        grad_w_out, grad_w_z, grad_w_x = (
            lax.psum_scatter(g.astype(BF16), "dp", scatter_dimension=dim, tiled=True).astype(F32)
            for g, dim in ((contract_rows(gated_low, dy_work), 1), (contract_rows(normed, d_inner_z_low), 0),
                           (contract_rows(normed, d_inner_x_low), 0)))
        small += (grad_gain,)
        (grad_x_proj, grad_dt_proj, grad_conv_weight, grad_conv_bias, grad_dt_bias, grad_skip, grad_gain) = cut(
            lax.psum(flatten(small), "dp"), small)
    return (out_tokens, in_grad, grad_gain, grad_w_x, grad_w_z, grad_conv_weight, grad_conv_bias, grad_x_proj,
            grad_dt_proj, grad_dt_bias, grad_skip, grad_w_out)


def solution(mesh):
    in_specs = (
        P("dp", None),
        P("dp", None),
        P(),
        P(None, "tensor"),
        P(None, "tensor"),
        P(None, "tensor"),
        P("tensor"),
        P("tensor", None),
        P(None, "tensor"),
        P("tensor"),
        P("tensor"),
        P("tensor", None),
        P("dp", None),
        P("dp"),
        P("dp"),
    )
    out_specs = (
        P("dp", "tensor"),
        P("dp", "tensor"),
        P("tensor"),
        P("dp", "tensor"),
        P("dp", "tensor"),
        P(None, "tensor"),
        P("tensor"),
        P("tensor", None),
        P(None, "tensor"),
        P("tensor"),
        P("tensor"),
        P("tensor", "dp"),
    )
    return jax.shard_map(body, mesh=mesh, in_specs=in_specs, out_specs=out_specs, check_vma=False)
```
